32 devices in a mesh: seq: 8 (over z, x), tp: 4 (over y, core).
Axes of the slice: x: 2, y: 2, z: 4, core: 2. Of those that a mesh axis runs over, the one named last changes fastest.
Arguments:
- tokens: bfloat16 [2, 2048, 2048], P(None, 'seq'), may hold values from -6 to 6
- positions: int32 [2, 2048], P(None, 'seq'), may hold values from 0 to 4095
- corpus: int32 [2, 2048], P(None, 'seq'), may hold values from 0 to 7, never falling along the last dimension, each value on 1 to 512 neighbouring positions
- corpus_weight: int32 [8], replicated, may hold values from 1 to 4
- gain_one: float32 [2048], replicated, may hold values from 0.1 to 1.9
- w_query: bfloat16 [2048, 2048], P(None, 'tp'), may hold values from -0.125 to 0.125
- w_key: bfloat16 [2048, 512], P(None, 'tp'), may hold values from -0.125 to 0.125
- w_value: bfloat16 [2048, 512], P(None, 'tp'), may hold values from -0.125 to 0.125
- gain_query: float32 [64], replicated, may hold values from 0.1 to 1.9
- gain_key: float32 [64], replicated, may hold values from 0.1 to 1.9
- w_out: bfloat16 [2048, 2048], P('tp'), may hold values from -2 to 2
- gain_two: float32 [2048], replicated, may hold values from 0.1 to 1.9
- w_gate: bfloat16 [2048, 8192], P(None, 'tp'), may hold values from -0.125 to 0.125
- w_up: bfloat16 [2048, 8192], P(None, 'tp'), may hold values from -0.125 to 0.125
- w_down: bfloat16 [8192, 2048], P('tp'), may hold values from -0.25 to 0.25
- cotangent: bfloat16 [2, 2048, 2048], P(None, 'seq'), may hold values from -6 to 6
Outputs:
- out: bfloat16 [2, 2048, 2048], P(None, 'seq')
- grad_tokens: bfloat16 [2, 2048, 2048], P(None, 'seq')
- grad_gain_one: float32 [2048], P('tp')
- grad_query: float32 [2048, 2048], P(None, 'tp')
- grad_key: float32 [2048, 512], P(None, 'tp')
- grad_value: float32 [2048, 512], P(None, 'tp')
- grad_gain_query: float32 [64], P('tp')
- grad_gain_key: float32 [64], P('tp')
- grad_out: float32 [2048, 2048], P('tp')
- grad_gain_two: float32 [2048], P('tp')
- grad_gate: float32 [2048, 8192], P(None, 'tp')
- grad_up: float32 [2048, 8192], P(None, 'tp')
- grad_down: float32 [8192, 2048], P('tp')
The draws below stay inside these ranges and needn't reach their ends.
Inputs may be any that keep to these rules, and one draw needn't show every extreme that they name: Along each row the corpus never falls, every corpus 0 to 7 occurs in every row, and no corpus covers more than 512 positions of a row.
All inputs are finite; a program needn't handle non-finite values.
Results may differ from the reference program's by a relative error of at most 0.033.
Values may be sent and summed in bfloat16 or wider, within the bound.
A program may use at most 320 MiB of HBM per device.

```python
import math
import jax
import jax.numpy as jnp
import numpy as np
from jax import lax

D = 2048
HQ = 32
KVH = 8
HD = 64
FF = 8192
NCORP = 8
ROWS = 2
L = 2048
MOST = 512
N_TP = 4


def place_ends(result, rng, least, high):
    extent = result.shape
    spot = [jax.random.randint(jax.random.fold_in(rng, axis), (), 0, extent[axis]) for axis in range(len(extent))]
    result = result.at[tuple(spot)].set(least)
    longest = extent.index(max(extent))
    spot[longest] = (spot[longest] + 1) % extent[longest]
    return result.at[tuple(spot)].set(high)


def block_scale(key, dims, split, low, top_value):
    factor_of = 1.0
    for axis_at, blocks in split:
        heights = jax.random.uniform(jax.random.fold_in(jax.random.fold_in(key, 6), axis_at), (blocks,), jnp.float32, low / len(split), top_value / len(split))
        factor_of = factor_of * jnp.repeat(jnp.exp(heights), dims[axis_at] // blocks).reshape((-1,) + (1,) * (len(dims) - 1 - axis_at))
    return factor_of


def profile(count, total, most, slope):
    loads = [(1 << 20) // math.isqrt(standing ** slope) + 1 for standing in range(2, count + 1)]
    rest, given = total - most - (count - 1), [1] * (count - 1)
    while rest > 0:
        candidates = [i for i in range(count - 1) if given[i] < most]
        pool, budget = sum([loads[i] for i in candidates]), rest
        for i in candidates:
            extra = min(most - given[i], max(1, budget * loads[i] // pool), rest)
            given[i] = given[i] + extra
            rest = rest - extra
    return np.array([most] + given)


def uneven(rng, number_of, total, most, lean):
    if number_of == 2:
        one = jax.random.randint(rng, (), max(1, total - most), min(most, total - 1) + 1)
        return jnp.stack([one, total - one])
    lengths = jnp.asarray(profile(number_of, total, most, lean), jnp.int32)
    couples = (number_of - 1) // 2
    donor, sink = lengths[1:1 + 2 * couples:2], lengths[2:2 + 2 * couples:2]
    room = jnp.minimum(donor - 1, most - sink)
    passed = jax.random.randint(jax.random.fold_in(rng, 1), (couples,), 0, 1 << 20) % (room + 1)
    lengths = lengths.at[1:1 + 2 * couples:2].set(donor - passed).at[2:2 + 2 * couples:2].set(sink + passed)
    return lengths[jax.random.permutation(jax.random.fold_in(rng, 2), number_of)]


def normal_values(key, extent, width, bound, pieces=(), kind=jnp.bfloat16):
    level = block_scale(key, extent, pieces, -0.22, 0.18) if pieces else 1.0
    entries = jax.random.normal(key, extent, jnp.float32) * width * level
    return jnp.minimum(jnp.maximum(entries, -bound), bound).astype(kind)


def setup_inputs(seed: int = 0) -> dict:
    arg_keys = jax.random.split(jax.random.key(seed), 17)
    return {
        "tokens": normal_values(arg_keys[0], (ROWS, L, D), 1.0, 6.0, ((1, 8),)),
        "positions": place_ends(jax.random.randint(arg_keys[1], (ROWS, L), 0, 4096), jax.random.fold_in(arg_keys[1], 1), 0, 4095).astype(jnp.int32),
        "corpus": jax.vmap(lambda own: jnp.searchsorted(jnp.cumsum(uneven(own, NCORP, L, MOST, 2)), jnp.arange(L), side="right"))(jax.random.split(arg_keys[2], ROWS)).reshape((ROWS, L)).astype(jnp.int32),
        "corpus_weight": place_ends(jax.random.randint(arg_keys[3], (NCORP,), 1, 5), jax.random.fold_in(arg_keys[3], 1), 1, 4).astype(jnp.int32),
        "gain_one": jnp.clip(1.0 + 0.18 * jax.random.normal(arg_keys[4], (D,), jnp.float32), 0.1, 1.9),
        "w_query": normal_values(arg_keys[5], (D, HQ * HD), D ** -0.5, 0.125, ((1, 4),)),
        "w_key": normal_values(arg_keys[6], (D, KVH * HD), D ** -0.5, 0.125, ((1, 4),)),
        "w_value": normal_values(arg_keys[7], (D, KVH * HD), D ** -0.5, 0.125, ((1, 4),)),
        "gain_query": jnp.clip(1.0 + 0.18 * jax.random.normal(arg_keys[8], (HD,), jnp.float32), 0.1, 1.9),
        "gain_key": jnp.clip(1.0 + 0.18 * jax.random.normal(arg_keys[9], (HD,), jnp.float32), 0.1, 1.9),
        "w_out": normal_values(arg_keys[10], (HQ * HD, D), (max(HQ * HD // 256, 1)) ** -0.5, 2.0, ((0, 4),)),
        "gain_two": jnp.clip(1.0 + 0.18 * jax.random.normal(arg_keys[11], (D,), jnp.float32), 0.1, 1.9),
        "w_gate": normal_values(arg_keys[12], (D, FF), D ** -0.5, 0.125, ((1, 4),)),
        "w_up": normal_values(arg_keys[13], (D, FF), D ** -0.5, 0.125, ((1, 4),)),
        "w_down": normal_values(arg_keys[14], (FF, D), (max(FF // 16, 1)) ** -0.5, 0.25, ((0, 4),)),
        "cotangent": normal_values(arg_keys[15], (ROWS, L, D), 1.0, 6.0, ((1, 8),)),
    }


EPS = 1e-05
EPS_HEAD = 1e-06
ROPE_BASE = 10000.0
PRECISE = lax.Precision.HIGHEST

@jax.custom_vjp
def low(v):
    return lax.optimization_barrier(v.astype(jnp.bfloat16)).astype(jnp.float32)

@jax.custom_vjp
def low_back(v):
    return v

def low_keep(v):
    return (low(v), None)

def low_pass(kept, grad):
    return (grad,)

def back_keep(v):
    return (v, None)

def back_low(kept, grad):
    return (low(grad),)
low.defvjp(low_keep, low_pass)
low_back.defvjp(back_keep, back_low)

def rope_tables(positions):
    half = HD // 2
    rates = ROPE_BASE ** (-jnp.arange(half, dtype=jnp.float32) * 2.0 / HD)
    angle = positions.astype(jnp.float32)[:, None] * rates[None, :]
    return (jnp.cos(angle), jnp.sin(angle))

def rotate(vector, cosine, sine):
    half = vector.shape[-1] // 2
    first = vector[..., :half]
    second = vector[..., half:]
    return jnp.concatenate([first * cosine - second * sine, second * cosine + first * sine], axis=-1)

def norm(vector, gain, epsilon):
    inverse = lax.rsqrt(lax.optimization_barrier(jnp.mean(vector * vector, axis=-1, keepdims=True)) + epsilon)
    return vector * inverse * gain

def layer_row(params, inputs):
    gain_one, w_query, w_key, w_value, gain_query, gain_key, w_out, gain_two, w_gate, w_up, w_down = params
    row_tokens, row_positions = inputs
    length = row_tokens.shape[0]
    cosine, sine = rope_tables(row_positions)
    cosine = cosine[:, None, :]
    sine = sine[:, None, :]
    a_one = low(norm(row_tokens, gain_one, EPS))
    query = jnp.dot(a_one, w_query, precision=PRECISE).reshape(length, HQ, HD)
    key = jnp.dot(a_one, w_key, precision=PRECISE).reshape(length, KVH, HD)
    value = jnp.dot(a_one, w_value, precision=PRECISE).reshape(length, KVH, HD)
    query = low(rotate(norm(low_back(query), gain_query, EPS_HEAD), cosine, sine))
    key = low(rotate(norm(low_back(key), gain_key, EPS_HEAD), cosine, sine))
    value = low(low_back(value))
    group = HQ // KVH
    key = jnp.repeat(key, group, axis=1)
    value = jnp.repeat(value, group, axis=1)
    scores = low_back(jnp.einsum('qhd,khd->hqk', query, key, precision=PRECISE) * HD ** (-0.5))
    causal = jnp.arange(length)[:, None] >= jnp.arange(length)[None, :]
    scores = jnp.where(causal[None, :, :], scores, -jnp.inf)
    probs = low(jax.nn.softmax(scores, axis=-1))
    attended = jnp.einsum('hqk,khd->qhd', probs, value, precision=PRECISE)
    attended = low(low_back(attended)).reshape(length, N_TP, HQ * HD // N_TP)
    partial_att = jnp.einsum('lgc,gcd->gld', attended, w_out.reshape(N_TP, HQ * HD // N_TP, D), precision=PRECISE)
    resid = row_tokens + low_back(lax.optimization_barrier(jnp.sum(low(partial_att), axis=0)))
    a_two = low(norm(resid, gain_two, EPS))
    gate = low_back(jnp.dot(a_two, w_gate, precision=PRECISE))
    up = low_back(jnp.dot(a_two, w_up, precision=PRECISE))
    hidden = low(jax.nn.silu(gate) * up).reshape(length, N_TP, FF // N_TP)
    partial_ffn = jnp.einsum('lgf,gfd->gld', hidden, w_down.reshape(N_TP, FF // N_TP, D), precision=PRECISE)
    return resid + low_back(lax.optimization_barrier(jnp.sum(low(partial_ffn), axis=0)))

def reference(tokens, positions, corpus, corpus_weight, gain_one, w_query, w_key, w_value, gain_query, gain_key, w_out, gain_two, w_gate, w_up, w_down, cotangent):
    params = (gain_one.astype(jnp.float32), w_query.astype(jnp.float32), w_key.astype(jnp.float32), w_value.astype(jnp.float32), gain_query.astype(jnp.float32), gain_key.astype(jnp.float32), w_out.astype(jnp.float32), gain_two.astype(jnp.float32), w_gate.astype(jnp.float32), w_up.astype(jnp.float32), w_down.astype(jnp.float32))
    x_all = tokens.astype(jnp.float32)

    def forward(x_in, weights):
        row_fn = jax.checkpoint(lambda inputs: layer_row(weights, inputs))
        return lax.map(row_fn, (x_in, positions))
    out, pullback = jax.vjp(forward, x_all, params)
    onehot = (corpus[..., None] == jnp.arange(NCORP, dtype=jnp.int32)).astype(jnp.float32)
    counts = lax.optimization_barrier(jnp.sum(onehot, axis=(0, 1)))
    weight_scale = corpus_weight.astype(jnp.float32) * (ROWS * L / NCORP) / counts
    token_scale = lax.optimization_barrier(jnp.sum(onehot * weight_scale, axis=-1))
    grad = cotangent.astype(jnp.float32) * token_scale[..., None]
    d_tokens, d_params = pullback(grad)
    g_one, g_query, g_key, g_value, g_gq, g_gk, g_out, g_two, g_gate, g_up, g_down = d_params
    return (out.astype(jnp.bfloat16), d_tokens.astype(jnp.bfloat16), g_one, g_query, g_key, g_value, g_gq, g_gk, g_out, g_two, g_gate, g_up, g_down)
```

```python
import functools

import jax
import jax.numpy as jnp
from jax import lax
from jax.sharding import PartitionSpec as P

HD = 64
NCORP = 8


EPS = 1e-05
EPS_HEAD = 1e-06
ROPE_BASE = 10000.0
BF = jnp.bfloat16
F32 = jnp.float32


def rope_tables(positions):
    half = HD // 2
    rates = ROPE_BASE ** (-jnp.arange(half, dtype=jnp.float32) * 2.0 / HD)
    angle = positions.astype(jnp.float32)[:, None] * rates[None, :]
    return (jnp.cos(angle), jnp.sin(angle))


def rotate(vector, cosine, sine):
    half = vector.shape[-1] // 2
    first = vector[..., :half]
    second = vector[..., half:]
    return jnp.concatenate(
        [first * cosine - second * sine, second * cosine + first * sine], axis=-1
    )


def unrotate(grads, cosine, sine):
    half = grads.shape[-1] // 2
    first = grads[..., :half]
    second = grads[..., half:]
    return jnp.concatenate(
        [first * cosine + second * sine, second * cosine - first * sine], axis=-1
    )


def norm_rows(vector, gain):
    inverse = lax.rsqrt(jnp.mean(vector * vector, axis=-1, keepdims=True) + EPS)
    normed = vector * inverse
    return (normed, inverse, (normed * gain).astype(jnp.bfloat16))


def head_norm(vector, gain):
    inverse = lax.rsqrt(jnp.mean(vector * vector, axis=-1, keepdims=True) + EPS_HEAD)
    normed = vector * inverse
    return (normed, inverse, normed * gain)


def norm_back(d_scaled, normed, inverse, gain):
    scaled = d_scaled * gain
    return inverse * (scaled - normed * jnp.mean(scaled * normed, axis=-1, keepdims=True))


def dot(a, b):
    return jnp.dot(a, b, preferred_element_type=F32)


def dot_tn(a, b):
    return lax.dot_general(a, b, (((0,), (0,)), ((), ())), preferred_element_type=F32)


def dot_nt(a, b):
    return lax.dot_general(a, b, (((1,), (1,)), ((), ())), preferred_element_type=F32)


def take(array, start, size, axis=0):
    return lax.dynamic_slice_in_dim(array, start, size, axis)


class Links:
    def __init__(self):
        self.seq = lax.axis_size("seq")
        self.tp = lax.axis_size("tp")
        self.nodes = self.seq // 2
        self.bits = self.tp.bit_length() - 1
        rank = lax.axis_index("seq")
        self.node = rank // 2
        self.side = rank % 2
        self.t = lax.axis_index("tp")

    def swap_side(self, value):
        return lax.ppermute(value, "seq", [(s, s ^ 1) for s in range(self.seq)])

    def swap_bit(self, value, bit):
        return lax.ppermute(value, "tp", [(r, r ^ (1 << bit)) for r in range(self.tp)])

    def hop(self, value, step, low, high):
        pairs = [(2 * n + d, 2 * (n + step) + d) for n in range(low, high) for d in range(2)]
        return lax.ppermute(value, "seq", pairs)

    def relative(self, rows):
        share = rows.shape[0] // self.tp
        return jnp.concatenate(
            [take(rows, (self.t ^ j) * share, share) for j in range(self.tp)], axis=0
        )

    def scatter_tp(self, blocks):
        held = dict(enumerate(blocks))
        for bit in range(self.bits):
            keep = [j for j in held if not (j >> bit) & 1]
            send = jnp.stack([held[j | (1 << bit)] for j in keep])
            got = self.swap_bit(send, bit)
            last = bit == self.bits - 1
            held = {
                j: (
                    held[j].astype(F32) + got[k].astype(F32)
                    if last
                    else (held[j].astype(F32) + got[k].astype(F32)).astype(BF)
                )
                for k, j in enumerate(keep)
            }
        return held[0]

    def scatter_all(self, part):
        share = part.shape[0] // (2 * self.tp)
        blocks = part.reshape(2, self.tp, share, -1)
        held = {j: blocks[:, j] for j in range(self.tp)}
        for bit in range(self.bits):
            keep = [j for j in held if not (j >> bit) & 1]
            send = jnp.stack([held[j | (1 << bit)] for j in keep])
            got = self.swap_bit(send, bit)
            held = {
                j: (held[j].astype(F32) + got[k].astype(F32)).astype(BF)
                for k, j in enumerate(keep)
            }
        mine = held[0]
        got = self.swap_side(mine[1])
        return mine[0].astype(F32) + got.astype(F32)

    def gather_tp(self, mine):
        held = mine[None]
        for bit in reversed(range(self.bits)):
            got = self.swap_bit(held, bit)
            held = jnp.stack([held, got], axis=1).reshape((-1,) + mine.shape)
        return held

    def gather_all(self, mine):
        top = self.bits - 1
        half = mine.shape[0] // 2
        across = self.swap_side(mine)
        over = self.swap_bit(mine, top)
        far = jnp.concatenate(
            [self.swap_bit(across[:half], top), self.swap_side(over[half:])], axis=0
        )
        held = jnp.stack([jnp.stack([mine, over]), jnp.stack([across, far])])
        for bit in reversed(range(top)):
            got = self.swap_bit(held, bit)
            held = jnp.stack([held, got], axis=2).reshape((2, -1) + mine.shape)
        return held.reshape(-1, mine.shape[-1])

    def natural(self, held):
        return jnp.concatenate(
            [lax.dynamic_index_in_dim(held, self.t ^ r, 0, False) for r in range(self.tp)], axis=0
        )

    def sum_line(self, part):
        count = self.nodes
        size = part.shape[0] // count

        def chunk(index):
            return take(part, jnp.clip(index, 0, count - 1) * size, size)

        up = down = None
        for step in range(1, count):
            send_up = chunk(self.node + count - step)
            send_down = chunk(self.node - count + step)
            if up is not None:
                send_up = (send_up.astype(F32) + up.astype(F32)).astype(BF)
                send_down = (send_down.astype(F32) + down.astype(F32)).astype(BF)
            up = self.hop(send_up, 1, 0, step)
            down = self.hop(send_down, -1, count - step, count)
        own = (chunk(self.node).astype(F32) + up.astype(F32) + down.astype(F32)).astype(BF)
        ups, downs = [own], [own]
        for step in range(1, count):
            ups.append(self.hop(ups[-1], 1, step - 1, count - 1))
            downs.append(self.hop(downs[-1], -1, 1, count - step + 1))
        return [own] + [ups[k] + downs[count - k] for k in range(1, count)]

    def finish(self, pieces, axis):
        count = self.nodes
        size, cols = pieces[0].shape
        shape = (count * size, 2 * cols) if axis == 1 else (2 * count * size, cols)
        result = jnp.zeros(shape, F32)
        for k, piece in enumerate(pieces):
            other = self.swap_side(piece)
            row = ((self.node + count - k) % count) * size
            for data, side in ((piece, self.side), (other, 1 - self.side)):
                where = (row, side * cols) if axis == 1 else (row + side * count * size, 0)
                result = lax.dynamic_update_slice(result, data.astype(F32), where)
        return result


def per_device(
    tokens,
    positions,
    corpus,
    corpus_weight,
    gain_one,
    w_query,
    w_key,
    w_value,
    gain_query,
    gain_key,
    w_out,
    gain_two,
    w_gate,
    w_up,
    w_down,
    cotangent,
):
    net = Links()
    rows, per_row, width = tokens.shape
    count = rows * per_row
    share = count // net.tp
    total_len = per_row * net.seq
    side, node, t = net.side, net.node, net.t
    scale = HD ** (-0.5)
    q_cols = w_query.shape[1] // 2
    shared = (w_key.shape[1] // HD) % 2 == 1
    k_cols = w_key.shape[1] if shared else w_key.shape[1] // 2
    k_grad = w_key.shape[1] // 2
    heads, kv_heads = q_cols // HD, k_cols // HD
    group = heads // kv_heads
    both = 2 * count

    x_rows = tokens.reshape(count, width).astype(F32)
    inverse_one = lax.rsqrt(jnp.mean(x_rows * x_rows, axis=-1, keepdims=True) + EPS)
    a_one = (x_rows * inverse_one * gain_one).astype(BF)

    def halves(w):
        cols = w.shape[1] // 2
        return take(w, side * cols, cols, 1), take(w, (1 - side) * cols, cols, 1)

    wq, wk, wv = halves(w_query), halves(w_key), halves(w_value)
    w_back = jnp.concatenate([wq[0], wk[0], wv[0]], axis=1)
    if shared:
        wk, wv = (w_key, w_key), (w_value, w_value)
    w_own = jnp.concatenate([wq[0], wk[0], wv[0]], axis=1)
    w_other = jnp.concatenate([wq[1], wk[1], wv[1]], axis=1)
    raw_other = net.swap_side(dot(a_one, w_other).astype(BF))
    raw_own = dot(a_one, w_own).astype(BF)
    raw = jnp.concatenate([raw_own, raw_other], axis=0).astype(F32)
    pos_own = positions.reshape(count)
    pos_both = jnp.concatenate([pos_own, net.swap_side(pos_own)])
    cosine, sine = rope_tables(pos_both)
    cos_heads, sin_heads = cosine[:, None, :], sine[:, None, :]
    q_normed, q_inverse, q_scaled = head_norm(
        raw[:, :q_cols].reshape(both, heads, HD), gain_query
    )
    query = rotate(q_scaled, cos_heads, sin_heads).astype(BF)
    k_normed, k_inverse, k_scaled = head_norm(
        raw[:, q_cols : q_cols + k_cols].reshape(both, kv_heads, HD), gain_key
    )
    key = rotate(k_scaled, cos_heads, sin_heads).astype(BF)
    value = raw[:, q_cols + k_cols :].reshape(both, kv_heads, HD).astype(BF)

    kv_own = jnp.concatenate([key, value], axis=-1).reshape(
        2, rows, per_row, kv_heads, 2 * HD
    )
    pieces = [kv_own] + [
        net.hop(kv_own, step, 0, net.nodes - step) for step in range(1, net.nodes)
    ]
    kv = jnp.stack(pieces)
    kv = kv.transpose(2, 4, 0, 1, 3, 5).reshape(rows, kv_heads, net.nodes * 2 * per_row, 2 * HD)
    offset = jnp.arange(per_row, dtype=jnp.int32)
    sides = jnp.stack([side, 1 - side]).astype(jnp.int32)
    q_index = (node * 2 * per_row + sides[:, None] * per_row + offset[None, :]).reshape(-1)
    piece_node = node - jnp.arange(net.nodes, dtype=jnp.int32)
    k_index = piece_node[:, None, None] * 2 * per_row + (
        sides[None, :, None] * per_row + offset[None, None, :]
    )
    k_index = jnp.where(piece_node[:, None, None] >= 0, k_index, total_len).reshape(-1)
    causal = k_index[None, :] <= q_index[:, None]

    def by_head(v):
        v = v.reshape(2, rows, per_row, kv_heads, group, HD)
        return v.transpose(1, 3, 4, 0, 2, 5).reshape(rows, kv_heads, group, 2 * per_row, HD)

    def by_token(v):
        v = v.reshape(rows, kv_heads, group, 2, per_row, HD)
        return v.transpose(3, 0, 4, 1, 2, 5).reshape(2, count, heads * HD)

    q_heads = by_head(query)
    scores = (
        jnp.einsum("rhgqd,rhjd->rhgqj", q_heads, kv[..., :HD], preferred_element_type=F32) * scale
    )
    weight = jnp.where(causal, jnp.exp(scores), 0.0)
    total = jnp.sum(weight, axis=-1)
    summed = jnp.einsum(
        "rhgqj,rhjd->rhgqd", weight.astype(BF), kv[..., HD:], preferred_element_type=F32
    )
    o_float = summed / total[..., None]
    o_low = by_token(o_float.astype(BF))

    att = jnp.concatenate([o_low[0], net.swap_side(o_low[1])], axis=1)
    out_rows = w_out.shape[0] // 2
    w_out_own = take(w_out, side * out_rows, out_rows)
    w_out_rel = jnp.concatenate([w_out_own, take(w_out, (1 - side) * out_rows, out_rows)], axis=0)
    att_part = dot(net.relative(att), w_out_rel).astype(BF)
    att_sum = net.scatter_tp([att_part[j * share : (j + 1) * share] for j in range(net.tp)])
    x_share = take(x_rows, t * share, share)
    inverse_one_share = take(inverse_one, t * share, share)
    resid = x_share + att_sum
    normed_two, inverse_two, a_two_share = norm_rows(resid, gain_two)
    a_two = net.gather_all(a_two_share)

    onehot = (corpus.reshape(count)[:, None] == jnp.arange(NCORP, dtype=jnp.int32)).astype(F32)
    counts = lax.psum(jnp.sum(onehot, axis=0), "seq")
    weight_scale = corpus_weight.astype(F32) * (rows * total_len / NCORP) / counts
    token_scale = jnp.sum(onehot * weight_scale, axis=-1, keepdims=True)
    grad = cotangent.reshape(count, width).astype(F32) * token_scale
    low_own = net.relative(grad.astype(BF)).reshape(net.tp, share, width)
    even = net.swap_side(low_own[0::2])
    odd = net.swap_bit(even, 0)
    low_other = jnp.stack([even, odd], axis=1)
    grad_low = jnp.concatenate(
        [low_own.reshape(count, width), low_other.reshape(count, width)], axis=0
    )
    grad_share = take(grad, t * share, share)

    ff = w_gate.shape[1] // 2
    gate_w, up_w = take(w_gate, side * ff, ff, 1), take(w_up, side * ff, ff, 1)
    down_w = take(w_down, side * ff, ff)
    d_hidden = dot_nt(grad_low, down_w)
    gate = dot(a_two, gate_w)
    up = dot(a_two, up_w)
    sigma = jax.nn.sigmoid(gate)
    hidden = (gate * sigma * up).astype(BF)
    d_up = (d_hidden * gate * sigma).astype(BF)
    d_gate = (d_hidden * up * sigma * (1.0 + gate * (1.0 - sigma))).astype(BF)
    down_part = dot_tn(hidden, grad_low).astype(BF)
    gate_part = dot_tn(a_two, d_gate).astype(BF)
    up_part = dot_tn(a_two, d_up).astype(BF)
    grad_down = net.finish(net.sum_line(down_part), 0)
    d_a_two = net.scatter_all((dot_nt(d_gate, gate_w) + dot_nt(d_up, up_w)).astype(BF))
    grad_gate = net.finish(net.sum_line(gate_part), 1)
    grad_up = net.finish(net.sum_line(up_part), 1)

    d_resid = grad_share + norm_back(d_a_two, normed_two, inverse_two, gain_two)
    gain_two_part = jnp.sum(d_a_two * normed_two, axis=0)
    branch_low = net.gather_all(d_resid.astype(BF))

    ffn = net.scatter_all(dot(hidden, down_w).astype(BF))
    out = net.natural(net.gather_tp((resid + ffn).astype(BF))).reshape(rows, per_row, width)

    d_att = dot_nt(branch_low, w_out_own).astype(BF)
    out_part = dot_tn(
        jnp.concatenate([net.relative(o_low[0]), net.relative(o_low[1])], axis=0), branch_low
    ).astype(BF)
    grad_out = net.finish(net.sum_line(out_part), 0)
    d_att = d_att.reshape(2, net.tp, share, heads * HD)
    do_heads = by_head(jnp.stack([net.natural(d_att[0]), net.natural(d_att[1])]))
    delta = jnp.sum(do_heads.astype(F32) * o_float, axis=-1)
    probs = weight / total[..., None]
    d_probs = jnp.einsum(
        "rhgqd,rhjd->rhgqj", do_heads, kv[..., HD:], preferred_element_type=F32
    )
    d_scores = (probs * (d_probs - delta[..., None])).astype(BF)
    d_q_sum = (
        jnp.einsum("rhgqj,rhjd->rhgqd", d_scores, kv[..., :HD], preferred_element_type=F32) * scale
    )
    d_k = jnp.einsum("rhgqj,rhgqd->rhjd", d_scores, q_heads, preferred_element_type=F32) * scale
    d_v = jnp.einsum("rhgqj,rhgqd->rhjd", probs.astype(BF), do_heads, preferred_element_type=F32)
    d_kv = jnp.concatenate([d_k, d_v], axis=-1)
    d_kv = d_kv.reshape(rows, kv_heads, net.nodes, 2, per_row, 2 * HD).transpose(2, 3, 0, 4, 1, 5)
    d_kv_own = d_kv[0]
    for step in range(1, net.nodes):
        got = net.hop(d_kv[step].astype(BF), -step, step, net.nodes)
        d_kv_own = d_kv_own + got.astype(F32)
    if shared:
        d_kv_own = d_kv_own + net.swap_side(d_kv_own.astype(BF))[::-1].astype(F32)
    d_kv_own = d_kv_own.reshape(both, kv_heads, 2 * HD)
    d_k_rot = unrotate(d_kv_own[..., :HD], cos_heads, sin_heads)
    gain_key_part = jnp.sum(d_k_rot * k_normed, axis=(0, 1))
    d_key = norm_back(d_k_rot, k_normed, k_inverse, gain_key).reshape(both, k_cols)
    d_value = d_kv_own[..., HD:].reshape(both, k_cols)
    d_q_rot = unrotate(
        by_token(d_q_sum).reshape(both, heads, HD), cos_heads, sin_heads
    )
    gain_query_part = jnp.sum(d_q_rot * q_normed, axis=(0, 1))
    d_query = norm_back(d_q_rot, q_normed, q_inverse, gain_query).reshape(both, q_cols)
    if shared:
        gain_key_part = 0.5 * gain_key_part
        d_key = take(d_key, side * k_grad, k_grad, 1)
        d_value = take(d_value, side * k_grad, k_grad, 1)
    d_raw = jnp.concatenate([d_query, d_key, d_value], axis=1).astype(BF)

    mine = take(a_one.reshape(2, count // 2, width), t % 2, 1)[0]
    got = net.swap_side(mine)
    got_other = net.swap_bit(got, 0)
    a_one_other = jnp.where(
        t % 2 == 0, jnp.stack([got, got_other]), jnp.stack([got_other, got])
    ).reshape(count, width)
    a_one_both = jnp.concatenate([a_one, a_one_other], axis=0)
    raw_part = dot_tn(a_one_both, d_raw).astype(BF)
    raw_sum = net.sum_line(raw_part)
    d_a_one_part = dot_nt(d_raw, w_back).astype(BF).reshape(2, count, width)
    d_a_one = net.scatter_all(
        jnp.concatenate([net.relative(d_a_one_part[0]), net.relative(d_a_one_part[1])], axis=0)
    )
    normed_one = x_share * inverse_one_share
    gain_one_part = jnp.sum(d_a_one * normed_one, axis=0)
    d_x = d_resid + norm_back(d_a_one, normed_one, inverse_one_share, gain_one)
    d_tokens = net.natural(net.gather_tp(d_x.astype(BF))).reshape(rows, per_row, width)
    cuts = (q_cols, q_cols + k_grad)
    grad_query = net.finish([p[:, : cuts[0]] for p in raw_sum], 1)
    grad_key = net.finish([p[:, cuts[0] : cuts[1]] for p in raw_sum], 1)
    grad_value = net.finish([p[:, cuts[1] :] for p in raw_sum], 1)

    gains = lax.psum(
        jnp.concatenate([gain_one_part, gain_two_part, gain_query_part, gain_key_part]),
        ("seq", "tp"),
    )

    def gain_share(start, size):
        mine = size // net.tp
        return take(gains, start + t * mine, mine)

    return (
        out,
        d_tokens,
        gain_share(0, width),
        grad_query,
        grad_key,
        grad_value,
        gain_share(2 * width, HD),
        gain_share(2 * width + HD, HD),
        grad_out,
        gain_share(width, width),
        grad_gate,
        grad_up,
        grad_down,
    )


def solution(mesh):
    placed = (
        P(None, "seq", None),
        P(None, "seq"),
        P(None, "seq"),
        P(),
        P(),
        P(None, "tp"),
        P(None, "tp"),
        P(None, "tp"),
        P(),
        P(),
        P("tp", None),
        P(),
        P(None, "tp"),
        P(None, "tp"),
        P("tp", None),
        P(None, "seq", None),
    )
    return jax.shard_map(
        per_device,
        mesh=mesh,
        in_specs=placed,
        out_specs=(
            P(None, "seq", None),
            P(None, "seq", None),
            P("tp"),
            P(None, "tp"),
            P(None, "tp"),
            P(None, "tp"),
            P("tp"),
            P("tp"),
            P("tp", None),
            P("tp"),
            P(None, "tp"),
            P(None, "tp"),
            P("tp", None),
        ),
        check_vma=False,
    )
```

```python
import functools

import jax
import jax.numpy as jnp
from jax import lax
from jax.experimental import pallas as pl
from jax.experimental.pallas import tpu as pltpu
from jax.sharding import PartitionSpec as P

HD = 64
NCORP = 8


EPS = 1e-05
EPS_HEAD = 1e-06
ROPE_BASE = 10000.0
BF = jnp.bfloat16
F32 = jnp.float32
MESH = pl.DeviceIdType.MESH
LAG = 2
AHEAD = 3


def rope_tables(positions):
    half = HD // 2
    rates = ROPE_BASE ** (-jnp.arange(half, dtype=jnp.float32) * 2.0 / HD)
    angle = positions.astype(jnp.float32)[:, None] * rates[None, :]
    return (jnp.cos(angle), jnp.sin(angle))


def rotate(vector, cosine, sine):
    half = vector.shape[-1] // 2
    first = vector[..., :half]
    second = vector[..., half:]
    return jnp.concatenate(
        [first * cosine - second * sine, second * cosine + first * sine], axis=-1
    )


def unrotate(grads, cosine, sine):
    half = grads.shape[-1] // 2
    first = grads[..., :half]
    second = grads[..., half:]
    return jnp.concatenate(
        [first * cosine + second * sine, second * cosine - first * sine], axis=-1
    )


def norm_rows(vector, gain):
    inverse = lax.rsqrt(jnp.mean(vector * vector, axis=-1, keepdims=True) + EPS)
    normed = vector * inverse
    return (normed, inverse, (normed * gain).astype(jnp.bfloat16))


def head_norm(vector, gain):
    inverse = lax.rsqrt(jnp.mean(vector * vector, axis=-1, keepdims=True) + EPS_HEAD)
    normed = vector * inverse
    return (normed, inverse, normed * gain)


def norm_back(d_scaled, normed, inverse, gain):
    scaled = d_scaled * gain
    return inverse * (scaled - normed * jnp.mean(scaled * normed, axis=-1, keepdims=True))


def dot(a, b):
    return jnp.dot(a, b, preferred_element_type=F32)


def dot_tn(a, b):
    return lax.dot_general(a, b, (((0,), (0,)), ((), ())), preferred_element_type=F32)


def dot_nt(a, b):
    return lax.dot_general(a, b, (((1,), (1,)), ((), ())), preferred_element_type=F32)


def take(array, start, size, axis=0):
    return lax.dynamic_slice_in_dim(array, start, size, axis)


class Links:
    def __init__(self):
        self.seq = lax.axis_size("seq")
        self.tp = lax.axis_size("tp")
        self.nodes = self.seq // 2
        self.bits = self.tp.bit_length() - 1
        rank = lax.axis_index("seq")
        self.node = rank // 2
        self.side = rank % 2
        self.t = lax.axis_index("tp")

    def swap_side(self, value):
        return lax.ppermute(value, "seq", [(s, s ^ 1) for s in range(self.seq)])

    def swap_bit(self, value, bit):
        return lax.ppermute(value, "tp", [(r, r ^ (1 << bit)) for r in range(self.tp)])

    def hop(self, value, step, low, high):
        pairs = [(2 * n + d, 2 * (n + step) + d) for n in range(low, high) for d in range(2)]
        return lax.ppermute(value, "seq", pairs)

    def relative(self, rows):
        share = rows.shape[0] // self.tp
        return jnp.concatenate(
            [take(rows, (self.t ^ j) * share, share) for j in range(self.tp)], axis=0
        )

    def scatter_tp(self, blocks):
        held = dict(enumerate(blocks))
        for bit in range(self.bits):
            keep = [j for j in held if not (j >> bit) & 1]
            send = jnp.stack([held[j | (1 << bit)] for j in keep])
            got = self.swap_bit(send, bit)
            last = bit == self.bits - 1
            held = {
                j: (
                    held[j].astype(F32) + got[k].astype(F32)
                    if last
                    else (held[j].astype(F32) + got[k].astype(F32)).astype(BF)
                )
                for k, j in enumerate(keep)
            }
        return held[0]

    def scatter_all(self, part):
        share = part.shape[0] // (2 * self.tp)
        blocks = part.reshape(2, self.tp, share, -1)
        held = {j: blocks[:, j] for j in range(self.tp)}
        for bit in range(self.bits):
            keep = [j for j in held if not (j >> bit) & 1]
            send = jnp.stack([held[j | (1 << bit)] for j in keep])
            got = self.swap_bit(send, bit)
            held = {
                j: (held[j].astype(F32) + got[k].astype(F32)).astype(BF)
                for k, j in enumerate(keep)
            }
        mine = held[0]
        got = self.swap_side(mine[1])
        return mine[0].astype(F32) + got.astype(F32)

    def gather_tp(self, mine):
        held = mine[None]
        for bit in reversed(range(self.bits)):
            got = self.swap_bit(held, bit)
            held = jnp.stack([held, got], axis=1).reshape((-1,) + mine.shape)
        return held

    def gather_all(self, mine):
        top = self.bits - 1
        half = mine.shape[0] // 2
        across = self.swap_side(mine)
        over = self.swap_bit(mine, top)
        far = jnp.concatenate(
            [self.swap_bit(across[:half], top), self.swap_side(over[half:])], axis=0
        )
        held = jnp.stack([jnp.stack([mine, over]), jnp.stack([across, far])])
        for bit in reversed(range(top)):
            got = self.swap_bit(held, bit)
            held = jnp.stack([held, got], axis=2).reshape((2, -1) + mine.shape)
        return held.reshape(-1, mine.shape[-1])

    def natural(self, held):
        return jnp.concatenate(
            [lax.dynamic_index_in_dim(held, self.t ^ r, 0, False) for r in range(self.tp)], axis=0
        )


def line_kernel(nodes, shapes, axes, prow, pcol, *refs):
    n = len(shapes)
    parts, outs = refs[:n], refs[n : 2 * n]
    red, own, own_sem, red_send, red_recv, fin_send, fin_recv, x_send, x_recv, put_sem = refs[2 * n :]
    half = red.shape[1]
    rank = lax.axis_index("seq")
    node, side = rank // 2, rank % 2
    last = nodes - 1

    barrier = pltpu.get_barrier_semaphore()
    for delta in (1, -1):

        @pl.when((node + delta >= 0) & (node + delta <= last))
        def _():
            pl.semaphore_signal(
                barrier, 1, device_id={"seq": rank + 2 * delta}, device_id_type=MESH
            )

    pl.semaphore_signal(barrier, 1, device_id={"seq": rank + 1 - 2 * side}, device_id_type=MESH)
    ends = jnp.where(node == 0, 1, 0) + jnp.where(node == last, 1, 0)
    pl.semaphore_wait(barrier, 3 - ends)

    def with_piece(b, j, act):
        p = 2 * j + b
        base = 0
        for i, (rows, cols) in enumerate(shapes):
            tall = rows // prow
            size = tall * (cols // pcol)

            @pl.when((p >= base) & (p < base + size))
            def _(i=i, base=base, tall=tall, rows=rows, cols=cols):
                q = p - base
                row = pl.multiple_of((q % tall) * prow, prow)
                col = pl.multiple_of((q // tall) * pcol, pcol)
                out_row = row + side * rows if axes[i] == 0 else row
                out_col = col + side * cols if axes[i] == 1 else col
                act(
                    parts[i].at[pl.ds(row, prow), pl.ds(col, pcol)],
                    outs[i].at[
                        pl.ds(pl.multiple_of(out_row, prow), prow),
                        pl.ds(pl.multiple_of(out_col, pcol), pcol),
                    ],
                )

            base += size

    def remote(src, dst, send, recv, target):
        return pltpu.make_async_remote_copy(
            src, dst, send, recv, device_id={"seq": target}, device_id_type=MESH
        )

    def stream(b, i):
        v = node if b == 0 else last - node
        ahead = rank + 2 if b == 0 else rank - 2
        behind = rank - 2 if b == 0 else rank + 2
        across = rank + 1 - 2 * side

        f = i - LAG * v + AHEAD - 1

        @pl.when((v > 0) & (f >= 0) & (f < half))
        def _():
            with_piece(
                b,
                f,
                lambda src, dst: pltpu.make_async_copy(
                    src, own.at[b, f % AHEAD], own_sem.at[b, f % AHEAD]
                ).start(),
            )

        j = i - LAG * v

        @pl.when((v == 0) & (j >= 0) & (j < half))
        def _():
            with_piece(
                b,
                j,
                lambda src, dst: remote(
                    src, red.at[b, j], red_send.at[b, j], red_recv.at[b, j], ahead
                ).start(),
            )

        @pl.when((v > 0) & (j >= 0) & (j < half))
        def _():
            pltpu.make_async_copy(
                own.at[b, j % AHEAD], own.at[b, j % AHEAD], own_sem.at[b, j % AHEAD]
            ).wait()
            remote(
                red.at[b, j], red.at[b, j], red_send.at[b, j], red_recv.at[b, j], behind
            ).wait_recv()
            red[b, j] = (red[b, j].astype(F32) + own[b, j % AHEAD].astype(F32)).astype(BF)

            @pl.when(v < last)
            def _():
                remote(
                    red.at[b, j], red.at[b, j], red_send.at[b, j], red_recv.at[b, j], ahead
                ).start()

            @pl.when(v == last)
            def _():
                def act(src, dst):
                    remote(red.at[b, j], dst, fin_send.at[b, j], fin_recv.at[b, j], behind).start()
                    remote(red.at[b, j], dst, x_send.at[b, j], x_recv.at[b, j], across).start()
                    pltpu.make_async_copy(red.at[b, j], dst, put_sem.at[b, j]).start()

                with_piece(b, j, act)

        g = i - LAG * last - LAG * (last - v)

        @pl.when((v < last) & (g >= 0) & (g < half))
        def _():
            remote(
                red.at[b, g], red.at[b, g], fin_send.at[b, g], fin_recv.at[b, g], ahead
            ).wait_recv()

            def act(src, dst):
                @pl.when(v > 0)
                def _():
                    remote(dst, dst, fin_send.at[b, g], fin_recv.at[b, g], behind).start()

                remote(dst, dst, x_send.at[b, g], x_recv.at[b, g], across).start()

            with_piece(b, g, act)

    @pl.loop(0, half + 2 * LAG * last)
    def _(i):
        for b in range(2):
            stream(b, i)

    @pl.loop(0, half)
    def _(j):
        for b in range(2):
            v = node if b == 0 else last - node
            probe = red.at[b, j]

            @pl.when(v < last)
            def _():
                remote(probe, probe, red_send.at[b, j], red_recv.at[b, j], rank).wait_send()

            @pl.when(v > 0)
            def _():
                remote(probe, probe, fin_send.at[b, j], fin_recv.at[b, j], rank).wait_send()

            @pl.when(v == last)
            def _():
                pltpu.make_async_copy(probe, probe, put_sem.at[b, j]).wait()

            remote(probe, probe, x_send.at[b, j], x_recv.at[b, j], rank).wait()


def sum_line(parts, axes, nodes, prow, pcol, ident):
    shapes = [p.shape for p in parts]
    pieces = sum((r // prow) * (c // pcol) for r, c in shapes)
    half = pieces // 2
    assert pieces % 2 == 0
    outs = [
        jax.ShapeDtypeStruct((2 * r, c) if a == 0 else (r, 2 * c), BF)
        for (r, c), a in zip(shapes, axes)
    ]
    anywhere = pl.BlockSpec(memory_space=pl.ANY)
    dma = pltpu.SemaphoreType.DMA
    vmem = 2 * (half + AHEAD) * prow * pcol * 2
    return pl.pallas_call(
        functools.partial(line_kernel, nodes, shapes, axes, prow, pcol),
        out_shape=outs,
        in_specs=[anywhere] * len(parts),
        out_specs=[anywhere] * len(parts),
        scratch_shapes=[
            pltpu.VMEM((2, half, prow, pcol), BF),
            pltpu.VMEM((2, AHEAD, prow, pcol), BF),
            dma((2, AHEAD)),
        ]
        + [dma((2, half))] * 7,
        compiler_params=pltpu.CompilerParams(
            collective_id=ident, has_side_effects=True, vmem_limit_bytes=vmem + (6 << 20)
        ),
        cost_estimate=pl.CostEstimate(
            flops=0, bytes_accessed=64 * pieces * prow * pcol, transcendentals=0
        ),
        name="sum_line",
    )(*parts)


def per_device(
    tokens,
    positions,
    corpus,
    corpus_weight,
    gain_one,
    w_query,
    w_key,
    w_value,
    gain_query,
    gain_key,
    w_out,
    gain_two,
    w_gate,
    w_up,
    w_down,
    cotangent,
):
    net = Links()
    rows, per_row, width = tokens.shape
    count = rows * per_row
    share = count // net.tp
    total_len = per_row * net.seq
    side, node, t = net.side, net.node, net.t
    scale = HD ** (-0.5)
    q_cols = w_query.shape[1] // 2
    shared = (w_key.shape[1] // HD) % 2 == 1
    k_cols = w_key.shape[1] if shared else w_key.shape[1] // 2
    k_grad = w_key.shape[1] // 2
    heads, kv_heads = q_cols // HD, k_cols // HD
    group = heads // kv_heads
    both = 2 * count

    x_rows = tokens.reshape(count, width).astype(F32)
    inverse_one = lax.rsqrt(jnp.mean(x_rows * x_rows, axis=-1, keepdims=True) + EPS)
    a_one = (x_rows * inverse_one * gain_one).astype(BF)

    def halves(w):
        cols = w.shape[1] // 2
        return take(w, side * cols, cols, 1), take(w, (1 - side) * cols, cols, 1)

    wq, wk, wv = halves(w_query), halves(w_key), halves(w_value)
    w_back = jnp.concatenate([wq[0], wk[0], wv[0]], axis=1)
    if shared:
        wk, wv = (w_key, w_key), (w_value, w_value)
    w_own = jnp.concatenate([wq[0], wk[0], wv[0]], axis=1)
    w_other = jnp.concatenate([wq[1], wk[1], wv[1]], axis=1)
    raw_other = net.swap_side(dot(a_one, w_other).astype(BF))
    raw_own = dot(a_one, w_own).astype(BF)
    raw = jnp.concatenate([raw_own, raw_other], axis=0).astype(F32)
    pos_own = positions.reshape(count)
    pos_both = jnp.concatenate([pos_own, net.swap_side(pos_own)])
    cosine, sine = rope_tables(pos_both)
    cos_heads, sin_heads = cosine[:, None, :], sine[:, None, :]
    q_normed, q_inverse, q_scaled = head_norm(
        raw[:, :q_cols].reshape(both, heads, HD), gain_query
    )
    query = rotate(q_scaled, cos_heads, sin_heads).astype(BF)
    k_normed, k_inverse, k_scaled = head_norm(
        raw[:, q_cols : q_cols + k_cols].reshape(both, kv_heads, HD), gain_key
    )
    key = rotate(k_scaled, cos_heads, sin_heads).astype(BF)
    value = raw[:, q_cols + k_cols :].reshape(both, kv_heads, HD).astype(BF)

    kv_own = jnp.concatenate([key, value], axis=-1).reshape(
        2, rows, per_row, kv_heads, 2 * HD
    )
    pieces = [kv_own] + [
        net.hop(kv_own, step, 0, net.nodes - step) for step in range(1, net.nodes)
    ]
    kv = jnp.stack(pieces)
    kv = kv.transpose(2, 4, 0, 1, 3, 5).reshape(rows, kv_heads, net.nodes * 2 * per_row, 2 * HD)
    offset = jnp.arange(per_row, dtype=jnp.int32)
    sides = jnp.stack([side, 1 - side]).astype(jnp.int32)
    q_index = (node * 2 * per_row + sides[:, None] * per_row + offset[None, :]).reshape(-1)
    piece_node = node - jnp.arange(net.nodes, dtype=jnp.int32)
    k_index = piece_node[:, None, None] * 2 * per_row + (
        sides[None, :, None] * per_row + offset[None, None, :]
    )
    k_index = jnp.where(piece_node[:, None, None] >= 0, k_index, total_len).reshape(-1)
    causal = k_index[None, :] <= q_index[:, None]

    def by_head(v):
        v = v.reshape(2, rows, per_row, kv_heads, group, HD)
        return v.transpose(1, 3, 4, 0, 2, 5).reshape(rows, kv_heads, group, 2 * per_row, HD)

    def by_token(v):
        v = v.reshape(rows, kv_heads, group, 2, per_row, HD)
        return v.transpose(3, 0, 4, 1, 2, 5).reshape(2, count, heads * HD)

    q_heads = by_head(query)
    scores = (
        jnp.einsum("rhgqd,rhjd->rhgqj", q_heads, kv[..., :HD], preferred_element_type=F32) * scale
    )
    weight = jnp.where(causal, jnp.exp(scores), 0.0)
    total = jnp.sum(weight, axis=-1)
    summed = jnp.einsum(
        "rhgqj,rhjd->rhgqd", weight.astype(BF), kv[..., HD:], preferred_element_type=F32
    )
    o_float = summed / total[..., None]
    o_low = by_token(o_float.astype(BF))

    att = jnp.concatenate([o_low[0], net.swap_side(o_low[1])], axis=1)
    out_rows = w_out.shape[0] // 2
    w_out_own = take(w_out, side * out_rows, out_rows)
    w_out_rel = jnp.concatenate([w_out_own, take(w_out, (1 - side) * out_rows, out_rows)], axis=0)
    att_part = dot(net.relative(att), w_out_rel).astype(BF)
    att_sum = net.scatter_tp([att_part[j * share : (j + 1) * share] for j in range(net.tp)])
    x_share = take(x_rows, t * share, share)
    inverse_one_share = take(inverse_one, t * share, share)
    resid = x_share + att_sum
    normed_two, inverse_two, a_two_share = norm_rows(resid, gain_two)
    a_two = net.gather_all(a_two_share)

    onehot = (corpus.reshape(count)[:, None] == jnp.arange(NCORP, dtype=jnp.int32)).astype(F32)
    counts = lax.psum(jnp.sum(onehot, axis=0), "seq")
    weight_scale = corpus_weight.astype(F32) * (rows * total_len / NCORP) / counts
    token_scale = jnp.sum(onehot * weight_scale, axis=-1, keepdims=True)
    grad = cotangent.reshape(count, width).astype(F32) * token_scale
    low_own = net.relative(grad.astype(BF)).reshape(net.tp, share, width)
    even = net.swap_side(low_own[0::2])
    odd = net.swap_bit(even, 0)
    low_other = jnp.stack([even, odd], axis=1)
    grad_low = jnp.concatenate(
        [low_own.reshape(count, width), low_other.reshape(count, width)], axis=0
    )
    grad_share = take(grad, t * share, share)

    ff = w_gate.shape[1] // 2
    gate_w, up_w = take(w_gate, side * ff, ff, 1), take(w_up, side * ff, ff, 1)
    down_w = take(w_down, side * ff, ff)
    d_hidden = dot_nt(grad_low, down_w)
    gate = dot(a_two, gate_w)
    up = dot(a_two, up_w)
    sigma = jax.nn.sigmoid(gate)
    hidden = (gate * sigma * up).astype(BF)
    d_up = (d_hidden * gate * sigma).astype(BF)
    d_gate = (d_hidden * up * sigma * (1.0 + gate * (1.0 - sigma))).astype(BF)
    down_part = dot_tn(hidden, grad_low).astype(BF)
    gate_part = dot_tn(a_two, d_gate).astype(BF)
    up_part = dot_tn(a_two, d_up).astype(BF)
    d_a_two = net.scatter_all((dot_nt(d_gate, gate_w) + dot_nt(d_up, up_w)).astype(BF))

    d_resid = grad_share + norm_back(d_a_two, normed_two, inverse_two, gain_two)
    gain_two_part = jnp.sum(d_a_two * normed_two, axis=0)
    branch_low = net.gather_all(d_resid.astype(BF))

    ffn = net.scatter_all(dot(hidden, down_w).astype(BF))
    out = net.natural(net.gather_tp((resid + ffn).astype(BF))).reshape(rows, per_row, width)

    d_att = dot_nt(branch_low, w_out_own).astype(BF)
    out_part = dot_tn(
        jnp.concatenate([net.relative(o_low[0]), net.relative(o_low[1])], axis=0), branch_low
    ).astype(BF)
    d_att = d_att.reshape(2, net.tp, share, heads * HD)
    do_heads = by_head(jnp.stack([net.natural(d_att[0]), net.natural(d_att[1])]))
    delta = jnp.sum(do_heads.astype(F32) * o_float, axis=-1)
    probs = weight / total[..., None]
    d_probs = jnp.einsum(
        "rhgqd,rhjd->rhgqj", do_heads, kv[..., HD:], preferred_element_type=F32
    )
    d_scores = (probs * (d_probs - delta[..., None])).astype(BF)
    d_q_sum = (
        jnp.einsum("rhgqj,rhjd->rhgqd", d_scores, kv[..., :HD], preferred_element_type=F32) * scale
    )
    d_k = jnp.einsum("rhgqj,rhgqd->rhjd", d_scores, q_heads, preferred_element_type=F32) * scale
    d_v = jnp.einsum("rhgqj,rhgqd->rhjd", probs.astype(BF), do_heads, preferred_element_type=F32)
    d_kv = jnp.concatenate([d_k, d_v], axis=-1)
    d_kv = d_kv.reshape(rows, kv_heads, net.nodes, 2, per_row, 2 * HD).transpose(2, 3, 0, 4, 1, 5)
    d_kv_own = d_kv[0]
    for step in range(1, net.nodes):
        got = net.hop(d_kv[step].astype(BF), -step, step, net.nodes)
        d_kv_own = d_kv_own + got.astype(F32)
    if shared:
        d_kv_own = d_kv_own + net.swap_side(d_kv_own.astype(BF))[::-1].astype(F32)
    d_kv_own = d_kv_own.reshape(both, kv_heads, 2 * HD)
    d_k_rot = unrotate(d_kv_own[..., :HD], cos_heads, sin_heads)
    gain_key_part = jnp.sum(d_k_rot * k_normed, axis=(0, 1))
    d_key = norm_back(d_k_rot, k_normed, k_inverse, gain_key).reshape(both, k_cols)
    d_value = d_kv_own[..., HD:].reshape(both, k_cols)
    d_q_rot = unrotate(
        by_token(d_q_sum).reshape(both, heads, HD), cos_heads, sin_heads
    )
    gain_query_part = jnp.sum(d_q_rot * q_normed, axis=(0, 1))
    d_query = norm_back(d_q_rot, q_normed, q_inverse, gain_query).reshape(both, q_cols)
    if shared:
        gain_key_part = 0.5 * gain_key_part
        d_key = take(d_key, side * k_grad, k_grad, 1)
        d_value = take(d_value, side * k_grad, k_grad, 1)
    d_raw = jnp.concatenate([d_query, d_key, d_value], axis=1).astype(BF)

    mine = take(a_one.reshape(2, count // 2, width), t % 2, 1)[0]
    got = net.swap_side(mine)
    got_other = net.swap_bit(got, 0)
    a_one_other = jnp.where(
        t % 2 == 0, jnp.stack([got, got_other]), jnp.stack([got_other, got])
    ).reshape(count, width)
    a_one_both = jnp.concatenate([a_one, a_one_other], axis=0)
    raw_part = dot_tn(a_one_both, d_raw).astype(BF)
    d_a_one_part = dot_nt(d_raw, w_back).astype(BF).reshape(2, count, width)
    d_a_one = net.scatter_all(
        jnp.concatenate([net.relative(d_a_one_part[0]), net.relative(d_a_one_part[1])], axis=0)
    )
    normed_one = x_share * inverse_one_share
    gain_one_part = jnp.sum(d_a_one * normed_one, axis=0)
    d_x = d_resid + norm_back(d_a_one, normed_one, inverse_one_share, gain_one)
    d_tokens = net.natural(net.gather_tp(d_x.astype(BF))).reshape(rows, per_row, width)
    piece_cols = min(ff, 1024)
    sums = sum_line(
        [gate_part, up_part, down_part, out_part, raw_part.reshape(-1, piece_cols)],
        [1, 1, 0, 0, 0],
        net.nodes,
        65536 // piece_cols,
        piece_cols,
        1,
    )
    grad_gate, grad_up, grad_down, grad_out = (v.astype(F32) for v in sums[:4])
    raw_sum = sums[4].reshape(2, width, -1)
    cuts = (q_cols, q_cols + k_grad)

    def columns(low, high):
        return jnp.concatenate([raw_sum[0, :, low:high], raw_sum[1, :, low:high]], axis=1).astype(F32)

    grad_query = columns(0, cuts[0])
    grad_key = columns(cuts[0], cuts[1])
    grad_value = columns(cuts[1], cuts[1] + k_grad)

    gains = lax.psum(
        jnp.concatenate([gain_one_part, gain_two_part, gain_query_part, gain_key_part]),
        ("seq", "tp"),
    )

    def gain_share(start, size):
        mine = size // net.tp
        return take(gains, start + t * mine, mine)

    return (
        out,
        d_tokens,
        gain_share(0, width),
        grad_query,
        grad_key,
        grad_value,
        gain_share(2 * width, HD),
        gain_share(2 * width + HD, HD),
        grad_out,
        gain_share(width, width),
        grad_gate,
        grad_up,
        grad_down,
    )


def solution(mesh):
    placed = (
        P(None, "seq", None),
        P(None, "seq"),
        P(None, "seq"),
        P(),
        P(),
        P(None, "tp"),
        P(None, "tp"),
        P(None, "tp"),
        P(),
        P(),
        P("tp", None),
        P(),
        P(None, "tp"),
        P(None, "tp"),
        P("tp", None),
        P(None, "seq", None),
    )
    return jax.shard_map(
        per_device,
        mesh=mesh,
        in_specs=placed,
        out_specs=(
            P(None, "seq", None),
            P(None, "seq", None),
            P("tp"),
            P(None, "tp"),
            P(None, "tp"),
            P(None, "tp"),
            P("tp"),
            P("tp"),
            P("tp", None),
            P("tp"),
            P(None, "tp"),
            P(None, "tp"),
            P("tp", None),
        ),
        check_vma=False,
    )
```

```python
import functools

import jax
import jax.numpy as jnp
from jax import lax
from jax.experimental import pallas as pl
from jax.experimental.pallas import tpu as pltpu
from jax.sharding import PartitionSpec as P

HD = 64
NCORP = 8


EPS = 1e-05
EPS_HEAD = 1e-06
ROPE_BASE = 10000.0
BF = jnp.bfloat16
F32 = jnp.float32
MESH = pl.DeviceIdType.MESH
LAG = 2
AHEAD = 3


def rope_tables(positions):
    half = HD // 2
    rates = ROPE_BASE ** (-jnp.arange(half, dtype=jnp.float32) * 2.0 / HD)
    angle = positions.astype(jnp.float32)[:, None] * rates[None, :]
    return (jnp.cos(angle), jnp.sin(angle))


def rotate(vector, cosine, sine):
    half = vector.shape[-1] // 2
    first = vector[..., :half]
    second = vector[..., half:]
    return jnp.concatenate(
        [first * cosine - second * sine, second * cosine + first * sine], axis=-1
    )


def unrotate(grads, cosine, sine):
    half = grads.shape[-1] // 2
    first = grads[..., :half]
    second = grads[..., half:]
    return jnp.concatenate(
        [first * cosine + second * sine, second * cosine - first * sine], axis=-1
    )


def norm_rows(vector, gain):
    inverse = lax.rsqrt(jnp.mean(vector * vector, axis=-1, keepdims=True) + EPS)
    normed = vector * inverse
    return (normed, inverse, (normed * gain).astype(jnp.bfloat16))


def head_norm(vector, gain):
    inverse = lax.rsqrt(jnp.mean(vector * vector, axis=-1, keepdims=True) + EPS_HEAD)
    normed = vector * inverse
    return (normed, inverse, normed * gain)


def norm_back(d_scaled, normed, inverse, gain):
    scaled = d_scaled * gain
    return inverse * (scaled - normed * jnp.mean(scaled * normed, axis=-1, keepdims=True))


def dot(a, b):
    return jnp.dot(a, b, preferred_element_type=F32)


def dot_tn(a, b):
    return lax.dot_general(a, b, (((0,), (0,)), ((), ())), preferred_element_type=F32)


def dot_nt(a, b):
    return lax.dot_general(a, b, (((1,), (1,)), ((), ())), preferred_element_type=F32)


def take(array, start, size, axis=0):
    return lax.dynamic_slice_in_dim(array, start, size, axis)


class Links:
    def __init__(self):
        self.seq = lax.axis_size("seq")
        self.tp = lax.axis_size("tp")
        self.nodes = self.seq // 2
        self.bits = self.tp.bit_length() - 1
        rank = lax.axis_index("seq")
        self.node = rank // 2
        self.side = rank % 2
        self.t = lax.axis_index("tp")

    def swap_side(self, value):
        return lax.ppermute(value, "seq", [(s, s ^ 1) for s in range(self.seq)])

    def swap_bit(self, value, bit):
        return lax.ppermute(value, "tp", [(r, r ^ (1 << bit)) for r in range(self.tp)])

    def hop(self, value, step, low, high):
        pairs = [(2 * n + d, 2 * (n + step) + d) for n in range(low, high) for d in range(2)]
        return lax.ppermute(value, "seq", pairs)

    def relative(self, rows):
        share = rows.shape[0] // self.tp
        return jnp.concatenate(
            [take(rows, (self.t ^ j) * share, share) for j in range(self.tp)], axis=0
        )

    def scatter_tp(self, blocks):
        held = dict(enumerate(blocks))
        for bit in range(self.bits):
            keep = [j for j in held if not (j >> bit) & 1]
            send = jnp.stack([held[j | (1 << bit)] for j in keep])
            got = self.swap_bit(send, bit)
            last = bit == self.bits - 1
            held = {
                j: (
                    held[j].astype(F32) + got[k].astype(F32)
                    if last
                    else (held[j].astype(F32) + got[k].astype(F32)).astype(BF)
                )
                for k, j in enumerate(keep)
            }
        return held[0]

    def scatter_all(self, part):
        share = part.shape[0] // (2 * self.tp)
        blocks = part.reshape(2, self.tp, share, -1)
        held = {j: blocks[:, j] for j in range(self.tp)}
        for bit in range(self.bits):
            keep = [j for j in held if not (j >> bit) & 1]
            send = jnp.stack([held[j | (1 << bit)] for j in keep])
            got = self.swap_bit(send, bit)
            held = {
                j: (held[j].astype(F32) + got[k].astype(F32)).astype(BF)
                for k, j in enumerate(keep)
            }
        mine = held[0]
        got = self.swap_side(mine[1])
        return mine[0].astype(F32) + got.astype(F32)

    def gather_tp(self, mine):
        held = mine[None]
        for bit in reversed(range(self.bits)):
            got = self.swap_bit(held, bit)
            held = jnp.stack([held, got], axis=1).reshape((-1,) + mine.shape)
        return held

    def gather_all(self, mine):
        top = self.bits - 1
        half = mine.shape[0] // 2
        across = self.swap_side(mine)
        over = self.swap_bit(mine, top)
        far = jnp.concatenate(
            [self.swap_bit(across[:half], top), self.swap_side(over[half:])], axis=0
        )
        held = jnp.stack([jnp.stack([mine, over]), jnp.stack([across, far])])
        for bit in reversed(range(top)):
            got = self.swap_bit(held, bit)
            held = jnp.stack([held, got], axis=2).reshape((2, -1) + mine.shape)
        return held.reshape(-1, mine.shape[-1])

    def natural(self, held):
        return jnp.concatenate(
            [lax.dynamic_index_in_dim(held, self.t ^ r, 0, False) for r in range(self.tp)], axis=0
        )


def line_kernel(nodes, shapes, axes, prow, pcol, *refs):
    n = len(shapes)
    parts, outs = refs[:n], refs[n : 2 * n]
    red, own, own_sem, red_send, red_recv, fin_send, fin_recv, x_send, x_recv, put_sem = refs[2 * n :]
    half = red.shape[1]
    rank = lax.axis_index("seq")
    node, side = rank // 2, rank % 2
    last = nodes - 1

    barrier = pltpu.get_barrier_semaphore()
    for delta in (1, -1):

        @pl.when((node + delta >= 0) & (node + delta <= last))
        def _():
            pl.semaphore_signal(
                barrier, 1, device_id={"seq": rank + 2 * delta}, device_id_type=MESH
            )

    pl.semaphore_signal(barrier, 1, device_id={"seq": rank + 1 - 2 * side}, device_id_type=MESH)
    ends = jnp.where(node == 0, 1, 0) + jnp.where(node == last, 1, 0)
    pl.semaphore_wait(barrier, 3 - ends)

    def with_piece(b, j, act):
        p = 2 * j + b
        base = 0
        for i, (rows, cols) in enumerate(shapes):
            tall = rows // prow
            size = tall * (cols // pcol)

            @pl.when((p >= base) & (p < base + size))
            def _(i=i, base=base, tall=tall, rows=rows, cols=cols):
                q = p - base
                row = pl.multiple_of((q % tall) * prow, prow)
                col = pl.multiple_of((q // tall) * pcol, pcol)
                out_row = row + side * rows if axes[i] == 0 else row
                out_col = col + side * cols if axes[i] == 1 else col
                act(
                    parts[i].at[pl.ds(row, prow), pl.ds(col, pcol)],
                    outs[i].at[
                        pl.ds(pl.multiple_of(out_row, prow), prow),
                        pl.ds(pl.multiple_of(out_col, pcol), pcol),
                    ],
                )

            base += size

    def remote(src, dst, send, recv, target):
        return pltpu.make_async_remote_copy(
            src, dst, send, recv, device_id={"seq": target}, device_id_type=MESH
        )

    def stream(b, i):
        v = node if b == 0 else last - node
        ahead = rank + 2 if b == 0 else rank - 2
        behind = rank - 2 if b == 0 else rank + 2
        across = rank + 1 - 2 * side

        f = i - LAG * v + AHEAD - 1

        @pl.when((v > 0) & (f >= 0) & (f < half))
        def _():
            with_piece(
                b,
                f,
                lambda src, dst: pltpu.make_async_copy(
                    src, own.at[b, f % AHEAD], own_sem.at[b, f % AHEAD]
                ).start(),
            )

        j = i - LAG * v

        @pl.when((v == 0) & (j >= 0) & (j < half))
        def _():
            with_piece(
                b,
                j,
                lambda src, dst: remote(
                    src, red.at[b, j], red_send.at[b, j], red_recv.at[b, j], ahead
                ).start(),
            )

        @pl.when((v > 0) & (j >= 0) & (j < half))
        def _():
            pltpu.make_async_copy(
                own.at[b, j % AHEAD], own.at[b, j % AHEAD], own_sem.at[b, j % AHEAD]
            ).wait()
            remote(
                red.at[b, j], red.at[b, j], red_send.at[b, j], red_recv.at[b, j], behind
            ).wait_recv()
            red[b, j] = (red[b, j].astype(F32) + own[b, j % AHEAD].astype(F32)).astype(BF)

            @pl.when(v < last)
            def _():
                remote(
                    red.at[b, j], red.at[b, j], red_send.at[b, j], red_recv.at[b, j], ahead
                ).start()

            @pl.when(v == last)
            def _():
                def act(src, dst):
                    remote(red.at[b, j], dst, fin_send.at[b, j], fin_recv.at[b, j], behind).start()
                    remote(red.at[b, j], dst, x_send.at[b, j], x_recv.at[b, j], across).start()
                    pltpu.make_async_copy(red.at[b, j], dst, put_sem.at[b, j]).start()

                with_piece(b, j, act)

        g = i - LAG * last - LAG * (last - v)

        @pl.when((v < last) & (g >= 0) & (g < half))
        def _():
            remote(
                red.at[b, g], red.at[b, g], fin_send.at[b, g], fin_recv.at[b, g], ahead
            ).wait_recv()

            def act(src, dst):
                @pl.when(v > 0)
                def _():
                    remote(dst, dst, fin_send.at[b, g], fin_recv.at[b, g], behind).start()

                remote(dst, dst, x_send.at[b, g], x_recv.at[b, g], across).start()

            with_piece(b, g, act)

    @pl.loop(0, half + 2 * LAG * last)
    def _(i):
        for b in range(2):
            stream(b, i)

    @pl.loop(0, half)
    def _(j):
        for b in range(2):
            v = node if b == 0 else last - node
            probe = red.at[b, j]

            @pl.when(v < last)
            def _():
                remote(probe, probe, red_send.at[b, j], red_recv.at[b, j], rank).wait_send()

            @pl.when(v > 0)
            def _():
                remote(probe, probe, fin_send.at[b, j], fin_recv.at[b, j], rank).wait_send()

            @pl.when(v == last)
            def _():
                pltpu.make_async_copy(probe, probe, put_sem.at[b, j]).wait()

            remote(probe, probe, x_send.at[b, j], x_recv.at[b, j], rank).wait()


def sum_line(parts, axes, nodes, prow, pcol, ident):
    shapes = [p.shape for p in parts]
    pieces = sum((r // prow) * (c // pcol) for r, c in shapes)
    half = pieces // 2
    assert pieces % 2 == 0
    outs = [
        jax.ShapeDtypeStruct((2 * r, c) if a == 0 else (r, 2 * c), BF)
        for (r, c), a in zip(shapes, axes)
    ]
    anywhere = pl.BlockSpec(memory_space=pl.ANY)
    dma = pltpu.SemaphoreType.DMA
    vmem = 2 * (half + AHEAD) * prow * pcol * 2
    return pl.pallas_call(
        functools.partial(line_kernel, nodes, shapes, axes, prow, pcol),
        out_shape=outs,
        in_specs=[anywhere] * len(parts),
        out_specs=[anywhere] * len(parts),
        scratch_shapes=[
            pltpu.VMEM((2, half, prow, pcol), BF),
            pltpu.VMEM((2, AHEAD, prow, pcol), BF),
            dma((2, AHEAD)),
        ]
        + [dma((2, half))] * 7,
        compiler_params=pltpu.CompilerParams(
            collective_id=ident, has_side_effects=True, vmem_limit_bytes=vmem + (6 << 20)
        ),
        cost_estimate=pl.CostEstimate(
            flops=0, bytes_accessed=64 * pieces * prow * pcol, transcendentals=0
        ),
        name="sum_line",
    )(*parts)


def remote_copy(src, dst, send, recv, **where):
    return pltpu.make_async_remote_copy(
        src, dst, send, recv, device_id=where, device_id_type=MESH
    )


def attend_kernel(
    nodes,
    bits,
    kv_heads,
    q_ref,
    kv_ref,
    count_ref,
    cot_ref,
    x_ref,
    gain_ref,
    w_ref,
    att_ref,
    log_ref,
    counts_ref,
    cot_out,
    resid_ref,
    a_out,
    kv_in,
    acc,
    weight_sum,
    att_in,
    parts,
    got,
    a_mine,
    kv_send,
    kv_recv,
    count_send,
    count_recv,
    cot_send,
    cot_recv,
    att_sem,
    sum_send,
    sum_recv,
    all_send,
    all_recv,
    own_sem,
):
    tp = 1 << bits
    seq = 2 * nodes
    rank, t = lax.axis_index("seq"), lax.axis_index("tp")
    node, side = rank // 2, rank % 2
    across = rank + 1 - 2 * side
    n_q, wide = q_ref.shape[0], q_ref.shape[1]
    n_rows = kv_ref.shape[0]
    heads = n_q // n_rows
    group = heads // kv_heads
    span = wide // 2
    share, width = x_ref.shape
    top = bits - 1

    def flip(bit):
        return t + (1 << bit) * (1 - 2 * ((t // (1 << bit)) % 2))

    def block_of(j):
        other = t
        for bit in range(bits):
            if (j >> bit) & 1:
                other = other + (1 << bit) * (1 - 2 * ((t // (1 << bit)) % 2))
        return other

    barrier = pltpu.get_barrier_semaphore()
    for step in range(1, seq):
        pl.semaphore_signal(
            barrier, 1, device_id={"seq": (rank + step) % seq}, device_id_type=MESH
        )
    for bit in range(bits):
        pl.semaphore_signal(barrier, 1, device_id={"tp": flip(bit)}, device_id_type=MESH)
    pl.semaphore_wait(barrier, seq - 1 + bits)

    for step in range(1, nodes):

        @pl.when(node + step < nodes)
        def _():
            remote_copy(
                kv_ref,
                kv_in.at[step - 1],
                kv_send.at[step - 1],
                kv_recv.at[step - 1],
                seq=rank + 2 * step,
            ).start()

    counts_ref[0] = count_ref[...]
    count_copies = [
        remote_copy(
            count_ref,
            counts_ref.at[step],
            count_send.at[step - 1],
            count_recv.at[step - 1],
            seq=(rank + step) % seq,
        )
        for step in range(1, seq)
    ]
    for copy in count_copies:
        copy.start()
    cot_copies = []
    for j in range(0, tp, 2):
        rows = pl.ds(pl.multiple_of(block_of(j) * share, share), share)
        cot_copies.append(
            remote_copy(
                cot_ref.at[rows], cot_out.at[j], cot_send.at[j], cot_recv.at[j], seq=across
            )
        )
        cot_copies[-1].start()

    def attend(kv_at, diagonal):
        @pl.loop(0, n_q)
        def _(i):
            kv = kv_at(i // heads, (i % heads) // group)
            scores = lax.dot_general(
                q_ref[i], kv, (((1,), (1,)), ((), ())), preferred_element_type=F32
            )
            weight = jnp.exp2(scores * (HD**-0.5 * 1.4426950408889634))
            if diagonal:
                q_at = lax.broadcasted_iota(jnp.int32, (wide, wide), 0)
                k_at = lax.broadcasted_iota(jnp.int32, (wide, wide), 1)
                q_at = jnp.where(q_at < span, q_at + span * side, q_at - span * side)
                k_at = jnp.where(k_at < span, k_at + span * side, k_at - span * side)
                weight = jnp.where(k_at <= q_at, weight, 0.0)
            sums = weight[:, :128]
            for c in range(128, wide, 128):
                sums = sums + weight[:, c : c + 128]
            values = jnp.dot(weight.astype(BF), kv, preferred_element_type=F32)
            if diagonal:
                weight_sum[i] = sums
                acc[i] = values
            else:
                weight_sum[i] += sums
                acc[i] += values

    attend(lambda r, h: kv_ref[r, h], True)
    for step in range(1, nodes):

        @pl.when(node >= step)
        def _():
            remote_copy(
                kv_ref,
                kv_in.at[step - 1],
                kv_send.at[step - 1],
                kv_recv.at[step - 1],
                seq=rank,
            ).wait_recv()
            attend(lambda r, h: kv_in[step - 1, r, h], False)

    att_copy = remote_copy(
        att_ref.at[1], att_in, att_sem.at[0], att_sem.at[1], seq=across
    )
    lane = lax.broadcasted_iota(jnp.int32, (span, 2 * HD), 1)
    for d in (1, 0):
        for r in range(n_rows):
            for h in range(0, heads, 2):
                out = []
                for k in range(2):
                    i = r * heads + h + k
                    at = pl.ds(d * span, span)
                    total = jnp.sum(weight_sum[i, at, :], axis=-1, keepdims=True)
                    log_ref[i, at, :] = jnp.log2(total)
                    out.append(acc[i, at, :] / total)
                both = jnp.where(lane < HD, pltpu.roll(out[0], HD, 1), out[1])
                att_ref[d, pl.ds(r * span, span), pl.ds(h * HD, 2 * HD)] = both.astype(BF)
        if d == 1:
            att_copy.start()

    half = w_ref.shape[0] // 2
    w_mine = w_ref[pl.ds(pl.multiple_of(side * half, half), half), :]
    w_other = w_ref[pl.ds(pl.multiple_of((1 - side) * half, half), half), :]

    def project(j, add):
        rows = pl.ds(pl.multiple_of(block_of(j) * share, share), share)
        if not add:
            parts[j] = jnp.dot(att_ref[0, rows, :], w_mine, preferred_element_type=F32)
        else:
            parts[j] += jnp.dot(att_in[rows, :], w_other, preferred_element_type=F32)

    for j in range(tp):
        project(j, False)
    att_copy.wait()
    order = sorted(range(tp), key=lambda j: -(j & 1))
    for j in order:
        project(j, True)

    held = list(range(tp))
    slot = 0
    for bit in range(bits):
        keep = [j for j in held if not (j >> bit) & 1]
        copies = []
        for j in keep:
            a_mine[slot] = parts[j | (1 << bit)].astype(BF)
            copies.append(
                remote_copy(
                    a_mine.at[slot], got.at[slot], sum_send.at[slot], sum_recv.at[slot],
                    tp=flip(bit),
                )
            )
            copies[-1].start()
            slot += 1
        for k, j in enumerate(keep):
            copies[k].wait()
            parts[j] += got[slot - len(keep) + k].astype(F32)
        held = keep
    resid = x_ref[...].astype(F32) + parts[0]
    resid_ref[...] = resid
    inverse = lax.rsqrt(jnp.mean(resid * resid, axis=-1, keepdims=True) + EPS)
    a_mine[slot] = (resid * inverse * gain_ref[...]).astype(BF)
    mine = a_mine.at[slot]

    started = []

    def send(src, dst, k, **where):
        copy = remote_copy(src, dst, all_send.at[k], all_recv.at[k], **where)
        copy.start()
        started.append(copy)
        return copy

    up = 1 << top
    cut = share // 2
    low, high = pl.ds(0, cut), pl.ds(cut, cut)
    by_side = send(mine, a_out.at[1, 0], 0, seq=across)
    by_top = send(mine, a_out.at[0, up], 1, tp=flip(top))
    put = pltpu.make_async_copy(mine, a_out.at[0, 0], own_sem)
    put.start()
    k = 4
    for copy in cot_copies:
        copy.wait()
    cot_copies = []
    for j in range(0, tp, 2):
        cot_copies.append(
            remote_copy(
                cot_out.at[j], cot_out.at[j + 1], cot_send.at[j + 1], cot_recv.at[j + 1],
                tp=flip(0),
            )
        )
        cot_copies[-1].start()
    pending = {}
    for bit in reversed(range(top)):
        have = [j for j in range(tp) if j % (2 << bit) == 0]
        if bit == top - 1:
            pending[0, 0] = send(mine, a_out.at[0, 1 << bit], k, tp=flip(bit))
            k += 1
            by_side.wait_recv()
            far_low = send(a_out.at[1, 0, low], a_out.at[1, up, low], 2, tp=flip(top))
            pending[1, 0] = send(a_out.at[1, 0], a_out.at[1, 1 << bit], k, tp=flip(bit))
            k += 1
            by_top.wait_recv()
            far_high = send(a_out.at[0, up, high], a_out.at[1, up, high], 3, seq=across)
            pending[0, up] = send(a_out.at[0, up], a_out.at[0, up | 1 << bit], k, tp=flip(bit))
            k += 1
            far_low.wait_recv()
            far_high.wait_recv()
            pending[1, up] = send(a_out.at[1, up], a_out.at[1, up | 1 << bit], k, tp=flip(bit))
            k += 1
        else:
            for d in range(2):
                for j in have:
                    pending[d, j] = send(
                        a_out.at[d, j], a_out.at[d, j | 1 << bit], k, tp=flip(bit)
                    )
                    k += 1
        for copy in pending.values():
            copy.wait_recv()
        pending = {}
    for copy in started:
        copy.wait_send()
    put.wait()
    for copy in count_copies + cot_copies:
        copy.wait()
    for step in range(1, nodes):

        @pl.when(node + step < nodes)
        def _():
            remote_copy(
                kv_ref,
                kv_in.at[step - 1],
                kv_send.at[step - 1],
                kv_recv.at[step - 1],
                seq=rank,
            ).wait_send()


def attend(nodes, bits, kv_heads, q, kv, count, cotangent, x_share, gain, w_out, ident):
    tp = 1 << bits
    seq = 2 * nodes
    n_q, wide, _ = q.shape
    n_rows = kv.shape[0]
    heads = n_q // n_rows
    share, width = x_share.shape
    vmem = pl.BlockSpec(memory_space=pltpu.VMEM)
    anywhere = pl.BlockSpec(memory_space=pl.ANY)
    dma = pltpu.SemaphoreType.DMA
    tokens = tp * share
    messages = 4 + 2 * (tp - 2)
    return pl.pallas_call(
        functools.partial(attend_kernel, nodes, bits, kv_heads),
        out_shape=[
            jax.ShapeDtypeStruct((2, tokens, heads * HD), BF),
            jax.ShapeDtypeStruct((n_q, wide, 1), F32),
            jax.ShapeDtypeStruct((seq,) + count.shape, F32),
            jax.ShapeDtypeStruct((tp, share, width), BF),
            jax.ShapeDtypeStruct((share, width), F32),
            jax.ShapeDtypeStruct((2, tp, share, width), BF),
            jax.ShapeDtypeStruct((nodes - 1,) + kv.shape, BF),
        ],
        in_specs=[vmem, vmem, vmem, anywhere, vmem, vmem, vmem],
        out_specs=[vmem, vmem, vmem, anywhere, vmem, anywhere, vmem],
        scratch_shapes=[
            pltpu.VMEM((n_q, wide, 2 * HD), F32),
            pltpu.VMEM((n_q, wide, 128), F32),
            pltpu.VMEM((tokens, heads * HD), BF),
            pltpu.VMEM((tp, share, width), F32),
            pltpu.VMEM((tp - 1, share, width), BF),
            pltpu.VMEM((tp, share, width), BF),
            dma((nodes - 1,)),
            dma((nodes - 1,)),
            dma((seq - 1,)),
            dma((seq - 1,)),
            dma((tp,)),
            dma((tp,)),
            dma((2,)),
            dma((tp - 1,)),
            dma((tp - 1,)),
            dma((messages,)),
            dma((messages,)),
            dma,
        ],
        compiler_params=pltpu.CompilerParams(
            collective_id=ident, has_side_effects=True, vmem_limit_bytes=48 << 20
        ),
        cost_estimate=pl.CostEstimate(
            flops=0, bytes_accessed=200 << 20, transcendentals=0
        ),
        name="attend",
    )(q, kv, count, cotangent, x_share, gain, w_out)


def per_device(
    tokens,
    positions,
    corpus,
    corpus_weight,
    gain_one,
    w_query,
    w_key,
    w_value,
    gain_query,
    gain_key,
    w_out,
    gain_two,
    w_gate,
    w_up,
    w_down,
    cotangent,
):
    net = Links()
    rows, per_row, width = tokens.shape
    count = rows * per_row
    share = count // net.tp
    total_len = per_row * net.seq
    side, node, t = net.side, net.node, net.t
    scale = HD ** (-0.5)
    q_cols = w_query.shape[1] // 2
    shared = (w_key.shape[1] // HD) % 2 == 1
    k_cols = w_key.shape[1] if shared else w_key.shape[1] // 2
    k_grad = w_key.shape[1] // 2
    heads, kv_heads = q_cols // HD, k_cols // HD
    group = heads // kv_heads
    both = 2 * count

    x_rows = tokens.reshape(count, width).astype(F32)
    inverse_one = lax.rsqrt(jnp.mean(x_rows * x_rows, axis=-1, keepdims=True) + EPS)
    a_one = (x_rows * inverse_one * gain_one).astype(BF)

    def halves(w):
        cols = w.shape[1] // 2
        return take(w, side * cols, cols, 1), take(w, (1 - side) * cols, cols, 1)

    wq, wk, wv = halves(w_query), halves(w_key), halves(w_value)
    w_back = jnp.concatenate([wq[0], wk[0], wv[0]], axis=1)
    if shared:
        wk, wv = (w_key, w_key), (w_value, w_value)
    w_own = jnp.concatenate([wq[0], wk[0], wv[0]], axis=1)
    w_other = jnp.concatenate([wq[1], wk[1], wv[1]], axis=1)
    raw_other = net.swap_side(dot(a_one, w_other).astype(BF))
    raw_own = dot(a_one, w_own).astype(BF)
    raw = jnp.concatenate([raw_own, raw_other], axis=0).astype(F32)
    pos_own = positions.reshape(count)
    pos_both = jnp.concatenate([pos_own, net.swap_side(pos_own)])
    cosine, sine = rope_tables(pos_both)
    cos_heads, sin_heads = cosine[:, None, :], sine[:, None, :]
    q_normed, q_inverse, q_scaled = head_norm(
        raw[:, :q_cols].reshape(both, heads, HD), gain_query
    )
    query = rotate(q_scaled, cos_heads, sin_heads).astype(BF)
    k_normed, k_inverse, k_scaled = head_norm(
        raw[:, q_cols : q_cols + k_cols].reshape(both, kv_heads, HD), gain_key
    )
    key = rotate(k_scaled, cos_heads, sin_heads).astype(BF)
    value = raw[:, q_cols + k_cols :].reshape(both, kv_heads, HD).astype(BF)

    def by_head(v, depth):
        v = v.reshape(2, rows, per_row, -1, depth).transpose(1, 3, 0, 2, 4)
        return v.reshape(rows, -1, 2 * per_row, depth)

    def by_token(v):
        v = v.reshape(rows, heads, 2, per_row, HD)
        return v.transpose(2, 0, 3, 1, 4).reshape(2, count, heads * HD)

    q_heads = by_head(query, HD)
    q_padded = jnp.pad(q_heads, ((0, 0), (0, 0), (0, 0), (0, HD)))
    kv_own = by_head(jnp.concatenate([key, value], axis=-1), 2 * HD)
    onehot = (corpus.reshape(count)[:, None] == jnp.arange(NCORP, dtype=jnp.int32)).astype(F32)
    own_counts = jnp.zeros((8, 128), F32).at[0, :NCORP].set(jnp.sum(onehot, axis=0))
    x_share = take(tokens.reshape(count, width), t * share, share)
    cot_rows = cotangent.reshape(count, width)
    o_low, log_total, all_counts, cot_other, resid, a_two, kv_in = attend(
        net.nodes,
        net.bits,
        kv_heads,
        q_padded.reshape(rows * heads, 2 * per_row, 2 * HD),
        kv_own,
        own_counts,
        cot_rows,
        x_share,
        gain_two[None],
        w_out,
        2,
    )
    a_two = a_two.reshape(both, width)
    x_share = x_share.astype(F32)
    inverse_one_share = take(inverse_one, t * share, share)
    inverse_two = lax.rsqrt(jnp.mean(resid * resid, axis=-1, keepdims=True) + EPS)
    normed_two = resid * inverse_two
    w_out_own = take(w_out, side * (w_out.shape[0] // 2), w_out.shape[0] // 2)

    counts = jnp.sum(all_counts, axis=0)[0, :NCORP]
    weight_scale = corpus_weight.astype(F32) * (rows * total_len / NCORP) / counts
    corpus_other = net.swap_side(corpus.reshape(count))
    onehot_other = (corpus_other[:, None] == jnp.arange(NCORP, dtype=jnp.int32)).astype(F32)
    scale_own = jnp.sum(onehot * weight_scale, axis=-1, keepdims=True)
    scale_other = jnp.sum(onehot_other * weight_scale, axis=-1, keepdims=True)
    cot_both = jnp.concatenate([net.relative(cot_rows), cot_other.reshape(count, width)], axis=0)
    scale_both = jnp.concatenate([net.relative(scale_own), net.relative(scale_other)], axis=0)
    grad_low = (cot_both.astype(F32) * scale_both).astype(BF)
    grad_share = cot_both[:share].astype(F32) * scale_both[:share]

    ff = w_gate.shape[1] // 2
    gate_w, up_w = take(w_gate, side * ff, ff, 1), take(w_up, side * ff, ff, 1)
    down_w = take(w_down, side * ff, ff)
    d_hidden = dot_nt(grad_low, down_w)
    gate = dot(a_two, gate_w)
    up = dot(a_two, up_w)
    sigma = jax.nn.sigmoid(gate)
    hidden = (gate * sigma * up).astype(BF)
    d_up = (d_hidden * gate * sigma).astype(BF)
    d_gate = (d_hidden * up * sigma * (1.0 + gate * (1.0 - sigma))).astype(BF)
    down_part = dot_tn(hidden, grad_low).astype(BF)
    gate_part = dot_tn(a_two, d_gate).astype(BF)
    up_part = dot_tn(a_two, d_up).astype(BF)
    d_a_two = net.scatter_all((dot_nt(d_gate, gate_w) + dot_nt(d_up, up_w)).astype(BF))

    d_resid = grad_share + norm_back(d_a_two, normed_two, inverse_two, gain_two)
    gain_two_part = jnp.sum(d_a_two * normed_two, axis=0)
    branch_low = net.gather_all(d_resid.astype(BF))

    ffn = net.scatter_all(dot(hidden, down_w).astype(BF))
    out = net.natural(net.gather_tp((resid + ffn).astype(BF))).reshape(rows, per_row, width)

    d_att = dot_nt(branch_low, w_out_own).astype(BF)
    out_part = dot_tn(
        jnp.concatenate([net.relative(o_low[0]), net.relative(o_low[1])], axis=0), branch_low
    ).astype(BF)
    d_att = d_att.reshape(2, net.tp, share, heads * HD)
    d_att = jnp.concatenate([net.natural(d_att[0]), net.natural(d_att[1])], axis=0)
    delta = by_head(
        jnp.sum((d_att.astype(F32) * o_low.reshape(both, -1).astype(F32)).reshape(both, heads, HD), axis=-1),
        1,
    ).reshape(rows, kv_heads, group, 2 * per_row)
    do_heads = by_head(d_att, HD).reshape(rows, kv_heads, group, 2 * per_row, HD)
    q_heads = q_heads.reshape(rows, kv_heads, group, 2 * per_row, HD)
    offset = jnp.arange(per_row, dtype=jnp.int32)
    sides = jnp.stack([side, 1 - side]).astype(jnp.int32)
    q_index = (node * 2 * per_row + sides[:, None] * per_row + offset[None, :]).reshape(-1)
    piece_node = node - jnp.arange(net.nodes, dtype=jnp.int32)
    k_index = piece_node[:, None] * 2 * per_row + (
        sides[:, None] * per_row + offset[None, :]
    ).reshape(1, -1)
    k_index = jnp.where(piece_node[:, None] >= 0, k_index, total_len).reshape(-1)
    causal = k_index[None, :] <= q_index[:, None]
    have = (piece_node[1:] >= 0)[:, None, None, None, None]
    kv = jnp.concatenate([kv_own[None], jnp.where(have, kv_in, 0)], axis=0)
    kv = kv.transpose(1, 2, 0, 3, 4).reshape(rows, kv_heads, -1, 2 * HD)
    scores = (
        jnp.einsum("rhgqd,rhjd->rhgqj", q_heads, kv[..., :HD], preferred_element_type=F32) * scale
    )
    log_total = log_total.reshape(rows, kv_heads, group, 2 * per_row, 1) * 0.6931471805599453
    probs = jnp.where(causal, jnp.exp(scores - log_total), 0.0)
    d_probs = jnp.einsum(
        "rhgqd,rhjd->rhgqj", do_heads, kv[..., HD:], preferred_element_type=F32
    )
    d_scores = (probs * (d_probs - delta[..., None])).astype(BF)
    d_q_sum = (
        jnp.einsum("rhgqj,rhjd->rhgqd", d_scores, kv[..., :HD], preferred_element_type=F32) * scale
    )
    d_k = jnp.einsum("rhgqj,rhgqd->rhjd", d_scores, q_heads, preferred_element_type=F32) * scale
    d_v = jnp.einsum("rhgqj,rhgqd->rhjd", probs.astype(BF), do_heads, preferred_element_type=F32)
    d_kv = jnp.concatenate([d_k, d_v], axis=-1)
    d_kv = d_kv.reshape(rows, kv_heads, net.nodes, 2, per_row, 2 * HD).transpose(2, 3, 0, 4, 1, 5)
    d_kv_own = d_kv[0]
    for step in range(1, net.nodes):
        got = net.hop(d_kv[step].astype(BF), -step, step, net.nodes)
        d_kv_own = d_kv_own + got.astype(F32)
    if shared:
        d_kv_own = d_kv_own + net.swap_side(d_kv_own.astype(BF))[::-1].astype(F32)
    d_kv_own = d_kv_own.reshape(both, kv_heads, 2 * HD)
    d_k_rot = unrotate(d_kv_own[..., :HD], cos_heads, sin_heads)
    gain_key_part = jnp.sum(d_k_rot * k_normed, axis=(0, 1))
    d_key = norm_back(d_k_rot, k_normed, k_inverse, gain_key).reshape(both, k_cols)
    d_value = d_kv_own[..., HD:].reshape(both, k_cols)
    d_q_rot = unrotate(
        by_token(d_q_sum).reshape(both, heads, HD), cos_heads, sin_heads
    )
    gain_query_part = jnp.sum(d_q_rot * q_normed, axis=(0, 1))
    d_query = norm_back(d_q_rot, q_normed, q_inverse, gain_query).reshape(both, q_cols)
    if shared:
        gain_key_part = 0.5 * gain_key_part
        d_key = take(d_key, side * k_grad, k_grad, 1)
        d_value = take(d_value, side * k_grad, k_grad, 1)
    d_raw = jnp.concatenate([d_query, d_key, d_value], axis=1).astype(BF)

    mine = take(a_one.reshape(2, count // 2, width), t % 2, 1)[0]
    got = net.swap_side(mine)
    got_other = net.swap_bit(got, 0)
    a_one_other = jnp.where(
        t % 2 == 0, jnp.stack([got, got_other]), jnp.stack([got_other, got])
    ).reshape(count, width)
    a_one_both = jnp.concatenate([a_one, a_one_other], axis=0)
    raw_part = dot_tn(a_one_both, d_raw).astype(BF)
    d_a_one_part = dot_nt(d_raw, w_back).astype(BF).reshape(2, count, width)
    d_a_one = net.scatter_all(
        jnp.concatenate([net.relative(d_a_one_part[0]), net.relative(d_a_one_part[1])], axis=0)
    )
    normed_one = x_share * inverse_one_share
    gain_one_part = jnp.sum(d_a_one * normed_one, axis=0)
    d_x = d_resid + norm_back(d_a_one, normed_one, inverse_one_share, gain_one)
    d_tokens = net.natural(net.gather_tp(d_x.astype(BF))).reshape(rows, per_row, width)
    piece_cols = min(ff, 1024)
    sums = sum_line(
        [gate_part, up_part, down_part, out_part, raw_part.reshape(-1, piece_cols)],
        [1, 1, 0, 0, 0],
        net.nodes,
        65536 // piece_cols,
        piece_cols,
        1,
    )
    grad_gate, grad_up, grad_down, grad_out = (v.astype(F32) for v in sums[:4])
    raw_sum = sums[4].reshape(2, width, -1)
    cuts = (q_cols, q_cols + k_grad)

    def columns(low, high):
        return jnp.concatenate([raw_sum[0, :, low:high], raw_sum[1, :, low:high]], axis=1).astype(F32)

    grad_query = columns(0, cuts[0])
    grad_key = columns(cuts[0], cuts[1])
    grad_value = columns(cuts[1], cuts[1] + k_grad)

    gains = lax.psum(
        jnp.concatenate([gain_one_part, gain_two_part, gain_query_part, gain_key_part]),
        ("seq", "tp"),
    )

    def gain_share(start, size):
        mine = size // net.tp
        return take(gains, start + t * mine, mine)

    return (
        out,
        d_tokens,
        gain_share(0, width),
        grad_query,
        grad_key,
        grad_value,
        gain_share(2 * width, HD),
        gain_share(2 * width + HD, HD),
        grad_out,
        gain_share(width, width),
        grad_gate,
        grad_up,
        grad_down,
    )


def solution(mesh):
    placed = (
        P(None, "seq", None),
        P(None, "seq"),
        P(None, "seq"),
        P(),
        P(),
        P(None, "tp"),
        P(None, "tp"),
        P(None, "tp"),
        P(),
        P(),
        P("tp", None),
        P(),
        P(None, "tp"),
        P(None, "tp"),
        P("tp", None),
        P(None, "seq", None),
    )
    return jax.shard_map(
        per_device,
        mesh=mesh,
        in_specs=placed,
        out_specs=(
            P(None, "seq", None),
            P(None, "seq", None),
            P("tp"),
            P(None, "tp"),
            P(None, "tp"),
            P(None, "tp"),
            P("tp"),
            P("tp"),
            P("tp", None),
            P("tp"),
            P(None, "tp"),
            P(None, "tp"),
            P("tp", None),
        ),
        check_vma=False,
    )
```

```python
import functools

import jax
import jax.numpy as jnp
from jax import lax
from jax.experimental import pallas as pl
from jax.experimental.pallas import tpu as pltpu
from jax.sharding import PartitionSpec as P

HD = 64
NCORP = 8


EPS = 1e-05
EPS_HEAD = 1e-06
ROPE_BASE = 10000.0
BF = jnp.bfloat16
F32 = jnp.float32
MESH = pl.DeviceIdType.MESH
LAG = 2
AHEAD = 3


def rope_tables(positions):
    half = HD // 2
    rates = ROPE_BASE ** (-jnp.arange(half, dtype=jnp.float32) * 2.0 / HD)
    angle = positions.astype(jnp.float32)[:, None] * rates[None, :]
    return (jnp.cos(angle), jnp.sin(angle))


def rotate(vector, cosine, sine):
    half = vector.shape[-1] // 2
    first = vector[..., :half]
    second = vector[..., half:]
    return jnp.concatenate(
        [first * cosine - second * sine, second * cosine + first * sine], axis=-1
    )


def head_norm(vector, gain):
    inverse = lax.rsqrt(jnp.mean(vector * vector, axis=-1, keepdims=True) + EPS_HEAD)
    normed = vector * inverse
    return (normed, inverse, normed * gain)


def dot(a, b):
    return jnp.dot(a, b, preferred_element_type=F32)


def dot_tn(a, b):
    return lax.dot_general(a, b, (((0,), (0,)), ((), ())), preferred_element_type=F32)


def dot_nt(a, b):
    return lax.dot_general(a, b, (((1,), (1,)), ((), ())), preferred_element_type=F32)


def take(array, start, size, axis=0):
    return lax.dynamic_slice_in_dim(array, start, size, axis)


class Links:
    def __init__(self):
        self.seq = lax.axis_size("seq")
        self.tp = lax.axis_size("tp")
        self.nodes = self.seq // 2
        self.bits = self.tp.bit_length() - 1
        rank = lax.axis_index("seq")
        self.node = rank // 2
        self.side = rank % 2
        self.t = lax.axis_index("tp")

    def swap_side(self, value):
        return lax.ppermute(value, "seq", [(s, s ^ 1) for s in range(self.seq)])

    def swap_bit(self, value, bit):
        return lax.ppermute(value, "tp", [(r, r ^ (1 << bit)) for r in range(self.tp)])

    def relative(self, rows):
        share = rows.shape[0] // self.tp
        return jnp.concatenate(
            [take(rows, (self.t ^ j) * share, share) for j in range(self.tp)], axis=0
        )


def remote_copy(src, dst, send, recv, **where):
    return pltpu.make_async_remote_copy(
        src, dst, send, recv, device_id=where, device_id_type=MESH
    )


def attend_kernel(
    nodes,
    bits,
    kv_heads,
    q_ref,
    kv_ref,
    count_ref,
    cot_ref,
    x_ref,
    gain_ref,
    w_ref,
    att_ref,
    log_ref,
    counts_ref,
    cot_out,
    resid_ref,
    a_out,
    kv_in,
    acc,
    weight_sum,
    att_in,
    parts,
    got,
    a_mine,
    kv_send,
    kv_recv,
    count_send,
    count_recv,
    cot_send,
    cot_recv,
    att_sem,
    sum_send,
    sum_recv,
    all_send,
    all_recv,
    own_sem,
):
    tp = 1 << bits
    seq = 2 * nodes
    rank, t = lax.axis_index("seq"), lax.axis_index("tp")
    node, side = rank // 2, rank % 2
    across = rank + 1 - 2 * side
    n_q, wide = q_ref.shape[0], q_ref.shape[1]
    n_rows = kv_ref.shape[0]
    heads = n_q // n_rows
    group = heads // kv_heads
    span = wide // 2
    share, width = x_ref.shape
    top = bits - 1

    def flip(bit):
        return t + (1 << bit) * (1 - 2 * ((t // (1 << bit)) % 2))

    def block_of(j):
        other = t
        for bit in range(bits):
            if (j >> bit) & 1:
                other = other + (1 << bit) * (1 - 2 * ((t // (1 << bit)) % 2))
        return other

    barrier = pltpu.get_barrier_semaphore()
    for step in range(1, seq):
        pl.semaphore_signal(
            barrier, 1, device_id={"seq": (rank + step) % seq}, device_id_type=MESH
        )
    for bit in range(bits):
        pl.semaphore_signal(barrier, 1, device_id={"tp": flip(bit)}, device_id_type=MESH)
    pl.semaphore_wait(barrier, seq - 1 + bits)

    for step in range(1, nodes):

        @pl.when(node + step < nodes)
        def _():
            remote_copy(
                kv_ref,
                kv_in.at[step - 1],
                kv_send.at[step - 1],
                kv_recv.at[step - 1],
                seq=rank + 2 * step,
            ).start()

    counts_ref[0] = count_ref[...]
    count_copies = [
        remote_copy(
            count_ref,
            counts_ref.at[step],
            count_send.at[step - 1],
            count_recv.at[step - 1],
            seq=(rank + step) % seq,
        )
        for step in range(1, seq)
    ]
    for copy in count_copies:
        copy.start()
    cot_copies = []
    for j in range(0, tp, 2):
        rows = pl.ds(pl.multiple_of(block_of(j) * share, share), share)
        cot_copies.append(
            remote_copy(
                cot_ref.at[rows], cot_out.at[j], cot_send.at[j], cot_recv.at[j], seq=across
            )
        )
        cot_copies[-1].start()

    def attend(kv_at, diagonal):
        @pl.loop(0, n_q)
        def _(i):
            kv = kv_at(i // heads, (i % heads) // group)
            scores = lax.dot_general(
                q_ref[i], kv, (((1,), (1,)), ((), ())), preferred_element_type=F32
            )
            weight = jnp.exp2(scores * (HD**-0.5 * 1.4426950408889634))
            if diagonal:
                q_at = lax.broadcasted_iota(jnp.int32, (wide, wide), 0)
                k_at = lax.broadcasted_iota(jnp.int32, (wide, wide), 1)
                q_at = jnp.where(q_at < span, q_at + span * side, q_at - span * side)
                k_at = jnp.where(k_at < span, k_at + span * side, k_at - span * side)
                weight = jnp.where(k_at <= q_at, weight, 0.0)
            sums = weight[:, :128]
            for c in range(128, wide, 128):
                sums = sums + weight[:, c : c + 128]
            values = jnp.dot(weight.astype(BF), kv, preferred_element_type=F32)
            if diagonal:
                weight_sum[i] = sums
                acc[i] = values
            else:
                weight_sum[i] += sums
                acc[i] += values

    attend(lambda r, h: kv_ref[r, h], True)
    for step in range(1, nodes):

        @pl.when(node >= step)
        def _():
            remote_copy(
                kv_ref,
                kv_in.at[step - 1],
                kv_send.at[step - 1],
                kv_recv.at[step - 1],
                seq=rank,
            ).wait_recv()
            attend(lambda r, h: kv_in[step - 1, r, h], False)

    att_copy = remote_copy(
        att_ref.at[1], att_in, att_sem.at[0], att_sem.at[1], seq=across
    )
    lane = lax.broadcasted_iota(jnp.int32, (span, 2 * HD), 1)
    for d in (1, 0):
        for r in range(n_rows):
            for h in range(0, heads, 2):
                out = []
                for k in range(2):
                    i = r * heads + h + k
                    at = pl.ds(d * span, span)
                    total = jnp.sum(weight_sum[i, at, :], axis=-1, keepdims=True)
                    log_ref[i, at, :] = jnp.log2(total)
                    out.append(acc[i, at, :] / total)
                both = jnp.where(lane < HD, pltpu.roll(out[0], HD, 1), out[1])
                att_ref[d, pl.ds(r * span, span), pl.ds(h * HD, 2 * HD)] = both.astype(BF)
        if d == 1:
            att_copy.start()

    half = w_ref.shape[0] // 2
    w_mine = w_ref[pl.ds(pl.multiple_of(side * half, half), half), :]
    w_other = w_ref[pl.ds(pl.multiple_of((1 - side) * half, half), half), :]

    def project(j, add):
        rows = pl.ds(pl.multiple_of(block_of(j) * share, share), share)
        if not add:
            parts[j] = jnp.dot(att_ref[0, rows, :], w_mine, preferred_element_type=F32)
        else:
            parts[j] += jnp.dot(att_in[rows, :], w_other, preferred_element_type=F32)

    for j in range(tp):
        project(j, False)
    att_copy.wait()
    order = sorted(range(tp), key=lambda j: -(j & 1))
    for j in order:
        project(j, True)

    held = list(range(tp))
    slot = 0
    for bit in range(bits):
        keep = [j for j in held if not (j >> bit) & 1]
        copies = []
        for j in keep:
            a_mine[slot] = parts[j | (1 << bit)].astype(BF)
            copies.append(
                remote_copy(
                    a_mine.at[slot], got.at[slot], sum_send.at[slot], sum_recv.at[slot],
                    tp=flip(bit),
                )
            )
            copies[-1].start()
            slot += 1
        for k, j in enumerate(keep):
            copies[k].wait()
            parts[j] += got[slot - len(keep) + k].astype(F32)
        held = keep
    resid = x_ref[...].astype(F32) + parts[0]
    resid_ref[...] = resid
    inverse = lax.rsqrt(jnp.mean(resid * resid, axis=-1, keepdims=True) + EPS)
    a_mine[slot] = (resid * inverse * gain_ref[...]).astype(BF)
    mine = a_mine.at[slot]

    started = []

    def send(src, dst, k, **where):
        copy = remote_copy(src, dst, all_send.at[k], all_recv.at[k], **where)
        copy.start()
        started.append(copy)
        return copy

    up = 1 << top
    cut = share // 2
    low, high = pl.ds(0, cut), pl.ds(cut, cut)
    by_side = send(mine, a_out.at[1, 0], 0, seq=across)
    by_top = send(mine, a_out.at[0, up], 1, tp=flip(top))
    put = pltpu.make_async_copy(mine, a_out.at[0, 0], own_sem)
    put.start()
    k = 4
    for copy in cot_copies:
        copy.wait()
    cot_copies = []
    for j in range(0, tp, 2):
        cot_copies.append(
            remote_copy(
                cot_out.at[j], cot_out.at[j + 1], cot_send.at[j + 1], cot_recv.at[j + 1],
                tp=flip(0),
            )
        )
        cot_copies[-1].start()
    pending = {}
    for bit in reversed(range(top)):
        have = [j for j in range(tp) if j % (2 << bit) == 0]
        if bit == top - 1:
            pending[0, 0] = send(mine, a_out.at[0, 1 << bit], k, tp=flip(bit))
            k += 1
            by_side.wait_recv()
            far_low = send(a_out.at[1, 0, low], a_out.at[1, up, low], 2, tp=flip(top))
            pending[1, 0] = send(a_out.at[1, 0], a_out.at[1, 1 << bit], k, tp=flip(bit))
            k += 1
            by_top.wait_recv()
            far_high = send(a_out.at[0, up, high], a_out.at[1, up, high], 3, seq=across)
            pending[0, up] = send(a_out.at[0, up], a_out.at[0, up | 1 << bit], k, tp=flip(bit))
            k += 1
            far_low.wait_recv()
            far_high.wait_recv()
            pending[1, up] = send(a_out.at[1, up], a_out.at[1, up | 1 << bit], k, tp=flip(bit))
            k += 1
        else:
            for d in range(2):
                for j in have:
                    pending[d, j] = send(
                        a_out.at[d, j], a_out.at[d, j | 1 << bit], k, tp=flip(bit)
                    )
                    k += 1
        for copy in pending.values():
            copy.wait_recv()
        pending = {}
    for copy in started:
        copy.wait_send()
    put.wait()
    for copy in count_copies + cot_copies:
        copy.wait()
    for step in range(1, nodes):

        @pl.when(node + step < nodes)
        def _():
            remote_copy(
                kv_ref,
                kv_in.at[step - 1],
                kv_send.at[step - 1],
                kv_recv.at[step - 1],
                seq=rank,
            ).wait_send()


def attend(nodes, bits, kv_heads, q, kv, count, cotangent, x_share, gain, w_out, ident):
    tp = 1 << bits
    seq = 2 * nodes
    n_q, wide, _ = q.shape
    n_rows = kv.shape[0]
    heads = n_q // n_rows
    share, width = x_share.shape
    vmem = pl.BlockSpec(memory_space=pltpu.VMEM)
    anywhere = pl.BlockSpec(memory_space=pl.ANY)
    dma = pltpu.SemaphoreType.DMA
    tokens = tp * share
    messages = 4 + 2 * (tp - 2)
    return pl.pallas_call(
        functools.partial(attend_kernel, nodes, bits, kv_heads),
        out_shape=[
            jax.ShapeDtypeStruct((2, tokens, heads * HD), BF),
            jax.ShapeDtypeStruct((n_q, wide, 1), F32),
            jax.ShapeDtypeStruct((seq,) + count.shape, F32),
            jax.ShapeDtypeStruct((tp, share, width), BF),
            jax.ShapeDtypeStruct((share, width), F32),
            jax.ShapeDtypeStruct((2, tp, share, width), BF),
            jax.ShapeDtypeStruct((nodes - 1,) + kv.shape, BF),
        ],
        in_specs=[vmem, vmem, vmem, anywhere, vmem, vmem, vmem],
        out_specs=[vmem, vmem, vmem, anywhere, vmem, anywhere, vmem],
        scratch_shapes=[
            pltpu.VMEM((n_q, wide, 2 * HD), F32),
            pltpu.VMEM((n_q, wide, 128), F32),
            pltpu.VMEM((tokens, heads * HD), BF),
            pltpu.VMEM((tp, share, width), F32),
            pltpu.VMEM((tp - 1, share, width), BF),
            pltpu.VMEM((tp, share, width), BF),
            dma((nodes - 1,)),
            dma((nodes - 1,)),
            dma((seq - 1,)),
            dma((seq - 1,)),
            dma((tp,)),
            dma((tp,)),
            dma((2,)),
            dma((tp - 1,)),
            dma((tp - 1,)),
            dma((messages,)),
            dma((messages,)),
            dma,
        ],
        compiler_params=pltpu.CompilerParams(
            collective_id=ident, has_side_effects=True, vmem_limit_bytes=48 << 20
        ),
        cost_estimate=pl.CostEstimate(
            flops=0, bytes_accessed=200 << 20, transcendentals=0
        ),
        name="attend",
    )(q, kv, count, cotangent, x_share, gain, w_out)


def backward_kernel(nodes, bits, axes, prow, pcol, *refs):
    names = (
        "gate_part", "up_part", "down_part", "two_part", "ffn_part", "resid", "grad", "x",
        "gain_two", "gain_one", "gain_q", "gain_k", "w_out", "w_back", "a_one", "q", "kv", "kv_in",
        "att", "log", "raw_q", "raw_k", "cosine", "sine", "gate_sum", "up_sum", "down_sum",
        "out_sum", "raw_sum", "out", "tokens", "gains", "two_in", "ffn_in", "one_in", "red", "own",
        "hold", "temp", "low", "w_rows", "w_in", "a_in", "q_in", "d_out", "d_q", "d_kv", "kv_all",
        "att_in", "d_att", "delta", "d_raw", "raw_part", "out_part", "kv_back", "kv_far",
        "d_resid", "fresh", "gain_rows", "gain_box", "gain_all", "log_in", "own_sem", "red_send",
        "red_recv", "fin_send", "fin_recv", "x_send", "x_recv", "put_sem", "load_sem", "sum_send",
        "sum_recv", "hold_sem", "temp_sem", "low_send", "low_recv", "kv_send", "kv_recv",
        "tok_send", "tok_recv", "tok_put", "gain_send", "gain_recv",
    )
    assert len(names) == len(refs)
    R = dict(zip(names, refs))
    tp, seq = 1 << bits, 2 * nodes
    top = bits - 1
    rank, t = lax.axis_index("seq"), lax.axis_index("tp")
    node, side = rank // 2, rank % 2
    across = rank + 1 - 2 * side
    last = nodes - 1
    me = rank * tp + t
    total = seq * tp
    share, width = R["x"].shape
    n_q, wide, _ = R["q"].shape
    n_rows = R["kv"].shape[0]
    heads = n_q // n_rows
    span = wide // 2
    half = R["red"].shape[1]

    def flip(bit):
        return t + (1 << bit) * (1 - 2 * ((t // (1 << bit)) % 2))

    def block_of(j):
        other = t
        for bit in range(bits):
            if (j >> bit) & 1:
                other = other + (1 << bit) * (1 - 2 * ((t // (1 << bit)) % 2))
        return other

    def block_rows(j):
        return pl.ds(pl.multiple_of(block_of(j) * share, share), share)

    barrier = pltpu.get_barrier_semaphore()

    @pl.loop(1, total)
    def _(k):
        other = (me + k) % total
        pl.semaphore_signal(
            barrier, 1, device_id={"seq": other // tp, "tp": other % tp}, device_id_type=MESH
        )

    pl.semaphore_wait(barrier, total - 1)

    parts = [R[k] for k in ("gate_part", "up_part", "down_part", "out_part", "raw_part")]
    outs = [R[k] for k in ("gate_sum", "up_sum", "down_sum", "out_sum", "raw_sum")]
    red, own = R["red"], R["own"]
    own_sem, put_sem = R["own_sem"], R["put_sem"]
    red_sems = R["red_send"], R["red_recv"]
    fin_sems = R["fin_send"], R["fin_recv"]
    x_sems = R["x_send"], R["x_recv"]

    def with_piece(b, j, act):
        p = 2 * j + b
        base = 0
        for i, part in enumerate(parts):
            rows, cols = part.shape
            tall = rows // prow
            size = tall * (cols // pcol)

            @pl.when((p >= base) & (p < base + size))
            def _(i=i, base=base, tall=tall, rows=rows, cols=cols):
                q = p - base
                row = pl.multiple_of((q % tall) * prow, prow)
                col = pl.multiple_of((q // tall) * pcol, pcol)
                out_row = row + side * rows if axes[i] == 0 else row
                out_col = col + side * cols if axes[i] == 1 else col
                act(
                    parts[i].at[pl.ds(row, prow), pl.ds(col, pcol)],
                    outs[i].at[
                        pl.ds(pl.multiple_of(out_row, prow), prow),
                        pl.ds(pl.multiple_of(out_col, pcol), pcol),
                    ],
                )

            base += size

    def along(src, dst, sems, b, j, target):
        return remote_copy(src, dst, sems[0].at[b, j], sems[1].at[b, j], seq=target)

    def placed(j):
        if gap == 0:
            return j, (j >= 0) & (j < half)
        after = j >= late + gap
        return jnp.where(after, j - gap, j), ((j >= 0) & (j < late)) | (
            after & (j < half + gap)
        )

    def stream(b, i):
        v = node if b == 0 else last - node
        ahead = rank + 2 if b == 0 else rank - 2
        behind = rank - 2 if b == 0 else rank + 2
        f, there = placed(i - LAG * v + AHEAD - 1)

        @pl.when((v > 0) & there)
        def _():
            with_piece(
                b,
                f,
                lambda src, dst: pltpu.make_async_copy(
                    src, own.at[b, f % AHEAD], own_sem.at[b, f % AHEAD]
                ).start(),
            )

        j, there = placed(i - LAG * v)

        @pl.when((v == 0) & there)
        def _():
            with_piece(
                b, j, lambda src, dst: along(src, red.at[b, j], red_sems, b, j, ahead).start()
            )

        @pl.when((v > 0) & there)
        def _():
            mine = own.at[b, j % AHEAD]
            pltpu.make_async_copy(mine, mine, own_sem.at[b, j % AHEAD]).wait()
            along(red.at[b, j], red.at[b, j], red_sems, b, j, behind).wait_recv()
            red[b, j] = (red[b, j].astype(F32) + own[b, j % AHEAD].astype(F32)).astype(BF)

            @pl.when(v < last)
            def _():
                along(red.at[b, j], red.at[b, j], red_sems, b, j, ahead).start()

            @pl.when(v == last)
            def _():
                def act(src, dst):
                    along(red.at[b, j], dst, fin_sems, b, j, behind).start()
                    along(red.at[b, j], dst, x_sems, b, j, across).start()
                    pltpu.make_async_copy(red.at[b, j], dst, put_sem.at[b, j]).start()

                with_piece(b, j, act)

        g, there = placed(i - LAG * last - LAG * (last - v))

        @pl.when((v < last) & there)
        def _():
            along(red.at[b, g], red.at[b, g], fin_sems, b, g, ahead).wait_recv()

            def act(src, dst):
                @pl.when(v > 0)
                def _():
                    along(dst, dst, fin_sems, b, g, behind).start()

                along(dst, dst, x_sems, b, g, across).start()

            with_piece(b, g, act)

    hold, temp = R["hold"], R["temp"]
    sources = [R["two_part"], R["ffn_part"], None]
    boxes = [R["two_in"], R["ffn_in"], R["one_in"]]

    def messages(bit):
        base = sum(tp >> b for b in range(bit))
        keep = [(d, j) for d in range(2) for j in range(0, tp, 2 << bit)]
        return [(base + k, d, j) for k, (d, j) in enumerate(keep)]

    def sum_copy(n, m, src, **where):
        return remote_copy(
            src, boxes[n].at[m], R["sum_send"].at[n, m], R["sum_recv"].at[n, m], **where
        )

    def sum_start(n, bit):
        for m, d, j in messages(bit):
            far = j | 1 << bit
            if bit == 0 and n < 2:
                src = sources[n].at[d, far]
                pltpu.make_async_copy(
                    sources[n].at[d, j], hold.at[d, j // 2], R["hold_sem"].at[d, j // 2]
                ).start()
            elif bit == 0:
                src = temp.at[d, j // 2]
            else:
                src = hold.at[d, far // 2]
            sum_copy(n, m, src, tp=flip(bit)).start()

    def sum_add(n, bit):
        for m, d, j in messages(bit):
            copy = sum_copy(n, m, temp.at[d, j // 2], tp=flip(bit))
            copy.wait()
        for m, d, j in messages(bit):
            pltpu.make_async_copy(
                boxes[n].at[m], temp.at[d, j // 2], R["temp_sem"].at[d, j // 2]
            ).start()
        for m, d, j in messages(bit):
            k = j // 2
            if bit == 0 and n < 2:
                pltpu.make_async_copy(
                    hold.at[d, k], hold.at[d, k], R["hold_sem"].at[d, k]
                ).wait()
            pltpu.make_async_copy(temp.at[d, k], temp.at[d, k], R["temp_sem"].at[d, k]).wait()
            hold[d, k] = (hold[d, k].astype(F32) + temp[d, k].astype(F32)).astype(BF)

    final = 2 * (tp - 1)

    def side_start(n):
        sum_copy(n, final, hold.at[1, 0], seq=across).start()

    def side_finish(n):
        sum_copy(n, final, hold.at[1, 0], seq=across).wait()
        load = pltpu.make_async_copy(boxes[n].at[final], temp.at[0, 0], R["temp_sem"].at[0, 0])
        load.start()
        load.wait()
        return hold[0, 0].astype(F32) + temp[0, 0].astype(F32)

    ends = [R["out"], R["tokens"]]

    def token_copy(n, k, src, j, bit):
        return remote_copy(
            src,
            ends[n].at[block_of(j)],
            R["tok_send"].at[n, k],
            R["tok_recv"].at[n, k],
            tp=flip(bit),
        )

    def token_messages(bit):
        base = sum(tp >> (b + 1) for b in range(bit + 1, bits))
        return [(base + k, j) for k, j in enumerate(range(0, tp, 2 << bit))]

    def tokens_start(n, bit):
        for k, j in token_messages(bit):
            src = R["fresh"].at[n] if j == 0 else ends[n].at[block_of(j)]
            token_copy(n, k, src, j, bit).start()

    def tokens_wait(n, bit):
        for k, j in token_messages(bit):
            token_copy(n, k, R["fresh"].at[n], j, bit).wait()

    def tokens_put(n):
        return pltpu.make_async_copy(R["fresh"].at[n], ends[n].at[t], R["tok_put"].at[n])

    loads = [
        (R["w_out"].at[pl.ds(pl.multiple_of(side * heads * HD, heads * HD), heads * HD)], R["w_rows"]),
        (R["w_back"], R["w_in"]),
        (R["a_one"], R["a_in"]),
        (R["q"], R["q_in"]),
        (R["kv"], R["kv_all"].at[0]),
        (R["kv_in"], R["kv_all"].at[pl.ds(1, nodes - 1)]),
        (R["att"], R["att_in"]),
        (R["log"], R["log_in"]),
    ]

    def load(k):
        return pltpu.make_async_copy(loads[k][0], loads[k][1], R["load_sem"].at[k])

    def begin():
        sum_start(0, 0)
        for k in range(len(loads)):
            load(k).start()
        R["d_kv"][...] = jnp.zeros_like(R["d_kv"])
        R["d_q"][...] = jnp.zeros_like(R["d_q"])

    def normed(v):
        inverse = lax.rsqrt(jnp.mean(v * v, axis=-1, keepdims=True) + EPS)
        return v * inverse, inverse

    low = R["low"]

    def low_copy(k, src, dst, **where):
        return remote_copy(src, dst, R["low_send"].at[k], R["low_recv"].at[k], **where)

    up = 1 << top
    low_side = low_copy(0, low.at[0, 0], low.at[1, 0], seq=across)
    low_top = low_copy(1, low.at[0, 0], low.at[0, up], tp=flip(top))
    low_far = low_copy(2, low.at[1, 0], low.at[1, up], tp=flip(top))

    def low_bit(bit):
        base = 3 + sum(tp >> b for b in range(bit + 1, top))
        return [
            low_copy(base + k, low.at[d, j], low.at[d, j | 1 << bit], tp=flip(bit))
            for k, (d, j) in enumerate(
                (d, j) for d in range(2) for j in range(0, tp, 2 << bit)
            )
        ]

    def second_norm():
        d_a = side_finish(0)
        n_two, inverse = normed(R["resid"][...])
        R["gain_rows"][1:2, :] = jnp.sum(d_a * n_two, axis=0, keepdims=True)
        e = d_a * R["gain_two"][...]
        d_resid = R["grad"][...] + inverse * (
            e - n_two * jnp.mean(e * n_two, axis=-1, keepdims=True)
        )
        R["d_resid"][...] = d_resid
        low[0, 0] = d_resid.astype(BF)
        low_side.start()
        low_top.start()

    lane = lax.broadcasted_iota(jnp.int32, (span, 2 * HD), 1)

    def attended_back():
        for k in (0, 6):
            load(k).wait()
        for d in range(2):
            for j in range(tp):
                R["d_att"][d, block_rows(j), :] = lax.dot_general(
                    low[d, j], R["w_rows"][...], (((1,), (1,)), ((), ())), preferred_element_type=F32
                ).astype(BF)
        ones = jnp.ones((8, 2 * HD), F32)
        for d in range(2):
            for r in range(n_rows):
                for h in range(heads):
                    cols = pl.ds((h // 2) * 2 * HD, 2 * HD)
                    grads = R["d_att"][d, pl.ds(r * span, span), cols].astype(F32)
                    values = R["att_in"][d, pl.ds(r * span, span), cols].astype(F32)
                    if h % 2 == 0:
                        grads = pltpu.roll(grads, HD, 1)
                        values = pltpu.roll(values, HD, 1)
                    grads = jnp.where(lane < HD, 0.0, grads)
                    i = r * heads + h
                    R["d_out"][i, pl.ds(d * span, span), :] = grads.astype(BF)
                    R["delta"][i, :, pl.ds(d * span, span)] = lax.dot_general(
                        ones,
                        grads * values,
                        (((1,), (1,)), ((), ())),
                        precision=lax.Precision.HIGHEST,
                        preferred_element_type=F32,
                    )

    def out_gradient():
        chunk = 512
        for c in range(0, width, chunk):
            sums = None
            for d in range(2):
                for j in range(tp):
                    term = lax.dot_general(
                        R["att_in"][d, block_rows(j), :],
                        low[d, j, :, c : c + chunk],
                        (((0,), (0,)), ((), ())),
                        preferred_element_type=F32,
                    )
                    sums = term if sums is None else sums + term
            R["out_part"][:, c : c + chunk] = sums.astype(BF)

    def attention_block(piece, i, diagonal):
        r = i // heads
        kv = R["kv_all"][piece, r, 0]
        q, d_out = R["q_in"][i], R["d_out"][i]
        nt = (((1,), (1,)), ((), ()))
        scores = lax.dot_general(kv, q, nt, preferred_element_type=F32)
        probs = jnp.exp2(scores * (HD**-0.5 * 1.4426950408889634) - R["log_in"][i])
        if diagonal:
            k_at = lax.broadcasted_iota(jnp.int32, (wide, wide), 0)
            q_at = lax.broadcasted_iota(jnp.int32, (wide, wide), 1)
            q_at = jnp.where(q_at < span, q_at + span * side, q_at - span * side)
            k_at = jnp.where(k_at < span, k_at + span * side, k_at - span * side)
            probs = jnp.where(k_at <= q_at, probs, 0.0)
        d_probs = lax.dot_general(kv, d_out, nt, preferred_element_type=F32)
        d_scores = (probs * (d_probs - R["delta"][i, 0:1, :])).astype(BF)
        R["d_kv"][piece, r] += jnp.dot(d_scores, q, preferred_element_type=F32) + jnp.dot(
            probs.astype(BF), d_out, preferred_element_type=F32
        ) * (HD**0.5)
        R["d_q"][i] += lax.dot_general(
            kv, d_scores, (((0,), (0,)), ((), ())), preferred_element_type=F32
        )

    def kv_copy(step):
        return remote_copy(
            R["kv_back"].at[step - 1],
            R["kv_far"].at[step - 1],
            R["kv_send"].at[step - 1],
            R["kv_recv"].at[step - 1],
            seq=rank - 2 * step,
        )

    def kv_send():
        for step in range(1, nodes):

            @pl.when(node >= step)
            def _():
                R["kv_back"][step - 1] = R["d_kv"][step].astype(BF)
                kv_copy(step).start()

    def kv_sum():
        for step in range(1, nodes):

            @pl.when(node + step < nodes)
            def _():
                kv_copy(step).wait_recv()
                R["d_kv"][0] += R["kv_far"][step - 1].astype(F32)

            @pl.when(node >= step)
            def _():
                kv_copy(step).wait_send()

    def head_back(grads, raw, gain, at):
        lanes = 2 * HD
        low_lane = lane < HD // 2
        swapped = jnp.where(
            low_lane, pltpu.roll(grads, lanes - HD // 2, 1), pltpu.roll(grads, HD // 2, 1)
        )
        rotated = grads * R["cosine"][at, :] + swapped * R["sine"][at, :]
        inverse = lax.rsqrt(jnp.sum(raw * raw, axis=-1, keepdims=True) * (1.0 / HD) + EPS_HEAD)
        n = raw * inverse
        e = rotated * gain
        back = inverse * (e - n * (jnp.sum(e * n, axis=-1, keepdims=True) * (1.0 / HD)))
        return back, jnp.sum(rotated * n, axis=0, keepdims=True)

    def heads_back():
        scale = HD**-0.5
        gain_q = jnp.zeros((1, 2 * HD), F32)
        gain_k = jnp.zeros((1, 2 * HD), F32)
        for r in range(n_rows):
            for d in range(2):
                at = pl.ds(d * n_rows * span + r * span, span)
                for h in range(0, heads, 2):
                    pair = []
                    for k in range(2):
                        i = r * heads + h + k
                        grads = R["d_q"][i, :, pl.ds(d * span, span)].T * scale
                        raw = R["raw_q"][i, pl.ds(d * span, span), :].astype(F32)
                        back, gain = head_back(grads, raw, R["gain_q"][...], at)
                        gain_q = gain_q + gain
                        pair.append(back)
                    R["d_raw"][at, pl.ds(h * HD, 2 * HD)] = jnp.where(
                        lane < HD, pair[0], pltpu.roll(pair[1], HD, 1)
                    ).astype(BF)
                grads = R["d_kv"][0, r, pl.ds(d * span, span), :] * scale
                raw = R["raw_k"][r, pl.ds(d * span, span), :].astype(F32)
                back, gain = head_back(grads, raw, R["gain_k"][...], at)
                gain_k = gain_k + gain
                R["d_raw"][at, pl.ds(heads * HD, 2 * HD)] = jnp.where(
                    lane < HD, back, grads
                ).astype(BF)
        R["gain_rows"][2:3, 0 : 2 * HD] = gain_q
        R["gain_rows"][3:4, 0 : 2 * HD] = gain_k

    def raw_gradient():
        load(2).wait()
        chunk = 512
        for c in range(0, width, chunk):
            R["raw_part"][:, c : c + chunk] = lax.dot_general(
                R["d_raw"][...],
                R["a_in"][:, c : c + chunk],
                (((0,), (0,)), ((), ())),
                preferred_element_type=F32,
            ).astype(BF)

    def first_part():
        load(1).wait()
        for d in range(2):
            for j in range(tp):
                rows = pl.ds(
                    pl.multiple_of((d * tp + block_of(j)) * share, share), share
                )
                value = lax.dot_general(
                    R["d_raw"][rows, :],
                    R["w_in"][...],
                    (((1,), (1,)), ((), ())),
                    preferred_element_type=F32,
                ).astype(BF)
                if j % 2:
                    temp[d, j // 2] = value
                else:
                    hold[d, j // 2] = value
        sum_start(2, 0)

    def out_end():
        R["fresh"][0] = (R["resid"][...] + side_finish(1)).astype(BF)
        tokens_put(0).start()
        tokens_start(0, top)

    def first_norm():
        d_a = side_finish(2)
        n_one, inverse = normed(R["x"][...].astype(F32))
        R["gain_rows"][0:1, :] = jnp.sum(d_a * n_one, axis=0, keepdims=True)
        e = d_a * R["gain_one"][...]
        d_x = R["d_resid"][...] + inverse * (
            e - n_one * jnp.mean(e * n_one, axis=-1, keepdims=True)
        )
        R["fresh"][1] = d_x.astype(BF)
        tokens_put(1).start()
        tokens_start(1, top)
        part = width // tp
        for k in range(tp):
            R["gain_box"][k] = jnp.zeros((8, part), F32)
            R["gain_box"][k, 0:2, :] = R["gain_rows"][0:2, k * part : (k + 1) * part]
            R["gain_box"][k, 2:4, 0 : 2 * HD] = R["gain_rows"][2:4, 0 : 2 * HD]

        @pl.loop(1, total)
        def _(k):
            other = (me + k) % total
            remote_copy(
                R["gain_box"].at[other % tp],
                R["gain_all"].at[k],
                R["gain_send"].at[k],
                R["gain_recv"].at[k],
                seq=other // tp,
                tp=other % tp,
            ).start()

        R["gain_all"][0] = R["gain_box"][t]

    def gains_end():
        @pl.loop(1, total)
        def _(k):
            remote_copy(
                R["gain_box"].at[0],
                R["gain_all"].at[k],
                R["gain_send"].at[k],
                R["gain_recv"].at[k],
                seq=rank,
                tp=t,
            ).wait()

        R["gains"][...] = jnp.sum(R["gain_all"][...], axis=0)

    tasks = {}

    def task(step, *acts):
        tasks.setdefault(step, []).extend(acts)
        return step

    def sums_tasks(n, step):
        for bit in range(bits):
            step += 2 if bit == 0 else 5
            following = (
                (lambda bit=bit: sum_start(n, bit + 1)) if bit < top else (lambda: side_start(n))
            )
            task(step, lambda bit=bit: sum_add(n, bit), following)
        return step + 5

    def token_tasks(n, step):
        for bit in reversed(range(bits)):
            step += 3
            task(step, lambda bit=bit: tokens_wait(n, bit))
            if bit:
                task(step, lambda bit=bit: tokens_start(n, bit - 1))
        task(step, lambda: tokens_put(n).wait())
        return step

    step = task(0, begin)
    step = task(sums_tasks(0, step), second_norm)
    step = task(step + 4, low_side.wait, low_top.wait, low_far.start)
    step += 3
    task(step, low_far.wait)
    for bit in reversed(range(top)):
        task(step, lambda bit=bit: [c.start() for c in low_bit(bit)])
        step += 2
        task(step, lambda bit=bit: [c.wait() for c in low_bit(bit)])
    task(step, attended_back)
    step = task(step + 1, out_gradient, lambda: sum_start(1, 0))
    token_tasks(0, task(sums_tasks(1, step), out_end))
    step = task(step + 1, *[load(k).wait for k in (3, 4, 5, 7)])
    first_block = step
    per_step = 2
    step += (nodes * n_q) // per_step
    task(step, kv_send)
    step = task(step + 6, kv_sum, heads_back)
    step = task(step + 1, raw_gradient)
    raw_ready = step
    step = task(step + 1, first_part)
    step = task(sums_tasks(2, step), first_norm)
    task(token_tasks(1, step), gains_end)

    late = half - (R["raw_part"].shape[0] // prow) * (width // pcol) // 2
    gap = max(0, raw_ready + 1 - late)
    steps = max(half + gap + 2 * LAG * last, max(tasks) + 1)

    @pl.loop(0, steps)
    def _(i):
        for b in range(2):
            stream(b, i)
        for at, acts in sorted(tasks.items()):

            @pl.when(i == at)
            def _(acts=acts):
                for act in acts:
                    act()

        for k in range(per_step):
            n = (i - first_block) * per_step + k

            @pl.when((n >= 0) & (n < n_q))
            def _(n=n):
                attention_block(0, n, True)

            @pl.when((n >= n_q) & (n < n_q * nodes) & (node >= n // n_q))
            def _(n=n):
                attention_block(n // n_q, n % n_q, False)

    @pl.loop(0, half)
    def _(j):
        for b in range(2):
            v = node if b == 0 else last - node
            probe = red.at[b, j]

            @pl.when(v < last)
            def _():
                along(probe, probe, red_sems, b, j, rank).wait_send()

            @pl.when(v > 0)
            def _():
                along(probe, probe, fin_sems, b, j, rank).wait_send()

            @pl.when(v == last)
            def _():
                pltpu.make_async_copy(probe, probe, put_sem.at[b, j]).wait()

            along(probe, probe, x_sems, b, j, rank).wait()


def backward(nodes, bits, ident, values):
    tp, seq = 1 << bits, 2 * nodes
    share, width = values["x"].shape
    ff = values["gate_part"].shape[1]
    n_q, wide, _ = values["q"].shape
    n_rows = values["kv"].shape[0]
    heads = n_q // n_rows
    tokens = tp * share
    prow, pcol = 64, ff
    cols = (heads + 2) * HD
    shapes = [(width, ff), (width, ff), (ff, width), (heads * HD, width), (cols, width)]
    axes = [1, 1, 0, 0, 0]
    pieces = sum((r // prow) * (c // pcol) for r, c in shapes)
    half = pieces // 2
    assert pieces % 2 == 0
    vmem = pl.BlockSpec(memory_space=pltpu.VMEM)
    anywhere = pl.BlockSpec(memory_space=pl.ANY)
    dma = pltpu.SemaphoreType.DMA
    inside = ("resid", "grad", "x", "gain_two", "gain_one", "gain_q", "gain_k")
    inside += ("raw_q", "raw_k", "cosine", "sine")
    sums = [
        jax.ShapeDtypeStruct((2 * r, c) if a == 0 else (r, 2 * c), BF)
        for (r, c), a in zip(shapes, axes)
    ]
    ends = [jax.ShapeDtypeStruct((tp, share, width), BF)] * 2
    boxes = [jax.ShapeDtypeStruct((2 * tp - 1, share, width), BF)] * 3
    gains = jax.ShapeDtypeStruct((8, width // tp), F32)
    kv = values["kv"].shape
    total = seq * tp
    low_messages = 3 + 2 * (tp - 2)
    return pl.pallas_call(
        functools.partial(backward_kernel, nodes, bits, axes, prow, pcol),
        out_shape=sums + ends + [gains] + boxes,
        in_specs=[vmem if k in inside else anywhere for k in values],
        out_specs=[anywhere] * 7 + [vmem] + [anywhere] * 3,
        scratch_shapes=[
            pltpu.VMEM((2, half, prow, pcol), BF),
            pltpu.VMEM((2, AHEAD, prow, pcol), BF),
            pltpu.VMEM((2, tp // 2, share, width), BF),
            pltpu.VMEM((2, tp // 2, share, width), BF),
            pltpu.VMEM((2, tp, share, width), BF),
            pltpu.VMEM((heads * HD, width), BF),
            pltpu.VMEM((width, cols), BF),
            pltpu.VMEM((2 * tokens, width), BF),
            pltpu.VMEM((n_q, wide, 2 * HD), BF),
            pltpu.VMEM((n_q, wide, 2 * HD), BF),
            pltpu.VMEM((n_q, 2 * HD, wide), F32),
            pltpu.VMEM((nodes, n_rows, wide, 2 * HD), F32),
            pltpu.VMEM((nodes,) + kv, BF),
            pltpu.VMEM((2, tokens, heads * HD), BF),
            pltpu.VMEM((2, tokens, heads * HD), BF),
            pltpu.VMEM((n_q, 8, wide), F32),
            pltpu.VMEM((2 * tokens, cols), BF),
            pltpu.VMEM((cols, width), BF),
            pltpu.VMEM((heads * HD, width), BF),
            pltpu.VMEM((nodes - 1, n_rows, wide, 2 * HD), BF),
            pltpu.VMEM((nodes - 1, n_rows, wide, 2 * HD), BF),
            pltpu.VMEM((share, width), F32),
            pltpu.VMEM((2, share, width), BF),
            pltpu.VMEM((8, width), F32),
            pltpu.VMEM((tp, 8, width // tp), F32),
            pltpu.VMEM((total, 8, width // tp), F32),
            pltpu.VMEM((n_q, 1, wide), F32),
            dma((2, AHEAD)),
        ]
        + [dma((2, half))] * 7
        + [
            dma((8,)),
            dma((3, 2 * tp - 1)),
            dma((3, 2 * tp - 1)),
            dma((2, tp // 2)),
            dma((2, tp // 2)),
            dma((low_messages,)),
            dma((low_messages,)),
            dma((nodes - 1,)),
            dma((nodes - 1,)),
            dma((2, tp - 1)),
            dma((2, tp - 1)),
            dma((2,)),
            dma((total,)),
            dma((total,)),
        ],
        compiler_params=pltpu.CompilerParams(
            collective_id=ident, has_side_effects=True, vmem_limit_bytes=61 << 20
        ),
        cost_estimate=pl.CostEstimate(
            flops=0, bytes_accessed=1 << 30, transcendentals=0
        ),
        name="backward",
    )(*values.values())[:8]


def per_device(
    tokens,
    positions,
    corpus,
    corpus_weight,
    gain_one,
    w_query,
    w_key,
    w_value,
    gain_query,
    gain_key,
    w_out,
    gain_two,
    w_gate,
    w_up,
    w_down,
    cotangent,
):
    net = Links()
    rows, per_row, width = tokens.shape
    count = rows * per_row
    share = count // net.tp
    total_len = per_row * net.seq
    side, node, t = net.side, net.node, net.t
    scale = HD ** (-0.5)
    q_cols = w_query.shape[1] // 2
    shared = (w_key.shape[1] // HD) % 2 == 1
    k_cols = w_key.shape[1] if shared else w_key.shape[1] // 2
    heads, kv_heads = q_cols // HD, k_cols // HD
    group = heads // kv_heads
    both = 2 * count

    x_rows = tokens.reshape(count, width).astype(F32)
    inverse_one = lax.rsqrt(jnp.mean(x_rows * x_rows, axis=-1, keepdims=True) + EPS)
    a_one = (x_rows * inverse_one * gain_one).astype(BF)

    def halves(w):
        cols = w.shape[1] // 2
        return take(w, side * cols, cols, 1), take(w, (1 - side) * cols, cols, 1)

    wq, wk, wv = halves(w_query), halves(w_key), halves(w_value)
    if shared:
        wk, wv = (w_key, w_key), (w_value, w_value)
    w_own = jnp.concatenate([wq[0], wk[0], wv[0]], axis=1)
    w_other = jnp.concatenate([wq[1], wk[1], wv[1]], axis=1)
    raw_other = net.swap_side(dot(a_one, w_other).astype(BF))
    raw_own = dot(a_one, w_own).astype(BF)
    raw_low = jnp.concatenate([raw_own, raw_other], axis=0)
    raw = raw_low.astype(F32)
    pos_own = positions.reshape(count)
    pos_both = jnp.concatenate([pos_own, net.swap_side(pos_own)])
    cosine, sine = rope_tables(pos_both)
    cos_heads, sin_heads = cosine[:, None, :], sine[:, None, :]
    q_normed, q_inverse, q_scaled = head_norm(
        raw[:, :q_cols].reshape(both, heads, HD), gain_query
    )
    query = rotate(q_scaled, cos_heads, sin_heads).astype(BF)
    k_normed, k_inverse, k_scaled = head_norm(
        raw[:, q_cols : q_cols + k_cols].reshape(both, kv_heads, HD), gain_key
    )
    key = rotate(k_scaled, cos_heads, sin_heads).astype(BF)
    value = raw[:, q_cols + k_cols :].reshape(both, kv_heads, HD).astype(BF)

    def by_head(v, depth):
        v = v.reshape(2, rows, per_row, -1, depth).transpose(1, 3, 0, 2, 4)
        return v.reshape(rows, -1, 2 * per_row, depth)

    q_heads = by_head(query, HD)
    q_padded = jnp.pad(q_heads, ((0, 0), (0, 0), (0, 0), (0, HD)))
    q_padded = q_padded.reshape(rows * heads, 2 * per_row, 2 * HD)
    assert kv_heads == 1
    kv_own = by_head(jnp.concatenate([key, value], axis=-1), 2 * HD)
    onehot = (corpus.reshape(count)[:, None] == jnp.arange(NCORP, dtype=jnp.int32)).astype(F32)
    own_counts = jnp.zeros((8, 128), F32).at[0, :NCORP].set(jnp.sum(onehot, axis=0))
    x_share = take(tokens.reshape(count, width), t * share, share)
    cot_rows = cotangent.reshape(count, width)
    o_low, log_total, all_counts, cot_other, resid, a_two, kv_in = attend(
        net.nodes,
        net.bits,
        kv_heads,
        q_padded,
        kv_own,
        own_counts,
        cot_rows,
        x_share,
        gain_two[None],
        w_out,
        2,
    )
    a_two = a_two.reshape(both, width)

    counts = jnp.sum(all_counts, axis=0)[0, :NCORP]
    weight_scale = corpus_weight.astype(F32) * (rows * total_len / NCORP) / counts
    corpus_other = net.swap_side(corpus.reshape(count))
    onehot_other = (corpus_other[:, None] == jnp.arange(NCORP, dtype=jnp.int32)).astype(F32)
    scale_own = jnp.sum(onehot * weight_scale, axis=-1, keepdims=True)
    scale_other = jnp.sum(onehot_other * weight_scale, axis=-1, keepdims=True)
    cot_both = jnp.concatenate([net.relative(cot_rows), cot_other.reshape(count, width)], axis=0)
    scale_both = jnp.concatenate([net.relative(scale_own), net.relative(scale_other)], axis=0)
    grad_low = (cot_both.astype(F32) * scale_both).astype(BF)
    grad_share = cot_both[:share].astype(F32) * scale_both[:share]

    ff = w_gate.shape[1] // 2
    gate_w, up_w = take(w_gate, side * ff, ff, 1), take(w_up, side * ff, ff, 1)
    down_w = take(w_down, side * ff, ff)
    d_hidden = dot_nt(grad_low, down_w)
    gate = dot(a_two, gate_w)
    up = dot(a_two, up_w)
    sigma = jax.nn.sigmoid(gate)
    hidden = (gate * sigma * up).astype(BF)
    d_up = (d_hidden * gate * sigma).astype(BF)
    d_gate = (d_hidden * up * sigma * (1.0 + gate * (1.0 - sigma))).astype(BF)
    down_part = dot_tn(hidden, grad_low).astype(BF)
    gate_part = dot_tn(a_two, d_gate).astype(BF)
    up_part = dot_tn(a_two, d_up).astype(BF)
    blocks = (2, net.tp, share, width)
    two_part = (dot_nt(d_gate, gate_w) + dot_nt(d_up, up_w)).astype(BF).reshape(blocks)
    ffn_part = dot(hidden, down_w).astype(BF).reshape(blocks)

    mine = take(a_one.reshape(2, count // 2, width), t % 2, 1)[0]
    got = net.swap_side(mine)
    got_other = net.swap_bit(got, 0)
    a_one_other = jnp.where(
        t % 2 == 0, jnp.stack([got, got_other]), jnp.stack([got_other, got])
    ).reshape(count, width)

    def lanes(v):
        return jnp.pad(v, [(0, 0)] * (v.ndim - 1) + [(0, 2 * HD - v.shape[-1])])

    def by_pair(v):
        return lanes(by_head(v, HD)).reshape(-1, 2 * per_row, 2 * HD)

    sums = backward(
        net.nodes,
        net.bits,
        3,
        dict(
            gate_part=gate_part,
            up_part=up_part,
            down_part=down_part,
            two_part=two_part,
            ffn_part=ffn_part,
            resid=resid,
            grad=grad_share,
            x=x_share,
            gain_two=gain_two[None],
            gain_one=gain_one[None],
            gain_q=lanes(gain_query[None]),
            gain_k=lanes(gain_key[None]),
            w_out=w_out,
            w_back=w_own,
            a_one=jnp.concatenate([a_one, a_one_other], axis=0),
            q=q_padded,
            kv=kv_own,
            kv_in=kv_in,
            att=o_low,
            log=log_total.reshape(-1, 1, 2 * per_row),
            raw_q=by_pair(raw_low[:, :q_cols]),
            raw_k=by_pair(raw_low[:, q_cols : q_cols + k_cols]),
            cosine=lanes(jnp.concatenate([cosine, cosine], axis=1)),
            sine=lanes(jnp.concatenate([sine, -sine], axis=1)),
        ),
    )
    grad_gate, grad_up, grad_down, grad_out = (v.astype(F32) for v in sums[:4])
    raw_sum = sums[4].reshape(2, -1, width)
    out, d_tokens = (v.reshape(rows, per_row, width) for v in sums[5:7])
    gains = sums[7]

    def columns(low, high, add=False):
        both_sides = raw_sum[0, low:high], raw_sum[1, low:high]
        if add:
            return (both_sides[0].astype(F32) + both_sides[1].astype(F32)).T
        return jnp.concatenate(both_sides, axis=0).astype(F32).T

    grad_query = columns(0, q_cols)
    grad_key = columns(q_cols, q_cols + k_cols, shared)
    grad_value = columns(q_cols + k_cols, q_cols + 2 * k_cols, shared)
    head_share = HD // net.tp

    return (
        out,
        d_tokens,
        gains[0],
        grad_query,
        grad_key,
        grad_value,
        take(gains[2], t * head_share, head_share),
        take(gains[3], t * head_share, head_share),
        grad_out,
        gains[1],
        grad_gate,
        grad_up,
        grad_down,
    )


def solution(mesh):
    placed = (
        P(None, "seq", None),
        P(None, "seq"),
        P(None, "seq"),
        P(),
        P(),
        P(None, "tp"),
        P(None, "tp"),
        P(None, "tp"),
        P(),
        P(),
        P("tp", None),
        P(),
        P(None, "tp"),
        P(None, "tp"),
        P("tp", None),
        P(None, "seq", None),
    )
    return jax.shard_map(
        per_device,
        mesh=mesh,
        in_specs=placed,
        out_specs=(
            P(None, "seq", None),
            P(None, "seq", None),
            P("tp"),
            P(None, "tp"),
            P(None, "tp"),
            P(None, "tp"),
            P("tp"),
            P("tp"),
            P("tp", None),
            P("tp"),
            P(None, "tp"),
            P(None, "tp"),
            P("tp", None),
        ),
        check_vma=False,
    )
```

```python
import functools

import jax
import jax.numpy as jnp
from jax import lax
from jax.experimental import pallas as pl
from jax.experimental.pallas import tpu as pltpu
from jax.sharding import PartitionSpec as P

HD = 64
NCORP = 8


EPS = 1e-05
EPS_HEAD = 1e-06
ROPE_BASE = 10000.0
BF = jnp.bfloat16
F32 = jnp.float32
MESH = pl.DeviceIdType.MESH
LAG = 2
AHEAD = 3
KEPT = 6


def rope_tables(positions):
    half = HD // 2
    rates = ROPE_BASE ** (-jnp.arange(half, dtype=jnp.float32) * 2.0 / HD)
    angle = positions.astype(jnp.float32)[:, None] * rates[None, :]
    return (jnp.cos(angle), jnp.sin(angle))


def rotate(vector, cosine, sine):
    half = vector.shape[-1] // 2
    first = vector[..., :half]
    second = vector[..., half:]
    return jnp.concatenate(
        [first * cosine - second * sine, second * cosine + first * sine], axis=-1
    )


def head_norm(vector, gain):
    inverse = lax.rsqrt(jnp.mean(vector * vector, axis=-1, keepdims=True) + EPS_HEAD)
    normed = vector * inverse
    return (normed, inverse, normed * gain)


def dot(a, b):
    return jnp.dot(a, b, preferred_element_type=F32)


def dot_tn(a, b):
    return lax.dot_general(a, b, (((0,), (0,)), ((), ())), preferred_element_type=F32)


def dot_nt(a, b):
    return lax.dot_general(a, b, (((1,), (1,)), ((), ())), preferred_element_type=F32)


def take(array, start, size, axis=0):
    return lax.dynamic_slice_in_dim(array, start, size, axis)


class Links:
    def __init__(self):
        self.seq = lax.axis_size("seq")
        self.tp = lax.axis_size("tp")
        self.nodes = self.seq // 2
        self.bits = self.tp.bit_length() - 1
        rank = lax.axis_index("seq")
        self.node = rank // 2
        self.side = rank % 2
        self.t = lax.axis_index("tp")

    def swap_side(self, value):
        return lax.ppermute(value, "seq", [(s, s ^ 1) for s in range(self.seq)])

    def swap_bit(self, value, bit):
        return lax.ppermute(value, "tp", [(r, r ^ (1 << bit)) for r in range(self.tp)])

    def relative(self, rows):
        share = rows.shape[0] // self.tp
        return jnp.concatenate(
            [take(rows, (self.t ^ j) * share, share) for j in range(self.tp)], axis=0
        )


def remote_copy(src, dst, send, recv, **where):
    return pltpu.make_async_remote_copy(
        src, dst, send, recv, device_id=where, device_id_type=MESH
    )


def attend_kernel(
    nodes,
    bits,
    kv_heads,
    q_ref,
    kv_ref,
    count_ref,
    cot_ref,
    x_ref,
    gain_ref,
    w_ref,
    att_ref,
    log_ref,
    counts_ref,
    cot_out,
    resid_ref,
    a_out,
    kv_in,
    acc,
    weight_sum,
    att_in,
    parts,
    got,
    a_mine,
    kv_send,
    kv_recv,
    count_send,
    count_recv,
    cot_send,
    cot_recv,
    att_sem,
    sum_send,
    sum_recv,
    all_send,
    all_recv,
    own_sem,
):
    tp = 1 << bits
    seq = 2 * nodes
    rank, t = lax.axis_index("seq"), lax.axis_index("tp")
    node, side = rank // 2, rank % 2
    across = rank + 1 - 2 * side
    n_q, wide = q_ref.shape[0], q_ref.shape[1]
    n_rows = kv_ref.shape[0]
    heads = n_q // n_rows
    group = heads // kv_heads
    span = wide // 2
    share, width = x_ref.shape
    top = bits - 1

    def flip(bit):
        return t + (1 << bit) * (1 - 2 * ((t // (1 << bit)) % 2))

    def block_of(j):
        other = t
        for bit in range(bits):
            if (j >> bit) & 1:
                other = other + (1 << bit) * (1 - 2 * ((t // (1 << bit)) % 2))
        return other

    barrier = pltpu.get_barrier_semaphore()
    for step in range(1, seq):
        pl.semaphore_signal(
            barrier, 1, device_id={"seq": (rank + step) % seq}, device_id_type=MESH
        )
    for bit in range(bits):
        pl.semaphore_signal(barrier, 1, device_id={"tp": flip(bit)}, device_id_type=MESH)
    pl.semaphore_wait(barrier, seq - 1 + bits)

    for step in range(1, nodes):

        @pl.when(node + step < nodes)
        def _():
            remote_copy(
                kv_ref,
                kv_in.at[step - 1],
                kv_send.at[step - 1],
                kv_recv.at[step - 1],
                seq=rank + 2 * step,
            ).start()

    counts_ref[0] = count_ref[...]
    count_copies = [
        remote_copy(
            count_ref,
            counts_ref.at[step],
            count_send.at[step - 1],
            count_recv.at[step - 1],
            seq=(rank + step) % seq,
        )
        for step in range(1, seq)
    ]
    for copy in count_copies:
        copy.start()
    cot_copies = []
    for j in range(0, tp, 2):
        rows = pl.ds(pl.multiple_of(block_of(j) * share, share), share)
        cot_copies.append(
            remote_copy(
                cot_ref.at[rows], cot_out.at[j], cot_send.at[j], cot_recv.at[j], seq=across
            )
        )
        cot_copies[-1].start()

    def attend(kv_at, diagonal):
        @pl.loop(0, n_q)
        def _(i):
            kv = kv_at(i // heads, (i % heads) // group)
            scores = lax.dot_general(
                q_ref[i], kv, (((1,), (1,)), ((), ())), preferred_element_type=F32
            )
            weight = jnp.exp2(scores * (HD**-0.5 * 1.4426950408889634))
            if diagonal:
                q_at = lax.broadcasted_iota(jnp.int32, (wide, wide), 0)
                k_at = lax.broadcasted_iota(jnp.int32, (wide, wide), 1)
                q_at = jnp.where(q_at < span, q_at + span * side, q_at - span * side)
                k_at = jnp.where(k_at < span, k_at + span * side, k_at - span * side)
                weight = jnp.where(k_at <= q_at, weight, 0.0)
            sums = weight[:, :128]
            for c in range(128, wide, 128):
                sums = sums + weight[:, c : c + 128]
            values = jnp.dot(weight.astype(BF), kv, preferred_element_type=F32)
            if diagonal:
                weight_sum[i] = sums
                acc[i] = values
            else:
                weight_sum[i] += sums
                acc[i] += values

    attend(lambda r, h: kv_ref[r, h], True)
    for step in range(1, nodes):

        @pl.when(node >= step)
        def _():
            remote_copy(
                kv_ref,
                kv_in.at[step - 1],
                kv_send.at[step - 1],
                kv_recv.at[step - 1],
                seq=rank,
            ).wait_recv()
            attend(lambda r, h: kv_in[step - 1, r, h], False)

    att_copy = remote_copy(
        att_ref.at[1], att_in, att_sem.at[0], att_sem.at[1], seq=across
    )
    lane = lax.broadcasted_iota(jnp.int32, (span, 2 * HD), 1)
    for d in (1, 0):
        for r in range(n_rows):
            for h in range(0, heads, 2):
                out = []
                for k in range(2):
                    i = r * heads + h + k
                    at = pl.ds(d * span, span)
                    total = jnp.sum(weight_sum[i, at, :], axis=-1, keepdims=True)
                    log_ref[i, at, :] = jnp.log2(total)
                    out.append(acc[i, at, :] / total)
                both = jnp.where(lane < HD, pltpu.roll(out[0], HD, 1), out[1])
                att_ref[d, pl.ds(r * span, span), pl.ds(h * HD, 2 * HD)] = both.astype(BF)
        if d == 1:
            att_copy.start()

    half = w_ref.shape[0] // 2
    w_mine = w_ref[pl.ds(pl.multiple_of(side * half, half), half), :]
    w_other = w_ref[pl.ds(pl.multiple_of((1 - side) * half, half), half), :]

    def project(j, add):
        rows = pl.ds(pl.multiple_of(block_of(j) * share, share), share)
        if not add:
            parts[j] = jnp.dot(att_ref[0, rows, :], w_mine, preferred_element_type=F32)
        else:
            parts[j] += jnp.dot(att_in[rows, :], w_other, preferred_element_type=F32)

    for j in range(tp):
        project(j, False)
    att_copy.wait()
    order = sorted(range(tp), key=lambda j: -(j & 1))
    for j in order:
        project(j, True)

    held = list(range(tp))
    slot = 0
    for bit in range(bits):
        keep = [j for j in held if not (j >> bit) & 1]
        copies = []
        for j in keep:
            a_mine[slot] = parts[j | (1 << bit)].astype(BF)
            copies.append(
                remote_copy(
                    a_mine.at[slot], got.at[slot], sum_send.at[slot], sum_recv.at[slot],
                    tp=flip(bit),
                )
            )
            copies[-1].start()
            slot += 1
        for k, j in enumerate(keep):
            copies[k].wait()
            parts[j] += got[slot - len(keep) + k].astype(F32)
        held = keep
    resid = x_ref[...].astype(F32) + parts[0]
    resid_ref[...] = resid
    inverse = lax.rsqrt(jnp.mean(resid * resid, axis=-1, keepdims=True) + EPS)
    a_mine[slot] = (resid * inverse * gain_ref[...]).astype(BF)
    mine = a_mine.at[slot]

    started = []

    def send(src, dst, k, **where):
        copy = remote_copy(src, dst, all_send.at[k], all_recv.at[k], **where)
        copy.start()
        started.append(copy)
        return copy

    up = 1 << top
    cut = share // 2
    low, high = pl.ds(0, cut), pl.ds(cut, cut)
    by_side = send(mine, a_out.at[1, 0], 0, seq=across)
    by_top = send(mine, a_out.at[0, up], 1, tp=flip(top))
    put = pltpu.make_async_copy(mine, a_out.at[0, 0], own_sem)
    put.start()
    k = 4
    for copy in cot_copies:
        copy.wait()
    cot_copies = []
    for j in range(0, tp, 2):
        cot_copies.append(
            remote_copy(
                cot_out.at[j], cot_out.at[j + 1], cot_send.at[j + 1], cot_recv.at[j + 1],
                tp=flip(0),
            )
        )
        cot_copies[-1].start()
    pending = {}
    for bit in reversed(range(top)):
        have = [j for j in range(tp) if j % (2 << bit) == 0]
        if bit == top - 1:
            pending[0, 0] = send(mine, a_out.at[0, 1 << bit], k, tp=flip(bit))
            k += 1
            by_side.wait_recv()
            far_low = send(a_out.at[1, 0, low], a_out.at[1, up, low], 2, tp=flip(top))
            pending[1, 0] = send(a_out.at[1, 0], a_out.at[1, 1 << bit], k, tp=flip(bit))
            k += 1
            by_top.wait_recv()
            far_high = send(a_out.at[0, up, high], a_out.at[1, up, high], 3, seq=across)
            pending[0, up] = send(a_out.at[0, up], a_out.at[0, up | 1 << bit], k, tp=flip(bit))
            k += 1
            far_low.wait_recv()
            far_high.wait_recv()
            pending[1, up] = send(a_out.at[1, up], a_out.at[1, up | 1 << bit], k, tp=flip(bit))
            k += 1
        else:
            for d in range(2):
                for j in have:
                    pending[d, j] = send(
                        a_out.at[d, j], a_out.at[d, j | 1 << bit], k, tp=flip(bit)
                    )
                    k += 1
        for copy in pending.values():
            copy.wait_recv()
        pending = {}
    for copy in started:
        copy.wait_send()
    put.wait()
    for copy in count_copies + cot_copies:
        copy.wait()
    for step in range(1, nodes):

        @pl.when(node + step < nodes)
        def _():
            remote_copy(
                kv_ref,
                kv_in.at[step - 1],
                kv_send.at[step - 1],
                kv_recv.at[step - 1],
                seq=rank,
            ).wait_send()


def attend(nodes, bits, kv_heads, q, kv, count, cotangent, x_share, gain, w_out, ident):
    tp = 1 << bits
    seq = 2 * nodes
    n_q, wide, _ = q.shape
    n_rows = kv.shape[0]
    heads = n_q // n_rows
    share, width = x_share.shape
    vmem = pl.BlockSpec(memory_space=pltpu.VMEM)
    anywhere = pl.BlockSpec(memory_space=pl.ANY)
    dma = pltpu.SemaphoreType.DMA
    tokens = tp * share
    messages = 4 + 2 * (tp - 2)
    return pl.pallas_call(
        functools.partial(attend_kernel, nodes, bits, kv_heads),
        out_shape=[
            jax.ShapeDtypeStruct((2, tokens, heads * HD), BF),
            jax.ShapeDtypeStruct((n_q, wide, 1), F32),
            jax.ShapeDtypeStruct((seq,) + count.shape, F32),
            jax.ShapeDtypeStruct((tp, share, width), BF),
            jax.ShapeDtypeStruct((share, width), F32),
            jax.ShapeDtypeStruct((2, tp, share, width), BF),
            jax.ShapeDtypeStruct((nodes - 1,) + kv.shape, BF),
        ],
        in_specs=[vmem, vmem, vmem, anywhere, vmem, vmem, vmem],
        out_specs=[vmem, vmem, vmem, anywhere, vmem, anywhere, vmem],
        scratch_shapes=[
            pltpu.VMEM((n_q, wide, 2 * HD), F32),
            pltpu.VMEM((n_q, wide, 128), F32),
            pltpu.VMEM((tokens, heads * HD), BF),
            pltpu.VMEM((tp, share, width), F32),
            pltpu.VMEM((tp - 1, share, width), BF),
            pltpu.VMEM((tp, share, width), BF),
            dma((nodes - 1,)),
            dma((nodes - 1,)),
            dma((seq - 1,)),
            dma((seq - 1,)),
            dma((tp,)),
            dma((tp,)),
            dma((2,)),
            dma((tp - 1,)),
            dma((tp - 1,)),
            dma((messages,)),
            dma((messages,)),
            dma,
        ],
        compiler_params=pltpu.CompilerParams(
            collective_id=ident, has_side_effects=True, vmem_limit_bytes=48 << 20
        ),
        cost_estimate=pl.CostEstimate(
            flops=0, bytes_accessed=200 << 20, transcendentals=0
        ),
        name="attend",
    )(q, kv, count, cotangent, x_share, gain, w_out)


def backward_kernel(nodes, bits, *refs):
    names = (
        "a_two", "grad_low", "w_gate", "w_up", "w_down", "resid", "grad", "x", "gain_two",
        "gain_one", "gain_q", "gain_k", "w_out", "w_back", "a_one", "q", "kv", "kv_in", "att",
        "log", "raw_q", "raw_k", "cosine", "sine", "gate_sum", "up_sum", "down_sum", "out_sum",
        "q_sum", "kv_sum", "out", "tokens", "gains", "two_in", "ffn_in", "one_in", "gate_part",
        "up_part", "down_part", "red", "own", "hold", "temp", "low", "a_in", "a_t", "w_rows",
        "q_in", "d_out", "d_q", "d_kv", "kv_all", "att_in", "d_att", "delta", "d_raw", "q_part",
        "kv_part", "out_part", "kv_back", "kv_far", "d_resid", "fresh", "gain_rows", "gain_box",
        "gain_all", "log_in", "hidden", "d_pair", "w_strip", "w_cols", "stage", "stage_down",
        "own_sem", "red_send", "red_recv", "fin_send", "fin_recv", "x_send", "x_recv", "put_sem",
        "load_sem", "sum_send", "sum_recv", "temp_sem", "low_send", "low_recv", "kv_send",
        "kv_recv", "tok_send", "tok_recv", "tok_put", "gain_send", "gain_recv", "w_sem",
        "stage_sem",
    )
    assert len(names) == len(refs)
    R = dict(zip(names, refs))
    tp, seq = 1 << bits, 2 * nodes
    top = bits - 1
    rank, t = lax.axis_index("seq"), lax.axis_index("tp")
    node, side = rank // 2, rank % 2
    across = rank + 1 - 2 * side
    last = nodes - 1
    me = rank * tp + t
    total = seq * tp
    share, width = R["x"].shape
    n_q, wide, _ = R["q"].shape
    n_rows = R["kv"].shape[0]
    heads = n_q // n_rows
    span = wide // 2
    slots, prow, pcol = R["red"].shape[1:]
    half = R["red_send"].shape[1]
    ff = R["gate_part"].shape[1]
    chunks = ff // pcol
    tall = width // prow
    per_chunk = 3 * tall
    fed = chunks * per_chunk

    def strips(rows, step, body):
        @pl.loop(0, rows // step)
        def _(m):
            body(pl.ds(pl.multiple_of(m * step, step), step))

    def flip(bit):
        return t + (1 << bit) * (1 - 2 * ((t // (1 << bit)) % 2))

    def block_of(j):
        other = t
        for bit in range(bits):
            there = (j // (1 << bit)) % 2
            other = other + there * (1 << bit) * (1 - 2 * ((t // (1 << bit)) % 2))
        return other

    def block_rows(j):
        return pl.ds(pl.multiple_of(block_of(j) * share, share), share)

    barrier = pltpu.get_barrier_semaphore()

    @pl.loop(1, total)
    def _(k):
        other = (me + k) % total
        pl.semaphore_signal(
            barrier, 1, device_id={"seq": other // tp, "tp": other % tp}, device_id_type=MESH
        )

    pl.semaphore_wait(barrier, total - 1)

    red, own = R["red"], R["own"]
    own_sem, put_sem = R["own_sem"], R["put_sem"]
    red_sems = R["red_send"], R["red_recv"]
    fin_sems = R["fin_send"], R["fin_recv"]
    x_sems = R["x_send"], R["x_recv"]

    def with_piece(b, j, act):
        p = 2 * j + b
        chunk, k, kind = p // per_chunk, p % tall, (p % per_chunk) // tall
        along_chunk = pl.multiple_of(chunk * pcol, pcol)
        along_side = pl.multiple_of(side * ff + chunk * pcol, pcol)
        along_width = pl.ds(pl.multiple_of(k * prow, prow), prow)
        for i, name in enumerate(("gate", "up", "down")):

            @pl.when((p < fed) & (kind == i))
            def _(name=name):
                part, whole = R[name + "_part"], R[name + "_sum"]
                if name == "down":
                    act(
                        part.at[pl.ds(along_chunk, prow), along_width],
                        whole.at[pl.ds(along_side, prow), along_width],
                    )
                else:
                    act(
                        part.at[along_width, pl.ds(along_chunk, pcol)],
                        whole.at[along_width, pl.ds(along_side, pcol)],
                    )

        base = fed
        for name in ("out", "q", "kv"):
            part, whole = R[name + "_part"], R[name + "_sum"]
            size = part.shape[1] // pcol

            @pl.when((p >= base) & (p < base + size))
            def _(part=part, whole=whole, base=base):
                col = pl.ds(pl.multiple_of((p - base) * pcol, pcol), pcol)
                act(
                    part.at[:, col],
                    whole.at[pl.ds(pl.multiple_of(side * prow, prow), prow), col],
                )

            base += size

    def along(src, dst, sems, b, j, target):
        return remote_copy(src, dst, sems[0].at[b, j], sems[1].at[b, j], seq=target)

    def placed(j):
        if gap == 0:
            return j, (j >= 0) & (j < half)
        after = j >= late + gap
        return jnp.where(after, j - gap, j), ((j >= 0) & (j < late)) | (
            after & (j < half + gap)
        )

    def stream(b, i):
        v = node if b == 0 else last - node
        ahead = rank + 2 if b == 0 else rank - 2
        behind = rank - 2 if b == 0 else rank + 2
        f, there = placed(i - LAG * v + AHEAD - 1)

        @pl.when((v > 0) & there)
        def _():
            with_piece(
                b,
                f,
                lambda src, dst: pltpu.make_async_copy(
                    src, own.at[b, f % AHEAD], own_sem.at[b, f % AHEAD]
                ).start(),
            )

        j, there = placed(i - LAG * v)

        @pl.when((v == 0) & there)
        def _():
            with_piece(
                b, j, lambda src, dst: along(src, red.at[b, j % slots], red_sems, b, j, ahead).start()
            )

        @pl.when((v > 0) & there)
        def _():
            mine = own.at[b, j % AHEAD]
            pltpu.make_async_copy(mine, mine, own_sem.at[b, j % AHEAD]).wait()
            along(red.at[b, j % slots], red.at[b, j % slots], red_sems, b, j, behind).wait_recv()
            at = j % slots

            def add(r):
                red[b, at, r] = (
                    red[b, at, r].astype(F32) + own[b, j % AHEAD, r].astype(F32)
                ).astype(BF)

            strips(prow, 64, add)

            @pl.when(v < last)
            def _():
                along(red.at[b, j % slots], red.at[b, j % slots], red_sems, b, j, ahead).start()

            @pl.when((v == last) & (j >= KEPT))
            def _():
                along(red.at[b, 0], red.at[b, 0], x_sems, b, j - KEPT, across).wait_send()
                along(red.at[b, 0], red.at[b, 0], fin_sems, b, j - KEPT, behind).wait_send()
                pltpu.make_async_copy(red.at[b, 0], red.at[b, 0], put_sem.at[b, j - KEPT]).wait()

            @pl.when(v == last)
            def _():
                def act(src, dst):
                    along(red.at[b, j % slots], dst, fin_sems, b, j, behind).start()
                    along(red.at[b, j % slots], dst, x_sems, b, j, across).start()
                    pltpu.make_async_copy(red.at[b, j % slots], dst, put_sem.at[b, j]).start()

                with_piece(b, j, act)

        g, there = placed(i - LAG * last - LAG * (last - v))

        @pl.when((v < last) & there)
        def _():
            along(red.at[b, 0], red.at[b, 0], fin_sems, b, g, ahead).wait_recv()

            @pl.when(v > 0)
            def _():
                along(red.at[b, 0], red.at[b, 0], red_sems, b, g, ahead).wait_send()

            def act(src, dst):
                @pl.when(v > 0)
                def _():
                    along(dst, dst, fin_sems, b, g, behind).start()

                along(dst, dst, x_sems, b, g, across).start()

            with_piece(b, g, act)

    hold, temp = R["hold"], R["temp"]
    boxes = [R["two_in"], R["ffn_in"], R["one_in"]]

    def held(ref, d, k):
        return ref.at[pl.ds((d * (tp // 2) + k) * share, share)]

    def messages(bit):
        base = sum(tp >> b for b in range(bit))
        keep = [(d, j) for d in range(2) for j in range(0, tp, 2 << bit)]
        return [(base + k, d, j) for k, (d, j) in enumerate(keep)]

    def sum_copy(n, m, src, **where):
        return remote_copy(
            src, boxes[n].at[m], R["sum_send"].at[n, m], R["sum_recv"].at[n, m], **where
        )

    def sum_start(n, bit):
        for m, d, j in messages(bit):
            src = held(temp, d, j // 2) if bit == 0 else held(hold, d, (j | 1 << bit) // 2)
            sum_copy(n, m, src, tp=flip(bit)).start()

    def sum_add(n, bit):
        for m, d, j in messages(bit):
            sum_copy(n, m, held(temp, d, j // 2), tp=flip(bit)).wait()
        loads = []
        for m, d, j in messages(bit):
            k = j // 2
            loads.append(
                pltpu.make_async_copy(boxes[n].at[m], held(temp, d, k), R["temp_sem"].at[d, k])
            )
            loads[-1].start()
        for copy, (m, d, j) in zip(loads, messages(bit)):
            copy.wait()
            base = (d * (tp // 2) + j // 2) * share

            def add(r, base=base):
                at = pl.ds(pl.multiple_of(base + r.start, 16), 16)
                hold[at, :] = (hold[at, :].astype(F32) + temp[at, :].astype(F32)).astype(BF)

            strips(share, 16, add)

    final = 2 * (tp - 1)

    def side_start(n):
        sum_copy(n, final, held(hold, 1, 0), seq=across).start()

    def side_finish(n):
        sum_copy(n, final, held(hold, 1, 0), seq=across).wait()
        load = pltpu.make_async_copy(boxes[n].at[final], held(temp, 0, 0), R["temp_sem"].at[0, 0])
        load.start()
        load.wait()

    def side_sum(r):
        return hold[r, :].astype(F32) + temp[r, :].astype(F32)

    ends = [R["out"], R["tokens"]]

    def token_copy(n, k, src, j, bit):
        return remote_copy(
            src,
            ends[n].at[block_of(j)],
            R["tok_send"].at[n, k],
            R["tok_recv"].at[n, k],
            tp=flip(bit),
        )

    def token_messages(bit):
        base = sum(tp >> (b + 1) for b in range(bit + 1, bits))
        return [(base + k, j) for k, j in enumerate(range(0, tp, 2 << bit))]

    def tokens_start(n, bit):
        for k, j in token_messages(bit):
            src = R["fresh"].at[n] if j == 0 else ends[n].at[block_of(j)]
            token_copy(n, k, src, j, bit).start()

    def tokens_wait(n, bit):
        for k, j in token_messages(bit):
            token_copy(n, k, R["fresh"].at[n], j, bit).wait()

    def tokens_put(n):
        return pltpu.make_async_copy(R["fresh"].at[n], ends[n].at[t], R["tok_put"].at[n])

    def block(d, j):
        return pl.ds((d * tp + j) * share, share)

    loads = [
        (R["w_out"].at[pl.ds(pl.multiple_of(side * heads * HD, heads * HD), heads * HD)], R["w_rows"]),
        (R["w_back"], R["a_t"].at[:, pl.ds(0, R["w_back"].shape[1])]),
        (R["a_one"], R["a_in"]),
        (R["q"], R["q_in"]),
        (R["kv"], R["kv_all"].at[0]),
        (R["kv_in"], R["kv_all"].at[pl.ds(1, nodes - 1)]),
        (R["att"], R["att_in"]),
        (R["log"], R["log_in"]),
        (R["a_two"], R["low"]),
        (R["grad_low"], R["a_in"]),
    ]

    def load(k):
        return pltpu.make_async_copy(loads[k][0], loads[k][1], R["load_sem"].at[k])

    w_cols, w_sem = R["w_cols"], R["w_sem"]
    both = 2 * tp * share
    nt = (((1,), (1,)), ((), ()))
    tn = (((0,), (0,)), ((), ()))

    def chunk_loads(c):
        at = pl.multiple_of(side * ff + c * pcol, pcol)
        slot = c % 2
        down_at = pl.multiple_of(slot * pcol, pcol)
        return [
            pltpu.make_async_copy(
                R["w_gate"].at[:, pl.ds(at, pcol)], w_cols.at[slot, 0], w_sem.at[slot, 0]
            ),
            pltpu.make_async_copy(
                R["w_up"].at[:, pl.ds(at, pcol)], w_cols.at[slot, 1], w_sem.at[slot, 1]
            ),
            pltpu.make_async_copy(
                R["w_down"].at[pl.ds(at, pcol)],
                hold.at[pl.ds(down_at, pcol)],
                w_sem.at[slot, 2],
            ),
        ]

    def begin():
        load(8).start()
        for copy in chunk_loads(0):
            copy.start()
        load(9).start()
        for copy in chunk_loads(1):
            copy.start()
        for k in (0, 3, 4, 5, 6, 7):
            load(k).start()
        load(8).wait()
        load(9).wait()

    def chunk_forward(c):
        for copy in chunk_loads(c):
            copy.wait()
        slot = c % 2
        cols = pl.ds(pl.multiple_of(c * pcol, pcol), pcol)
        w_rows = hold.at[pl.ds(pl.multiple_of(slot * pcol, pcol), pcol)]

        def body(at):
            gate = jnp.dot(R["low"][at, :], w_cols[slot, 0], preferred_element_type=F32)
            up = jnp.dot(R["low"][at, :], w_cols[slot, 1], preferred_element_type=F32)
            d_hidden = lax.dot_general(
                R["a_in"][at, :], w_rows[...], nt, preferred_element_type=F32
            )
            sigma = 1.0 / (1.0 + jnp.exp(-gate))
            smooth = gate * sigma
            R["hidden"][at, cols] = (smooth * up).astype(BF)
            R["d_pair"][1, at, cols] = (d_hidden * smooth).astype(BF)
            R["d_pair"][0, at, cols] = (
                d_hidden * up * (sigma * (1.0 + gate - smooth))
            ).astype(BF)

        strips(both, 256, body)

        @pl.when(c + 2 < chunks)
        def _():
            for copy in chunk_loads(c + 2):
                copy.start()

    def turn():
        def body(at):
            R["a_t"][:, at] = R["low"][at, :].T

        strips(both, 256, body)

    def stage_copies(c):
        at = pl.ds(pl.multiple_of(c * pcol, pcol), pcol)
        sem = R["stage_sem"]
        return [
            pltpu.make_async_copy(R["stage"].at[0], R["gate_part"].at[:, at], sem.at[0]),
            pltpu.make_async_copy(R["stage"].at[1], R["up_part"].at[:, at], sem.at[1]),
            pltpu.make_async_copy(R["stage_down"], R["down_part"].at[at], sem.at[2]),
        ]

    def chunk_gradients(c):
        cols = pl.ds(pl.multiple_of(c * pcol, pcol), pcol)

        @pl.loop(0, 2)
        def _(k):
            def body(at):
                R["stage"][k, at, :] = jnp.dot(
                    R["a_t"][at, :], R["d_pair"][k, :, cols], preferred_element_type=F32
                ).astype(BF)

            strips(width, 512, body)

        def body(at):
            R["stage_down"][:, at] = lax.dot_general(
                R["hidden"][:, cols], R["a_in"][:, at], tn, preferred_element_type=F32
            ).astype(BF)

        strips(width, 512, body)
        for copy in stage_copies(c):
            copy.start()

    def staged(c):
        for copy in stage_copies(c):
            copy.wait()

    def row_loads(n):
        rows = pl.ds(pl.multiple_of(n * pcol, pcol), pcol)
        cols = pl.ds(pl.multiple_of(side * ff, ff), ff)
        return [
            pltpu.make_async_copy(
                R[name].at[rows, cols], R["w_strip"].at[n % 2, k], w_sem.at[n % 2, k]
            )
            for k, name in enumerate(("w_gate", "w_up"))
        ]

    def down_loads(n):
        return [
            pltpu.make_async_copy(
                R["w_down"].at[
                    pl.ds(pl.multiple_of(side * ff, ff), ff),
                    pl.ds(pl.multiple_of(n * pcol, pcol), pcol),
                ],
                w_cols.at[n % 2, 0, pl.ds(0, ff)],
                w_sem.at[n % 2, 0],
            )
        ]

    def start_all(copies):
        for copy in copies:
            copy.start()

    def by_columns(low_n, high_n, loads, product):
        @pl.loop(low_n, high_n)
        def _(n):
            for copy in loads(n):
                copy.wait()
            cols = pl.ds(pl.multiple_of(n * pcol, pcol), pcol)

            @pl.loop(0, 2)
            def _(d):
                at = pl.ds(pl.multiple_of(d * tp * share, tp * share), tp * share)
                value = product(at, n % 2).astype(BF)
                for j in range(tp):
                    rows = pl.ds(
                        pl.multiple_of((d * (tp // 2) + j // 2) * share, share), share
                    )
                    (temp if j % 2 else hold)[rows, cols] = value[j * share : (j + 1) * share]

            @pl.when(n + 2 < width // pcol)
            def _():
                start_all(loads(n + 2))

    def second_part(low_n, high_n):
        def product(at, slot):
            value = lax.dot_general(
                R["d_pair"][0, at, :], R["w_strip"][slot, 0], nt, preferred_element_type=F32
            )
            return value + lax.dot_general(
                R["d_pair"][1, at, :], R["w_strip"][slot, 1], nt, preferred_element_type=F32
            )

        by_columns(low_n, high_n, row_loads, product)

    def ffn_part(low_n, high_n):
        def product(at, slot):
            return jnp.dot(
                R["hidden"][at, :], w_cols[slot, 0, 0:ff, :], preferred_element_type=F32
            )

        by_columns(low_n, high_n, down_loads, product)

    def normed(v):
        inverse = lax.rsqrt(jnp.mean(v * v, axis=-1, keepdims=True) + EPS)
        return v * inverse, inverse

    low = R["low"]

    def low_at(d, j):
        return low.at[block(d, j)]

    def low_copy(k, src, dst, **where):
        return remote_copy(src, dst, R["low_send"].at[k], R["low_recv"].at[k], **where)

    up = 1 << top
    low_side = low_copy(0, low_at(0, 0), low_at(1, 0), seq=across)
    low_top = low_copy(1, low_at(0, 0), low_at(0, up), tp=flip(top))
    low_far = low_copy(2, low_at(1, 0), low_at(1, up), tp=flip(top))

    def low_bit(bit):
        base = 3 + sum(tp >> b for b in range(bit + 1, top))
        return [
            low_copy(base + k, low_at(d, j), low_at(d, j | 1 << bit), tp=flip(bit))
            for k, (d, j) in enumerate(
                (d, j) for d in range(2) for j in range(0, tp, 2 << bit)
            )
        ]

    def second_norm():
        side_finish(0)
        R["gain_rows"][...] = jnp.zeros_like(R["gain_rows"])

        def body(r):
            d_a = side_sum(r)
            n_two, inverse = normed(R["resid"][r, :])
            R["gain_rows"][1:2, :] += jnp.sum(d_a * n_two, axis=0, keepdims=True)
            e = d_a * R["gain_two"][...]
            d_resid = R["grad"][r, :] + inverse * (
                e - n_two * jnp.mean(e * n_two, axis=-1, keepdims=True)
            )
            R["d_resid"][r, :] = d_resid
            low[r, :] = d_resid.astype(BF)

        strips(share, 16, body)
        low_side.start()
        low_top.start()

    lane = lax.broadcasted_iota(jnp.int32, (span, 2 * HD), 1)

    def attended_back():
        for k in (0, 6):
            load(k).wait()
        R["d_kv"][...] = jnp.zeros_like(R["d_kv"])
        R["d_q"][...] = jnp.zeros_like(R["d_q"])
        @pl.loop(0, 2)
        def _(d):
            value = lax.dot_general(
                low[pl.ds(pl.multiple_of(d * tp * share, tp * share), tp * share), :],
                R["w_rows"][...],
                nt,
                preferred_element_type=F32,
            ).astype(BF)
            for j in range(tp):
                R["d_att"][d, block_rows(j), :] = value[j * share : (j + 1) * share]

        ones = jnp.ones((8, 2 * HD), F32)
        pairs = heads // 2

        @pl.loop(0, 2 * n_rows * pairs)
        def _(n):
            d, r, h = n // (n_rows * pairs), n // pairs % n_rows, n % pairs
            cols = pl.ds(pl.multiple_of(h * 2 * HD, 2 * HD), 2 * HD)
            rows = pl.ds(pl.multiple_of(r * span, span), span)
            at = pl.ds(pl.multiple_of(d * span, span), span)
            for k in range(2):
                grads = R["d_att"][d, rows, cols].astype(F32)
                values = R["att_in"][d, rows, cols].astype(F32)
                if k == 0:
                    grads = pltpu.roll(grads, HD, 1)
                    values = pltpu.roll(values, HD, 1)
                grads = jnp.where(lane < HD, 0.0, grads)
                i = r * heads + 2 * h + k
                R["d_out"][i, at, :] = grads.astype(BF)
                R["delta"][i, :, at] = lax.dot_general(
                    ones,
                    grads * values,
                    nt,
                    precision=lax.Precision.HIGHEST,
                    preferred_element_type=F32,
                )

    def put_folded(ref, c, value):
        rows, cols = value.shape
        at = pl.ds(pl.multiple_of(c // ref.shape[1] * rows, rows), rows)
        ref[at, pl.ds(pl.multiple_of(c % ref.shape[1], cols), cols)] = value.astype(BF)

    def out_gradient():
        chunk = 256

        @pl.loop(0, 2 * tp)
        def _(n):
            R["d_att"][n // tp, pl.ds(pl.multiple_of(n % tp * share, share), share), :] = R[
                "att_in"
            ][n // tp, block_rows(n % tp), :]

        @pl.loop(0, width // chunk)
        def _(n):
            c = pl.multiple_of(n * chunk, chunk)
            value = None
            for d in range(2):
                term = lax.dot_general(
                    R["d_att"][d],
                    low[d * tp * share : (d + 1) * tp * share, pl.ds(c, chunk)],
                    tn,
                    preferred_element_type=F32,
                )
                value = term if value is None else value + term
            put_folded(R["out_part"], c, value)

    def attention_block(piece, i, diagonal):
        r = i // heads
        kv = R["kv_all"][piece, r, 0]
        q, d_out = R["q_in"][i], R["d_out"][i]
        scores = lax.dot_general(kv, q, nt, preferred_element_type=F32)
        probs = jnp.exp2(scores * (HD**-0.5 * 1.4426950408889634) - R["log_in"][i])
        if diagonal:
            k_at = lax.broadcasted_iota(jnp.int32, (wide, wide), 0)
            q_at = lax.broadcasted_iota(jnp.int32, (wide, wide), 1)
            q_at = jnp.where(q_at < span, q_at + span * side, q_at - span * side)
            k_at = jnp.where(k_at < span, k_at + span * side, k_at - span * side)
            probs = jnp.where(k_at <= q_at, probs, 0.0)
        d_probs = lax.dot_general(kv, d_out, nt, preferred_element_type=F32)
        d_scores = (probs * (d_probs - R["delta"][i, 0:1, :])).astype(BF)
        R["d_kv"][piece, r] += jnp.dot(d_scores, q, preferred_element_type=F32) + jnp.dot(
            probs.astype(BF), d_out, preferred_element_type=F32
        ) * (HD**0.5)
        R["d_q"][i] += lax.dot_general(
            kv, d_scores, (((0,), (0,)), ((), ())), preferred_element_type=F32
        )

    def kv_copy(step):
        return remote_copy(
            R["kv_back"].at[step - 1],
            R["kv_far"].at[step - 1],
            R["kv_send"].at[step - 1],
            R["kv_recv"].at[step - 1],
            seq=rank - 2 * step,
        )

    def kv_send():
        for step in range(1, nodes):

            @pl.when(node >= step)
            def _():
                R["kv_back"][step - 1] = R["d_kv"][step].astype(BF)
                kv_copy(step).start()

    def kv_sum():
        for step in range(1, nodes):

            @pl.when(node + step < nodes)
            def _():
                kv_copy(step).wait_recv()
                R["d_kv"][0] += R["kv_far"][step - 1].astype(F32)

            @pl.when(node >= step)
            def _():
                kv_copy(step).wait_send()

    def head_back(grads, raw, gain, at):
        lanes = 2 * HD
        low_lane = lane < HD // 2
        swapped = jnp.where(
            low_lane, pltpu.roll(grads, lanes - HD // 2, 1), pltpu.roll(grads, HD // 2, 1)
        )
        rotated = grads * R["cosine"][at, :] + swapped * R["sine"][at, :]
        inverse = lax.rsqrt(jnp.sum(raw * raw, axis=-1, keepdims=True) * (1.0 / HD) + EPS_HEAD)
        n = raw * inverse
        e = rotated * gain
        back = inverse * (e - n * (jnp.sum(e * n, axis=-1, keepdims=True) * (1.0 / HD)))
        return back, jnp.sum(rotated * n, axis=0, keepdims=True)

    def heads_back():
        scale = HD**-0.5
        pairs = heads // 2

        @pl.loop(0, 2 * n_rows)
        def _(n):
            r, d = n // 2, n % 2
            at = pl.ds(pl.multiple_of((d * n_rows + r) * span, span), span)
            here = pl.ds(pl.multiple_of(d * span, span), span)

            @pl.loop(0, pairs)
            def _(h):
                pair = []
                for k in range(2):
                    i = r * heads + 2 * h + k
                    grads = R["d_q"][i, :, here].T * scale
                    raw = R["raw_q"][i, here, :].astype(F32)
                    back, gain = head_back(grads, raw, R["gain_q"][...], at)
                    R["gain_rows"][2:3, 0 : 2 * HD] += gain
                    pair.append(back)
                R["d_raw"][at, pl.ds(pl.multiple_of(h * 2 * HD, 2 * HD), 2 * HD)] = jnp.where(
                    lane < HD, pair[0], pltpu.roll(pair[1], HD, 1)
                ).astype(BF)

            grads = R["d_kv"][0, r, here, :] * scale
            raw = R["raw_k"][r, here, :].astype(F32)
            back, gain = head_back(grads, raw, R["gain_k"][...], at)
            R["gain_rows"][3:4, 0 : 2 * HD] += gain
            R["d_raw"][at, pl.ds(heads * HD, 2 * HD)] = jnp.where(lane < HD, back, grads).astype(
                BF
            )

    def raw_gradient():
        load(2).wait()
        chunk = 256
        cut = heads * HD

        @pl.loop(0, width // chunk)
        def _(n):
            c = pl.multiple_of(n * chunk, chunk)
            value = lax.dot_general(
                R["d_raw"][...], R["a_in"][:, pl.ds(c, chunk)], tn, preferred_element_type=F32
            )
            put_folded(R["q_part"], c, value[:cut])
            put_folded(R["kv_part"], c, value[cut:])

    def first_part():
        load(1).wait()

        @pl.loop(0, tp)
        def _(n):
            d, k = n // (tp // 2), n % (tp // 2)
            out_rows = pl.ds(pl.multiple_of(n * share, share), share)
            for j, ref in ((2 * k, hold), (2 * k + 1, temp)):
                rows = pl.ds(pl.multiple_of((d * tp + block_of(j)) * share, share), share)
                ref[out_rows, :] = lax.dot_general(
                    R["d_raw"][rows, :],
                    R["a_t"][:, 0 : R["w_back"].shape[1]],
                    nt,
                    preferred_element_type=F32,
                ).astype(BF)

        sum_start(2, 0)

    def out_end():
        side_finish(1)

        def body(r):
            R["fresh"][0, r, :] = (R["resid"][r, :] + side_sum(r)).astype(BF)

        strips(share, 16, body)
        tokens_put(0).start()
        tokens_start(0, top)

    def first_norm():
        side_finish(2)

        def body(r):
            d_a = side_sum(r)
            n_one, inverse = normed(R["x"][r, :].astype(F32))
            R["gain_rows"][0:1, :] += jnp.sum(d_a * n_one, axis=0, keepdims=True)
            e = d_a * R["gain_one"][...]
            d_x = R["d_resid"][r, :] + inverse * (
                e - n_one * jnp.mean(e * n_one, axis=-1, keepdims=True)
            )
            R["fresh"][1, r, :] = d_x.astype(BF)

        strips(share, 16, body)
        tokens_put(1).start()
        tokens_start(1, top)
        part = width // tp
        for k in range(tp):
            R["gain_box"][k] = jnp.zeros((8, part), F32)
            R["gain_box"][k, 0:2, :] = R["gain_rows"][0:2, k * part : (k + 1) * part]
            R["gain_box"][k, 2:4, 0 : 2 * HD] = R["gain_rows"][2:4, 0 : 2 * HD]

        @pl.loop(1, total)
        def _(k):
            other = (me + k) % total
            remote_copy(
                R["gain_box"].at[other % tp],
                R["gain_all"].at[k],
                R["gain_send"].at[k],
                R["gain_recv"].at[k],
                seq=other // tp,
                tp=other % tp,
            ).start()

        R["gain_all"][0] = R["gain_box"][t]

    def gains_end():
        @pl.loop(1, total)
        def _(k):
            remote_copy(
                R["gain_box"].at[0],
                R["gain_all"].at[k],
                R["gain_send"].at[k],
                R["gain_recv"].at[k],
                seq=rank,
                tp=t,
            ).wait()

        R["gains"][...] = jnp.zeros_like(R["gains"])

        @pl.loop(0, total)
        def _(k):
            R["gains"][...] += R["gain_all"][k]

    tasks = {}

    def task(step, *acts):
        tasks.setdefault(step, []).extend(acts)
        return step

    def sums_tasks(n, step):
        for bit in range(bits):
            step += 2 if bit == 0 else 5
            following = (
                (lambda bit=bit: sum_start(n, bit + 1)) if bit < top else (lambda: side_start(n))
            )
            task(step, lambda bit=bit: sum_add(n, bit), following)
        return step + 5

    def token_tasks(n, step):
        for bit in reversed(range(bits)):
            step += 3
            task(step, lambda bit=bit: tokens_wait(n, bit))
            if bit:
                task(step, lambda bit=bit: tokens_start(n, bit - 1))
        task(step, lambda: tokens_put(n).wait())
        return step

    n_rows_w = width // pcol
    first_move = 1
    task(0, begin)
    step = chunks
    task(step, lambda: start_all(row_loads(0)), lambda: start_all(row_loads(1)))
    task(step, lambda: second_part(0, n_rows_w // 2))
    task(step + 1, lambda: second_part(n_rows_w // 2, n_rows_w), lambda: sum_start(0, 0))
    task(step + 1, lambda: start_all(down_loads(0)), lambda: start_all(down_loads(1)))
    grads_at = step + 2
    grads_end = grads_at + chunks - 1
    assert grads_end <= per_chunk // 2
    task(grads_end, load(1).start, load(2).start)
    step = task(sums_tasks(0, step + 1), second_norm)
    task(step + 1, lambda: ffn_part(0, n_rows_w // 2))
    ffn_at = task(step + 2, lambda: ffn_part(n_rows_w // 2, n_rows_w), lambda: sum_start(1, 0))
    step = task(step + 4, low_side.wait, low_top.wait, low_far.start)
    step += 3
    task(step, low_far.wait)
    for bit in reversed(range(top)):
        task(step, lambda bit=bit: [c.start() for c in low_bit(bit)])
        step += 2
        task(step, lambda bit=bit: [c.wait() for c in low_bit(bit)])
    task(step, attended_back)
    step = task(step + 1, out_gradient)
    ffn_end = task(sums_tasks(1, ffn_at), out_end)
    token_tasks(0, ffn_end)
    step = task(step + 1, *[load(k).wait for k in (3, 4, 5, 7)])
    first_block = step
    per_step = 4
    step += -(-(nodes * n_q) // per_step)
    last_block = step
    task(step, kv_send)
    step = task(step + 5, kv_sum, heads_back)
    step = task(step + 1, raw_gradient)
    raw_ready = step
    step = task(max(step, ffn_end) + 1, first_part)
    step = task(sums_tasks(2, step), first_norm)
    task(token_tasks(1, step), gains_end)

    late = half - (R["q_part"].shape[1] + R["kv_part"].shape[1]) // pcol // 2
    gap = max(0, raw_ready + 1 - late - first_move)
    steps = max(first_move + half + gap + 2 * LAG * last, max(tasks) + 1)

    @pl.loop(0, steps)
    def _(i):
        for b in range(2):
            stream(b, i - first_move)
        for at, acts in sorted(tasks.items()):

            @pl.when(i == at)
            def _(acts=acts):
                for act in acts:
                    act()

        @pl.when(i < chunks)
        def _():
            chunk_forward(i)

        pl.when(i == 0)(turn)

        @pl.when((i == 0) | ((i >= grads_at) & (i < grads_end)))
        def _():
            c = jnp.where(i == 0, 0, i - grads_at + 1)
            chunk_gradients(c)
            staged(c)

        @pl.when((i >= first_block) & (i < last_block))
        def _():
            @pl.loop(0, per_step)
            def _(k):
                n = (i - first_block) * per_step + k
                piece = n // n_q

                @pl.when(n < n_q)
                def _():
                    attention_block(0, n, True)

                @pl.when((n >= n_q) & (n < n_q * nodes) & (node >= piece))
                def _():
                    attention_block(piece, n % n_q, False)

    @pl.loop(0, half)
    def _(j):
        for b in range(2):
            v = node if b == 0 else last - node
            probe = red.at[b, 0]

            @pl.when(v == 0)
            def _():
                along(probe, probe, red_sems, b, j, rank).wait_send()

            @pl.when((v > 0) & ((v < last) | (j >= half - KEPT)))
            def _():
                along(probe, probe, fin_sems, b, j, rank).wait_send()

            @pl.when((v == last) & (j >= half - KEPT))
            def _():
                pltpu.make_async_copy(probe, probe, put_sem.at[b, j]).wait()

            @pl.when((v < last) | (j >= half - KEPT))
            def _():
                along(probe, probe, x_sems, b, j, rank).wait_send()

            along(probe, probe, x_sems, b, j, rank).wait_recv()


def backward(nodes, bits, ident, values):
    tp, seq = 1 << bits, 2 * nodes
    share, width = values["x"].shape
    ff = values["w_gate"].shape[1] // 2
    n_q, wide, _ = values["q"].shape
    n_rows = values["kv"].shape[0]
    heads = n_q // n_rows
    tokens = tp * share
    piece = 256
    cols = (heads + 2) * HD
    small = [(piece, r * width // piece) for r in (heads * HD, heads * HD, 2 * HD)]
    shapes = [(width, 2 * ff), (width, 2 * ff), (2 * ff, width)]
    shapes += [(2 * r, c) for r, c in small]
    half = (3 * width * ff + sum(r * c for r, c in small)) // (2 * piece * piece)
    slots = 2 * LAG * (nodes - 1) + 2
    vmem = pl.BlockSpec(memory_space=pltpu.VMEM)
    anywhere = pl.BlockSpec(memory_space=pl.ANY)
    dma = pltpu.SemaphoreType.DMA
    inside = ("resid", "grad", "x", "gain_two", "gain_one", "gain_q", "gain_k")
    inside += ("raw_q", "raw_k", "cosine", "sine")
    kv = values["kv"].shape
    total = seq * tp
    messages = 3 + 2 * (tp - 2)
    outs = shapes + [(tp, share, width)] * 2 + [(8, width // tp)]
    outs += [(2 * tp - 1, share, width)] * 3 + [(width, ff), (width, ff), (ff, width)]
    scratch = [
        (2, slots, piece, piece),
        (2, AHEAD, piece, piece),
        (tokens, width),
        (tokens, width),
        (2 * tokens, width),
        (2 * tokens, width),
        (width, 2 * tokens),
        (heads * HD, width),
        (n_q, wide, 2 * HD),
        (n_q, wide, 2 * HD),
        (n_q, 2 * HD, wide, F32),
        (nodes, n_rows, wide, 2 * HD, F32),
        (nodes,) + kv,
        (2, tokens, heads * HD),
        (2, tokens, heads * HD),
        (n_q, 8, wide, F32),
        (2 * tokens, cols),
        small[1],
        small[2],
        small[0],
        (nodes - 1, n_rows, wide, 2 * HD),
        (nodes - 1, n_rows, wide, 2 * HD),
        (share, width, F32),
        (2, share, width),
        (8, width, F32),
        (tp, 8, width // tp, F32),
        (total, 8, width // tp, F32),
        (n_q, 1, wide, F32),
        (2 * tokens, ff),
        (2, 2 * tokens, ff),
        (2, 2, piece, ff),
        (2, 2, width, piece),
        (2, width, piece),
        (piece, width),
    ]
    sems = [(2, AHEAD)] + [(2, half)] * 7 + [(10,), (3, 2 * tp - 1), (3, 2 * tp - 1)]
    sems += [(2, tp // 2), (messages,), (messages,), (nodes - 1,), (nodes - 1,)]
    sems += [(2, tp - 1), (2, tp - 1), (2,), (total,), (total,), (2, 3), (3,)]
    return pl.pallas_call(
        functools.partial(backward_kernel, nodes, bits),
        out_shape=[
            jax.ShapeDtypeStruct(shape, F32 if k == 8 else BF) for k, shape in enumerate(outs)
        ],
        in_specs=[vmem if k in inside else anywhere for k in values],
        out_specs=[vmem if k == 8 else anywhere for k in range(len(outs))],
        scratch_shapes=[
            pltpu.VMEM(s[:-1], F32) if s[-1] is F32 else pltpu.VMEM(s, BF) for s in scratch
        ]
        + [dma(s) for s in sems],
        compiler_params=pltpu.CompilerParams(
            collective_id=ident, has_side_effects=True, vmem_limit_bytes=62 << 20
        ),
        cost_estimate=pl.CostEstimate(
            flops=0, bytes_accessed=1 << 30, transcendentals=0
        ),
        name="backward",
    )(*values.values())[:9]


def per_device(
    tokens,
    positions,
    corpus,
    corpus_weight,
    gain_one,
    w_query,
    w_key,
    w_value,
    gain_query,
    gain_key,
    w_out,
    gain_two,
    w_gate,
    w_up,
    w_down,
    cotangent,
):
    net = Links()
    rows, per_row, width = tokens.shape
    count = rows * per_row
    share = count // net.tp
    total_len = per_row * net.seq
    side, node, t = net.side, net.node, net.t
    scale = HD ** (-0.5)
    q_cols = w_query.shape[1] // 2
    shared = (w_key.shape[1] // HD) % 2 == 1
    k_cols = w_key.shape[1] if shared else w_key.shape[1] // 2
    heads, kv_heads = q_cols // HD, k_cols // HD
    group = heads // kv_heads
    both = 2 * count

    x_rows = tokens.reshape(count, width).astype(F32)
    inverse_one = lax.rsqrt(jnp.mean(x_rows * x_rows, axis=-1, keepdims=True) + EPS)
    a_one = (x_rows * inverse_one * gain_one).astype(BF)

    def halves(w):
        cols = w.shape[1] // 2
        return take(w, side * cols, cols, 1), take(w, (1 - side) * cols, cols, 1)

    wq, wk, wv = halves(w_query), halves(w_key), halves(w_value)
    if shared:
        wk, wv = (w_key, w_key), (w_value, w_value)
    w_own = jnp.concatenate([wq[0], wk[0], wv[0]], axis=1)
    w_other = jnp.concatenate([wq[1], wk[1], wv[1]], axis=1)
    raw_other = net.swap_side(dot(a_one, w_other).astype(BF))
    raw_own = dot(a_one, w_own).astype(BF)
    raw_low = jnp.concatenate([raw_own, raw_other], axis=0)
    raw = raw_low.astype(F32)
    pos_own = positions.reshape(count)
    pos_both = jnp.concatenate([pos_own, net.swap_side(pos_own)])
    cosine, sine = rope_tables(pos_both)
    cos_heads, sin_heads = cosine[:, None, :], sine[:, None, :]
    q_normed, q_inverse, q_scaled = head_norm(
        raw[:, :q_cols].reshape(both, heads, HD), gain_query
    )
    query = rotate(q_scaled, cos_heads, sin_heads).astype(BF)
    k_normed, k_inverse, k_scaled = head_norm(
        raw[:, q_cols : q_cols + k_cols].reshape(both, kv_heads, HD), gain_key
    )
    key = rotate(k_scaled, cos_heads, sin_heads).astype(BF)
    value = raw[:, q_cols + k_cols :].reshape(both, kv_heads, HD).astype(BF)

    def by_head(v, depth):
        v = v.reshape(2, rows, per_row, -1, depth).transpose(1, 3, 0, 2, 4)
        return v.reshape(rows, -1, 2 * per_row, depth)

    q_heads = by_head(query, HD)
    q_padded = jnp.pad(q_heads, ((0, 0), (0, 0), (0, 0), (0, HD)))
    q_padded = q_padded.reshape(rows * heads, 2 * per_row, 2 * HD)
    assert kv_heads == 1
    kv_own = by_head(jnp.concatenate([key, value], axis=-1), 2 * HD)
    onehot = (corpus.reshape(count)[:, None] == jnp.arange(NCORP, dtype=jnp.int32)).astype(F32)
    own_counts = jnp.zeros((8, 128), F32).at[0, :NCORP].set(jnp.sum(onehot, axis=0))
    x_share = take(tokens.reshape(count, width), t * share, share)
    cot_rows = cotangent.reshape(count, width)
    o_low, log_total, all_counts, cot_other, resid, a_two, kv_in = attend(
        net.nodes,
        net.bits,
        kv_heads,
        q_padded,
        kv_own,
        own_counts,
        cot_rows,
        x_share,
        gain_two[None],
        w_out,
        2,
    )
    a_two = a_two.reshape(both, width)

    counts = jnp.sum(all_counts, axis=0)[0, :NCORP]
    weight_scale = corpus_weight.astype(F32) * (rows * total_len / NCORP) / counts
    corpus_other = net.swap_side(corpus.reshape(count))
    onehot_other = (corpus_other[:, None] == jnp.arange(NCORP, dtype=jnp.int32)).astype(F32)
    scale_own = jnp.sum(onehot * weight_scale, axis=-1, keepdims=True)
    scale_other = jnp.sum(onehot_other * weight_scale, axis=-1, keepdims=True)
    cot_both = jnp.concatenate([net.relative(cot_rows), cot_other.reshape(count, width)], axis=0)
    scale_both = jnp.concatenate([net.relative(scale_own), net.relative(scale_other)], axis=0)
    grad_low = (cot_both.astype(F32) * scale_both).astype(BF)
    grad_share = cot_both[:share].astype(F32) * scale_both[:share]

    mine = take(a_one.reshape(2, count // 2, width), t % 2, 1)[0]
    got = net.swap_side(mine)
    got_other = net.swap_bit(got, 0)
    a_one_other = jnp.where(
        t % 2 == 0, jnp.stack([got, got_other]), jnp.stack([got_other, got])
    ).reshape(count, width)

    def lanes(v):
        return jnp.pad(v, [(0, 0)] * (v.ndim - 1) + [(0, 2 * HD - v.shape[-1])])

    def by_pair(v):
        return lanes(by_head(v, HD)).reshape(-1, 2 * per_row, 2 * HD)

    sums = backward(
        net.nodes,
        net.bits,
        3,
        dict(
            a_two=a_two,
            grad_low=grad_low,
            w_gate=w_gate,
            w_up=w_up,
            w_down=w_down,
            resid=resid,
            grad=grad_share,
            x=x_share,
            gain_two=gain_two[None],
            gain_one=gain_one[None],
            gain_q=lanes(gain_query[None]),
            gain_k=lanes(gain_key[None]),
            w_out=w_out,
            w_back=w_own,
            a_one=jnp.concatenate([a_one, a_one_other], axis=0),
            q=q_padded,
            kv=kv_own,
            kv_in=kv_in,
            att=o_low,
            log=log_total.reshape(-1, 1, 2 * per_row),
            raw_q=by_pair(raw_low[:, :q_cols]),
            raw_k=by_pair(raw_low[:, q_cols : q_cols + k_cols]),
            cosine=lanes(jnp.concatenate([cosine, cosine], axis=1)),
            sine=lanes(jnp.concatenate([sine, -sine], axis=1)),
        ),
    )
    grad_gate, grad_up, grad_down = (v.astype(F32) for v in sums[:3])

    def unfolded(v, height):
        v = v.reshape(2, -1, height, v.shape[1])
        return v.transpose(0, 2, 1, 3).reshape(2, height, width)

    grad_out = unfolded(sums[3], q_cols).reshape(2 * q_cols, width).astype(F32)
    q_sum = unfolded(sums[4], q_cols)
    kv_sum = unfolded(sums[5], 2 * k_cols)
    out, d_tokens = (v.reshape(rows, per_row, width) for v in sums[6:8])
    gains = sums[8]

    def columns(both_sides, add=False):
        if add:
            return (both_sides[0].astype(F32) + both_sides[1].astype(F32)).T
        return both_sides.reshape(-1, width).astype(F32).T

    grad_query = columns(q_sum)
    grad_key = columns(kv_sum[:, :k_cols], shared)
    grad_value = columns(kv_sum[:, k_cols:], shared)
    head_share = HD // net.tp

    return (
        out,
        d_tokens,
        gains[0],
        grad_query,
        grad_key,
        grad_value,
        take(gains[2], t * head_share, head_share),
        take(gains[3], t * head_share, head_share),
        grad_out,
        gains[1],
        grad_gate,
        grad_up,
        grad_down,
    )


def solution(mesh):
    placed = (
        P(None, "seq", None),
        P(None, "seq"),
        P(None, "seq"),
        P(),
        P(),
        P(None, "tp"),
        P(None, "tp"),
        P(None, "tp"),
        P(),
        P(),
        P("tp", None),
        P(),
        P(None, "tp"),
        P(None, "tp"),
        P("tp", None),
        P(None, "seq", None),
    )
    return jax.shard_map(
        per_device,
        mesh=mesh,
        in_specs=placed,
        out_specs=(
            P(None, "seq", None),
            P(None, "seq", None),
            P("tp"),
            P(None, "tp"),
            P(None, "tp"),
            P(None, "tp"),
            P("tp"),
            P("tp"),
            P("tp", None),
            P("tp"),
            P(None, "tp"),
            P(None, "tp"),
            P("tp", None),
        ),
        check_vma=False,
    )
```

```python
import functools

import jax
import jax.numpy as jnp
from jax import lax
from jax.experimental import pallas as pl
from jax.experimental.pallas import tpu as pltpu
from jax.sharding import PartitionSpec as P

HD = 64
NCORP = 8


EPS = 1e-05
EPS_HEAD = 1e-06
ROPE_BASE = 10000.0
BF = jnp.bfloat16
F32 = jnp.float32
MESH = pl.DeviceIdType.MESH
LAG = 2
AHEAD = 3
KEPT = 6


def rope_tables(positions):
    half = HD // 2
    rates = ROPE_BASE ** (-jnp.arange(half, dtype=jnp.float32) * 2.0 / HD)
    angle = positions.astype(jnp.float32)[:, None] * rates[None, :]
    return (jnp.cos(angle), jnp.sin(angle))


def rotate(vector, cosine, sine):
    half = vector.shape[-1] // 2
    first = vector[..., :half]
    second = vector[..., half:]
    return jnp.concatenate(
        [first * cosine - second * sine, second * cosine + first * sine], axis=-1
    )


def head_norm(vector, gain):
    inverse = lax.rsqrt(jnp.mean(vector * vector, axis=-1, keepdims=True) + EPS_HEAD)
    normed = vector * inverse
    return (normed, inverse, normed * gain)


def dot(a, b):
    return jnp.dot(a, b, preferred_element_type=F32)


def dot_tn(a, b):
    return lax.dot_general(a, b, (((0,), (0,)), ((), ())), preferred_element_type=F32)


def dot_nt(a, b):
    return lax.dot_general(a, b, (((1,), (1,)), ((), ())), preferred_element_type=F32)


def take(array, start, size, axis=0):
    return lax.dynamic_slice_in_dim(array, start, size, axis)


class Links:
    def __init__(self):
        self.seq = lax.axis_size("seq")
        self.tp = lax.axis_size("tp")
        self.nodes = self.seq // 2
        self.bits = self.tp.bit_length() - 1
        rank = lax.axis_index("seq")
        self.node = rank // 2
        self.side = rank % 2
        self.t = lax.axis_index("tp")

    def swap_side(self, value):
        return lax.ppermute(value, "seq", [(s, s ^ 1) for s in range(self.seq)])

    def swap_bit(self, value, bit):
        return lax.ppermute(value, "tp", [(r, r ^ (1 << bit)) for r in range(self.tp)])

    def relative(self, rows):
        share = rows.shape[0] // self.tp
        return jnp.concatenate(
            [take(rows, (self.t ^ j) * share, share) for j in range(self.tp)], axis=0
        )


def remote_copy(src, dst, send, recv, **where):
    return pltpu.make_async_remote_copy(
        src, dst, send, recv, device_id=where, device_id_type=MESH
    )


def attend_kernel(
    nodes,
    bits,
    kv_heads,
    q_ref,
    kv_ref,
    count_ref,
    cot_ref,
    x_ref,
    gain_ref,
    w_ref,
    att_ref,
    log_ref,
    counts_ref,
    cot_out,
    resid_ref,
    a_out,
    kv_in,
    acc,
    weight_sum,
    att_in,
    parts,
    got,
    a_mine,
    kv_send,
    kv_recv,
    count_send,
    count_recv,
    cot_send,
    cot_recv,
    att_sem,
    sum_send,
    sum_recv,
    all_send,
    all_recv,
    own_sem,
):
    tp = 1 << bits
    seq = 2 * nodes
    rank, t = lax.axis_index("seq"), lax.axis_index("tp")
    node, side = rank // 2, rank % 2
    across = rank + 1 - 2 * side
    n_q, wide = q_ref.shape[0], q_ref.shape[1]
    n_rows = kv_ref.shape[0]
    heads = n_q // n_rows
    group = heads // kv_heads
    span = wide // 2
    share, width = x_ref.shape
    top = bits - 1

    def flip(bit):
        return t + (1 << bit) * (1 - 2 * ((t // (1 << bit)) % 2))

    def block_of(j):
        other = t
        for bit in range(bits):
            if (j >> bit) & 1:
                other = other + (1 << bit) * (1 - 2 * ((t // (1 << bit)) % 2))
        return other

    barrier = pltpu.get_barrier_semaphore()
    for step in range(1, seq):
        pl.semaphore_signal(
            barrier, 1, device_id={"seq": (rank + step) % seq}, device_id_type=MESH
        )
    for bit in range(bits):
        pl.semaphore_signal(barrier, 1, device_id={"tp": flip(bit)}, device_id_type=MESH)
    pl.semaphore_wait(barrier, seq - 1 + bits)

    for step in range(1, nodes):

        @pl.when(node + step < nodes)
        def _():
            remote_copy(
                kv_ref,
                kv_in.at[step - 1],
                kv_send.at[step - 1],
                kv_recv.at[step - 1],
                seq=rank + 2 * step,
            ).start()

    counts_ref[0] = count_ref[...]
    count_copies = [
        remote_copy(
            count_ref,
            counts_ref.at[step],
            count_send.at[step - 1],
            count_recv.at[step - 1],
            seq=(rank + step) % seq,
        )
        for step in range(1, seq)
    ]
    for copy in count_copies:
        copy.start()
    cot_copies = []
    for j in range(0, tp, 2):
        rows = pl.ds(pl.multiple_of(block_of(j) * share, share), share)
        cot_copies.append(
            remote_copy(
                cot_ref.at[rows], cot_out.at[j], cot_send.at[j], cot_recv.at[j], seq=across
            )
        )
        cot_copies[-1].start()

    def attend(kv_at, diagonal):
        @pl.loop(0, n_q)
        def _(i):
            kv = kv_at(i // heads, (i % heads) // group)
            scores = lax.dot_general(
                q_ref[i], kv, (((1,), (1,)), ((), ())), preferred_element_type=F32
            )
            weight = jnp.exp2(scores * (HD**-0.5 * 1.4426950408889634))
            if diagonal:
                q_at = lax.broadcasted_iota(jnp.int32, (wide, wide), 0)
                k_at = lax.broadcasted_iota(jnp.int32, (wide, wide), 1)
                q_at = jnp.where(q_at < span, q_at + span * side, q_at - span * side)
                k_at = jnp.where(k_at < span, k_at + span * side, k_at - span * side)
                weight = jnp.where(k_at <= q_at, weight, 0.0)
            sums = weight[:, :128]
            for c in range(128, wide, 128):
                sums = sums + weight[:, c : c + 128]
            values = jnp.dot(weight.astype(BF), kv, preferred_element_type=F32)
            if diagonal:
                weight_sum[i] = sums
                acc[i] = values
            else:
                weight_sum[i] += sums
                acc[i] += values

    attend(lambda r, h: kv_ref[r, h], True)
    for step in range(1, nodes):

        @pl.when(node >= step)
        def _():
            remote_copy(
                kv_ref,
                kv_in.at[step - 1],
                kv_send.at[step - 1],
                kv_recv.at[step - 1],
                seq=rank,
            ).wait_recv()
            attend(lambda r, h: kv_in[step - 1, r, h], False)

    att_copy = remote_copy(
        att_ref.at[1], att_in, att_sem.at[0], att_sem.at[1], seq=across
    )
    lane = lax.broadcasted_iota(jnp.int32, (span, 2 * HD), 1)
    for d in (1, 0):
        for r in range(n_rows):
            for h in range(0, heads, 2):
                out = []
                for k in range(2):
                    i = r * heads + h + k
                    at = pl.ds(d * span, span)
                    total = jnp.sum(weight_sum[i, at, :], axis=-1, keepdims=True)
                    log_ref[i, at, :] = jnp.log2(total)
                    out.append(acc[i, at, :] / total)
                both = jnp.where(lane < HD, pltpu.roll(out[0], HD, 1), out[1])
                att_ref[d, pl.ds(r * span, span), pl.ds(h * HD, 2 * HD)] = both.astype(BF)
        if d == 1:
            att_copy.start()

    half = w_ref.shape[0] // 2
    w_mine = w_ref[pl.ds(pl.multiple_of(side * half, half), half), :]
    w_other = w_ref[pl.ds(pl.multiple_of((1 - side) * half, half), half), :]

    def project(j, add):
        rows = pl.ds(pl.multiple_of(block_of(j) * share, share), share)
        if not add:
            parts[j] = jnp.dot(att_ref[0, rows, :], w_mine, preferred_element_type=F32)
        else:
            parts[j] += jnp.dot(att_in[rows, :], w_other, preferred_element_type=F32)

    for j in range(tp):
        project(j, False)
    att_copy.wait()
    order = sorted(range(tp), key=lambda j: -(j & 1))
    for j in order:
        project(j, True)

    held = list(range(tp))
    slot = 0
    for bit in range(bits):
        keep = [j for j in held if not (j >> bit) & 1]
        copies = []
        for j in keep:
            a_mine[slot] = parts[j | (1 << bit)].astype(BF)
            copies.append(
                remote_copy(
                    a_mine.at[slot], got.at[slot], sum_send.at[slot], sum_recv.at[slot],
                    tp=flip(bit),
                )
            )
            copies[-1].start()
            slot += 1
        for k, j in enumerate(keep):
            copies[k].wait()
            parts[j] += got[slot - len(keep) + k].astype(F32)
        held = keep
    resid = x_ref[...].astype(F32) + parts[0]
    resid_ref[...] = resid
    inverse = lax.rsqrt(jnp.mean(resid * resid, axis=-1, keepdims=True) + EPS)
    a_mine[slot] = (resid * inverse * gain_ref[...]).astype(BF)
    mine = a_mine.at[slot]

    started = []

    def send(src, dst, k, **where):
        copy = remote_copy(src, dst, all_send.at[k], all_recv.at[k], **where)
        copy.start()
        started.append(copy)
        return copy

    up = 1 << top
    cut = share // 2
    low, high = pl.ds(0, cut), pl.ds(cut, cut)
    by_side = send(mine, a_out.at[1, 0], 0, seq=across)
    by_top = send(mine, a_out.at[0, up], 1, tp=flip(top))
    put = pltpu.make_async_copy(mine, a_out.at[0, 0], own_sem)
    put.start()
    k = 4
    for copy in cot_copies:
        copy.wait()
    cot_copies = []
    for j in range(0, tp, 2):
        cot_copies.append(
            remote_copy(
                cot_out.at[j], cot_out.at[j + 1], cot_send.at[j + 1], cot_recv.at[j + 1],
                tp=flip(0),
            )
        )
        cot_copies[-1].start()
    pending = {}
    for bit in reversed(range(top)):
        have = [j for j in range(tp) if j % (2 << bit) == 0]
        if bit == top - 1:
            pending[0, 0] = send(mine, a_out.at[0, 1 << bit], k, tp=flip(bit))
            k += 1
            by_side.wait_recv()
            far_low = send(a_out.at[1, 0, low], a_out.at[1, up, low], 2, tp=flip(top))
            pending[1, 0] = send(a_out.at[1, 0], a_out.at[1, 1 << bit], k, tp=flip(bit))
            k += 1
            by_top.wait_recv()
            far_high = send(a_out.at[0, up, high], a_out.at[1, up, high], 3, seq=across)
            pending[0, up] = send(a_out.at[0, up], a_out.at[0, up | 1 << bit], k, tp=flip(bit))
            k += 1
            far_low.wait_recv()
            far_high.wait_recv()
            pending[1, up] = send(a_out.at[1, up], a_out.at[1, up | 1 << bit], k, tp=flip(bit))
            k += 1
        else:
            for d in range(2):
                for j in have:
                    pending[d, j] = send(
                        a_out.at[d, j], a_out.at[d, j | 1 << bit], k, tp=flip(bit)
                    )
                    k += 1
        for copy in pending.values():
            copy.wait_recv()
        pending = {}
    for copy in started:
        copy.wait_send()
    put.wait()
    for copy in count_copies + cot_copies:
        copy.wait()
    for step in range(1, nodes):

        @pl.when(node + step < nodes)
        def _():
            remote_copy(
                kv_ref,
                kv_in.at[step - 1],
                kv_send.at[step - 1],
                kv_recv.at[step - 1],
                seq=rank,
            ).wait_send()


def attend(nodes, bits, kv_heads, q, kv, count, cotangent, x_share, gain, w_out, ident):
    tp = 1 << bits
    seq = 2 * nodes
    n_q, wide, _ = q.shape
    n_rows = kv.shape[0]
    heads = n_q // n_rows
    share, width = x_share.shape
    vmem = pl.BlockSpec(memory_space=pltpu.VMEM)
    anywhere = pl.BlockSpec(memory_space=pl.ANY)
    dma = pltpu.SemaphoreType.DMA
    tokens = tp * share
    messages = 4 + 2 * (tp - 2)
    return pl.pallas_call(
        functools.partial(attend_kernel, nodes, bits, kv_heads),
        out_shape=[
            jax.ShapeDtypeStruct((2, tokens, heads * HD), BF),
            jax.ShapeDtypeStruct((n_q, wide, 1), F32),
            jax.ShapeDtypeStruct((seq,) + count.shape, F32),
            jax.ShapeDtypeStruct((tp, share, width), BF),
            jax.ShapeDtypeStruct((share, width), F32),
            jax.ShapeDtypeStruct((2, tp, share, width), BF),
            jax.ShapeDtypeStruct((nodes - 1,) + kv.shape, BF),
        ],
        in_specs=[vmem, vmem, vmem, anywhere, vmem, vmem, vmem],
        out_specs=[vmem, vmem, vmem, anywhere, vmem, anywhere, vmem],
        scratch_shapes=[
            pltpu.VMEM((n_q, wide, 2 * HD), F32),
            pltpu.VMEM((n_q, wide, 128), F32),
            pltpu.VMEM((tokens, heads * HD), BF),
            pltpu.VMEM((tp, share, width), F32),
            pltpu.VMEM((tp - 1, share, width), BF),
            pltpu.VMEM((tp, share, width), BF),
            dma((nodes - 1,)),
            dma((nodes - 1,)),
            dma((seq - 1,)),
            dma((seq - 1,)),
            dma((tp,)),
            dma((tp,)),
            dma((2,)),
            dma((tp - 1,)),
            dma((tp - 1,)),
            dma((messages,)),
            dma((messages,)),
            dma,
        ],
        compiler_params=pltpu.CompilerParams(
            collective_id=ident, has_side_effects=True, vmem_limit_bytes=48 << 20
        ),
        cost_estimate=pl.CostEstimate(
            flops=0, bytes_accessed=200 << 20, transcendentals=0
        ),
        name="attend",
    )(q, kv, count, cotangent, x_share, gain, w_out)


def backward_kernel(nodes, bits, *refs):
    names = (
        "a_two", "cot", "cot_far", "scale", "w_gate", "w_up", "w_down", "resid", "x", "gain_two",
        "gain_one", "gain_q", "gain_k", "w_out", "w_back", "a_one", "a_near", "a_far", "q", "kv", "kv_in", "att",
        "log", "raw_q", "raw_k", "cosine", "sine", "gate_sum", "up_sum", "down_sum", "out_sum",
        "q_sum", "kv_sum", "out", "tokens", "gains", "two_in", "ffn_in", "one_in", "gate_part",
        "up_part", "down_part", "red", "own", "hold", "temp", "low", "a_in", "a_t", "w_rows",
        "q_in", "d_out", "d_q", "d_kv", "kv_all", "att_in", "d_att", "delta", "d_raw", "q_part",
        "kv_part", "out_part", "kv_back", "kv_far", "d_resid", "fresh", "gain_rows", "gain_box",
        "gain_all", "log_in", "cot_in", "hidden", "d_pair", "w_strip", "w_cols", "stage", "stage_down",
        "own_sem", "red_send", "red_recv", "fin_send", "fin_recv", "x_send", "x_recv", "put_sem",
        "load_sem", "sum_send", "sum_recv", "temp_sem", "low_send", "low_recv", "kv_send",
        "kv_recv", "tok_send", "tok_recv", "tok_put", "gain_send", "gain_recv", "w_sem",
        "stage_sem",
    )
    assert len(names) == len(refs)
    R = dict(zip(names, refs))
    tp, seq = 1 << bits, 2 * nodes
    top = bits - 1
    rank, t = lax.axis_index("seq"), lax.axis_index("tp")
    node, side = rank // 2, rank % 2
    across = rank + 1 - 2 * side
    last = nodes - 1
    me = rank * tp + t
    total = seq * tp
    share, width = R["x"].shape
    n_q, wide, _ = R["q"].shape
    n_rows = R["kv"].shape[0]
    heads = n_q // n_rows
    span = wide // 2
    slots, prow, pcol = R["red"].shape[1:]
    half = R["red_send"].shape[1]
    ff = R["gate_part"].shape[1]
    chunks = ff // pcol
    tall = width // prow
    per_chunk = 3 * tall
    fed = chunks * per_chunk

    def strips(rows, step, body):
        @pl.loop(0, rows // step)
        def _(m):
            body(pl.ds(pl.multiple_of(m * step, step), step))

    def flip(bit):
        return t + (1 << bit) * (1 - 2 * ((t // (1 << bit)) % 2))

    def block_of(j):
        other = t
        for bit in range(bits):
            there = (j // (1 << bit)) % 2
            other = other + there * (1 << bit) * (1 - 2 * ((t // (1 << bit)) % 2))
        return other

    def block_rows(j):
        return pl.ds(pl.multiple_of(block_of(j) * share, share), share)

    barrier = pltpu.get_barrier_semaphore()

    @pl.loop(1, total)
    def _(k):
        other = (me + k) % total
        pl.semaphore_signal(
            barrier, 1, device_id={"seq": other // tp, "tp": other % tp}, device_id_type=MESH
        )

    pl.semaphore_wait(barrier, total - 1)

    red, own = R["red"], R["own"]
    own_sem, put_sem = R["own_sem"], R["put_sem"]
    red_sems = R["red_send"], R["red_recv"]
    fin_sems = R["fin_send"], R["fin_recv"]
    x_sems = R["x_send"], R["x_recv"]

    def with_piece(b, j, act):
        p = 2 * j + b
        chunk, k, kind = p // per_chunk, p % tall, (p % per_chunk) // tall
        along_chunk = pl.multiple_of(chunk * pcol, pcol)
        along_side = pl.multiple_of(side * ff + chunk * pcol, pcol)
        along_width = pl.ds(pl.multiple_of(k * prow, prow), prow)
        for i, name in enumerate(("gate", "up", "down")):

            @pl.when((p < fed) & (kind == i))
            def _(name=name):
                part, whole = R[name + "_part"], R[name + "_sum"]
                if name == "down":
                    act(
                        part.at[pl.ds(along_chunk, prow), along_width],
                        whole.at[pl.ds(along_side, prow), along_width],
                    )
                else:
                    act(
                        part.at[along_width, pl.ds(along_chunk, pcol)],
                        whole.at[along_width, pl.ds(along_side, pcol)],
                    )

        base = fed
        for name in ("out", "q", "kv"):
            part, whole = R[name + "_part"], R[name + "_sum"]
            size = part.shape[1] // pcol

            @pl.when((p >= base) & (p < base + size))
            def _(part=part, whole=whole, base=base, name=name):
                col = pl.ds(pl.multiple_of((p - base) * pcol, pcol), pcol)
                row = side * prow if name == "out" else 0
                act(part.at[:, col], whole.at[pl.ds(pl.multiple_of(row, prow), prow), col])

            base += size

    def along(src, dst, sems, b, j, target):
        return remote_copy(src, dst, sems[0].at[b, j], sems[1].at[b, j], seq=target)

    def placed(j):
        if gap == 0:
            return j, (j >= 0) & (j < half)
        after = j >= late + gap
        return jnp.where(after, j - gap, j), ((j >= 0) & (j < late)) | (
            after & (j < half + gap)
        )

    def stream(b, i):
        v = node if b == 0 else last - node
        ahead = rank + 2 if b == 0 else rank - 2
        behind = rank - 2 if b == 0 else rank + 2
        f, there = placed(i - LAG * v + AHEAD - 1)

        @pl.when((v > 0) & there)
        def _():
            with_piece(
                b,
                f,
                lambda src, dst: pltpu.make_async_copy(
                    src, own.at[b, f % AHEAD], own_sem.at[b, f % AHEAD]
                ).start(),
            )

        j, there = placed(i - LAG * v)

        @pl.when((v == 0) & there)
        def _():
            with_piece(
                b, j, lambda src, dst: along(src, red.at[b, j % slots], red_sems, b, j, ahead).start()
            )

        @pl.when((v > 0) & there)
        def _():
            mine = own.at[b, j % AHEAD]
            pltpu.make_async_copy(mine, mine, own_sem.at[b, j % AHEAD]).wait()
            along(red.at[b, j % slots], red.at[b, j % slots], red_sems, b, j, behind).wait_recv()
            at = j % slots

            def add(r):
                red[b, at, r] = (
                    red[b, at, r].astype(F32) + own[b, j % AHEAD, r].astype(F32)
                ).astype(BF)

            strips(prow, 64, add)

            @pl.when(v < last)
            def _():
                along(red.at[b, j % slots], red.at[b, j % slots], red_sems, b, j, ahead).start()

            @pl.when((v == last) & (j >= KEPT))
            def _():
                @pl.when(j - KEPT < late)
                def _():
                    along(red.at[b, 0], red.at[b, 0], x_sems, b, j - KEPT, across).wait_send()

                along(red.at[b, 0], red.at[b, 0], fin_sems, b, j - KEPT, behind).wait_send()
                pltpu.make_async_copy(red.at[b, 0], red.at[b, 0], put_sem.at[b, j - KEPT]).wait()

            @pl.when(v == last)
            def _():
                def act(src, dst):
                    along(red.at[b, j % slots], dst, fin_sems, b, j, behind).start()

                    @pl.when(j < late)
                    def _():
                        along(red.at[b, j % slots], dst, x_sems, b, j, across).start()

                    pltpu.make_async_copy(red.at[b, j % slots], dst, put_sem.at[b, j]).start()

                with_piece(b, j, act)

        g, there = placed(i - LAG * last - LAG * (last - v))

        @pl.when((v < last) & there)
        def _():
            along(red.at[b, 0], red.at[b, 0], fin_sems, b, g, ahead).wait_recv()

            @pl.when(v > 0)
            def _():
                along(red.at[b, 0], red.at[b, 0], red_sems, b, g, ahead).wait_send()

            def act(src, dst):
                @pl.when(v > 0)
                def _():
                    along(dst, dst, fin_sems, b, g, behind).start()

                @pl.when(g < late)
                def _():
                    along(dst, dst, x_sems, b, g, across).start()

            with_piece(b, g, act)

    hold, temp = R["hold"], R["temp"]
    boxes = [R["two_in"], R["ffn_in"], R["one_in"]]

    def held(ref, d, k):
        return ref.at[pl.ds((d * (tp // 2) + k) * share, share)]

    def messages(bit):
        base = sum(tp >> b for b in range(bit))
        keep = [(d, j) for d in range(2) for j in range(0, tp, 2 << bit)]
        return [(base + k, d, j) for k, (d, j) in enumerate(keep)]

    def sum_copy(n, m, src, **where):
        return remote_copy(
            src, boxes[n].at[m], R["sum_send"].at[n, m], R["sum_recv"].at[n, m], **where
        )

    def sum_start(n, bit):
        for m, d, j in messages(bit):
            src = held(temp, d, j // 2) if bit == 0 else held(hold, d, (j | 1 << bit) // 2)
            sum_copy(n, m, src, tp=flip(bit)).start()

    def sum_add(n, bit):
        for m, d, j in messages(bit):
            sum_copy(n, m, held(temp, d, j // 2), tp=flip(bit)).wait()
        loads = []
        for m, d, j in messages(bit):
            k = j // 2
            loads.append(
                pltpu.make_async_copy(boxes[n].at[m], held(temp, d, k), R["temp_sem"].at[d, k])
            )
            loads[-1].start()
        for copy, (m, d, j) in zip(loads, messages(bit)):
            copy.wait()
            base = (d * (tp // 2) + j // 2) * share

            def add(r, base=base):
                at = pl.ds(pl.multiple_of(base + r.start, 16), 16)
                hold[at, :] = (hold[at, :].astype(F32) + temp[at, :].astype(F32)).astype(BF)

            strips(share, 16, add)

    final = 2 * (tp - 1)

    def side_start(n):
        sum_copy(n, final, held(hold, 1, 0), seq=across).start()

    def side_finish(n):
        sum_copy(n, final, held(hold, 1, 0), seq=across).wait()
        load = pltpu.make_async_copy(boxes[n].at[final], held(temp, 0, 0), R["temp_sem"].at[0, 0])
        load.start()
        load.wait()

    def side_sum(r):
        return hold[r, :].astype(F32) + temp[r, :].astype(F32)

    ends = [R["out"], R["tokens"]]

    def token_copy(n, k, src, j, bit):
        return remote_copy(
            src,
            ends[n].at[block_of(j)],
            R["tok_send"].at[n, k],
            R["tok_recv"].at[n, k],
            tp=flip(bit),
        )

    def token_messages(bit):
        base = sum(tp >> (b + 1) for b in range(bit + 1, bits))
        return [(base + k, j) for k, j in enumerate(range(0, tp, 2 << bit))]

    def tokens_start(n, bit):
        for k, j in token_messages(bit):
            src = R["fresh"].at[n] if j == 0 else ends[n].at[block_of(j)]
            token_copy(n, k, src, j, bit).start()

    def tokens_wait(n, bit):
        for k, j in token_messages(bit):
            token_copy(n, k, R["fresh"].at[n], j, bit).wait()

    def tokens_put(n):
        return pltpu.make_async_copy(R["fresh"].at[n], ends[n].at[t], R["tok_put"].at[n])

    def block(d, j):
        return pl.ds((d * tp + j) * share, share)

    def a_at(k):
        return pl.multiple_of(tp * share + k * (tp * share // 2), tp * share // 2)

    loads = [
        (R["w_out"].at[pl.ds(pl.multiple_of(side * heads * HD, heads * HD), heads * HD)], R["w_rows"]),
        (R["w_back"], R["a_t"].at[:, pl.ds(0, R["w_back"].shape[1])]),
        (R["a_one"], R["a_in"].at[pl.ds(0, tp * share)]),
        (R["q"], R["q_in"]),
        (R["kv"], R["kv_all"].at[0]),
        (R["kv_in"], R["kv_all"].at[pl.ds(1, nodes - 1)]),
        (R["att"], R["att_in"]),
        (R["log"], R["log_in"]),
        (R["a_two"], R["low"]),
        (R["cot_far"], R["a_in"].at[pl.ds(tp * share, tp * share)]),
        (R["cot"].at[block_rows(0)], R["cot_in"]),
        (R["a_near"], R["a_in"].at[pl.ds(a_at(t % 2), tp * share // 2)]),
        (R["a_far"], R["a_in"].at[pl.ds(a_at(1 - t % 2), tp * share // 2)]),
    ] + [(R["cot"].at[block_rows(j)], R["a_in"].at[block(0, j)]) for j in range(tp)]

    def load(k):
        return pltpu.make_async_copy(loads[k][0], loads[k][1], R["load_sem"].at[k])

    w_cols, w_sem = R["w_cols"], R["w_sem"]
    both = 2 * tp * share
    nt = (((1,), (1,)), ((), ()))
    tn = (((0,), (0,)), ((), ()))

    def chunk_loads(c):
        at = pl.multiple_of(side * ff + c * pcol, pcol)
        slot = c % 2
        down_at = pl.multiple_of(slot * pcol, pcol)
        return [
            pltpu.make_async_copy(
                R["w_gate"].at[:, pl.ds(at, pcol)], w_cols.at[slot, 0], w_sem.at[slot, 0]
            ),
            pltpu.make_async_copy(
                R["w_up"].at[:, pl.ds(at, pcol)], w_cols.at[slot, 1], w_sem.at[slot, 1]
            ),
            pltpu.make_async_copy(
                R["w_down"].at[pl.ds(at, pcol)],
                hold.at[pl.ds(down_at, pcol)],
                w_sem.at[slot, 2],
            ),
        ]

    def begin():
        load(8).start()
        for copy in chunk_loads(0):
            copy.start()
        early = (9, *range(13, 13 + tp))
        for k in early:
            load(k).start()
        for copy in chunk_loads(1):
            copy.start()
        for k in (0, 3, 4, 5, 6, 7, 10):
            load(k).start()
        load(8).wait()
        for k in early:
            load(k).wait()

        def body(r):
            R["a_in"][r, :] = (R["a_in"][r, :].astype(F32) * R["scale"][r, :]).astype(BF)

        strips(both, 32, body)

    def chunk_ready(c):
        for copy in chunk_loads(c):
            copy.wait()

    def chunk_next(c):
        @pl.when(c + 2 < chunks)
        def _():
            for copy in chunk_loads(c + 2):
                copy.start()

    def chunk_forward(c, at):
        slot = c % 2
        cols = pl.ds(pl.multiple_of(c * pcol, pcol), pcol)
        w_rows = hold.at[pl.ds(pl.multiple_of(slot * pcol, pcol), pcol)]

        gate = jnp.dot(R["low"][at, :], w_cols[slot, 0], preferred_element_type=F32)
        up = jnp.dot(R["low"][at, :], w_cols[slot, 1], preferred_element_type=F32)
        d_hidden = lax.dot_general(R["a_in"][at, :], w_rows[...], nt, preferred_element_type=F32)
        sigma = 1.0 / (1.0 + jnp.exp(-gate))
        smooth = gate * sigma
        R["hidden"][at, cols] = (smooth * up).astype(BF)
        R["d_pair"][1, at, cols] = (d_hidden * smooth).astype(BF)
        R["d_pair"][0, at, cols] = (d_hidden * up * (sigma * (1.0 + gate - smooth))).astype(BF)

    def turn():
        def body(at):
            R["a_t"][:, at] = R["low"][at, :].T

        strips(both, 256, body)

    def stage_copies(c):
        at = pl.ds(pl.multiple_of(c * pcol, pcol), pcol)
        sem = R["stage_sem"]
        return [
            pltpu.make_async_copy(R["stage"].at[0], R["gate_part"].at[:, at], sem.at[0]),
            pltpu.make_async_copy(R["stage"].at[1], R["up_part"].at[:, at], sem.at[1]),
            pltpu.make_async_copy(R["stage_down"], R["down_part"].at[at], sem.at[2]),
        ]

    def chunk_gradients(c):
        cols = pl.ds(pl.multiple_of(c * pcol, pcol), pcol)

        @pl.loop(0, 2)
        def _(k):
            def body(at):
                R["stage"][k, at, :] = jnp.dot(
                    R["a_t"][at, :], R["d_pair"][k, :, cols], preferred_element_type=F32
                ).astype(BF)

            strips(width, 1024, body)

        for copy in stage_copies(c)[:2]:
            copy.start()

    def chunk_down(c):
        cols = pl.ds(pl.multiple_of(c * pcol, pcol), pcol)

        def body(at):
            R["stage_down"][:, at] = lax.dot_general(
                R["hidden"][:, cols], R["a_in"][:, at], tn, preferred_element_type=F32
            ).astype(BF)

        strips(width, 1024, body)
        stage_copies(c)[2].start()

    def staged(c):
        for copy in stage_copies(c):
            copy.wait()

    def row_loads(n):
        rows = pl.ds(pl.multiple_of(n * pcol, pcol), pcol)
        cols = pl.ds(pl.multiple_of(side * ff, ff), ff)
        return [
            pltpu.make_async_copy(
                R[name].at[rows, cols], R["w_strip"].at[n % 2, k], w_sem.at[n % 2, k]
            )
            for k, name in enumerate(("w_gate", "w_up"))
        ]

    def down_loads(n):
        return [
            pltpu.make_async_copy(
                R["w_down"].at[
                    pl.ds(pl.multiple_of(side * ff, ff), ff),
                    pl.ds(pl.multiple_of(n * pcol, pcol), pcol),
                ],
                w_cols.at[n % 2, 0, pl.ds(0, ff)],
                w_sem.at[n % 2, 0],
            )
        ]

    def start_all(copies):
        for copy in copies:
            copy.start()

    def by_columns(low_n, high_n, loads, product):
        @pl.loop(low_n, high_n)
        def _(n):
            for copy in loads(n):
                copy.wait()
            cols = pl.ds(pl.multiple_of(n * pcol, pcol), pcol)

            @pl.loop(0, 2)
            def _(d):
                at = pl.ds(pl.multiple_of(d * tp * share, tp * share), tp * share)
                value = product(at, n % 2).astype(BF)
                for j in range(tp):
                    rows = pl.ds(
                        pl.multiple_of((d * (tp // 2) + j // 2) * share, share), share
                    )
                    (temp if j % 2 else hold)[rows, cols] = value[j * share : (j + 1) * share]

            @pl.when(n + 2 < width // pcol)
            def _():
                start_all(loads(n + 2))

    def second_part(low_n, high_n):
        def product(at, slot):
            value = lax.dot_general(
                R["d_pair"][0, at, :], R["w_strip"][slot, 0], nt, preferred_element_type=F32
            )
            return value + lax.dot_general(
                R["d_pair"][1, at, :], R["w_strip"][slot, 1], nt, preferred_element_type=F32
            )

        by_columns(low_n, high_n, row_loads, product)

    def ffn_part(low_n, high_n):
        def product(at, slot):
            return jnp.dot(
                R["hidden"][at, :], w_cols[slot, 0, 0:ff, :], preferred_element_type=F32
            )

        by_columns(low_n, high_n, down_loads, product)

    def normed(v):
        inverse = lax.rsqrt(jnp.mean(v * v, axis=-1, keepdims=True) + EPS)
        return v * inverse, inverse

    low = R["low"]

    def low_at(d, j):
        return low.at[block(d, j)]

    def low_copy(k, src, dst, **where):
        return remote_copy(src, dst, R["low_send"].at[k], R["low_recv"].at[k], **where)

    up = 1 << top
    low_side = low_copy(0, low_at(0, 0), low_at(1, 0), seq=across)
    low_top = low_copy(1, low_at(0, 0), low_at(0, up), tp=flip(top))
    low_far = low_copy(2, low_at(1, 0), low_at(1, up), tp=flip(top))

    def low_bit(bit):
        base = 3 + sum(tp >> b for b in range(bit + 1, top))
        return [
            low_copy(base + k, low_at(d, j), low_at(d, j | 1 << bit), tp=flip(bit))
            for k, (d, j) in enumerate(
                (d, j) for d in range(2) for j in range(0, tp, 2 << bit)
            )
        ]

    def second_norm():
        side_finish(0)
        load(10).wait()
        R["gain_rows"][...] = jnp.zeros_like(R["gain_rows"])

        def body(r):
            d_a = side_sum(r)
            n_two, inverse = normed(R["resid"][r, :])
            R["gain_rows"][1:2, :] += jnp.sum(d_a * n_two, axis=0, keepdims=True)
            e = d_a * R["gain_two"][...]
            d_resid = R["cot_in"][r, :].astype(F32) * R["scale"][r, :] + inverse * (
                e - n_two * jnp.mean(e * n_two, axis=-1, keepdims=True)
            )
            R["d_resid"][r, :] = d_resid
            low[r, :] = d_resid.astype(BF)

        strips(share, 16, body)
        low_side.start()
        low_top.start()

    lane = lax.broadcasted_iota(jnp.int32, (span, 2 * HD), 1)

    def attended_back():
        for k in (0, 6):
            load(k).wait()
        R["d_kv"][...] = jnp.zeros_like(R["d_kv"])
        R["d_q"][...] = jnp.zeros_like(R["d_q"])
        @pl.loop(0, 2)
        def _(d):
            value = lax.dot_general(
                low[pl.ds(pl.multiple_of(d * tp * share, tp * share), tp * share), :],
                R["w_rows"][...],
                nt,
                preferred_element_type=F32,
            ).astype(BF)
            for j in range(tp):
                at = pl.ds(pl.multiple_of((d * tp + block_of(j)) * share, share), share)
                R["d_att"][at, :] = value[j * share : (j + 1) * share]

        ones = jnp.ones((8, 2 * HD), F32)
        pairs = heads // 2

        @pl.loop(0, 2 * n_rows * pairs)
        def _(n):
            d, r, h = n // (n_rows * pairs), n // pairs % n_rows, n % pairs
            cols = pl.ds(pl.multiple_of(h * 2 * HD, 2 * HD), 2 * HD)
            rows = pl.ds(pl.multiple_of(r * span, span), span)
            at = pl.ds(pl.multiple_of(d * span, span), span)
            d_rows = pl.ds(pl.multiple_of((d * n_rows + r) * span, span), span)
            for k in range(2):
                grads = R["d_att"][d_rows, cols].astype(F32)
                values = R["att_in"][d, rows, cols].astype(F32)
                if k == 0:
                    grads = pltpu.roll(grads, HD, 1)
                    values = pltpu.roll(values, HD, 1)
                grads = jnp.where(lane < HD, 0.0, grads)
                i = r * heads + 2 * h + k
                R["d_out"][i, at, :] = grads.astype(BF)
                R["delta"][i, :, at] = lax.dot_general(
                    ones,
                    grads * values,
                    nt,
                    precision=lax.Precision.HIGHEST,
                    preferred_element_type=F32,
                )

    def put_folded(ref, c, value):
        rows, cols = value.shape
        at = pl.ds(pl.multiple_of(c // ref.shape[1] * rows, rows), rows)
        ref[at, pl.ds(pl.multiple_of(c % ref.shape[1], cols), cols)] = value.astype(BF)

    def out_gradient():
        chunk = width // 2

        @pl.loop(0, 2 * tp)
        def _(n):
            R["d_att"][pl.ds(pl.multiple_of(n * share, share), share), :] = R["att_in"][
                n // tp, block_rows(n % tp), :
            ]

        @pl.loop(0, width // chunk)
        def _(n):
            c = pl.multiple_of(n * chunk, chunk)
            value = lax.dot_general(
                R["d_att"][...], low[:, pl.ds(c, chunk)], tn, preferred_element_type=F32
            )
            put_folded(R["out_part"], c, value)

    def attention_block(piece, i, diagonal):
        r = i // heads
        kv = R["kv_all"][piece, r, 0]
        q, d_out = R["q_in"][i], R["d_out"][i]
        scores = lax.dot_general(kv, q, nt, preferred_element_type=F32)
        probs = jnp.exp2(scores * (HD**-0.5 * 1.4426950408889634) - R["log_in"][i])
        if diagonal:
            k_at = lax.broadcasted_iota(jnp.int32, (wide, wide), 0)
            q_at = lax.broadcasted_iota(jnp.int32, (wide, wide), 1)
            q_at = jnp.where(q_at < span, q_at + span * side, q_at - span * side)
            k_at = jnp.where(k_at < span, k_at + span * side, k_at - span * side)
            probs = jnp.where(k_at <= q_at, probs, 0.0)
        d_probs = lax.dot_general(kv, d_out, nt, preferred_element_type=F32)
        d_scores = (probs * (d_probs - R["delta"][i, 0:1, :])).astype(BF)
        R["d_kv"][piece, r] += jnp.dot(d_scores, q, preferred_element_type=F32) + jnp.dot(
            probs.astype(BF), d_out, preferred_element_type=F32
        ) * (HD**0.5)
        R["d_q"][i] += lax.dot_general(
            kv, d_scores, (((0,), (0,)), ((), ())), preferred_element_type=F32
        )

    def kv_copy(step):
        return remote_copy(
            R["kv_back"].at[step - 1],
            R["kv_far"].at[step - 1],
            R["kv_send"].at[step - 1],
            R["kv_recv"].at[step - 1],
            seq=rank - 2 * step,
        )

    def kv_send():
        for step in range(1, nodes):

            @pl.when(node >= step)
            def _():
                R["kv_back"][step - 1] = R["d_kv"][step].astype(BF)
                kv_copy(step).start()

    def kv_sum():
        for step in range(1, nodes):

            @pl.when(node + step < nodes)
            def _():
                kv_copy(step).wait_recv()
                R["d_kv"][0] += R["kv_far"][step - 1].astype(F32)

            @pl.when(node >= step)
            def _():
                kv_copy(step).wait_send()

    def head_back(grads, raw, gain, at):
        lanes = 2 * HD
        low_lane = lane < HD // 2
        swapped = jnp.where(
            low_lane, pltpu.roll(grads, lanes - HD // 2, 1), pltpu.roll(grads, HD // 2, 1)
        )
        rotated = grads * R["cosine"][at, :] + swapped * R["sine"][at, :]
        inverse = lax.rsqrt(jnp.sum(raw * raw, axis=-1, keepdims=True) * (1.0 / HD) + EPS_HEAD)
        n = raw * inverse
        e = rotated * gain
        back = inverse * (e - n * (jnp.sum(e * n, axis=-1, keepdims=True) * (1.0 / HD)))
        return back, jnp.sum(rotated * n, axis=0, keepdims=True)

    def heads_back():
        scale = HD**-0.5
        pairs = heads // 2

        @pl.loop(0, 2 * n_rows)
        def _(n):
            r, d = n // 2, n % 2
            at = pl.ds(pl.multiple_of((d * n_rows + r) * span, span), span)
            here = pl.ds(pl.multiple_of(d * span, span), span)

            @pl.loop(0, pairs)
            def _(h):
                pair = []
                for k in range(2):
                    i = r * heads + 2 * h + k
                    grads = R["d_q"][i, :, here].T * scale
                    raw = R["raw_q"][i, here, :].astype(F32)
                    back, gain = head_back(grads, raw, R["gain_q"][...], at)
                    R["gain_rows"][2:3, 0 : 2 * HD] += gain
                    pair.append(back)
                R["d_raw"][at, pl.ds(pl.multiple_of(h * 2 * HD, 2 * HD), 2 * HD)] = jnp.where(
                    lane < HD, pair[0], pltpu.roll(pair[1], HD, 1)
                ).astype(BF)

            grads = R["d_kv"][0, r, here, :] * scale
            raw = R["raw_k"][r, here, :].astype(F32)
            back, gain = head_back(grads, raw, R["gain_k"][...], at)
            R["gain_rows"][3:4, 0 : 2 * HD] += gain
            R["d_raw"][at, pl.ds(heads * HD, 2 * HD)] = jnp.where(lane < HD, back, grads).astype(
                BF
            )

    def raw_gradient():
        for k in (2, 11, 12):
            load(k).wait()
        chunk = width // 2
        cut = heads * HD

        @pl.loop(0, width // chunk)
        def _(n):
            c = pl.multiple_of(n * chunk, chunk)
            value = lax.dot_general(
                R["d_raw"][...], R["a_in"][:, pl.ds(c, chunk)], tn, preferred_element_type=F32
            )
            put_folded(R["q_part"], c, value[:cut])
            put_folded(R["kv_part"], c, value[cut:])

    def first_part(low_n, high_n):
        inner = R["w_back"].shape[1]
        rel = R["hidden"]
        chunk = 512

        if low_n == 0:
            load(1).wait()

            @pl.loop(0, 2 * tp)
            def _(n):
                rows = pl.multiple_of((n // tp * tp + block_of(n % tp)) * share, share)
                rel[pl.ds(pl.multiple_of(n * share, share), share), 0:inner] = R["d_raw"][
                    pl.ds(rows, share), :
                ]

        @pl.loop(low_n, high_n)
        def _(n):
            cols = pl.ds(pl.multiple_of(n * chunk, chunk), chunk)

            @pl.loop(0, 2)
            def _(d):
                at = pl.ds(pl.multiple_of(d * tp * share, tp * share), tp * share)
                value = lax.dot_general(
                    rel[at, 0:inner], R["a_t"][cols, 0:inner], nt, preferred_element_type=F32
                ).astype(BF)
                for j in range(tp):
                    rows = pl.ds(
                        pl.multiple_of((d * (tp // 2) + j // 2) * share, share), share
                    )
                    (temp if j % 2 else hold)[rows, cols] = value[j * share : (j + 1) * share]

    def out_end():
        side_finish(1)

        def body(r):
            R["fresh"][0, r, :] = (R["resid"][r, :] + side_sum(r)).astype(BF)

        strips(share, 16, body)
        tokens_put(0).start()
        tokens_start(0, top)

    def first_norm():
        side_finish(2)

        def body(r):
            d_a = side_sum(r)
            n_one, inverse = normed(R["x"][r, :].astype(F32))
            R["gain_rows"][0:1, :] += jnp.sum(d_a * n_one, axis=0, keepdims=True)
            e = d_a * R["gain_one"][...]
            d_x = R["d_resid"][r, :] + inverse * (
                e - n_one * jnp.mean(e * n_one, axis=-1, keepdims=True)
            )
            R["fresh"][1, r, :] = d_x.astype(BF)

        strips(share, 16, body)
        tokens_put(1).start()
        tokens_start(1, top)
        part = width // tp
        for k in range(tp):
            R["gain_box"][k] = jnp.zeros((8, part), F32)
            R["gain_box"][k, 0:2, :] = R["gain_rows"][0:2, k * part : (k + 1) * part]
            R["gain_box"][k, 2:4, 0 : 2 * HD] = R["gain_rows"][2:4, 0 : 2 * HD]

        @pl.loop(1, total)
        def _(k):
            other = (me + k) % total
            remote_copy(
                R["gain_box"].at[other % tp],
                R["gain_all"].at[k],
                R["gain_send"].at[k],
                R["gain_recv"].at[k],
                seq=other // tp,
                tp=other % tp,
            ).start()

        R["gain_all"][0] = R["gain_box"][t]

    def gains_end():
        @pl.loop(1, total)
        def _(k):
            remote_copy(
                R["gain_box"].at[0],
                R["gain_all"].at[k],
                R["gain_send"].at[k],
                R["gain_recv"].at[k],
                seq=rank,
                tp=t,
            ).wait()

        R["gains"][...] = jnp.zeros_like(R["gains"])

        @pl.loop(0, total)
        def _(k):
            R["gains"][...] += R["gain_all"][k]

    tasks = {}

    def task(step, *acts):
        tasks.setdefault(step, []).extend(acts)
        return step

    def sums_tasks(n, step):
        for bit in range(bits):
            step += 2 if bit == 0 else 5
            following = (
                (lambda bit=bit: sum_start(n, bit + 1)) if bit < top else (lambda: side_start(n))
            )
            task(step, lambda bit=bit: sum_add(n, bit), following)
        return step + 5

    def token_tasks(n, step):
        for bit in reversed(range(bits)):
            step += 3
            task(step, lambda bit=bit: tokens_wait(n, bit))
            if bit:
                task(step, lambda bit=bit: tokens_start(n, bit - 1))
        task(step, lambda: tokens_put(n).wait())
        return step

    n_rows_w = width // pcol
    first_move = 1
    halves = 2 * chunks - 1
    task(0, begin)
    step = halves
    task(step, lambda: start_all(row_loads(0)), lambda: start_all(row_loads(1)))
    for k in range(4):
        step = task(
            halves + k, lambda k=k: second_part(n_rows_w * k // 4, n_rows_w * (k + 1) // 4)
        )
    task(step, lambda: sum_start(0, 0))
    task(step, lambda: start_all(down_loads(0)), lambda: start_all(down_loads(1)))
    grads_at = step + 1
    grads_end = grads_at + 2 * (chunks - 1)
    assert grads_at + 1 < first_move + per_chunk // 2
    task(grads_end, load(1).start, load(2).start, load(11).start, load(12).start)
    step = task(sums_tasks(0, step), second_norm)
    task(max(step, grads_end) + 1, lambda: ffn_part(0, n_rows_w // 2))
    ffn_at = task(
        max(step, grads_end) + 2,
        lambda: ffn_part(n_rows_w // 2, n_rows_w),
        lambda: sum_start(1, 0),
    )
    step = task(step + 4, low_side.wait, low_top.wait, low_far.start)
    step += 3
    task(step, low_far.wait)
    for bit in reversed(range(top)):
        task(step, lambda bit=bit: [c.start() for c in low_bit(bit)])
        step += 2
        task(step, lambda bit=bit: [c.wait() for c in low_bit(bit)])
    task(step, attended_back)
    ffn_end = task(sums_tasks(1, ffn_at), out_end)
    token_tasks(0, ffn_end)
    step = task(step + 1, *[load(k).wait for k in (3, 4, 5, 7)])
    first_block = step
    per_step = 4
    step += -(-(nodes * n_q) // per_step)
    last_block = step
    task(step, kv_send)
    task(step + 2, out_gradient)
    step = task(step + 5, kv_sum, heads_back)
    step = task(step + 1, raw_gradient)
    raw_ready = step
    assert raw_ready > ffn_end
    task(step + 1, lambda: first_part(0, width // 1024))
    step = task(
        step + 2, lambda: first_part(width // 1024, width // 512), lambda: sum_start(2, 0)
    )
    step = task(sums_tasks(2, step), first_norm)
    task(token_tasks(1, step), gains_end)

    late = half - (R["q_part"].shape[1] + R["kv_part"].shape[1]) // pcol // 2
    gap = max(0, raw_ready + 1 - late - first_move)
    steps = max(first_move + half + gap + 2 * LAG * last, max(tasks) + 1)

    @pl.loop(0, steps)
    def _(i):
        for b in range(2):
            stream(b, i - first_move)
        for at, acts in sorted(tasks.items()):

            @pl.when(i == at)
            def _(acts=acts):
                for act in acts:
                    act()

        @pl.when(i < halves)
        def _():
            c = (i + 1) // 2

            @pl.when((i == 0) | (i % 2 == 1))
            def _():
                chunk_ready(c)

            @pl.loop(jnp.where((i == 0) | (i % 2 == 1), 0, 1), jnp.where(i % 2 == 1, 1, 2))
            def _(m):
                chunk_forward(c, pl.ds(pl.multiple_of(m * (both // 2), both // 2), both // 2))

            @pl.when(i % 2 == 0)
            def _():
                chunk_next(c)

        pl.when(i == 0)(turn)
        g = i - grads_at
        c = jnp.where(i == 0, 0, g // 2 + 1)
        within = (g >= 0) & (i < grads_end)

        @pl.when((i == 0) | (within & (g % 2 == 0)))
        def _():
            chunk_gradients(c)

        @pl.when((i == 0) | (within & (g % 2 == 1)))
        def _():
            chunk_down(c)
            staged(c)

        @pl.when((i >= first_block) & (i < last_block))
        def _():
            @pl.loop(0, per_step)
            def _(k):
                n = (i - first_block) * per_step + k
                piece = n // n_q

                @pl.when(n < n_q)
                def _():
                    attention_block(0, n, True)

                @pl.when((n >= n_q) & (n < n_q * nodes) & (node >= piece))
                def _():
                    attention_block(piece, n % n_q, False)

    @pl.loop(0, half)
    def _(j):
        for b in range(2):
            v = node if b == 0 else last - node
            probe = red.at[b, 0]

            @pl.when(v == 0)
            def _():
                along(probe, probe, red_sems, b, j, rank).wait_send()

            @pl.when((v > 0) & ((v < last) | (j >= half - KEPT)))
            def _():
                along(probe, probe, fin_sems, b, j, rank).wait_send()

            @pl.when((v == last) & (j >= half - KEPT))
            def _():
                pltpu.make_async_copy(probe, probe, put_sem.at[b, j]).wait()

            @pl.when((j < late) & ((v < last) | (j >= half - KEPT)))
            def _():
                along(probe, probe, x_sems, b, j, rank).wait_send()

            @pl.when(j < late)
            def _():
                along(probe, probe, x_sems, b, j, rank).wait_recv()


def backward(nodes, bits, ident, values):
    tp, seq = 1 << bits, 2 * nodes
    share, width = values["x"].shape
    ff = values["w_gate"].shape[1] // 2
    n_q, wide, _ = values["q"].shape
    n_rows = values["kv"].shape[0]
    heads = n_q // n_rows
    tokens = tp * share
    piece = 256
    cols = (heads + 2) * HD
    small = [(piece, r * width // piece) for r in (heads * HD, heads * HD, 2 * HD)]
    shapes = [(width, 2 * ff), (width, 2 * ff), (2 * ff, width)]
    shapes += [(2 * small[0][0], small[0][1])] + small[1:]
    half = (3 * width * ff + sum(r * c for r, c in small)) // (2 * piece * piece)
    slots = 2 * LAG * (nodes - 1) + 2
    vmem = pl.BlockSpec(memory_space=pltpu.VMEM)
    anywhere = pl.BlockSpec(memory_space=pl.ANY)
    dma = pltpu.SemaphoreType.DMA
    inside = ("scale", "resid", "x", "gain_two", "gain_one", "gain_q", "gain_k")
    inside += ("raw_q", "raw_k", "cosine", "sine")
    kv = values["kv"].shape
    total = seq * tp
    messages = 3 + 2 * (tp - 2)
    outs = shapes + [(tp, share, width)] * 2 + [(8, width // tp)]
    outs += [(2 * tp - 1, share, width)] * 3 + [(width, ff), (width, ff), (ff, width)]
    scratch = [
        (2, slots, piece, piece),
        (2, AHEAD, piece, piece),
        (tokens, width),
        (tokens, width),
        (2 * tokens, width),
        (2 * tokens, width),
        (width, 2 * tokens),
        (heads * HD, width),
        (n_q, wide, 2 * HD),
        (n_q, wide, 2 * HD),
        (n_q, 2 * HD, wide, F32),
        (nodes, n_rows, wide, 2 * HD, F32),
        (nodes,) + kv,
        (2, tokens, heads * HD),
        (2 * tokens, heads * HD),
        (n_q, 8, wide, F32),
        (2 * tokens, cols),
        small[1],
        small[2],
        small[0],
        (nodes - 1, n_rows, wide, 2 * HD),
        (nodes - 1, n_rows, wide, 2 * HD),
        (share, width, F32),
        (2, share, width),
        (8, width, F32),
        (tp, 8, width // tp, F32),
        (total, 8, width // tp, F32),
        (n_q, 1, wide, F32),
        (share, width),
        (2 * tokens, ff),
        (2, 2 * tokens, ff),
        (2, 2, piece, ff),
        (2, 2, width, piece),
        (2, width, piece),
        (piece, width),
    ]
    sems = [(2, AHEAD)] + [(2, half)] * 7 + [(13 + tp,), (3, 2 * tp - 1), (3, 2 * tp - 1)]
    sems += [(2, tp // 2), (messages,), (messages,), (nodes - 1,), (nodes - 1,)]
    sems += [(2, tp - 1), (2, tp - 1), (2,), (total,), (total,), (2, 3), (3,)]
    return pl.pallas_call(
        functools.partial(backward_kernel, nodes, bits),
        out_shape=[
            jax.ShapeDtypeStruct(shape, F32 if k == 8 else BF) for k, shape in enumerate(outs)
        ],
        in_specs=[vmem if k in inside else anywhere for k in values],
        out_specs=[vmem if k == 8 else anywhere for k in range(len(outs))],
        scratch_shapes=[
            pltpu.VMEM(s[:-1], F32) if s[-1] is F32 else pltpu.VMEM(s, BF) for s in scratch
        ]
        + [dma(s) for s in sems],
        compiler_params=pltpu.CompilerParams(
            collective_id=ident, has_side_effects=True, vmem_limit_bytes=62 << 20
        ),
        cost_estimate=pl.CostEstimate(
            flops=0, bytes_accessed=1 << 30, transcendentals=0
        ),
        name="backward",
    )(*values.values())[:9]


def per_device(
    tokens,
    positions,
    corpus,
    corpus_weight,
    gain_one,
    w_query,
    w_key,
    w_value,
    gain_query,
    gain_key,
    w_out,
    gain_two,
    w_gate,
    w_up,
    w_down,
    cotangent,
):
    net = Links()
    rows, per_row, width = tokens.shape
    count = rows * per_row
    share = count // net.tp
    total_len = per_row * net.seq
    side, node, t = net.side, net.node, net.t
    scale = HD ** (-0.5)
    q_cols = w_query.shape[1] // 2
    shared = (w_key.shape[1] // HD) % 2 == 1
    k_cols = w_key.shape[1] if shared else w_key.shape[1] // 2
    heads, kv_heads = q_cols // HD, k_cols // HD
    group = heads // kv_heads
    both = 2 * count

    x_rows = tokens.reshape(count, width).astype(F32)
    inverse_one = lax.rsqrt(jnp.mean(x_rows * x_rows, axis=-1, keepdims=True) + EPS)
    a_one = (x_rows * inverse_one * gain_one).astype(BF)

    def halves(w):
        cols = w.shape[1] // 2
        return take(w, side * cols, cols, 1), take(w, (1 - side) * cols, cols, 1)

    wq, wk, wv = halves(w_query), halves(w_key), halves(w_value)
    if shared:
        wk, wv = (w_key, w_key), (w_value, w_value)
    w_own = jnp.concatenate([wq[0], wk[0], wv[0]], axis=1)
    w_other = jnp.concatenate([wq[1], wk[1], wv[1]], axis=1)
    raw_other = net.swap_side(dot(a_one, w_other).astype(BF))
    raw_own = dot(a_one, w_own).astype(BF)
    raw_low = jnp.concatenate([raw_own, raw_other], axis=0)
    raw = raw_low.astype(F32)
    pos_own = positions.reshape(count)
    pos_both = jnp.concatenate([pos_own, net.swap_side(pos_own)])
    cosine, sine = rope_tables(pos_both)
    cos_heads, sin_heads = cosine[:, None, :], sine[:, None, :]
    q_normed, q_inverse, q_scaled = head_norm(
        raw[:, :q_cols].reshape(both, heads, HD), gain_query
    )
    query = rotate(q_scaled, cos_heads, sin_heads).astype(BF)
    k_normed, k_inverse, k_scaled = head_norm(
        raw[:, q_cols : q_cols + k_cols].reshape(both, kv_heads, HD), gain_key
    )
    key = rotate(k_scaled, cos_heads, sin_heads).astype(BF)
    value = raw[:, q_cols + k_cols :].reshape(both, kv_heads, HD).astype(BF)

    def by_head(v, depth):
        v = v.reshape(2, rows, per_row, -1, depth).transpose(1, 3, 0, 2, 4)
        return v.reshape(rows, -1, 2 * per_row, depth)

    q_heads = by_head(query, HD)
    q_padded = jnp.pad(q_heads, ((0, 0), (0, 0), (0, 0), (0, HD)))
    q_padded = q_padded.reshape(rows * heads, 2 * per_row, 2 * HD)
    assert kv_heads == 1
    kv_own = by_head(jnp.concatenate([key, value], axis=-1), 2 * HD)
    onehot = (corpus.reshape(count)[:, None] == jnp.arange(NCORP, dtype=jnp.int32)).astype(F32)
    own_counts = jnp.zeros((8, 128), F32).at[0, :NCORP].set(jnp.sum(onehot, axis=0))
    x_share = take(tokens.reshape(count, width), t * share, share)
    cot_rows = cotangent.reshape(count, width)
    o_low, log_total, all_counts, cot_other, resid, a_two, kv_in = attend(
        net.nodes,
        net.bits,
        kv_heads,
        q_padded,
        kv_own,
        own_counts,
        cot_rows,
        x_share,
        gain_two[None],
        w_out,
        2,
    )
    a_two = a_two.reshape(both, width)

    counts = jnp.sum(all_counts, axis=0)[0, :NCORP]
    weight_scale = corpus_weight.astype(F32) * (rows * total_len / NCORP) / counts
    corpus_other = net.swap_side(corpus.reshape(count))
    onehot_other = (corpus_other[:, None] == jnp.arange(NCORP, dtype=jnp.int32)).astype(F32)
    scale_own = jnp.sum(onehot * weight_scale, axis=-1, keepdims=True)
    scale_other = jnp.sum(onehot_other * weight_scale, axis=-1, keepdims=True)
    scale_both = jnp.concatenate([net.relative(scale_own), net.relative(scale_other)], axis=0)

    mine = take(a_one.reshape(2, count // 2, width), t % 2, 1)[0]
    got = net.swap_side(mine)
    got_other = net.swap_bit(got, 0)
    def lanes(v):
        return jnp.pad(v, [(0, 0)] * (v.ndim - 1) + [(0, 2 * HD - v.shape[-1])])

    def by_pair(v):
        return lanes(by_head(v, HD)).reshape(-1, 2 * per_row, 2 * HD)

    sums = backward(
        net.nodes,
        net.bits,
        3,
        dict(
            a_two=a_two,
            cot=cot_rows,
            cot_far=cot_other.reshape(count, width),
            scale=scale_both,
            w_gate=w_gate,
            w_up=w_up,
            w_down=w_down,
            resid=resid,
            x=x_share,
            gain_two=gain_two[None],
            gain_one=gain_one[None],
            gain_q=lanes(gain_query[None]),
            gain_k=lanes(gain_key[None]),
            w_out=w_out,
            w_back=w_own,
            a_one=a_one,
            a_near=got,
            a_far=got_other,
            q=q_padded,
            kv=kv_own,
            kv_in=kv_in,
            att=o_low,
            log=log_total.reshape(-1, 1, 2 * per_row),
            raw_q=by_pair(raw_low[:, :q_cols]),
            raw_k=by_pair(raw_low[:, q_cols : q_cols + k_cols]),
            cosine=lanes(jnp.concatenate([cosine, cosine], axis=1)),
            sine=lanes(jnp.concatenate([sine, -sine], axis=1)),
        ),
    )
    grad_gate, grad_up, grad_down = (v.astype(F32) for v in sums[:3])

    def sum_pair(mine):
        other = net.swap_side(mine)
        return jnp.where(
            side == 0, jnp.concatenate([mine, other]), jnp.concatenate([other, mine])
        )

    def unfolded(v, height):
        v = v.reshape(2, -1, height, v.shape[1])
        return v.transpose(0, 2, 1, 3).reshape(2, height, width)

    grad_out = unfolded(sums[3], q_cols).reshape(2 * q_cols, width).astype(F32)
    q_sum = unfolded(sum_pair(sums[4]), q_cols)
    kv_sum = unfolded(sum_pair(sums[5]), 2 * k_cols)
    out, d_tokens = (v.reshape(rows, per_row, width) for v in sums[6:8])
    gains = sums[8]

    def columns(both_sides, add=False):
        if add:
            return (both_sides[0].astype(F32) + both_sides[1].astype(F32)).T
        return both_sides.reshape(-1, width).astype(F32).T

    grad_query = columns(q_sum)
    grad_key = columns(kv_sum[:, :k_cols], shared)
    grad_value = columns(kv_sum[:, k_cols:], shared)
    head_share = HD // net.tp

    return (
        out,
        d_tokens,
        gains[0],
        grad_query,
        grad_key,
        grad_value,
        take(gains[2], t * head_share, head_share),
        take(gains[3], t * head_share, head_share),
        grad_out,
        gains[1],
        grad_gate,
        grad_up,
        grad_down,
    )


def solution(mesh):
    placed = (
        P(None, "seq", None),
        P(None, "seq"),
        P(None, "seq"),
        P(),
        P(),
        P(None, "tp"),
        P(None, "tp"),
        P(None, "tp"),
        P(),
        P(),
        P("tp", None),
        P(),
        P(None, "tp"),
        P(None, "tp"),
        P("tp", None),
        P(None, "seq", None),
    )
    return jax.shard_map(
        per_device,
        mesh=mesh,
        in_specs=placed,
        out_specs=(
            P(None, "seq", None),
            P(None, "seq", None),
            P("tp"),
            P(None, "tp"),
            P(None, "tp"),
            P(None, "tp"),
            P("tp"),
            P("tp"),
            P("tp", None),
            P("tp"),
            P(None, "tp"),
            P(None, "tp"),
            P("tp", None),
        ),
        check_vma=False,
    )
```

```python
import functools

import jax
import jax.numpy as jnp
from jax import lax
from jax.experimental import pallas as pl
from jax.experimental.pallas import tpu as pltpu
from jax.sharding import PartitionSpec as P

HD = 64
NCORP = 8


EPS = 1e-05
EPS_HEAD = 1e-06
ROPE_BASE = 10000.0
BF = jnp.bfloat16
F32 = jnp.float32
MESH = pl.DeviceIdType.MESH
LAG = 2
AHEAD = 3
KEPT = 6


def rope_tables(positions):
    half = HD // 2
    rates = ROPE_BASE ** (-jnp.arange(half, dtype=jnp.float32) * 2.0 / HD)
    angle = positions.astype(jnp.float32)[:, None] * rates[None, :]
    return (jnp.cos(angle), jnp.sin(angle))


def rotate(vector, cosine, sine):
    half = vector.shape[-1] // 2
    first = vector[..., :half]
    second = vector[..., half:]
    return jnp.concatenate(
        [first * cosine - second * sine, second * cosine + first * sine], axis=-1
    )


def head_norm(vector, gain):
    inverse = lax.rsqrt(jnp.mean(vector * vector, axis=-1, keepdims=True) + EPS_HEAD)
    normed = vector * inverse
    return (normed, inverse, normed * gain)


def dot(a, b):
    return jnp.dot(a, b, preferred_element_type=F32)


def dot_tn(a, b):
    return lax.dot_general(a, b, (((0,), (0,)), ((), ())), preferred_element_type=F32)


def dot_nt(a, b):
    return lax.dot_general(a, b, (((1,), (1,)), ((), ())), preferred_element_type=F32)


def take(array, start, size, axis=0):
    return lax.dynamic_slice_in_dim(array, start, size, axis)


class Links:
    def __init__(self):
        self.seq = lax.axis_size("seq")
        self.tp = lax.axis_size("tp")
        self.nodes = self.seq // 2
        self.bits = self.tp.bit_length() - 1
        rank = lax.axis_index("seq")
        self.node = rank // 2
        self.side = rank % 2
        self.t = lax.axis_index("tp")

    def swap_side(self, value):
        return lax.ppermute(value, "seq", [(s, s ^ 1) for s in range(self.seq)])

    def swap_bit(self, value, bit):
        return lax.ppermute(value, "tp", [(r, r ^ (1 << bit)) for r in range(self.tp)])

    def relative(self, rows):
        share = rows.shape[0] // self.tp
        return jnp.concatenate(
            [take(rows, (self.t ^ j) * share, share) for j in range(self.tp)], axis=0
        )


def remote_copy(src, dst, send, recv, **where):
    return pltpu.make_async_remote_copy(
        src, dst, send, recv, device_id=where, device_id_type=MESH
    )


def attend_kernel(nodes, bits, *refs):
    names = (
        "tokens", "w_query", "w_key", "w_value", "w_out", "cot", "gain_one", "gain_two", "gain_q", "gain_k",
        "cosine", "sine", "count",
        "q", "kv", "raw", "a_one", "att", "log", "counts", "cot_out", "resid", "a_out", "kv_in", "a_other",
        "tok", "wq", "wk", "wv", "wo", "raw_other", "acc", "weight_sum", "att_in", "att_rel", "hold", "temp", "got",
        "mine",
        "load_sem", "raw_sem", "kv_send", "kv_recv", "count_send", "count_recv", "cot_send", "cot_recv", "att_sem",
        "sum_send", "sum_recv", "all_send", "all_recv", "own_sem", "a_sem",
    )
    assert len(names) == len(refs)
    R = dict(zip(names, refs))
    tp, seq = 1 << bits, 2 * nodes
    top = bits - 1
    rank, t = lax.axis_index("seq"), lax.axis_index("tp")
    node, side = rank // 2, rank % 2
    across = rank + 1 - 2 * side
    n_q, wide, _ = R["q"].shape
    n_rows = R["kv"].shape[0]
    heads = n_q // n_rows
    q_cols = heads * HD
    span = wide // 2
    share, width = R["resid"].shape
    count = tp * share

    def strips(rows, step, body):
        @pl.loop(0, rows // step)
        def _(m):
            body(pl.ds(pl.multiple_of(m * step, step), step))

    def flip(bit):
        return t + (1 << bit) * (1 - 2 * ((t // (1 << bit)) % 2))

    def block_of(j):
        other = t
        for bit in range(bits):
            there = (j // (1 << bit)) % 2
            other = other + there * (1 << bit) * (1 - 2 * ((t // (1 << bit)) % 2))
        return other

    def block_rows(j):
        return pl.ds(pl.multiple_of(block_of(j) * share, share), share)

    half = R["w_out"].shape[0] // 2
    loads = [(R["tokens"], R["tok"]), (R["w_query"], R["wq"]), (R["w_key"], R["wk"])]
    loads += [(R["w_value"], R["wv"])]
    loads += [
        (
            R["w_out"].at[pl.ds(pl.multiple_of(at * half, half), half)],
            R["wo"].at[pl.ds(k * half, half)],
        )
        for k, at in enumerate((side, 1 - side))
    ]

    def load(k):
        return pltpu.make_async_copy(loads[k][0], loads[k][1], R["load_sem"].at[k])

    for k in range(6):
        load(k).start()

    barrier = pltpu.get_barrier_semaphore()
    for step in range(1, seq):
        pl.semaphore_signal(
            barrier, 1, device_id={"seq": (rank + step) % seq}, device_id_type=MESH
        )
    for bit in range(bits):
        pl.semaphore_signal(barrier, 1, device_id={"tp": flip(bit)}, device_id_type=MESH)

    load(0).wait()

    def first_norm(r):
        v = R["tok"][r, :].astype(F32)
        inverse = lax.rsqrt(jnp.mean(v * v, axis=-1, keepdims=True) + EPS)
        R["a_one"][r, :] = (v * inverse * R["gain_one"][...]).astype(BF)

    strips(count, 16, first_norm)
    for k in (1, 2, 3):
        load(k).wait()

    def project(r):
        a = R["a_one"][r, :]
        q = jnp.dot(a, R["wq"][...], preferred_element_type=F32)
        k = jnp.dot(a, R["wk"][...], preferred_element_type=F32)
        v = jnp.dot(a, R["wv"][...], preferred_element_type=F32)
        if k.shape[1] == HD:
            first = second = jnp.concatenate([k, v], axis=1)
        else:
            low = lax.broadcasted_iota(jnp.int32, k.shape, 1) < HD
            first = jnp.where(low, k, pltpu.roll(v, HD, 1))
            second = jnp.where(low, pltpu.roll(k, HD, 1), v)
        at_first = side == 0
        R["raw"][r, 0:q_cols] = jnp.where(at_first, q[:, :q_cols], q[:, q_cols:]).astype(BF)
        R["raw"][r, q_cols:] = jnp.where(at_first, first, second).astype(BF)
        R["raw_other"][r, 0:q_cols] = jnp.where(at_first, q[:, q_cols:], q[:, :q_cols]).astype(BF)
        R["raw_other"][r, q_cols:] = jnp.where(at_first, second, first).astype(BF)

    strips(count, 256, project)
    pl.semaphore_wait(barrier, seq - 1 + bits)
    raw_copy = remote_copy(
        R["raw_other"],
        R["raw"].at[pl.ds(count, count)],
        R["raw_sem"].at[0],
        R["raw_sem"].at[1],
        seq=across,
    )
    raw_copy.start()
    R["counts"][0] = R["count"][...]
    count_copies = [
        remote_copy(
            R["count"],
            R["counts"].at[step],
            R["count_send"].at[step - 1],
            R["count_recv"].at[step - 1],
            seq=(rank + step) % seq,
        )
        for step in range(1, seq)
    ]
    for copy in count_copies:
        copy.start()

    lane = lax.broadcasted_iota(jnp.int32, (span, 2 * HD), 1)

    def head(v, gain, at):
        v = jnp.where(lane < HD, v, 0.0)
        inverse = lax.rsqrt(jnp.sum(v * v, axis=-1, keepdims=True) * (1.0 / HD) + EPS_HEAD)
        v = v * inverse * gain
        swapped = jnp.where(
            lane < HD // 2, pltpu.roll(v, 2 * HD - HD // 2, 1), pltpu.roll(v, HD // 2, 1)
        )
        return v * R["cosine"][at, :] - swapped * R["sine"][at, :]

    def head_rows(d):
        here = pl.ds(d * span, span)

        @pl.loop(0, n_rows)
        def _(r):
            at = pl.ds(pl.multiple_of((d * n_rows + r) * span, span), span)

            @pl.loop(0, heads // 2)
            def _(h):
                pair = R["raw"][at, pl.ds(pl.multiple_of(h * 2 * HD, 2 * HD), 2 * HD)].astype(F32)
                i = r * heads + 2 * h
                R["q"][i, here, :] = head(pair, R["gain_q"][...], at).astype(BF)
                R["q"][i + 1, here, :] = head(
                    pltpu.roll(pair, HD, 1), R["gain_q"][...], at
                ).astype(BF)

            pair = R["raw"][at, q_cols:].astype(F32)
            R["kv"][r, 0, here, :] = jnp.where(
                lane < HD, head(pair, R["gain_k"][...], at), pair
            ).astype(BF)

    head_rows(0)
    raw_copy.wait()
    head_rows(1)

    def kv_copy(step):
        return remote_copy(
            R["kv"],
            R["kv_in"].at[step - 1],
            R["kv_send"].at[step - 1],
            R["kv_recv"].at[step - 1],
            seq=rank + 2 * step,
        )

    for step in range(1, nodes):
        pl.when(node + step < nodes)(kv_copy(step).start)
    cot_copies = [
        remote_copy(
            R["cot"].at[block_rows(j)],
            R["cot_out"].at[j],
            R["cot_send"].at[j],
            R["cot_recv"].at[j],
            seq=across,
        )
        for j in range(0, tp, 2)
    ]
    for copy in cot_copies:
        copy.start()

    def attend(kv_at, diagonal):
        @pl.loop(0, n_q)
        def _(i):
            kv = kv_at(i // heads)
            scores = lax.dot_general(
                R["q"][i], kv, (((1,), (1,)), ((), ())), preferred_element_type=F32
            )
            weight = jnp.exp2(scores * (HD**-0.5 * 1.4426950408889634))
            if diagonal:
                q_at = lax.broadcasted_iota(jnp.int32, (wide, wide), 0)
                k_at = lax.broadcasted_iota(jnp.int32, (wide, wide), 1)
                q_at = jnp.where(q_at < span, q_at + span * side, q_at - span * side)
                k_at = jnp.where(k_at < span, k_at + span * side, k_at - span * side)
                weight = jnp.where(k_at <= q_at, weight, 0.0)
            sums = weight[:, :128]
            for c in range(128, wide, 128):
                sums = sums + weight[:, c : c + 128]
            values = jnp.dot(weight.astype(BF), kv, preferred_element_type=F32)
            if diagonal:
                R["weight_sum"][i] = sums
                R["acc"][i] = values
            else:
                R["weight_sum"][i] += sums
                R["acc"][i] += values

    attend(lambda r: R["kv"][r, 0], True)

    @pl.loop(1, nodes)
    def _(step):
        @pl.when(node >= step)
        def _():
            kv_copy(step).wait_recv()
            attend(lambda r: R["kv_in"][step - 1, r, 0], False)

    att_copy = remote_copy(
        R["att"].at[1], R["att_in"], R["att_sem"].at[0], R["att_sem"].at[1], seq=across
    )

    def finish(d):
        at = pl.ds(d * span, span)

        @pl.loop(0, n_rows * (heads // 2))
        def _(n):
            r, h = n // (heads // 2), n % (heads // 2)
            out = []
            for k in range(2):
                i = r * heads + 2 * h + k
                total = jnp.sum(R["weight_sum"][i, at, :], axis=-1, keepdims=True)
                out.append(R["acc"][i, at, :] / total)
            both = jnp.where(lane < HD, pltpu.roll(out[0], HD, 1), out[1])
            rows = pl.ds(pl.multiple_of(r * span, span), span)
            R["att"][d, rows, pl.ds(pl.multiple_of(h * 2 * HD, 2 * HD), 2 * HD)] = both.astype(BF)

    finish(1)
    att_copy.start()
    half_rows = pl.multiple_of(t % 2 * (count // 2), count // 2)
    a_half = pl.ds(half_rows, count // 2)
    a_copy = remote_copy(
        R["a_one"].at[a_half],
        R["a_other"].at[a_half],
        R["a_sem"].at[0],
        R["a_sem"].at[1],
        seq=across,
    )
    a_copy.start()
    finish(0)
    ones = jnp.ones((8, 2 * HD), F32)

    @pl.loop(0, n_q)
    def _(i):
        total = lax.dot_general(
            ones,
            R["weight_sum"][i],
            (((1,), (1,)), ((), ())),
            precision=lax.Precision.HIGHEST,
            preferred_element_type=F32,
        )
        R["log"][i] = jnp.log2(total)[0:1]

    @pl.loop(0, tp)
    def _(j):
        at = pl.ds(pl.multiple_of(j * share, share), share)
        R["att_rel"][at, 0:q_cols] = R["att"][0, block_rows(j), :]

    att_copy.wait()

    @pl.loop(0, tp)
    def _(j):
        at = pl.ds(pl.multiple_of(j * share, share), share)
        R["att_rel"][at, q_cols:] = R["att_in"][block_rows(j), :]

    for k in (4, 5):
        load(k).wait()
    hold, temp, got, mine = R["hold"], R["temp"], R["got"], R["mine"]
    chunk = 512

    @pl.loop(0, width // chunk)
    def _(n):
        cols = pl.ds(pl.multiple_of(n * chunk, chunk), chunk)
        value = jnp.dot(
            R["att_rel"][...], R["wo"][:, cols], preferred_element_type=F32
        ).astype(BF)
        for j in range(tp):
            (temp if j % 2 else hold)[j // 2, :, cols] = value[j * share : (j + 1) * share]

    slot = 0
    for bit in range(bits):
        keep = list(range(0, tp, 2 << bit))
        copies = []
        for k, j in enumerate(keep):
            src = temp.at[j // 2] if bit == 0 else hold.at[(j | 1 << bit) // 2]
            copies.append(
                remote_copy(
                    src,
                    got.at[slot + k],
                    R["sum_send"].at[slot + k],
                    R["sum_recv"].at[slot + k],
                    tp=flip(bit),
                )
            )
            copies[-1].start()
        for k, j in enumerate(keep):
            copies[k].wait()

            def add(r, k=k, j=j):
                hold[j // 2, r, :] = (
                    hold[j // 2, r, :].astype(F32) + got[slot + k, r, :].astype(F32)
                ).astype(BF)

            strips(share, 32, add)
        slot += len(keep)

    def second_norm(r):
        at = pl.ds(pl.multiple_of(t * share + r.start, 16), 16)
        resid = R["tok"][at, :].astype(F32) + hold[0, r, :].astype(F32)
        R["resid"][r, :] = resid
        inverse = lax.rsqrt(jnp.mean(resid * resid, axis=-1, keepdims=True) + EPS)
        mine[r, :] = (resid * inverse * R["gain_two"][...]).astype(BF)

    strips(share, 16, second_norm)

    a_out = R["a_out"]
    started = []

    def send(src, dst, k, **where):
        copy = remote_copy(src, dst, R["all_send"].at[k], R["all_recv"].at[k], **where)
        copy.start()
        started.append(copy)
        return copy

    up = 1 << top
    cut = share // 2
    low, high = pl.ds(0, cut), pl.ds(cut, cut)
    by_side = send(mine, a_out.at[1, 0], 0, seq=across)
    by_top = send(mine, a_out.at[0, up], 1, tp=flip(top))
    put = pltpu.make_async_copy(mine, a_out.at[0, 0], R["own_sem"])
    put.start()
    k = 4
    for copy in cot_copies:
        copy.wait()
    cot_copies = []
    for j in range(0, tp, 2):
        cot_copies.append(
            remote_copy(
                R["cot_out"].at[j],
                R["cot_out"].at[j + 1],
                R["cot_send"].at[j + 1],
                R["cot_recv"].at[j + 1],
                tp=flip(0),
            )
        )
        cot_copies[-1].start()
    pending = {}
    for bit in reversed(range(top)):
        have = [j for j in range(tp) if j % (2 << bit) == 0]
        if bit == top - 1:
            pending[0, 0] = send(mine, a_out.at[0, 1 << bit], k, tp=flip(bit))
            k += 1
            by_side.wait_recv()
            far_low = send(a_out.at[1, 0, low], a_out.at[1, up, low], 2, tp=flip(top))
            pending[1, 0] = send(a_out.at[1, 0], a_out.at[1, 1 << bit], k, tp=flip(bit))
            k += 1
            by_top.wait_recv()
            far_high = send(a_out.at[0, up, high], a_out.at[1, up, high], 3, seq=across)
            pending[0, up] = send(a_out.at[0, up], a_out.at[0, up | 1 << bit], k, tp=flip(bit))
            k += 1
            far_low.wait_recv()
            far_high.wait_recv()
            pending[1, up] = send(a_out.at[1, up], a_out.at[1, up | 1 << bit], k, tp=flip(bit))
            k += 1
        else:
            for d in range(2):
                for j in have:
                    pending[d, j] = send(
                        a_out.at[d, j], a_out.at[d, j | 1 << bit], k, tp=flip(bit)
                    )
                    k += 1
        for copy in pending.values():
            copy.wait_recv()
        pending = {}
    a_copy.wait()
    a_next = remote_copy(
        R["a_other"].at[a_half],
        R["a_other"].at[a_half],
        R["a_sem"].at[2],
        R["a_sem"].at[3],
        tp=flip(0),
    )
    a_next.start()
    for copy in started:
        copy.wait_send()
    put.wait()
    for copy in count_copies + cot_copies:
        copy.wait()
    a_next.wait()
    for step in range(1, nodes):
        pl.when(node + step < nodes)(kv_copy(step).wait_send)


def attend(nodes, bits, ident, values):
    tp, seq = 1 << bits, 2 * nodes
    tokens, width = values["tokens"].shape
    share = tokens // tp
    q_all, k_all = values["w_query"].shape[1], values["w_key"].shape[1]
    heads = q_all // 2 // HD
    rows, wide = values["rows"], 2 * tokens // values["rows"]
    n_q = rows * heads
    cols = (heads + 2) * HD
    inputs = {k: v for k, v in values.items() if k != "rows"}
    inside = ("gain_one", "gain_two", "gain_q", "gain_k", "cosine", "sine", "count")
    vmem = pl.BlockSpec(memory_space=pltpu.VMEM)
    anywhere = pl.BlockSpec(memory_space=pl.ANY)
    dma = pltpu.SemaphoreType.DMA
    messages = 4 + 2 * (tp - 2)
    kv = (rows, 1, wide, 2 * HD)
    outs = [
        ((n_q, wide, 2 * HD), BF, vmem),
        (kv, BF, vmem),
        ((2 * tokens, cols), BF, vmem),
        ((tokens, width), BF, vmem),
        ((2, tokens, heads * HD), BF, vmem),
        ((n_q, 1, wide), F32, vmem),
        ((seq,) + values["count"].shape, F32, vmem),
        ((tp, share, width), BF, anywhere),
        ((share, width), F32, vmem),
        ((2, tp, share, width), BF, anywhere),
        ((nodes - 1,) + kv, BF, vmem),
        ((tokens, width), BF, anywhere),
    ]
    scratch = [
        ((tokens, width), BF),
        ((width, q_all), BF),
        ((width, k_all), BF),
        ((width, k_all), BF),
        ((q_all, width), BF),
        ((tokens, cols), BF),
        ((n_q, wide, 2 * HD), F32),
        ((n_q, wide, 128), F32),
        ((tokens, heads * HD), BF),
        ((tokens, q_all), BF),
        ((tp // 2, share, width), BF),
        ((tp // 2, share, width), BF),
        ((tp - 1, share, width), BF),
        ((share, width), BF),
    ]
    sems = [(6,), (2,), (nodes - 1,), (nodes - 1,), (seq - 1,), (seq - 1,), (tp,), (tp,), (2,)]
    sems += [(tp - 1,), (tp - 1,), (messages,), (messages,), (), (4,)]
    return pl.pallas_call(
        functools.partial(attend_kernel, nodes, bits),
        out_shape=[jax.ShapeDtypeStruct(shape, kind) for shape, kind, _ in outs],
        in_specs=[vmem if k in inside else anywhere for k in inputs],
        out_specs=[place for _, _, place in outs],
        scratch_shapes=[pltpu.VMEM(shape, kind) for shape, kind in scratch]
        + [dma(s) for s in sems],
        compiler_params=pltpu.CompilerParams(
            collective_id=ident, has_side_effects=True, vmem_limit_bytes=56 << 20
        ),
        cost_estimate=pl.CostEstimate(
            flops=0, bytes_accessed=200 << 20, transcendentals=0
        ),
        name="attend",
    )(*inputs.values())


def backward_kernel(nodes, bits, *refs):
    names = (
        "a_two", "cot", "cot_far", "scale", "w_gate", "w_up", "w_down", "resid", "x", "gain_two",
        "gain_one", "gain_q", "gain_k", "w_out", "w_back", "a_one", "a_other", "q", "kv", "kv_in", "att",
        "log", "raw", "cosine", "sine", "gate_sum", "up_sum", "down_sum", "out_sum",
        "q_sum", "kv_sum", "out", "tokens", "gains", "two_in", "ffn_in", "one_in", "gate_part",
        "up_part", "down_part", "red", "own", "hold", "temp", "low", "a_in", "a_t", "w_rows",
        "q_in", "d_out", "d_q", "d_kv", "kv_all", "att_in", "d_att", "delta", "d_raw", "q_part",
        "kv_part", "out_part", "kv_back", "kv_far", "d_resid", "fresh", "gain_rows", "gain_box",
        "gain_all", "log_in", "cot_in", "hidden", "d_pair", "w_strip", "w_cols", "stage", "stage_down",
        "own_sem", "red_send", "red_recv", "fin_send", "fin_recv", "x_send", "x_recv", "put_sem",
        "load_sem", "sum_send", "sum_recv", "temp_sem", "low_send", "low_recv", "kv_send",
        "kv_recv", "tok_send", "tok_recv", "tok_put", "gain_send", "gain_recv", "w_sem",
        "stage_sem",
    )
    assert len(names) == len(refs)
    R = dict(zip(names, refs))
    tp, seq = 1 << bits, 2 * nodes
    top = bits - 1
    rank, t = lax.axis_index("seq"), lax.axis_index("tp")
    node, side = rank // 2, rank % 2
    across = rank + 1 - 2 * side
    last = nodes - 1
    me = rank * tp + t
    total = seq * tp
    share, width = R["x"].shape
    n_q, wide, _ = R["q"].shape
    n_rows = R["kv"].shape[0]
    heads = n_q // n_rows
    span = wide // 2
    slots, prow, pcol = R["red"].shape[1:]
    half = R["red_send"].shape[1]
    ff = R["gate_part"].shape[1]
    chunks = ff // pcol
    tall = width // prow
    per_chunk = 3 * tall
    fed = chunks * per_chunk

    def strips(rows, step, body):
        @pl.loop(0, rows // step)
        def _(m):
            body(pl.ds(pl.multiple_of(m * step, step), step))

    def flip(bit):
        return t + (1 << bit) * (1 - 2 * ((t // (1 << bit)) % 2))

    def block_of(j):
        other = t
        for bit in range(bits):
            there = (j // (1 << bit)) % 2
            other = other + there * (1 << bit) * (1 - 2 * ((t // (1 << bit)) % 2))
        return other

    def block_rows(j):
        return pl.ds(pl.multiple_of(block_of(j) * share, share), share)

    barrier = pltpu.get_barrier_semaphore()

    @pl.loop(1, total)
    def _(k):
        other = (me + k) % total
        pl.semaphore_signal(
            barrier, 1, device_id={"seq": other // tp, "tp": other % tp}, device_id_type=MESH
        )

    pl.semaphore_wait(barrier, total - 1)

    red, own = R["red"], R["own"]
    own_sem, put_sem = R["own_sem"], R["put_sem"]
    red_sems = R["red_send"], R["red_recv"]
    fin_sems = R["fin_send"], R["fin_recv"]
    x_sems = R["x_send"], R["x_recv"]

    def with_piece(b, j, act):
        p = 2 * j + b
        chunk, k, kind = p // per_chunk, p % tall, (p % per_chunk) // tall
        along_chunk = pl.multiple_of(chunk * pcol, pcol)
        along_side = pl.multiple_of(side * ff + chunk * pcol, pcol)
        along_width = pl.ds(pl.multiple_of(k * prow, prow), prow)
        for i, name in enumerate(("gate", "up", "down")):

            @pl.when((p < fed) & (kind == i))
            def _(name=name):
                part, whole = R[name + "_part"], R[name + "_sum"]
                if name == "down":
                    act(
                        part.at[pl.ds(along_chunk, prow), along_width],
                        whole.at[pl.ds(along_side, prow), along_width],
                    )
                else:
                    act(
                        part.at[along_width, pl.ds(along_chunk, pcol)],
                        whole.at[along_width, pl.ds(along_side, pcol)],
                    )

        base = fed
        for name in ("out", "q", "kv"):
            part, whole = R[name + "_part"], R[name + "_sum"]
            size = part.shape[1] // pcol

            @pl.when((p >= base) & (p < base + size))
            def _(part=part, whole=whole, base=base, name=name):
                col = pl.ds(pl.multiple_of((p - base) * pcol, pcol), pcol)
                row = 0 if name == "q" else side * prow
                act(part.at[:, col], whole.at[pl.ds(pl.multiple_of(row, prow), prow), col])

            base += size

    def along(src, dst, sems, b, j, target):
        return remote_copy(src, dst, sems[0].at[b, j], sems[1].at[b, j], seq=target)

    def placed(j):
        if gap == 0:
            return j, (j >= 0) & (j < half)
        after = j >= late + gap
        return jnp.where(after, j - gap, j), ((j >= 0) & (j < late)) | (
            after & (j < half + gap)
        )

    def crosses(j):
        return (j < late) | (j >= late_end)

    def stream(b, i):
        v = node if b == 0 else last - node
        ahead = rank + 2 if b == 0 else rank - 2
        behind = rank - 2 if b == 0 else rank + 2
        f, there = placed(i - LAG * v + AHEAD - 1)

        @pl.when((v > 0) & there)
        def _():
            with_piece(
                b,
                f,
                lambda src, dst: pltpu.make_async_copy(
                    src, own.at[b, f % AHEAD], own_sem.at[b, f % AHEAD]
                ).start(),
            )

        j, there = placed(i - LAG * v)

        @pl.when((v == 0) & there)
        def _():
            with_piece(
                b, j, lambda src, dst: along(src, red.at[b, j % slots], red_sems, b, j, ahead).start()
            )

        @pl.when((v > 0) & there)
        def _():
            mine = own.at[b, j % AHEAD]
            pltpu.make_async_copy(mine, mine, own_sem.at[b, j % AHEAD]).wait()
            along(red.at[b, j % slots], red.at[b, j % slots], red_sems, b, j, behind).wait_recv()
            at = j % slots

            def add(r):
                red[b, at, r] = (
                    red[b, at, r].astype(F32) + own[b, j % AHEAD, r].astype(F32)
                ).astype(BF)

            strips(prow, 64, add)

            @pl.when(v < last)
            def _():
                along(red.at[b, j % slots], red.at[b, j % slots], red_sems, b, j, ahead).start()

            @pl.when((v == last) & (j >= KEPT))
            def _():
                @pl.when(crosses(j - KEPT))
                def _():
                    along(red.at[b, 0], red.at[b, 0], x_sems, b, j - KEPT, across).wait_send()

                along(red.at[b, 0], red.at[b, 0], fin_sems, b, j - KEPT, behind).wait_send()
                pltpu.make_async_copy(red.at[b, 0], red.at[b, 0], put_sem.at[b, j - KEPT]).wait()

            @pl.when(v == last)
            def _():
                def act(src, dst):
                    along(red.at[b, j % slots], dst, fin_sems, b, j, behind).start()

                    @pl.when(crosses(j))
                    def _():
                        along(red.at[b, j % slots], dst, x_sems, b, j, across).start()

                    pltpu.make_async_copy(red.at[b, j % slots], dst, put_sem.at[b, j]).start()

                with_piece(b, j, act)

        g, there = placed(i - LAG * last - LAG * (last - v))

        @pl.when((v < last) & there)
        def _():
            along(red.at[b, 0], red.at[b, 0], fin_sems, b, g, ahead).wait_recv()

            @pl.when(v > 0)
            def _():
                along(red.at[b, 0], red.at[b, 0], red_sems, b, g, ahead).wait_send()

            def act(src, dst):
                @pl.when(v > 0)
                def _():
                    along(dst, dst, fin_sems, b, g, behind).start()

                @pl.when(crosses(g))
                def _():
                    along(dst, dst, x_sems, b, g, across).start()

            with_piece(b, g, act)

    hold, temp = R["hold"], R["temp"]
    boxes = [R["two_in"], R["ffn_in"], R["one_in"]]

    def held(ref, d, k):
        return ref.at[pl.ds((d * (tp // 2) + k) * share, share)]

    def messages(bit):
        base = sum(tp >> b for b in range(bit))
        keep = [(d, j) for d in range(2) for j in range(0, tp, 2 << bit)]
        return [(base + k, d, j) for k, (d, j) in enumerate(keep)]

    def sum_copy(n, m, src, **where):
        return remote_copy(
            src, boxes[n].at[m], R["sum_send"].at[n, m], R["sum_recv"].at[n, m], **where
        )

    def sum_start(n, bit):
        for m, d, j in messages(bit):
            src = held(temp, d, j // 2) if bit == 0 else held(hold, d, (j | 1 << bit) // 2)
            sum_copy(n, m, src, tp=flip(bit)).start()

    def sum_add(n, bit):
        for m, d, j in messages(bit):
            sum_copy(n, m, held(temp, d, j // 2), tp=flip(bit)).wait()
        loads = []
        for m, d, j in messages(bit):
            k = j // 2
            loads.append(
                pltpu.make_async_copy(boxes[n].at[m], held(temp, d, k), R["temp_sem"].at[d, k])
            )
            loads[-1].start()
        for copy, (m, d, j) in zip(loads, messages(bit)):
            copy.wait()
            base = (d * (tp // 2) + j // 2) * share

            def add(r, base=base):
                at = pl.ds(pl.multiple_of(base + r.start, 16), 16)
                hold[at, :] = (hold[at, :].astype(F32) + temp[at, :].astype(F32)).astype(BF)

            strips(share, 16, add)

    final = 2 * (tp - 1)

    def side_start(n):
        sum_copy(n, final, held(hold, 1, 0), seq=across).start()

    def side_finish(n):
        sum_copy(n, final, held(hold, 1, 0), seq=across).wait()
        load = pltpu.make_async_copy(boxes[n].at[final], held(temp, 0, 0), R["temp_sem"].at[0, 0])
        load.start()
        load.wait()

    def side_sum(r):
        return hold[r, :].astype(F32) + temp[r, :].astype(F32)

    ends = [R["out"], R["tokens"]]

    def token_copy(n, k, src, j, bit):
        return remote_copy(
            src,
            ends[n].at[block_of(j)],
            R["tok_send"].at[n, k],
            R["tok_recv"].at[n, k],
            tp=flip(bit),
        )

    def token_messages(bit):
        base = sum(tp >> (b + 1) for b in range(bit + 1, bits))
        return [(base + k, j) for k, j in enumerate(range(0, tp, 2 << bit))]

    def tokens_start(n, bit):
        for k, j in token_messages(bit):
            src = R["fresh"].at[n] if j == 0 else ends[n].at[block_of(j)]
            token_copy(n, k, src, j, bit).start()

    def tokens_wait(n, bit):
        for k, j in token_messages(bit):
            token_copy(n, k, R["fresh"].at[n], j, bit).wait()

    def tokens_put(n):
        return pltpu.make_async_copy(R["fresh"].at[n], ends[n].at[t], R["tok_put"].at[n])

    def block(d, j):
        return pl.ds((d * tp + j) * share, share)

    loads = [
        (R["w_out"].at[pl.ds(pl.multiple_of(side * heads * HD, heads * HD), heads * HD)], R["w_rows"]),
        (R["w_back"], R["a_t"].at[:, pl.ds(0, R["w_back"].shape[1])]),
        (R["a_one"], R["a_in"].at[pl.ds(0, tp * share)]),
        (R["q"], R["q_in"]),
        (R["kv"], R["kv_all"].at[0]),
        (R["kv_in"], R["kv_all"].at[pl.ds(1, nodes - 1)]),
        (R["att"], R["att_in"]),
        (R["log"], R["log_in"]),
        (R["a_two"], R["low"]),
        (R["cot_far"], R["a_in"].at[pl.ds(tp * share, tp * share)]),
        (R["cot"].at[block_rows(0)], R["cot_in"]),
        (R["a_other"], R["a_in"].at[pl.ds(tp * share, tp * share)]),
    ] + [(R["cot"].at[block_rows(j)], R["a_in"].at[block(0, j)]) for j in range(tp)]

    def load(k):
        return pltpu.make_async_copy(loads[k][0], loads[k][1], R["load_sem"].at[k])

    w_cols, w_sem = R["w_cols"], R["w_sem"]
    both = 2 * tp * share
    nt = (((1,), (1,)), ((), ()))
    tn = (((0,), (0,)), ((), ()))

    def chunk_loads(c):
        at = pl.multiple_of(side * ff + c * pcol, pcol)
        slot = c % 2
        down_at = pl.multiple_of(slot * pcol, pcol)
        return [
            pltpu.make_async_copy(
                R["w_gate"].at[:, pl.ds(at, pcol)], w_cols.at[slot, 0], w_sem.at[slot, 0]
            ),
            pltpu.make_async_copy(
                R["w_up"].at[:, pl.ds(at, pcol)], w_cols.at[slot, 1], w_sem.at[slot, 1]
            ),
            pltpu.make_async_copy(
                R["w_down"].at[pl.ds(at, pcol)],
                hold.at[pl.ds(down_at, pcol)],
                w_sem.at[slot, 2],
            ),
        ]

    def begin():
        load(8).start()
        for copy in chunk_loads(0):
            copy.start()
        early = (9, *range(12, 12 + tp))
        for k in early:
            load(k).start()
        for copy in chunk_loads(1):
            copy.start()
        for k in (0, 3, 4, 5, 6, 7, 10):
            load(k).start()
        load(8).wait()
        for k in early:
            load(k).wait()

        def body(r):
            R["a_in"][r, :] = (R["a_in"][r, :].astype(F32) * R["scale"][r, :]).astype(BF)

        strips(both, 32, body)

    def chunk_ready(c):
        for copy in chunk_loads(c):
            copy.wait()

    def chunk_next(c):
        @pl.when(c + 2 < chunks)
        def _():
            for copy in chunk_loads(c + 2):
                copy.start()

    def chunk_forward(c, at):
        slot = c % 2
        cols = pl.ds(pl.multiple_of(c * pcol, pcol), pcol)
        w_rows = hold.at[pl.ds(pl.multiple_of(slot * pcol, pcol), pcol)]

        gate = jnp.dot(R["low"][at, :], w_cols[slot, 0], preferred_element_type=F32)
        up = jnp.dot(R["low"][at, :], w_cols[slot, 1], preferred_element_type=F32)
        d_hidden = lax.dot_general(R["a_in"][at, :], w_rows[...], nt, preferred_element_type=F32)
        sigma = 1.0 / (1.0 + jnp.exp(-gate))
        smooth = gate * sigma
        R["hidden"][at, cols] = (smooth * up).astype(BF)
        R["d_pair"][1, at, cols] = (d_hidden * smooth).astype(BF)
        R["d_pair"][0, at, cols] = (d_hidden * up * (sigma * (1.0 + gate - smooth))).astype(BF)

    def turn():
        def body(at):
            R["a_t"][:, at] = R["low"][at, :].T

        strips(both, 256, body)

    def stage_copies(c):
        at = pl.ds(pl.multiple_of(c * pcol, pcol), pcol)
        sem = R["stage_sem"]
        return [
            pltpu.make_async_copy(R["stage"].at[0], R["gate_part"].at[:, at], sem.at[0]),
            pltpu.make_async_copy(R["stage"].at[1], R["up_part"].at[:, at], sem.at[1]),
            pltpu.make_async_copy(R["stage_down"], R["down_part"].at[at], sem.at[2]),
        ]

    def chunk_gradients(c):
        cols = pl.ds(pl.multiple_of(c * pcol, pcol), pcol)

        @pl.loop(0, 2)
        def _(k):
            def body(at):
                R["stage"][k, at, :] = jnp.dot(
                    R["a_t"][at, :], R["d_pair"][k, :, cols], preferred_element_type=F32
                ).astype(BF)

            strips(width, 1024, body)

        for copy in stage_copies(c)[:2]:
            copy.start()

    def chunk_down(c):
        cols = pl.ds(pl.multiple_of(c * pcol, pcol), pcol)

        def body(at):
            R["stage_down"][:, at] = lax.dot_general(
                R["hidden"][:, cols], R["a_in"][:, at], tn, preferred_element_type=F32
            ).astype(BF)

        strips(width, 1024, body)
        stage_copies(c)[2].start()

    def staged(c):
        for copy in stage_copies(c):
            copy.wait()

    def row_loads(n):
        rows = pl.ds(pl.multiple_of(n * pcol, pcol), pcol)
        cols = pl.ds(pl.multiple_of(side * ff, ff), ff)
        return [
            pltpu.make_async_copy(
                R[name].at[rows, cols], R["w_strip"].at[n % 2, k], w_sem.at[n % 2, k]
            )
            for k, name in enumerate(("w_gate", "w_up"))
        ]

    def down_loads(n):
        return [
            pltpu.make_async_copy(
                R["w_down"].at[
                    pl.ds(pl.multiple_of(side * ff, ff), ff),
                    pl.ds(pl.multiple_of(n * pcol, pcol), pcol),
                ],
                w_cols.at[n % 2, 0, pl.ds(0, ff)],
                w_sem.at[n % 2, 0],
            )
        ]

    def start_all(copies):
        for copy in copies:
            copy.start()

    def by_columns(low_n, high_n, loads, product):
        @pl.loop(low_n, high_n)
        def _(n):
            for copy in loads(n):
                copy.wait()
            cols = pl.ds(pl.multiple_of(n * pcol, pcol), pcol)

            @pl.loop(0, 2)
            def _(d):
                at = pl.ds(pl.multiple_of(d * tp * share, tp * share), tp * share)
                value = product(at, n % 2).astype(BF)
                for j in range(tp):
                    rows = pl.ds(
                        pl.multiple_of((d * (tp // 2) + j // 2) * share, share), share
                    )
                    (temp if j % 2 else hold)[rows, cols] = value[j * share : (j + 1) * share]

            @pl.when(n + 2 < width // pcol)
            def _():
                start_all(loads(n + 2))

    def second_part(low_n, high_n):
        def product(at, slot):
            value = lax.dot_general(
                R["d_pair"][0, at, :], R["w_strip"][slot, 0], nt, preferred_element_type=F32
            )
            return value + lax.dot_general(
                R["d_pair"][1, at, :], R["w_strip"][slot, 1], nt, preferred_element_type=F32
            )

        by_columns(low_n, high_n, row_loads, product)

    def ffn_part(low_n, high_n):
        def product(at, slot):
            return jnp.dot(
                R["hidden"][at, :], w_cols[slot, 0, 0:ff, :], preferred_element_type=F32
            )

        by_columns(low_n, high_n, down_loads, product)

    def normed(v):
        inverse = lax.rsqrt(jnp.mean(v * v, axis=-1, keepdims=True) + EPS)
        return v * inverse, inverse

    low = R["low"]

    def low_at(d, j):
        return low.at[block(d, j)]

    def low_copy(k, src, dst, **where):
        return remote_copy(src, dst, R["low_send"].at[k], R["low_recv"].at[k], **where)

    up = 1 << top
    low_side = low_copy(0, low_at(0, 0), low_at(1, 0), seq=across)
    low_top = low_copy(1, low_at(0, 0), low_at(0, up), tp=flip(top))
    low_far = low_copy(2, low_at(1, 0), low_at(1, up), tp=flip(top))

    def low_bit(bit):
        base = 3 + sum(tp >> b for b in range(bit + 1, top))
        return [
            low_copy(base + k, low_at(d, j), low_at(d, j | 1 << bit), tp=flip(bit))
            for k, (d, j) in enumerate(
                (d, j) for d in range(2) for j in range(0, tp, 2 << bit)
            )
        ]

    def second_norm():
        side_finish(0)
        load(10).wait()
        R["gain_rows"][...] = jnp.zeros_like(R["gain_rows"])

        def body(r):
            d_a = side_sum(r)
            n_two, inverse = normed(R["resid"][r, :])
            R["gain_rows"][1:2, :] += jnp.sum(d_a * n_two, axis=0, keepdims=True)
            e = d_a * R["gain_two"][...]
            d_resid = R["cot_in"][r, :].astype(F32) * R["scale"][r, :] + inverse * (
                e - n_two * jnp.mean(e * n_two, axis=-1, keepdims=True)
            )
            R["d_resid"][r, :] = d_resid
            low[r, :] = d_resid.astype(BF)

        strips(share, 16, body)
        low_side.start()
        low_top.start()

    lane = lax.broadcasted_iota(jnp.int32, (span, 2 * HD), 1)

    def attended_back():
        for k in (0, 6):
            load(k).wait()
        R["d_kv"][...] = jnp.zeros_like(R["d_kv"])
        R["d_q"][...] = jnp.zeros_like(R["d_q"])
        @pl.loop(0, 2)
        def _(d):
            value = lax.dot_general(
                low[pl.ds(pl.multiple_of(d * tp * share, tp * share), tp * share), :],
                R["w_rows"][...],
                nt,
                preferred_element_type=F32,
            ).astype(BF)
            for j in range(tp):
                at = pl.ds(pl.multiple_of((d * tp + block_of(j)) * share, share), share)
                R["d_att"][at, :] = value[j * share : (j + 1) * share]

        ones = jnp.ones((8, 2 * HD), F32)
        pairs = heads // 2

        @pl.loop(0, 2 * n_rows * pairs)
        def _(n):
            d, r, h = n // (n_rows * pairs), n // pairs % n_rows, n % pairs
            cols = pl.ds(pl.multiple_of(h * 2 * HD, 2 * HD), 2 * HD)
            rows = pl.ds(pl.multiple_of(r * span, span), span)
            at = pl.ds(pl.multiple_of(d * span, span), span)
            d_rows = pl.ds(pl.multiple_of((d * n_rows + r) * span, span), span)
            for k in range(2):
                grads = R["d_att"][d_rows, cols].astype(F32)
                values = R["att_in"][d, rows, cols].astype(F32)
                if k == 0:
                    grads = pltpu.roll(grads, HD, 1)
                    values = pltpu.roll(values, HD, 1)
                grads = jnp.where(lane < HD, 0.0, grads)
                i = r * heads + 2 * h + k
                R["d_out"][i, at, :] = grads.astype(BF)
                R["delta"][i, :, at] = lax.dot_general(
                    ones,
                    grads * values,
                    nt,
                    precision=lax.Precision.HIGHEST,
                    preferred_element_type=F32,
                )

    def put_folded(ref, c, value):
        rows, cols = value.shape
        at = pl.ds(pl.multiple_of(c // ref.shape[1] * rows, rows), rows)
        ref[at, pl.ds(pl.multiple_of(c % ref.shape[1], cols), cols)] = value.astype(BF)

    def out_gradient():
        chunk = width // 2

        @pl.loop(0, 2 * tp)
        def _(n):
            R["d_att"][pl.ds(pl.multiple_of(n * share, share), share), :] = R["att_in"][
                n // tp, block_rows(n % tp), :
            ]

        @pl.loop(0, width // chunk)
        def _(n):
            c = pl.multiple_of(n * chunk, chunk)
            value = lax.dot_general(
                R["d_att"][...], low[:, pl.ds(c, chunk)], tn, preferred_element_type=F32
            )
            put_folded(R["out_part"], c, value)

    def attention_block(piece, i, diagonal):
        r = i // heads
        kv = R["kv_all"][piece, r, 0]
        q, d_out = R["q_in"][i], R["d_out"][i]
        scores = lax.dot_general(kv, q, nt, preferred_element_type=F32)
        probs = jnp.exp2(scores * (HD**-0.5 * 1.4426950408889634) - R["log_in"][i])
        if diagonal:
            k_at = lax.broadcasted_iota(jnp.int32, (wide, wide), 0)
            q_at = lax.broadcasted_iota(jnp.int32, (wide, wide), 1)
            q_at = jnp.where(q_at < span, q_at + span * side, q_at - span * side)
            k_at = jnp.where(k_at < span, k_at + span * side, k_at - span * side)
            probs = jnp.where(k_at <= q_at, probs, 0.0)
        d_probs = lax.dot_general(kv, d_out, nt, preferred_element_type=F32)
        d_scores = (probs * (d_probs - R["delta"][i, 0:1, :])).astype(BF)
        R["d_kv"][piece, r] += jnp.dot(d_scores, q, preferred_element_type=F32) + jnp.dot(
            probs.astype(BF), d_out, preferred_element_type=F32
        ) * (HD**0.5)
        R["d_q"][i] += lax.dot_general(
            kv, d_scores, (((0,), (0,)), ((), ())), preferred_element_type=F32
        )

    def kv_copy(step):
        return remote_copy(
            R["kv_back"].at[step - 1],
            R["kv_far"].at[step - 1],
            R["kv_send"].at[step - 1],
            R["kv_recv"].at[step - 1],
            seq=rank - 2 * step,
        )

    def kv_send():
        for step in range(1, nodes):

            @pl.when(node >= step)
            def _():
                R["kv_back"][step - 1] = R["d_kv"][step].astype(BF)
                kv_copy(step).start()

    def kv_sum():
        for step in range(1, nodes):

            @pl.when(node + step < nodes)
            def _():
                kv_copy(step).wait_recv()
                R["d_kv"][0] += R["kv_far"][step - 1].astype(F32)

            @pl.when(node >= step)
            def _():
                kv_copy(step).wait_send()

    def head_back(grads, raw, gain, at):
        lanes = 2 * HD
        low_lane = lane < HD // 2
        raw = jnp.where(lane < HD, raw, 0.0)
        swapped = jnp.where(
            low_lane, pltpu.roll(grads, lanes - HD // 2, 1), pltpu.roll(grads, HD // 2, 1)
        )
        rotated = grads * R["cosine"][at, :] + swapped * R["sine"][at, :]
        inverse = lax.rsqrt(jnp.sum(raw * raw, axis=-1, keepdims=True) * (1.0 / HD) + EPS_HEAD)
        n = raw * inverse
        e = rotated * gain
        back = inverse * (e - n * (jnp.sum(e * n, axis=-1, keepdims=True) * (1.0 / HD)))
        return back, jnp.sum(rotated * n, axis=0, keepdims=True)

    def heads_back():
        scale = HD**-0.5
        pairs = heads // 2

        @pl.loop(0, 2 * n_rows)
        def _(n):
            r, d = n // 2, n % 2
            at = pl.ds(pl.multiple_of((d * n_rows + r) * span, span), span)
            here = pl.ds(pl.multiple_of(d * span, span), span)

            @pl.loop(0, pairs)
            def _(h):
                pair = []
                both_raw = R["raw"][at, pl.ds(pl.multiple_of(h * 2 * HD, 2 * HD), 2 * HD)].astype(F32)
                for k in range(2):
                    i = r * heads + 2 * h + k
                    grads = R["d_q"][i, :, here].T * scale
                    raw = both_raw if k == 0 else pltpu.roll(both_raw, HD, 1)
                    back, gain = head_back(grads, raw, R["gain_q"][...], at)
                    R["gain_rows"][2:3, 0 : 2 * HD] += gain
                    pair.append(back)
                R["d_raw"][at, pl.ds(pl.multiple_of(h * 2 * HD, 2 * HD), 2 * HD)] = jnp.where(
                    lane < HD, pair[0], pltpu.roll(pair[1], HD, 1)
                ).astype(BF)

            grads = R["d_kv"][0, r, here, :] * scale
            raw = R["raw"][at, heads * HD :].astype(F32)
            back, gain = head_back(grads, raw, R["gain_k"][...], at)
            R["gain_rows"][3:4, 0 : 2 * HD] += gain
            R["d_raw"][at, pl.ds(heads * HD, 2 * HD)] = jnp.where(lane < HD, back, grads).astype(
                BF
            )

    def raw_gradient():
        for k in (2, 11):
            load(k).wait()
        chunk = width // 2
        cut = heads * HD

        @pl.loop(0, width // chunk)
        def _(n):
            c = pl.multiple_of(n * chunk, chunk)
            value = lax.dot_general(
                R["d_raw"][...], R["a_in"][:, pl.ds(c, chunk)], tn, preferred_element_type=F32
            )
            put_folded(R["q_part"], c, value[:cut])
            put_folded(R["kv_part"], c, value[cut:])

    def first_part(low_n, high_n):
        inner = R["w_back"].shape[1]
        rel = R["hidden"]
        chunk = 512

        if low_n == 0:
            load(1).wait()

            @pl.loop(0, 2 * tp)
            def _(n):
                rows = pl.multiple_of((n // tp * tp + block_of(n % tp)) * share, share)
                rel[pl.ds(pl.multiple_of(n * share, share), share), 0:inner] = R["d_raw"][
                    pl.ds(rows, share), :
                ]

        @pl.loop(low_n, high_n)
        def _(n):
            cols = pl.ds(pl.multiple_of(n * chunk, chunk), chunk)

            @pl.loop(0, 2)
            def _(d):
                at = pl.ds(pl.multiple_of(d * tp * share, tp * share), tp * share)
                value = lax.dot_general(
                    rel[at, 0:inner], R["a_t"][cols, 0:inner], nt, preferred_element_type=F32
                ).astype(BF)
                for j in range(tp):
                    rows = pl.ds(
                        pl.multiple_of((d * (tp // 2) + j // 2) * share, share), share
                    )
                    (temp if j % 2 else hold)[rows, cols] = value[j * share : (j + 1) * share]

    def out_end():
        side_finish(1)

        def body(r):
            R["fresh"][0, r, :] = (R["resid"][r, :] + side_sum(r)).astype(BF)

        strips(share, 16, body)
        tokens_put(0).start()
        tokens_start(0, top)

    def first_norm():
        side_finish(2)

        def body(r):
            d_a = side_sum(r)
            n_one, inverse = normed(R["x"][r, :].astype(F32))
            R["gain_rows"][0:1, :] += jnp.sum(d_a * n_one, axis=0, keepdims=True)
            e = d_a * R["gain_one"][...]
            d_x = R["d_resid"][r, :] + inverse * (
                e - n_one * jnp.mean(e * n_one, axis=-1, keepdims=True)
            )
            R["fresh"][1, r, :] = d_x.astype(BF)

        strips(share, 16, body)
        tokens_put(1).start()
        tokens_start(1, top)
        part = width // tp
        for k in range(tp):
            R["gain_box"][k] = jnp.zeros((8, part), F32)
            R["gain_box"][k, 0:2, :] = R["gain_rows"][0:2, k * part : (k + 1) * part]
            R["gain_box"][k, 2:4, 0 : 2 * HD] = R["gain_rows"][2:4, 0 : 2 * HD]

        @pl.loop(1, total)
        def _(k):
            other = (me + k) % total
            remote_copy(
                R["gain_box"].at[other % tp],
                R["gain_all"].at[k],
                R["gain_send"].at[k],
                R["gain_recv"].at[k],
                seq=other // tp,
                tp=other % tp,
            ).start()

        R["gain_all"][0] = R["gain_box"][t]

    def gains_end():
        @pl.loop(1, total)
        def _(k):
            remote_copy(
                R["gain_box"].at[0],
                R["gain_all"].at[k],
                R["gain_send"].at[k],
                R["gain_recv"].at[k],
                seq=rank,
                tp=t,
            ).wait()

        R["gains"][...] = jnp.zeros_like(R["gains"])

        @pl.loop(0, total)
        def _(k):
            R["gains"][...] += R["gain_all"][k]

    tasks = {}

    def task(step, *acts):
        tasks.setdefault(step, []).extend(acts)
        return step

    def sums_tasks(n, step):
        for bit in range(bits):
            step += 2 if bit == 0 else 5
            following = (
                (lambda bit=bit: sum_start(n, bit + 1)) if bit < top else (lambda: side_start(n))
            )
            task(step, lambda bit=bit: sum_add(n, bit), following)
        return step + 5

    def token_tasks(n, step):
        for bit in reversed(range(bits)):
            step += 3
            task(step, lambda bit=bit: tokens_wait(n, bit))
            if bit:
                task(step, lambda bit=bit: tokens_start(n, bit - 1))
        task(step, lambda: tokens_put(n).wait())
        return step

    n_rows_w = width // pcol
    first_move = 1
    halves = 2 * chunks - 1
    task(0, begin)
    step = halves
    task(step, lambda: start_all(row_loads(0)), lambda: start_all(row_loads(1)))
    for k in range(4):
        step = task(
            halves + k, lambda k=k: second_part(n_rows_w * k // 4, n_rows_w * (k + 1) // 4)
        )
    task(step, lambda: sum_start(0, 0))
    task(step, lambda: start_all(down_loads(0)), lambda: start_all(down_loads(1)))
    grads_at = step + 1
    grads_end = grads_at + 2 * (chunks - 1)
    assert grads_at + 1 < first_move + per_chunk // 2
    task(grads_end, load(1).start, load(2).start, load(11).start)
    step = task(sums_tasks(0, step), second_norm)
    task(max(step, grads_end) + 1, lambda: ffn_part(0, n_rows_w // 2))
    ffn_at = task(
        max(step, grads_end) + 2,
        lambda: ffn_part(n_rows_w // 2, n_rows_w),
        lambda: sum_start(1, 0),
    )
    step = task(step + 4, low_side.wait, low_top.wait, low_far.start)
    step += 3
    task(step, low_far.wait)
    for bit in reversed(range(top)):
        task(step, lambda bit=bit: [c.start() for c in low_bit(bit)])
        step += 2
        task(step, lambda bit=bit: [c.wait() for c in low_bit(bit)])
    task(step, attended_back)
    ffn_end = task(sums_tasks(1, ffn_at), out_end)
    token_tasks(0, ffn_end)
    step = task(step + 1, *[load(k).wait for k in (3, 4, 5, 7)])
    first_block = step
    per_step = 4
    step += -(-(nodes * n_q) // per_step)
    last_block = step
    task(step, kv_send)
    task(step + 2, out_gradient)
    step = task(step + 5, kv_sum, heads_back)
    step = task(step + 1, raw_gradient)
    raw_ready = step
    assert raw_ready > ffn_end
    task(step + 1, lambda: first_part(0, width // 1024))
    step = task(
        step + 2, lambda: first_part(width // 1024, width // 512), lambda: sum_start(2, 0)
    )
    step = task(sums_tasks(2, step), first_norm)
    task(token_tasks(1, step), gains_end)

    late = half - (R["q_part"].shape[1] + R["kv_part"].shape[1]) // pcol // 2
    late_end = late + R["q_part"].shape[1] // pcol // 2
    gap = max(0, raw_ready + 1 - late - first_move)
    steps = max(first_move + half + gap + 2 * LAG * last, max(tasks) + 1)

    @pl.loop(0, steps)
    def _(i):
        for b in range(2):
            stream(b, i - first_move)
        for at, acts in sorted(tasks.items()):

            @pl.when(i == at)
            def _(acts=acts):
                for act in acts:
                    act()

        @pl.when(i < halves)
        def _():
            c = (i + 1) // 2

            @pl.when((i == 0) | (i % 2 == 1))
            def _():
                chunk_ready(c)

            @pl.loop(jnp.where((i == 0) | (i % 2 == 1), 0, 1), jnp.where(i % 2 == 1, 1, 2))
            def _(m):
                chunk_forward(c, pl.ds(pl.multiple_of(m * (both // 2), both // 2), both // 2))

            @pl.when(i % 2 == 0)
            def _():
                chunk_next(c)

        pl.when(i == 0)(turn)
        g = i - grads_at
        c = jnp.where(i == 0, 0, g // 2 + 1)
        within = (g >= 0) & (i < grads_end)

        @pl.when((i == 0) | (within & (g % 2 == 0)))
        def _():
            chunk_gradients(c)

        @pl.when((i == 0) | (within & (g % 2 == 1)))
        def _():
            chunk_down(c)
            staged(c)

        @pl.when((i >= first_block) & (i < last_block))
        def _():
            @pl.loop(0, per_step)
            def _(k):
                n = (i - first_block) * per_step + k
                piece = n // n_q

                @pl.when(n < n_q)
                def _():
                    attention_block(0, n, True)

                @pl.when((n >= n_q) & (n < n_q * nodes) & (node >= piece))
                def _():
                    attention_block(piece, n % n_q, False)

    @pl.loop(0, half)
    def _(j):
        for b in range(2):
            v = node if b == 0 else last - node
            probe = red.at[b, 0]

            @pl.when(v == 0)
            def _():
                along(probe, probe, red_sems, b, j, rank).wait_send()

            @pl.when((v > 0) & ((v < last) | (j >= half - KEPT)))
            def _():
                along(probe, probe, fin_sems, b, j, rank).wait_send()

            @pl.when((v == last) & (j >= half - KEPT))
            def _():
                pltpu.make_async_copy(probe, probe, put_sem.at[b, j]).wait()

            @pl.when(crosses(j) & ((v < last) | (j >= half - KEPT)))
            def _():
                along(probe, probe, x_sems, b, j, rank).wait_send()

            @pl.when(crosses(j))
            def _():
                along(probe, probe, x_sems, b, j, rank).wait_recv()


def backward(nodes, bits, ident, values):
    tp, seq = 1 << bits, 2 * nodes
    share, width = values["x"].shape
    ff = values["w_gate"].shape[1] // 2
    n_q, wide, _ = values["q"].shape
    n_rows = values["kv"].shape[0]
    heads = n_q // n_rows
    tokens = tp * share
    piece = 256
    cols = (heads + 2) * HD
    small = [(piece, r * width // piece) for r in (heads * HD, heads * HD, 2 * HD)]
    shapes = [(width, 2 * ff), (width, 2 * ff), (2 * ff, width)]
    shapes += [(2 * small[0][0], small[0][1]), small[1], (2 * small[2][0], small[2][1])]
    half = (3 * width * ff + sum(r * c for r, c in small)) // (2 * piece * piece)
    slots = 2 * LAG * (nodes - 1) + 2
    vmem = pl.BlockSpec(memory_space=pltpu.VMEM)
    anywhere = pl.BlockSpec(memory_space=pl.ANY)
    dma = pltpu.SemaphoreType.DMA
    inside = ("scale", "resid", "x", "gain_two", "gain_one", "gain_q", "gain_k")
    inside += ("raw", "cosine", "sine")
    kv = values["kv"].shape
    total = seq * tp
    messages = 3 + 2 * (tp - 2)
    outs = shapes + [(tp, share, width)] * 2 + [(8, width // tp)]
    outs += [(2 * tp - 1, share, width)] * 3 + [(width, ff), (width, ff), (ff, width)]
    scratch = [
        (2, slots, piece, piece),
        (2, AHEAD, piece, piece),
        (tokens, width),
        (tokens, width),
        (2 * tokens, width),
        (2 * tokens, width),
        (width, 2 * tokens),
        (heads * HD, width),
        (n_q, wide, 2 * HD),
        (n_q, wide, 2 * HD),
        (n_q, 2 * HD, wide, F32),
        (nodes, n_rows, wide, 2 * HD, F32),
        (nodes,) + kv,
        (2, tokens, heads * HD),
        (2 * tokens, heads * HD),
        (n_q, 8, wide, F32),
        (2 * tokens, cols),
        small[1],
        small[2],
        small[0],
        (nodes - 1, n_rows, wide, 2 * HD),
        (nodes - 1, n_rows, wide, 2 * HD),
        (share, width, F32),
        (2, share, width),
        (8, width, F32),
        (tp, 8, width // tp, F32),
        (total, 8, width // tp, F32),
        (n_q, 1, wide, F32),
        (share, width),
        (2 * tokens, ff),
        (2, 2 * tokens, ff),
        (2, 2, piece, ff),
        (2, 2, width, piece),
        (2, width, piece),
        (piece, width),
    ]
    sems = [(2, AHEAD)] + [(2, half)] * 7 + [(12 + tp,), (3, 2 * tp - 1), (3, 2 * tp - 1)]
    sems += [(2, tp // 2), (messages,), (messages,), (nodes - 1,), (nodes - 1,)]
    sems += [(2, tp - 1), (2, tp - 1), (2,), (total,), (total,), (2, 3), (3,)]
    return pl.pallas_call(
        functools.partial(backward_kernel, nodes, bits),
        out_shape=[
            jax.ShapeDtypeStruct(shape, F32 if k == 8 else BF) for k, shape in enumerate(outs)
        ],
        in_specs=[vmem if k in inside else anywhere for k in values],
        out_specs=[vmem if k == 8 else anywhere for k in range(len(outs))],
        scratch_shapes=[
            pltpu.VMEM(s[:-1], F32) if s[-1] is F32 else pltpu.VMEM(s, BF) for s in scratch
        ]
        + [dma(s) for s in sems],
        compiler_params=pltpu.CompilerParams(
            collective_id=ident, has_side_effects=True, vmem_limit_bytes=62 << 20
        ),
        cost_estimate=pl.CostEstimate(
            flops=0, bytes_accessed=1 << 30, transcendentals=0
        ),
        name="backward",
    )(*values.values())[:9]


def widen(arrays):
    block = arrays[-1].shape[0]
    for array in arrays:
        block = min(block, array.shape[0])
    counts = [array.shape[0] // block for array in arrays]
    starts = [sum(counts[:k]) for k in range(len(arrays))]
    width = arrays[0].shape[1]

    def kernel(*refs):
        step = pl.program_id(0)
        for k, (start, size) in enumerate(zip(starts, counts)):

            @pl.when((step >= start) & (step < start + size))
            def _(k=k):
                refs[len(arrays) + k][...] = refs[k][...].astype(F32)

    specs = [
        pl.BlockSpec(
            (block, width), lambda i, start=start, size=size: (jnp.clip(i - start, 0, size - 1), 0)
        )
        for start, size in zip(starts, counts)
    ]
    return pl.pallas_call(
        kernel,
        grid=(sum(counts),),
        out_shape=[jax.ShapeDtypeStruct(a.shape, F32) for a in arrays],
        in_specs=specs,
        out_specs=specs,
        compiler_params=pltpu.CompilerParams(vmem_limit_bytes=56 << 20),
        cost_estimate=pl.CostEstimate(
            flops=0, bytes_accessed=6 * block * width * sum(counts), transcendentals=0
        ),
        name="widen",
    )(*arrays)


def turn_heads(mine, other, kv, q_cols, shared, width):
    side = (lax.axis_index("seq") % 2).reshape(1).astype(jnp.int32)
    chunk = 256

    def kernel(side_ref, mine_ref, other_ref, kv_ref, q_out, k_out, v_out):
        first = side_ref[0] == 0
        per = mine_ref.shape[1] // chunk
        lane = lax.broadcasted_iota(jnp.int32, (chunk, 2 * HD), 1)

        @pl.loop(0, width // chunk)
        def _(n):
            rows = pl.ds(pl.multiple_of(n * chunk, chunk), chunk)
            at = pl.ds(pl.multiple_of(n // per * q_cols, q_cols), q_cols)
            cols = pl.ds(pl.multiple_of(n % per * chunk, chunk), chunk)
            own = mine_ref[at, cols].astype(F32).T
            far = other_ref[at, cols].astype(F32).T
            q_out[rows, 0:q_cols] = jnp.where(first, own, far)
            q_out[rows, q_cols:] = jnp.where(first, far, own)

        height = 2 * HD
        per_kv = kv_ref.shape[1] // chunk
        stack = kv_ref.shape[0] // 2

        @pl.loop(0, width // chunk)
        def _(n):
            rows = pl.ds(pl.multiple_of(n * chunk, chunk), chunk)
            cols = pl.ds(pl.multiple_of(n % per_kv * chunk, chunk), chunk)
            pair = [
                kv_ref[
                    pl.ds(pl.multiple_of(s * stack + n // per_kv * height, height), height), cols
                ]
                .astype(F32)
                .T
                for s in range(2)
            ]
            if shared:
                both = pair[0] + pair[1]
                k_out[rows, :] = both[:, :HD]
                v_out[rows, :] = both[:, HD:]
            else:
                k_out[rows, :] = jnp.where(lane < HD, pair[0], pltpu.roll(pair[1], HD, 1))
                v_out[rows, :] = jnp.where(lane < HD, pltpu.roll(pair[0], HD, 1), pair[1])

    vmem = pl.BlockSpec(memory_space=pltpu.VMEM)
    k_cols = HD if shared else 2 * HD
    return pl.pallas_call(
        kernel,
        out_shape=[
            jax.ShapeDtypeStruct((width, c), F32) for c in (2 * q_cols, k_cols, k_cols)
        ],
        in_specs=[pl.BlockSpec(memory_space=pltpu.SMEM)] + [vmem] * 3,
        out_specs=[vmem] * 3,
        compiler_params=pltpu.CompilerParams(vmem_limit_bytes=40 << 20),
        name="turn_heads",
    )(side, mine, other, kv)


def per_device(
    tokens,
    positions,
    corpus,
    corpus_weight,
    gain_one,
    w_query,
    w_key,
    w_value,
    gain_query,
    gain_key,
    w_out,
    gain_two,
    w_gate,
    w_up,
    w_down,
    cotangent,
):
    net = Links()
    rows, per_row, width = tokens.shape
    count = rows * per_row
    share = count // net.tp
    total_len = per_row * net.seq
    side, node, t = net.side, net.node, net.t
    q_cols = w_query.shape[1] // 2
    shared = (w_key.shape[1] // HD) % 2 == 1
    k_cols = w_key.shape[1] if shared else w_key.shape[1] // 2
    both = 2 * count

    def lanes(v):
        return jnp.pad(v, [(0, 0)] * (v.ndim - 1) + [(0, 2 * HD - v.shape[-1])])

    pos_own = positions.reshape(count)
    corpus_own = corpus.reshape(count)
    told = net.swap_side(jnp.stack([pos_own, corpus_own]))
    cosine, sine = rope_tables(jnp.concatenate([pos_own, told[0]]))
    cosine = lanes(jnp.concatenate([cosine, cosine], axis=1))
    sine = lanes(jnp.concatenate([sine, -sine], axis=1))
    onehot = (corpus_own[:, None] == jnp.arange(NCORP, dtype=jnp.int32)).astype(F32)
    own_counts = jnp.zeros((8, 128), F32).at[0, :NCORP].set(jnp.sum(onehot, axis=0))
    token_rows = tokens.reshape(count, width)
    cot_rows = cotangent.reshape(count, width)
    gain_q, gain_k = lanes(gain_query[None]), lanes(gain_key[None])

    def half_of(w):
        cols = w.shape[1] // 2
        return take(w, side * cols, cols, 1)

    w_back = jnp.concatenate(
        [half_of(w_query)] + [w if shared else half_of(w) for w in (w_key, w_value)], axis=1
    )
    assert k_cols == HD

    q, kv, raw, a_one, att, log, all_counts, cot_other, resid, a_two, kv_in, a_other = attend(
        net.nodes,
        net.bits,
        2,
        dict(
            tokens=token_rows,
            w_query=w_query,
            w_key=w_key,
            w_value=w_value,
            w_out=w_out,
            cot=cot_rows,
            gain_one=gain_one[None],
            gain_two=gain_two[None],
            gain_q=gain_q,
            gain_k=gain_k,
            cosine=cosine,
            sine=sine,
            count=own_counts,
            rows=rows,
        ),
    )
    a_two = a_two.reshape(both, width)
    x_share = take(token_rows, t * share, share)

    counts = jnp.sum(all_counts, axis=0)[0, :NCORP]
    weight_scale = corpus_weight.astype(F32) * (rows * total_len / NCORP) / counts
    corpus_other = told[1]
    onehot_other = (corpus_other[:, None] == jnp.arange(NCORP, dtype=jnp.int32)).astype(F32)
    scale_own = jnp.sum(onehot * weight_scale, axis=-1, keepdims=True)
    scale_other = jnp.sum(onehot_other * weight_scale, axis=-1, keepdims=True)
    scale_both = jnp.concatenate([net.relative(scale_own), net.relative(scale_other)], axis=0)

    sums = backward(
        net.nodes,
        net.bits,
        3,
        dict(
            a_two=a_two,
            cot=cot_rows,
            cot_far=cot_other.reshape(count, width),
            scale=scale_both,
            w_gate=w_gate,
            w_up=w_up,
            w_down=w_down,
            resid=resid,
            x=x_share,
            gain_two=gain_two[None],
            gain_one=gain_one[None],
            gain_q=gain_q,
            gain_k=gain_k,
            w_out=w_out,
            w_back=w_back,
            a_one=a_one,
            a_other=a_other,
            q=q,
            kv=kv,
            kv_in=kv_in,
            att=att,
            log=log,
            raw=raw,
            cosine=cosine,
            sine=sine,
        ),
    )
    q_other = net.swap_side(sums[4])
    fold = width // sums[3].shape[1]
    grad_out = sums[3].reshape(2, fold, q_cols, -1).transpose(0, 2, 1, 3).reshape(2 * q_cols, width)
    grad_gate, grad_up, grad_down, grad_out = widen([*sums[:3], grad_out])
    grad_query, grad_key, grad_value = turn_heads(
        sums[4], q_other, sums[5], q_cols, shared, width
    )
    out, d_tokens = (v.reshape(rows, per_row, width) for v in sums[6:8])
    gains = sums[8]

    head_share = HD // net.tp

    return (
        out,
        d_tokens,
        gains[0],
        grad_query,
        grad_key,
        grad_value,
        take(gains[2], t * head_share, head_share),
        take(gains[3], t * head_share, head_share),
        grad_out,
        gains[1],
        grad_gate,
        grad_up,
        grad_down,
    )


def solution(mesh):
    placed = (
        P(None, "seq", None),
        P(None, "seq"),
        P(None, "seq"),
        P(),
        P(),
        P(None, "tp"),
        P(None, "tp"),
        P(None, "tp"),
        P(),
        P(),
        P("tp", None),
        P(),
        P(None, "tp"),
        P(None, "tp"),
        P("tp", None),
        P(None, "seq", None),
    )
    return jax.shard_map(
        per_device,
        mesh=mesh,
        in_specs=placed,
        out_specs=(
            P(None, "seq", None),
            P(None, "seq", None),
            P("tp"),
            P(None, "tp"),
            P(None, "tp"),
            P(None, "tp"),
            P("tp"),
            P("tp"),
            P("tp", None),
            P("tp"),
            P(None, "tp"),
            P(None, "tp"),
            P("tp", None),
        ),
        check_vma=False,
    )
```

```python
import functools

import jax
import jax.numpy as jnp
from jax import lax
from jax.experimental import pallas as pl
from jax.experimental.pallas import tpu as pltpu
from jax.sharding import PartitionSpec as P

HD = 64
NCORP = 8


EPS = 1e-05
EPS_HEAD = 1e-06
ROPE_BASE = 10000.0
BF = jnp.bfloat16
F32 = jnp.float32
MESH = pl.DeviceIdType.MESH
LAG = 2
AHEAD = 3
KEPT = 6
ROWS_AT_ONCE = 64
SCALE_ROWS = 128


def rope_tables(positions):
    half = HD // 2
    rates = ROPE_BASE ** (-jnp.arange(half, dtype=jnp.float32) * 2.0 / HD)
    angle = positions.astype(jnp.float32)[:, None] * rates[None, :]
    return (jnp.cos(angle), jnp.sin(angle))


def rotate(vector, cosine, sine):
    half = vector.shape[-1] // 2
    first = vector[..., :half]
    second = vector[..., half:]
    return jnp.concatenate(
        [first * cosine - second * sine, second * cosine + first * sine], axis=-1
    )


def head_norm(vector, gain):
    inverse = lax.rsqrt(jnp.mean(vector * vector, axis=-1, keepdims=True) + EPS_HEAD)
    normed = vector * inverse
    return (normed, inverse, normed * gain)


def dot(a, b):
    return jnp.dot(a, b, preferred_element_type=F32)


def dot_tn(a, b):
    return lax.dot_general(a, b, (((0,), (0,)), ((), ())), preferred_element_type=F32)


def dot_nt(a, b):
    return lax.dot_general(a, b, (((1,), (1,)), ((), ())), preferred_element_type=F32)


def take(array, start, size, axis=0):
    return lax.dynamic_slice_in_dim(array, start, size, axis)


class Links:
    def __init__(self):
        self.seq = lax.axis_size("seq")
        self.tp = lax.axis_size("tp")
        self.nodes = self.seq // 2
        self.bits = self.tp.bit_length() - 1
        rank = lax.axis_index("seq")
        self.node = rank // 2
        self.side = rank % 2
        self.t = lax.axis_index("tp")

    def swap_side(self, value):
        return lax.ppermute(value, "seq", [(s, s ^ 1) for s in range(self.seq)])

    def swap_bit(self, value, bit):
        return lax.ppermute(value, "tp", [(r, r ^ (1 << bit)) for r in range(self.tp)])

    def relative(self, rows):
        share = rows.shape[0] // self.tp
        return jnp.concatenate(
            [take(rows, (self.t ^ j) * share, share) for j in range(self.tp)], axis=0
        )


def remote_copy(src, dst, send, recv, **where):
    return pltpu.make_async_remote_copy(
        src, dst, send, recv, device_id=where, device_id_type=MESH
    )


def attend_kernel(nodes, bits, *refs):
    names = (
        "tokens", "w_query", "w_key", "w_value", "w_out", "cot", "gain_one", "gain_two", "gain_q", "gain_k",
        "cosine", "sine", "count",
        "q", "kv", "raw", "a_one", "att", "log", "counts", "cot_out", "resid", "a_out", "kv_in", "a_other", "w_kv",
        "tok", "wq", "wk", "wv", "wo", "raw_other", "acc", "weight_sum", "att_in", "att_rel", "hold", "temp", "got",
        "mine",
        "load_sem", "raw_sem", "kv_send", "kv_recv", "count_send", "count_recv", "cot_send", "cot_recv", "att_sem",
        "sum_send", "sum_recv", "all_send", "all_recv", "own_sem", "a_sem",
    )
    assert len(names) == len(refs)
    R = dict(zip(names, refs))
    tp, seq = 1 << bits, 2 * nodes
    top = bits - 1
    rank, t = lax.axis_index("seq"), lax.axis_index("tp")
    node, side = rank // 2, rank % 2
    across = rank + 1 - 2 * side
    n_q, wide, _ = R["q"].shape
    n_rows = R["kv"].shape[0]
    heads = n_q // n_rows
    q_cols = heads * HD
    span = wide // 2
    share, width = R["resid"].shape
    count = tp * share

    def strips(rows, step, body):
        @pl.loop(0, rows // step)
        def _(m):
            body(pl.ds(pl.multiple_of(m * step, step), step))

    def flip(bit):
        return t + (1 << bit) * (1 - 2 * ((t // (1 << bit)) % 2))

    def block_of(j):
        other = t
        for bit in range(bits):
            there = (j // (1 << bit)) % 2
            other = other + there * (1 << bit) * (1 - 2 * ((t // (1 << bit)) % 2))
        return other

    def block_rows(j):
        return pl.ds(pl.multiple_of(block_of(j) * share, share), share)

    half = R["w_out"].shape[0] // 2
    loads = [(R["tokens"], R["tok"]), (R["w_query"], R["wq"]), (R["w_key"], R["wk"])]
    loads += [(R["w_value"], R["wv"])]
    loads += [
        (
            R["w_out"].at[pl.ds(pl.multiple_of(at * half, half), half)],
            R["wo"].at[pl.ds(k * half, half)],
        )
        for k, at in enumerate((side, 1 - side))
    ]

    def load(k):
        return pltpu.make_async_copy(loads[k][0], loads[k][1], R["load_sem"].at[k])

    for k in range(6):
        load(k).start()

    barrier = pltpu.get_barrier_semaphore()
    for step in range(1, seq):
        pl.semaphore_signal(
            barrier, 1, device_id={"seq": (rank + step) % seq}, device_id_type=MESH
        )
    for bit in range(bits):
        pl.semaphore_signal(barrier, 1, device_id={"tp": flip(bit)}, device_id_type=MESH)

    load(0).wait()

    def first_norm(r):
        v = R["tok"][r, :].astype(F32)
        inverse = lax.rsqrt(jnp.mean(v * v, axis=-1, keepdims=True) + EPS)
        R["a_one"][r, :] = (v * inverse * R["gain_one"][...]).astype(BF)

    strips(count, 64, first_norm)
    for k in (1, 2, 3):
        load(k).wait()

    def pair_of(k, v, first):
        if k.shape[1] == HD:
            return jnp.concatenate([k, v], axis=1)
        low = lax.broadcasted_iota(jnp.int32, k.shape, 1) < HD
        return jnp.where(
            low,
            jnp.where(first, k, pltpu.roll(k, HD, 1)),
            jnp.where(first, pltpu.roll(v, HD, 1), v),
        )

    def project(r):
        a = R["a_one"][r, :]
        k = jnp.dot(a, R["wk"][...], preferred_element_type=F32)
        v = jnp.dot(a, R["wv"][...], preferred_element_type=F32)
        R["raw"][r, q_cols:] = pair_of(k, v, side == 0).astype(BF)
        R["raw_other"][r, q_cols:] = pair_of(k, v, side == 1).astype(BF)

    strips(count, 256, project)

    def queries(ref, half):
        cols = pl.ds(pl.multiple_of(half * q_cols, q_cols), q_cols)

        def body(r):
            ref[r, 0:q_cols] = jnp.dot(
                R["a_one"][r, :], R["wq"][:, cols], preferred_element_type=F32
            ).astype(BF)

        strips(count, 256, body)

    queries(R["raw_other"], 1 - side)
    pl.semaphore_wait(barrier, seq - 1 + bits)
    raw_copy = remote_copy(
        R["raw_other"],
        R["raw"].at[pl.ds(count, count)],
        R["raw_sem"].at[0],
        R["raw_sem"].at[1],
        seq=across,
    )
    raw_copy.start()
    queries(R["raw"], side)
    R["counts"][0] = R["count"][...]
    count_copies = [
        remote_copy(
            R["count"],
            R["counts"].at[step],
            R["count_send"].at[step - 1],
            R["count_recv"].at[step - 1],
            seq=(rank + step) % seq,
        )
        for step in range(1, seq)
    ]
    for copy in count_copies:
        copy.start()

    lane = lax.broadcasted_iota(jnp.int32, (span, 2 * HD), 1)

    def head(v, gain, at):
        v = jnp.where(lane < HD, v, 0.0)
        inverse = lax.rsqrt(jnp.sum(v * v, axis=-1, keepdims=True) * (1.0 / HD) + EPS_HEAD)
        v = v * inverse * gain
        swapped = jnp.where(
            lane < HD // 2, pltpu.roll(v, 2 * HD - HD // 2, 1), pltpu.roll(v, HD // 2, 1)
        )
        return v * R["cosine"][at, :] - swapped * R["sine"][at, :]

    def head_rows(d):
        here = pl.ds(d * span, span)

        @pl.loop(0, n_rows)
        def _(r):
            at = pl.ds(pl.multiple_of((d * n_rows + r) * span, span), span)

            @pl.loop(0, heads // 2)
            def _(h):
                pair = R["raw"][at, pl.ds(pl.multiple_of(h * 2 * HD, 2 * HD), 2 * HD)].astype(F32)
                i = r * heads + 2 * h
                R["q"][i, here, :] = head(pair, R["gain_q"][...], at).astype(BF)
                R["q"][i + 1, here, :] = head(
                    pltpu.roll(pair, HD, 1), R["gain_q"][...], at
                ).astype(BF)

            pair = R["raw"][at, q_cols:].astype(F32)
            R["kv"][r, 0, here, :] = jnp.where(
                lane < HD, head(pair, R["gain_k"][...], at), pair
            ).astype(BF)

    def kv_copy(step, d):
        here = pl.ds(d * span, span)
        return remote_copy(
            R["kv"].at[:, :, here],
            R["kv_in"].at[step - 1, :, :, here],
            R["kv_send"].at[d, step - 1],
            R["kv_recv"].at[d, step - 1],
            seq=rank + 2 * step,
        )

    head_rows(0)
    for step in range(1, nodes):
        pl.when(node + step < nodes)(kv_copy(step, 0).start)

    def w_pairs(r):
        R["w_kv"][r, :] = pair_of(
            R["wk"][r, :].astype(F32), R["wv"][r, :].astype(F32), side == 0
        ).astype(BF)

    strips(width, 256, w_pairs)
    raw_copy.wait()
    head_rows(1)
    for step in range(1, nodes):
        pl.when(node + step < nodes)(kv_copy(step, 1).start)
    cot_copies = [
        remote_copy(
            R["cot"].at[block_rows(j)],
            R["cot_out"].at[j],
            R["cot_send"].at[j],
            R["cot_recv"].at[j],
            seq=across,
        )
        for j in range(0, tp, 2)
    ]
    for copy in cot_copies:
        copy.start()

    def attend(kv_at, diagonal):
        @pl.loop(0, n_q)
        def _(i):
            kv = kv_at(i // heads)
            scores = lax.dot_general(
                R["q"][i], kv, (((1,), (1,)), ((), ())), preferred_element_type=F32
            )
            weight = jnp.exp2(scores * (HD**-0.5 * 1.4426950408889634))
            if diagonal:
                q_at = lax.broadcasted_iota(jnp.int32, (wide, wide), 0)
                k_at = lax.broadcasted_iota(jnp.int32, (wide, wide), 1)
                q_at = jnp.where(q_at < span, q_at + span * side, q_at - span * side)
                k_at = jnp.where(k_at < span, k_at + span * side, k_at - span * side)
                weight = jnp.where(k_at <= q_at, weight, 0.0)
            sums = weight[:, :128]
            for c in range(128, wide, 128):
                sums = sums + weight[:, c : c + 128]
            values = jnp.dot(weight.astype(BF), kv, preferred_element_type=F32)
            if diagonal:
                R["weight_sum"][i] = sums
                R["acc"][i] = values
            else:
                R["weight_sum"][i] += sums
                R["acc"][i] += values

    attend(lambda r: R["kv"][r, 0], True)

    @pl.loop(1, nodes)
    def _(step):
        @pl.when(node >= step)
        def _():
            for d in range(2):
                kv_copy(step, d).wait_recv()
            attend(lambda r: R["kv_in"][step - 1, r, 0], False)

    att_copy = remote_copy(
        R["att"].at[1], R["att_in"], R["att_sem"].at[0], R["att_sem"].at[1], seq=across
    )

    def finish(d):
        at = pl.ds(d * span, span)

        @pl.loop(0, n_rows * (heads // 2))
        def _(n):
            r, h = n // (heads // 2), n % (heads // 2)
            out = []
            for k in range(2):
                i = r * heads + 2 * h + k
                total = jnp.sum(R["weight_sum"][i, at, :], axis=-1, keepdims=True)
                out.append(R["acc"][i, at, :] / total)
            both = jnp.where(lane < HD, pltpu.roll(out[0], HD, 1), out[1])
            rows = pl.ds(pl.multiple_of(r * span, span), span)
            R["att"][d, rows, pl.ds(pl.multiple_of(h * 2 * HD, 2 * HD), 2 * HD)] = both.astype(BF)

    finish(1)
    att_copy.start()
    half_rows = pl.multiple_of(t % 2 * (count // 2), count // 2)
    a_half = pl.ds(half_rows, count // 2)
    a_copy = remote_copy(
        R["a_one"].at[a_half],
        R["a_other"].at[a_half],
        R["a_sem"].at[0],
        R["a_sem"].at[1],
        seq=across,
    )
    finish(0)
    ones = jnp.ones((8, 2 * HD), F32)

    @pl.loop(0, n_q)
    def _(i):
        total = lax.dot_general(
            ones,
            R["weight_sum"][i],
            (((1,), (1,)), ((), ())),
            precision=lax.Precision.HIGHEST,
            preferred_element_type=F32,
        )
        R["log"][i] = jnp.log2(total)[0:1]

    @pl.loop(0, tp)
    def _(j):
        at = pl.ds(pl.multiple_of(j * share, share), share)
        R["att_rel"][at, 0:q_cols] = R["att"][0, block_rows(j), :]

    att_copy.wait()
    a_copy.start()

    @pl.loop(0, tp)
    def _(j):
        at = pl.ds(pl.multiple_of(j * share, share), share)
        R["att_rel"][at, q_cols:] = R["att_in"][block_rows(j), :]

    for k in (4, 5):
        load(k).wait()
    hold, temp, got, mine = R["hold"], R["temp"], R["got"], R["mine"]
    chunk = 512

    @pl.loop(0, width // chunk)
    def _(n):
        cols = pl.ds(pl.multiple_of(n * chunk, chunk), chunk)
        value = jnp.dot(
            R["att_rel"][...], R["wo"][:, cols], preferred_element_type=F32
        ).astype(BF)
        for j in range(tp):
            (temp if j % 2 else hold)[j // 2, :, cols] = value[j * share : (j + 1) * share]

    slot = 0
    for bit in range(bits):
        keep = list(range(0, tp, 2 << bit))
        copies = []
        for k, j in enumerate(keep):
            src = temp.at[j // 2] if bit == 0 else hold.at[(j | 1 << bit) // 2]
            copies.append(
                remote_copy(
                    src,
                    got.at[slot + k],
                    R["sum_send"].at[slot + k],
                    R["sum_recv"].at[slot + k],
                    tp=flip(bit),
                )
            )
            copies[-1].start()
        for k, j in enumerate(keep):
            copies[k].wait()

            def add(r, k=k, j=j):
                hold[j // 2, r, :] = (
                    hold[j // 2, r, :].astype(F32) + got[slot + k, r, :].astype(F32)
                ).astype(BF)

            strips(share, 64, add)
        slot += len(keep)

    def second_norm(r):
        at = pl.ds(pl.multiple_of(t * share + r.start, 64), 64)
        resid = R["tok"][at, :].astype(F32) + hold[0, r, :].astype(F32)
        R["resid"][r, :] = resid
        inverse = lax.rsqrt(jnp.mean(resid * resid, axis=-1, keepdims=True) + EPS)
        mine[r, :] = (resid * inverse * R["gain_two"][...]).astype(BF)

    strips(share, 64, second_norm)

    a_out = R["a_out"]
    started = []

    def send(src, dst, k, **where):
        copy = remote_copy(src, dst, R["all_send"].at[k], R["all_recv"].at[k], **where)
        copy.start()
        started.append(copy)
        return copy

    up = 1 << top
    cut = share // 2
    low, high = pl.ds(0, cut), pl.ds(cut, cut)
    by_side = send(mine, a_out.at[1, 0], 0, seq=across)
    by_top = send(mine, a_out.at[0, up], 1, tp=flip(top))
    put = pltpu.make_async_copy(mine, a_out.at[0, 0], R["own_sem"])
    put.start()
    k = 4
    for copy in cot_copies:
        copy.wait()
    cot_copies = []
    for j in range(0, tp, 2):
        cot_copies.append(
            remote_copy(
                R["cot_out"].at[j],
                R["cot_out"].at[j + 1],
                R["cot_send"].at[j + 1],
                R["cot_recv"].at[j + 1],
                tp=flip(0),
            )
        )
        cot_copies[-1].start()
    pending = {}
    for bit in reversed(range(top)):
        have = [j for j in range(tp) if j % (2 << bit) == 0]
        if bit == top - 1:
            pending[0, 0] = send(mine, a_out.at[0, 1 << bit], k, tp=flip(bit))
            k += 1
            by_side.wait_recv()
            far_low = send(a_out.at[1, 0, low], a_out.at[1, up, low], 2, tp=flip(top))
            pending[1, 0] = send(a_out.at[1, 0], a_out.at[1, 1 << bit], k, tp=flip(bit))
            k += 1
            by_top.wait_recv()
            far_high = send(a_out.at[0, up, high], a_out.at[1, up, high], 3, seq=across)
            pending[0, up] = send(a_out.at[0, up], a_out.at[0, up | 1 << bit], k, tp=flip(bit))
            k += 1
            far_low.wait_recv()
            far_high.wait_recv()
            pending[1, up] = send(a_out.at[1, up], a_out.at[1, up | 1 << bit], k, tp=flip(bit))
            k += 1
        else:
            for d in range(2):
                for j in have:
                    pending[d, j] = send(
                        a_out.at[d, j], a_out.at[d, j | 1 << bit], k, tp=flip(bit)
                    )
                    k += 1
        for copy in pending.values():
            copy.wait_recv()
        pending = {}
    a_copy.wait()
    a_next = remote_copy(
        R["a_other"].at[a_half],
        R["a_other"].at[a_half],
        R["a_sem"].at[2],
        R["a_sem"].at[3],
        tp=flip(0),
    )
    a_next.start()
    for copy in started:
        copy.wait_send()
    put.wait()
    for copy in count_copies + cot_copies:
        copy.wait()
    a_next.wait()
    for step in range(1, nodes):
        for d in range(2):
            pl.when(node + step < nodes)(kv_copy(step, d).wait_send)


def attend(nodes, bits, ident, values):
    tp, seq = 1 << bits, 2 * nodes
    tokens, width = values["tokens"].shape
    share = tokens // tp
    q_all, k_all = values["w_query"].shape[1], values["w_key"].shape[1]
    heads = q_all // 2 // HD
    rows, wide = values["rows"], 2 * tokens // values["rows"]
    n_q = rows * heads
    cols = (heads + 2) * HD
    inputs = {k: v for k, v in values.items() if k != "rows"}
    inside = ("gain_one", "gain_two", "gain_q", "gain_k", "cosine", "sine", "count")
    vmem = pl.BlockSpec(memory_space=pltpu.VMEM)
    anywhere = pl.BlockSpec(memory_space=pl.ANY)
    dma = pltpu.SemaphoreType.DMA
    messages = 4 + 2 * (tp - 2)
    kv = (rows, 1, wide, 2 * HD)
    outs = [
        ((n_q, wide, 2 * HD), BF, vmem),
        (kv, BF, vmem),
        ((2 * tokens, cols), BF, vmem),
        ((tokens, width), BF, vmem),
        ((2, tokens, heads * HD), BF, vmem),
        ((n_q, 1, wide), F32, vmem),
        ((seq,) + values["count"].shape, F32, vmem),
        ((tp, share, width), BF, anywhere),
        ((share, width), F32, vmem),
        ((2, tp, share, width), BF, anywhere),
        ((nodes - 1,) + kv, BF, vmem),
        ((tokens, width), BF, anywhere),
        ((width, 2 * HD), BF, vmem),
    ]
    scratch = [
        ((tokens, width), BF),
        ((width, q_all), BF),
        ((width, k_all), BF),
        ((width, k_all), BF),
        ((q_all, width), BF),
        ((tokens, cols), BF),
        ((n_q, wide, 2 * HD), F32),
        ((n_q, wide, 128), F32),
        ((tokens, heads * HD), BF),
        ((tokens, q_all), BF),
        ((tp // 2, share, width), BF),
        ((tp // 2, share, width), BF),
        ((tp - 1, share, width), BF),
        ((share, width), BF),
    ]
    sems = [(6,), (2,), (2, nodes - 1), (2, nodes - 1), (seq - 1,), (seq - 1,), (tp,), (tp,), (2,)]
    sems += [(tp - 1,), (tp - 1,), (messages,), (messages,), (), (4,)]
    return pl.pallas_call(
        functools.partial(attend_kernel, nodes, bits),
        out_shape=[jax.ShapeDtypeStruct(shape, kind) for shape, kind, _ in outs],
        in_specs=[vmem if k in inside else anywhere for k in inputs],
        out_specs=[place for _, _, place in outs],
        scratch_shapes=[pltpu.VMEM(shape, kind) for shape, kind in scratch]
        + [dma(s) for s in sems],
        compiler_params=pltpu.CompilerParams(
            collective_id=ident, has_side_effects=True, vmem_limit_bytes=56 << 20
        ),
        cost_estimate=pl.CostEstimate(
            flops=0, bytes_accessed=200 << 20, transcendentals=0
        ),
        name="attend",
    )(*inputs.values())


def backward_kernel(nodes, bits, *refs):
    names = (
        "a_two", "cot", "cot_far", "scale", "w_gate", "w_up", "w_down", "resid", "tokens_in", "gain_two",
        "gain_one", "gain_q", "gain_k", "w_out", "w_query", "w_kv", "a_one", "a_other", "q", "kv", "kv_in", "att",
        "log", "raw", "cosine", "sine", "gate_sum", "up_sum", "down_sum", "out_sum",
        "q_sum", "kv_sum", "out", "tokens", "gains", "two_in", "ffn_in", "one_in", "gate_part",
        "up_part", "down_part", "red", "own", "hold", "temp", "low", "a_in", "a_t", "w_rows",
        "q_in", "d_out", "d_q", "d_kv", "kv_all", "att_in", "d_att", "delta", "d_raw", "q_part",
        "kv_part", "out_part", "kv_back", "kv_far", "d_resid", "fresh", "gain_rows", "gain_box",
        "gain_all", "log_in", "cot_in", "resid_in", "raw_in", "cos_in", "sin_in", "x_in", "hidden", "d_pair", "w_strip", "w_cols", "stage", "stage_down",
        "own_sem", "red_send", "red_recv", "fin_send", "fin_recv", "x_send", "x_recv", "put_sem",
        "load_sem", "sum_send", "sum_recv", "temp_sem", "low_send", "low_recv", "kv_send",
        "kv_recv", "tok_send", "tok_recv", "tok_put", "gain_send", "gain_recv", "w_sem",
        "stage_sem",
    )
    assert len(names) == len(refs)
    R = dict(zip(names, refs))
    tp, seq = 1 << bits, 2 * nodes
    top = bits - 1
    rank, t = lax.axis_index("seq"), lax.axis_index("tp")
    node, side = rank // 2, rank % 2
    across = rank + 1 - 2 * side
    last = nodes - 1
    me = rank * tp + t
    total = seq * tp
    share, width = R["resid"].shape
    n_q, wide, _ = R["q"].shape
    n_rows = R["kv"].shape[0]
    heads = n_q // n_rows
    span = wide // 2
    slots, prow, pcol = R["red"].shape[1:]
    half = R["red_send"].shape[1]
    ff = R["gate_part"].shape[1]
    chunks = ff // pcol
    tall = width // prow
    per_chunk = 3 * tall
    fed = chunks * per_chunk

    def strips(rows, step, body):
        @pl.loop(0, rows // step)
        def _(m):
            body(pl.ds(pl.multiple_of(m * step, step), step))

    def flip(bit):
        return t + (1 << bit) * (1 - 2 * ((t // (1 << bit)) % 2))

    def block_of(j):
        other = t
        for bit in range(bits):
            there = (j // (1 << bit)) % 2
            other = other + there * (1 << bit) * (1 - 2 * ((t // (1 << bit)) % 2))
        return other

    def block_rows(j):
        return pl.ds(pl.multiple_of(block_of(j) * share, share), share)

    barrier = pltpu.get_barrier_semaphore()

    @pl.loop(1, total)
    def _(k):
        other = (me + k) % total
        pl.semaphore_signal(
            barrier, 1, device_id={"seq": other // tp, "tp": other % tp}, device_id_type=MESH
        )

    pl.semaphore_wait(barrier, total - 1)

    red, own = R["red"], R["own"]
    own_sem, put_sem = R["own_sem"], R["put_sem"]
    red_sems = R["red_send"], R["red_recv"]
    fin_sems = R["fin_send"], R["fin_recv"]
    x_sems = R["x_send"], R["x_recv"]

    def with_piece(b, j, act):
        p = 2 * j + b
        chunk, k, kind = p // per_chunk, p % tall, (p % per_chunk) // tall
        along_chunk = pl.multiple_of(chunk * pcol, pcol)
        along_side = pl.multiple_of(side * ff + chunk * pcol, pcol)
        along_width = pl.ds(pl.multiple_of(k * prow, prow), prow)
        for i, name in enumerate(("gate", "up", "down")):

            @pl.when((p < fed) & (kind == i))
            def _(name=name):
                part, whole = R[name + "_part"], R[name + "_sum"]
                if name == "down":
                    act(
                        part.at[pl.ds(along_chunk, prow), along_width],
                        whole.at[pl.ds(along_side, prow), along_width],
                    )
                else:
                    act(
                        part.at[along_width, pl.ds(along_chunk, pcol)],
                        whole.at[along_width, pl.ds(along_side, pcol)],
                    )

        base = fed
        for name in ("out", "q", "kv"):
            part, whole = R[name + "_part"], R[name + "_sum"]
            size = part.shape[1] // pcol

            @pl.when((p >= base) & (p < base + size))
            def _(part=part, whole=whole, base=base, name=name):
                col = pl.ds(pl.multiple_of((p - base) * pcol, pcol), pcol)
                row = 0 if name == "q" else side * prow
                act(part.at[:, col], whole.at[pl.ds(pl.multiple_of(row, prow), prow), col])

            base += size

    def along(src, dst, sems, b, j, target):
        return remote_copy(src, dst, sems[0].at[b, j], sems[1].at[b, j], seq=target)

    def placed(j):
        if gap == 0:
            return j, (j >= 0) & (j < half)
        after = j >= late + gap
        return jnp.where(after, j - gap, j), ((j >= 0) & (j < late)) | (
            after & (j < half + gap)
        )

    def crosses(j):
        return (j < late) | (j >= late_end)

    def stream(b, i):
        v = node if b == 0 else last - node
        ahead = rank + 2 if b == 0 else rank - 2
        behind = rank - 2 if b == 0 else rank + 2
        f, there = placed(i - LAG * v + AHEAD - 1)

        @pl.when((v > 0) & there)
        def _():
            with_piece(
                b,
                f,
                lambda src, dst: pltpu.make_async_copy(
                    src, own.at[b, f % AHEAD], own_sem.at[b, f % AHEAD]
                ).start(),
            )

        j, there = placed(i - LAG * v)

        @pl.when((v == 0) & there)
        def _():
            with_piece(
                b, j, lambda src, dst: along(src, red.at[b, j % slots], red_sems, b, j, ahead).start()
            )

        @pl.when((v > 0) & there)
        def _():
            mine = own.at[b, j % AHEAD]
            pltpu.make_async_copy(mine, mine, own_sem.at[b, j % AHEAD]).wait()
            along(red.at[b, j % slots], red.at[b, j % slots], red_sems, b, j, behind).wait_recv()
            at = j % slots

            def add(r):
                red[b, at, r] = (
                    red[b, at, r].astype(F32) + own[b, j % AHEAD, r].astype(F32)
                ).astype(BF)

            strips(prow, 64, add)

            @pl.when(v < last)
            def _():
                along(red.at[b, j % slots], red.at[b, j % slots], red_sems, b, j, ahead).start()

            @pl.when((v == last) & (j >= KEPT))
            def _():
                @pl.when(crosses(j - KEPT))
                def _():
                    along(red.at[b, 0], red.at[b, 0], x_sems, b, j - KEPT, across).wait_send()

                along(red.at[b, 0], red.at[b, 0], fin_sems, b, j - KEPT, behind).wait_send()
                pltpu.make_async_copy(red.at[b, 0], red.at[b, 0], put_sem.at[b, j - KEPT]).wait()

            @pl.when(v == last)
            def _():
                def act(src, dst):
                    along(red.at[b, j % slots], dst, fin_sems, b, j, behind).start()

                    @pl.when(crosses(j))
                    def _():
                        along(red.at[b, j % slots], dst, x_sems, b, j, across).start()

                    pltpu.make_async_copy(red.at[b, j % slots], dst, put_sem.at[b, j]).start()

                with_piece(b, j, act)

        g, there = placed(i - LAG * last - LAG * (last - v))

        @pl.when((v < last) & there)
        def _():
            along(red.at[b, 0], red.at[b, 0], fin_sems, b, g, ahead).wait_recv()

            @pl.when(v > 0)
            def _():
                along(red.at[b, 0], red.at[b, 0], red_sems, b, g, ahead).wait_send()

            def act(src, dst):
                @pl.when(v > 0)
                def _():
                    along(dst, dst, fin_sems, b, g, behind).start()

                @pl.when(crosses(g))
                def _():
                    along(dst, dst, x_sems, b, g, across).start()

            with_piece(b, g, act)

    hold, temp = R["hold"], R["temp"]
    boxes = [R["two_in"], R["ffn_in"], R["one_in"]]

    def held(ref, d, k):
        return ref.at[pl.ds((d * (tp // 2) + k) * share, share)]

    def messages(bit):
        base = sum(tp >> b for b in range(bit))
        keep = [(d, j) for d in range(2) for j in range(0, tp, 2 << bit)]
        return [(base + k, d, j) for k, (d, j) in enumerate(keep)]

    def sum_copy(n, m, src, **where):
        return remote_copy(
            src, boxes[n].at[m], R["sum_send"].at[n, m], R["sum_recv"].at[n, m], **where
        )

    def sum_start(n, bit):
        for m, d, j in messages(bit):
            src = held(temp, d, j // 2) if bit == 0 else held(hold, d, (j | 1 << bit) // 2)
            sum_copy(n, m, src, tp=flip(bit)).start()

    def sum_add(n, bit):
        for m, d, j in messages(bit):
            sum_copy(n, m, held(temp, d, j // 2), tp=flip(bit)).wait()
        loads = []
        for m, d, j in messages(bit):
            k = j // 2
            loads.append(
                pltpu.make_async_copy(boxes[n].at[m], held(temp, d, k), R["temp_sem"].at[d, k])
            )
            loads[-1].start()
        for copy, (m, d, j) in zip(loads, messages(bit)):
            copy.wait()
            base = (d * (tp // 2) + j // 2) * share

            def add(r, base=base):
                at = pl.ds(pl.multiple_of(base + r.start, ROWS_AT_ONCE), ROWS_AT_ONCE)
                hold[at, :] = (hold[at, :].astype(F32) + temp[at, :].astype(F32)).astype(BF)

            strips(share, ROWS_AT_ONCE, add)

    final = 2 * (tp - 1)

    def side_start(n):
        sum_copy(n, final, held(hold, 1, 0), seq=across).start()

    def side_finish(n):
        sum_copy(n, final, held(hold, 1, 0), seq=across).wait()
        load = pltpu.make_async_copy(boxes[n].at[final], held(temp, 0, 0), R["temp_sem"].at[0, 0])
        load.start()
        load.wait()

    def side_sum(r):
        return hold[r, :].astype(F32) + temp[r, :].astype(F32)

    ends = [R["out"], R["tokens"]]

    def token_copy(n, k, src, j, bit):
        return remote_copy(
            src,
            ends[n].at[block_of(j)],
            R["tok_send"].at[n, k],
            R["tok_recv"].at[n, k],
            tp=flip(bit),
        )

    def token_messages(bit):
        base = sum(tp >> (b + 1) for b in range(bit + 1, bits))
        return [(base + k, j) for k, j in enumerate(range(0, tp, 2 << bit))]

    def tokens_start(n, bit):
        for k, j in token_messages(bit):
            src = R["fresh"].at[n] if j == 0 else ends[n].at[block_of(j)]
            token_copy(n, k, src, j, bit).start()

    def tokens_wait(n, bit):
        for k, j in token_messages(bit):
            token_copy(n, k, R["fresh"].at[n], j, bit).wait()

    def tokens_put(n):
        return pltpu.make_async_copy(R["fresh"].at[n], ends[n].at[t], R["tok_put"].at[n])

    def block(d, j):
        return pl.ds((d * tp + j) * share, share)

    loads = [
        (R["w_out"].at[pl.ds(pl.multiple_of(side * heads * HD, heads * HD), heads * HD)], R["w_rows"]),
        (
            R["w_query"].at[:, pl.ds(pl.multiple_of(side * heads * HD, heads * HD), heads * HD)],
            R["a_t"].at[:, pl.ds(0, heads * HD)],
        ),
        (R["a_one"], R["a_in"].at[pl.ds(0, tp * share)]),
        (R["q"], R["q_in"]),
        (R["kv"], R["kv_all"].at[0]),
        (R["kv_in"], R["kv_all"].at[pl.ds(1, nodes - 1)]),
        (R["att"], R["att_in"]),
        (R["log"], R["log_in"]),
        (R["a_two"], R["low"]),
        (R["cot_far"], R["a_in"].at[pl.ds(tp * share, tp * share)]),
        (R["cot"].at[block_rows(0)], R["cot_in"]),
        (R["a_other"], R["a_in"].at[pl.ds(tp * share, tp * share)]),
        (R["w_kv"], R["a_t"].at[:, pl.ds(heads * HD, 2 * HD)]),
    ] + [(R["cot"].at[block_rows(j)], R["a_in"].at[block(0, j)]) for j in range(tp)]
    first_plain = len(loads)
    loads += [(R["resid"], R["resid_in"]), (R["raw"], R["raw_in"])]
    loads += [(R["cosine"], R["cos_in"]), (R["sine"], R["sin_in"])]
    loads += [(R["tokens_in"].at[block_rows(0)], R["x_in"])]
    plain = range(first_plain, len(loads))

    def load(k):
        return pltpu.make_async_copy(loads[k][0], loads[k][1], R["load_sem"].at[k])

    w_cols, w_sem = R["w_cols"], R["w_sem"]
    both = 2 * tp * share
    nt = (((1,), (1,)), ((), ()))
    tn = (((0,), (0,)), ((), ()))

    def chunk_loads(c):
        at = pl.multiple_of(side * ff + c * pcol, pcol)
        slot = c % 2
        down_at = pl.multiple_of(slot * pcol, pcol)
        return [
            pltpu.make_async_copy(
                R["w_gate"].at[:, pl.ds(at, pcol)], w_cols.at[slot, 0], w_sem.at[slot, 0]
            ),
            pltpu.make_async_copy(
                R["w_up"].at[:, pl.ds(at, pcol)], w_cols.at[slot, 1], w_sem.at[slot, 1]
            ),
            pltpu.make_async_copy(
                R["w_down"].at[pl.ds(at, pcol)],
                hold.at[pl.ds(down_at, pcol)],
                w_sem.at[slot, 2],
            ),
        ]

    def begin():
        load(8).start()
        for copy in chunk_loads(0):
            copy.start()
        early = (9, *range(13, 13 + tp))
        for k in early:
            load(k).start()
        load(8).wait()
        for k in early:
            load(k).wait()

        def body(r):
            R["a_in"][r, :] = (R["a_in"][r, :].astype(F32) * R["scale"][r, :]).astype(BF)

        strips(both, SCALE_ROWS, body)
        for copy in chunk_loads(1):
            copy.start()
        for k in (0, 3, 4, 5, 6, 7, 10, *plain):
            load(k).start()

    def chunk_ready(c):
        for copy in chunk_loads(c):
            copy.wait()

    def chunk_next(c):
        @pl.when(c + 2 < chunks)
        def _():
            for copy in chunk_loads(c + 2):
                copy.start()

    def chunk_forward(c, at):
        slot = c % 2
        cols = pl.ds(pl.multiple_of(c * pcol, pcol), pcol)
        w_rows = hold.at[pl.ds(pl.multiple_of(slot * pcol, pcol), pcol)]

        gate = jnp.dot(R["low"][at, :], w_cols[slot, 0], preferred_element_type=F32)
        up = jnp.dot(R["low"][at, :], w_cols[slot, 1], preferred_element_type=F32)
        d_hidden = lax.dot_general(R["a_in"][at, :], w_rows[...], nt, preferred_element_type=F32)
        sigma = 1.0 / (1.0 + jnp.exp(-gate))
        smooth = gate * sigma
        R["hidden"][at, cols] = (smooth * up).astype(BF)
        R["d_pair"][1, at, cols] = (d_hidden * smooth).astype(BF)
        R["d_pair"][0, at, cols] = (d_hidden * up * (sigma * (1.0 + gate - smooth))).astype(BF)

    def turn():
        def body(at):
            R["a_t"][:, at] = R["low"][at, :].T

        strips(both, 256, body)

    def stage_copies(c):
        at = pl.ds(pl.multiple_of(c * pcol, pcol), pcol)
        sem = R["stage_sem"]
        return [
            pltpu.make_async_copy(R["stage"].at[0], R["gate_part"].at[:, at], sem.at[0]),
            pltpu.make_async_copy(R["stage"].at[1], R["up_part"].at[:, at], sem.at[1]),
            pltpu.make_async_copy(R["stage_down"], R["down_part"].at[at], sem.at[2]),
        ]

    def chunk_gradients(c):
        cols = pl.ds(pl.multiple_of(c * pcol, pcol), pcol)

        @pl.loop(0, 2)
        def _(k):
            def body(at):
                R["stage"][k, at, :] = jnp.dot(
                    R["a_t"][at, :], R["d_pair"][k, :, cols], preferred_element_type=F32
                ).astype(BF)

            strips(width, 1024, body)

        for copy in stage_copies(c)[:2]:
            copy.start()

    def chunk_down(c):
        cols = pl.ds(pl.multiple_of(c * pcol, pcol), pcol)

        def body(at):
            R["stage_down"][:, at] = lax.dot_general(
                R["hidden"][:, cols], R["a_in"][:, at], tn, preferred_element_type=F32
            ).astype(BF)

        strips(width, 1024, body)
        stage_copies(c)[2].start()

    def row_loads(n):
        rows = pl.ds(pl.multiple_of(n * pcol, pcol), pcol)
        cols = pl.ds(pl.multiple_of(side * ff, ff), ff)
        return [
            pltpu.make_async_copy(
                R[name].at[rows, cols], R["w_strip"].at[n % 2, k], w_sem.at[n % 2, k]
            )
            for k, name in enumerate(("w_gate", "w_up"))
        ]

    def down_loads(n):
        return [
            pltpu.make_async_copy(
                R["w_down"].at[
                    pl.ds(pl.multiple_of(side * ff, ff), ff),
                    pl.ds(pl.multiple_of(n * pcol, pcol), pcol),
                ],
                w_cols.at[n % 2, 0, pl.ds(0, ff)],
                w_sem.at[n % 2, 0],
            )
        ]

    def start_all(copies):
        for copy in copies:
            copy.start()

    def by_columns(low_n, high_n, loads, product):
        @pl.loop(low_n, high_n)
        def _(n):
            for copy in loads(n):
                copy.wait()
            cols = pl.ds(pl.multiple_of(n * pcol, pcol), pcol)

            @pl.loop(0, 2)
            def _(d):
                at = pl.ds(pl.multiple_of(d * tp * share, tp * share), tp * share)
                value = product(at, n % 2).astype(BF)
                for j in range(tp):
                    rows = pl.ds(
                        pl.multiple_of((d * (tp // 2) + j // 2) * share, share), share
                    )
                    (temp if j % 2 else hold)[rows, cols] = value[j * share : (j + 1) * share]

            @pl.when(n + 2 < width // pcol)
            def _():
                start_all(loads(n + 2))

    def second_part(low_n, high_n):
        def product(at, slot):
            value = lax.dot_general(
                R["d_pair"][0, at, :], R["w_strip"][slot, 0], nt, preferred_element_type=F32
            )
            return value + lax.dot_general(
                R["d_pair"][1, at, :], R["w_strip"][slot, 1], nt, preferred_element_type=F32
            )

        by_columns(low_n, high_n, row_loads, product)

    def ffn_part(low_n, high_n):
        def product(at, slot):
            return jnp.dot(
                R["hidden"][at, :], w_cols[slot, 0, 0:ff, :], preferred_element_type=F32
            )

        by_columns(low_n, high_n, down_loads, product)

    def normed(v):
        inverse = lax.rsqrt(jnp.mean(v * v, axis=-1, keepdims=True) + EPS)
        return v * inverse, inverse

    low = R["low"]

    def low_at(d, j):
        return low.at[block(d, j)]

    def low_copy(k, src, dst, **where):
        return remote_copy(src, dst, R["low_send"].at[k], R["low_recv"].at[k], **where)

    up = 1 << top
    low_side = low_copy(0, low_at(0, 0), low_at(1, 0), seq=across)
    low_top = low_copy(1, low_at(0, 0), low_at(0, up), tp=flip(top))
    low_far = low_copy(2, low_at(1, 0), low_at(1, up), tp=flip(top))

    def low_bit(bit):
        base = 3 + sum(tp >> b for b in range(bit + 1, top))
        return [
            low_copy(base + k, low_at(d, j), low_at(d, j | 1 << bit), tp=flip(bit))
            for k, (d, j) in enumerate(
                (d, j) for d in range(2) for j in range(0, tp, 2 << bit)
            )
        ]

    def second_norm():
        side_finish(0)
        for k in (10, *plain):
            load(k).wait()
        R["gain_rows"][...] = jnp.zeros_like(R["gain_rows"])

        def body(r):
            d_a = side_sum(r)
            n_two, inverse = normed(R["resid_in"][r, :])
            R["gain_rows"][1:2, :] += jnp.sum(d_a * n_two, axis=0, keepdims=True)
            e = d_a * R["gain_two"][...]
            d_resid = R["cot_in"][r, :].astype(F32) * R["scale"][r, :] + inverse * (
                e - n_two * jnp.mean(e * n_two, axis=-1, keepdims=True)
            )
            R["d_resid"][r, :] = d_resid
            low[r, :] = d_resid.astype(BF)

        strips(share, ROWS_AT_ONCE, body)
        low_side.start()
        low_top.start()

    lane = lax.broadcasted_iota(jnp.int32, (span, 2 * HD), 1)

    def attended_back():
        for k in (0, 6):
            load(k).wait()
        R["d_kv"][...] = jnp.zeros_like(R["d_kv"])
        R["d_q"][...] = jnp.zeros_like(R["d_q"])
        @pl.loop(0, 2)
        def _(d):
            value = lax.dot_general(
                low[pl.ds(pl.multiple_of(d * tp * share, tp * share), tp * share), :],
                R["w_rows"][...],
                nt,
                preferred_element_type=F32,
            ).astype(BF)
            for j in range(tp):
                at = pl.ds(pl.multiple_of((d * tp + block_of(j)) * share, share), share)
                R["d_att"][at, :] = value[j * share : (j + 1) * share]

        ones = jnp.ones((8, 2 * HD), F32)
        pairs = heads // 2

        @pl.loop(0, 2 * n_rows * pairs)
        def _(n):
            d, r, h = n // (n_rows * pairs), n // pairs % n_rows, n % pairs
            cols = pl.ds(pl.multiple_of(h * 2 * HD, 2 * HD), 2 * HD)
            rows = pl.ds(pl.multiple_of(r * span, span), span)
            at = pl.ds(pl.multiple_of(d * span, span), span)
            d_rows = pl.ds(pl.multiple_of((d * n_rows + r) * span, span), span)
            for k in range(2):
                grads = R["d_att"][d_rows, cols].astype(F32)
                values = R["att_in"][d, rows, cols].astype(F32)
                if k == 0:
                    grads = pltpu.roll(grads, HD, 1)
                    values = pltpu.roll(values, HD, 1)
                grads = jnp.where(lane < HD, 0.0, grads)
                i = r * heads + 2 * h + k
                R["d_out"][i, at, :] = grads.astype(BF)
                R["delta"][i, :, at] = lax.dot_general(
                    ones,
                    grads * values,
                    nt,
                    precision=lax.Precision.HIGHEST,
                    preferred_element_type=F32,
                )

    def put_folded(ref, c, value):
        rows, cols = value.shape
        at = pl.ds(pl.multiple_of(c // ref.shape[1] * rows, rows), rows)
        ref[at, pl.ds(pl.multiple_of(c % ref.shape[1], cols), cols)] = value.astype(BF)

    def out_gradient():
        chunk = width // 2

        @pl.loop(0, 2 * tp)
        def _(n):
            R["d_att"][pl.ds(pl.multiple_of(n * share, share), share), :] = R["att_in"][
                n // tp, block_rows(n % tp), :
            ]

        @pl.loop(0, width // chunk)
        def _(n):
            c = pl.multiple_of(n * chunk, chunk)
            value = lax.dot_general(
                R["d_att"][...], low[:, pl.ds(c, chunk)], tn, preferred_element_type=F32
            )
            put_folded(R["out_part"], c, value)

    def attention_block(piece, i, diagonal):
        r = i // heads
        kv = R["kv_all"][piece, r, 0]
        q, d_out = R["q_in"][i], R["d_out"][i]
        scores = lax.dot_general(kv, q, nt, preferred_element_type=F32)
        probs = jnp.exp2(scores * (HD**-0.5 * 1.4426950408889634) - R["log_in"][i])
        if diagonal:
            k_at = lax.broadcasted_iota(jnp.int32, (wide, wide), 0)
            q_at = lax.broadcasted_iota(jnp.int32, (wide, wide), 1)
            q_at = jnp.where(q_at < span, q_at + span * side, q_at - span * side)
            k_at = jnp.where(k_at < span, k_at + span * side, k_at - span * side)
            probs = jnp.where(k_at <= q_at, probs, 0.0)
        d_probs = lax.dot_general(kv, d_out, nt, preferred_element_type=F32)
        d_scores = (probs * (d_probs - R["delta"][i, 0:1, :])).astype(BF)
        R["d_kv"][piece, r] += jnp.dot(d_scores, q, preferred_element_type=F32) + jnp.dot(
            probs.astype(BF), d_out, preferred_element_type=F32
        ) * (HD**0.5)
        R["d_q"][i] += lax.dot_general(
            kv, d_scores, (((0,), (0,)), ((), ())), preferred_element_type=F32
        )

    def kv_copy(step):
        return remote_copy(
            R["kv_back"].at[step - 1],
            R["kv_far"].at[step - 1],
            R["kv_send"].at[step - 1],
            R["kv_recv"].at[step - 1],
            seq=rank - 2 * step,
        )

    def kv_send():
        for step in range(1, nodes):

            @pl.when(node >= step)
            def _():
                R["kv_back"][step - 1] = R["d_kv"][step].astype(BF)
                kv_copy(step).start()

    def kv_sum():
        for step in range(1, nodes):

            @pl.when(node + step < nodes)
            def _():
                kv_copy(step).wait_recv()
                R["d_kv"][0] += R["kv_far"][step - 1].astype(F32)

            @pl.when(node >= step)
            def _():
                kv_copy(step).wait_send()

    def head_back(grads, raw, gain, at):
        lanes = 2 * HD
        low_lane = lane < HD // 2
        raw = jnp.where(lane < HD, raw, 0.0)
        swapped = jnp.where(
            low_lane, pltpu.roll(grads, lanes - HD // 2, 1), pltpu.roll(grads, HD // 2, 1)
        )
        rotated = grads * R["cos_in"][at, :] + swapped * R["sin_in"][at, :]
        inverse = lax.rsqrt(jnp.sum(raw * raw, axis=-1, keepdims=True) * (1.0 / HD) + EPS_HEAD)
        n = raw * inverse
        e = rotated * gain
        back = inverse * (e - n * (jnp.sum(e * n, axis=-1, keepdims=True) * (1.0 / HD)))
        return back, jnp.sum(rotated * n, axis=0, keepdims=True)

    def heads_back():
        scale = HD**-0.5
        pairs = heads // 2

        @pl.loop(0, 2 * n_rows)
        def _(n):
            r, d = n // 2, n % 2
            at = pl.ds(pl.multiple_of((d * n_rows + r) * span, span), span)
            here = pl.ds(pl.multiple_of(d * span, span), span)

            @pl.loop(0, pairs)
            def _(h):
                pair = []
                both_raw = R["raw_in"][at, pl.ds(pl.multiple_of(h * 2 * HD, 2 * HD), 2 * HD)].astype(F32)
                for k in range(2):
                    i = r * heads + 2 * h + k
                    grads = R["d_q"][i, :, here].T * scale
                    raw = both_raw if k == 0 else pltpu.roll(both_raw, HD, 1)
                    back, gain = head_back(grads, raw, R["gain_q"][...], at)
                    R["gain_rows"][2:3, 0 : 2 * HD] += gain
                    pair.append(back)
                R["d_raw"][at, pl.ds(pl.multiple_of(h * 2 * HD, 2 * HD), 2 * HD)] = jnp.where(
                    lane < HD, pair[0], pltpu.roll(pair[1], HD, 1)
                ).astype(BF)

            grads = R["d_kv"][0, r, here, :] * scale
            raw = R["raw_in"][at, heads * HD :].astype(F32)
            back, gain = head_back(grads, raw, R["gain_k"][...], at)
            R["gain_rows"][3:4, 0 : 2 * HD] += gain
            R["d_raw"][at, pl.ds(heads * HD, 2 * HD)] = jnp.where(lane < HD, back, grads).astype(
                BF
            )

    def raw_gradient():
        for k in (2, 11):
            load(k).wait()
        chunk = width // 2
        cut = heads * HD

        @pl.loop(0, width // chunk)
        def _(n):
            c = pl.multiple_of(n * chunk, chunk)
            value = lax.dot_general(
                R["d_raw"][...], R["a_in"][:, pl.ds(c, chunk)], tn, preferred_element_type=F32
            )
            put_folded(R["q_part"], c, value[:cut])
            put_folded(R["kv_part"], c, value[cut:])

    def first_part(low_n, high_n):
        inner = (heads + 2) * HD
        rel = R["hidden"]
        chunk = 512

        if low_n == 0:
            load(1).wait()
            load(12).wait()

            @pl.loop(0, 2 * tp)
            def _(n):
                rows = pl.multiple_of((n // tp * tp + block_of(n % tp)) * share, share)
                rel[pl.ds(pl.multiple_of(n * share, share), share), 0:inner] = R["d_raw"][
                    pl.ds(rows, share), :
                ]

        @pl.loop(low_n, high_n)
        def _(n):
            cols = pl.ds(pl.multiple_of(n * chunk, chunk), chunk)

            @pl.loop(0, 2)
            def _(d):
                at = pl.ds(pl.multiple_of(d * tp * share, tp * share), tp * share)
                value = lax.dot_general(
                    rel[at, 0:inner], R["a_t"][cols, 0:inner], nt, preferred_element_type=F32
                ).astype(BF)
                for j in range(tp):
                    rows = pl.ds(
                        pl.multiple_of((d * (tp // 2) + j // 2) * share, share), share
                    )
                    (temp if j % 2 else hold)[rows, cols] = value[j * share : (j + 1) * share]

    def out_end():
        side_finish(1)

        def body(r):
            R["fresh"][0, r, :] = (R["resid_in"][r, :] + side_sum(r)).astype(BF)

        strips(share, ROWS_AT_ONCE, body)
        tokens_put(0).start()
        tokens_start(0, top)

    def first_norm():
        side_finish(2)

        def body(r):
            d_a = side_sum(r)
            n_one, inverse = normed(R["x_in"][r, :].astype(F32))
            R["gain_rows"][0:1, :] += jnp.sum(d_a * n_one, axis=0, keepdims=True)
            e = d_a * R["gain_one"][...]
            d_x = R["d_resid"][r, :] + inverse * (
                e - n_one * jnp.mean(e * n_one, axis=-1, keepdims=True)
            )
            R["fresh"][1, r, :] = d_x.astype(BF)

        strips(share, ROWS_AT_ONCE, body)
        tokens_put(1).start()
        tokens_start(1, top)
        part = width // tp
        for k in range(tp):
            R["gain_box"][k] = jnp.zeros((8, part), F32)
            R["gain_box"][k, 0:2, :] = R["gain_rows"][0:2, k * part : (k + 1) * part]
            R["gain_box"][k, 2:4, 0 : 2 * HD] = R["gain_rows"][2:4, 0 : 2 * HD]

        @pl.loop(1, total)
        def _(k):
            other = (me + k) % total
            remote_copy(
                R["gain_box"].at[other % tp],
                R["gain_all"].at[k],
                R["gain_send"].at[k],
                R["gain_recv"].at[k],
                seq=other // tp,
                tp=other % tp,
            ).start()

        R["gain_all"][0] = R["gain_box"][t]

    def gains_end():
        @pl.loop(1, total)
        def _(k):
            remote_copy(
                R["gain_box"].at[0],
                R["gain_all"].at[k],
                R["gain_send"].at[k],
                R["gain_recv"].at[k],
                seq=rank,
                tp=t,
            ).wait()

        R["gains"][...] = jnp.zeros_like(R["gains"])

        @pl.loop(0, total)
        def _(k):
            R["gains"][...] += R["gain_all"][k]

    tasks = {}

    def task(step, *acts):
        tasks.setdefault(step, []).extend(acts)
        return step

    def sums_tasks(n, step):
        for bit in range(bits):
            step += 2 if bit == 0 else 5
            following = (
                (lambda bit=bit: sum_start(n, bit + 1)) if bit < top else (lambda: side_start(n))
            )
            task(step, lambda bit=bit: sum_add(n, bit), following)
        return step + 5

    def token_tasks(n, step):
        for bit in reversed(range(bits)):
            step += 3
            task(step, lambda bit=bit: tokens_wait(n, bit))
            if bit:
                task(step, lambda bit=bit: tokens_start(n, bit - 1))
        task(step, lambda: tokens_put(n).wait())
        return step

    n_rows_w = width // pcol
    first_move = 1
    halves = 2 * chunks - 1
    task(0, begin)
    step = halves
    task(step, lambda: start_all(row_loads(0)), lambda: start_all(row_loads(1)))
    for k in range(4):
        step = task(
            halves + k, lambda k=k: second_part(n_rows_w * k // 4, n_rows_w * (k + 1) // 4)
        )
    task(step, lambda: sum_start(0, 0))
    task(step, lambda: start_all(down_loads(0)), lambda: start_all(down_loads(1)))
    grads_at = step + 1
    grads_end = grads_at + 2 * (chunks - 1)
    assert grads_at + 1 < first_move + per_chunk // 2
    task(grads_end, load(1).start, load(2).start, load(11).start, load(12).start)
    step = task(sums_tasks(0, step), second_norm)
    task(max(step, grads_end) + 1, lambda: ffn_part(0, n_rows_w // 2))
    ffn_at = task(
        max(step, grads_end) + 2,
        lambda: ffn_part(n_rows_w // 2, n_rows_w),
        lambda: sum_start(1, 0),
    )
    step = task(step + 4, low_side.wait, low_top.wait, low_far.start)
    step += 3
    task(step, low_far.wait)
    for bit in reversed(range(top)):
        task(step, lambda bit=bit: [c.start() for c in low_bit(bit)])
        step += 2
        task(step, lambda bit=bit: [c.wait() for c in low_bit(bit)])
    task(step, attended_back)
    ffn_end = task(sums_tasks(1, ffn_at), out_end)
    token_tasks(0, ffn_end)
    step = task(step + 1, *[load(k).wait for k in (3, 4, 5, 7)])
    first_block = step
    per_step = 4
    step += -(-(nodes * n_q) // per_step)
    last_block = step
    task(step, kv_send)
    task(step + 2, out_gradient)
    step = task(step + 5, kv_sum, heads_back)
    step = task(step + 1, raw_gradient)
    raw_ready = step
    assert raw_ready > ffn_end
    task(step + 1, lambda: first_part(0, width // 1024))
    step = task(
        step + 2, lambda: first_part(width // 1024, width // 512), lambda: sum_start(2, 0)
    )
    step = task(sums_tasks(2, step), first_norm)
    task(token_tasks(1, step), gains_end)

    late = half - (R["q_part"].shape[1] + R["kv_part"].shape[1]) // pcol // 2
    late_end = late + R["q_part"].shape[1] // pcol // 2
    gap = max(0, raw_ready + 1 - late - first_move)
    steps = max(first_move + half + gap + 2 * LAG * last, max(tasks) + 1)

    @pl.loop(0, steps)
    def _(i):
        for b in range(2):
            stream(b, i - first_move)
        for at, acts in sorted(tasks.items()):

            @pl.when(i == at)
            def _(acts=acts):
                for act in acts:
                    act()

        @pl.when(i < halves)
        def _():
            c = (i + 1) // 2

            @pl.when((i == 0) | (i % 2 == 1))
            def _():
                chunk_ready(c)

            @pl.loop(jnp.where((i == 0) | (i % 2 == 1), 0, 1), jnp.where(i % 2 == 1, 1, 2))
            def _(m):
                chunk_forward(c, pl.ds(pl.multiple_of(m * (both // 2), both // 2), both // 2))

            @pl.when(i % 2 == 0)
            def _():
                chunk_next(c)

        pl.when(i == 0)(turn)
        g = i - grads_at
        c = jnp.where(i < 2, 0, g // 2 + 1)
        within = (g >= 0) & (i < grads_end)

        @pl.when((i == 0) | (within & (g % 2 == 0)))
        def _():
            chunk_gradients(c)
            for copy in stage_copies(c)[:2]:
                copy.wait()

        @pl.when((i == 1) | (within & (g % 2 == 1)))
        def _():
            chunk_down(c)
            stage_copies(c)[2].wait()

        @pl.when((i >= first_block) & (i < last_block))
        def _():
            @pl.loop(0, per_step)
            def _(k):
                n = (i - first_block) * per_step + k
                piece = n // n_q

                @pl.when(n < n_q)
                def _():
                    attention_block(0, n, True)

                @pl.when((n >= n_q) & (n < n_q * nodes) & (node >= piece))
                def _():
                    attention_block(piece, n % n_q, False)

    @pl.loop(0, half)
    def _(j):
        for b in range(2):
            v = node if b == 0 else last - node
            probe = red.at[b, 0]

            @pl.when(v == 0)
            def _():
                along(probe, probe, red_sems, b, j, rank).wait_send()

            @pl.when((v > 0) & ((v < last) | (j >= half - KEPT)))
            def _():
                along(probe, probe, fin_sems, b, j, rank).wait_send()

            @pl.when((v == last) & (j >= half - KEPT))
            def _():
                pltpu.make_async_copy(probe, probe, put_sem.at[b, j]).wait()

            @pl.when(crosses(j) & ((v < last) | (j >= half - KEPT)))
            def _():
                along(probe, probe, x_sems, b, j, rank).wait_send()

            @pl.when(crosses(j))
            def _():
                along(probe, probe, x_sems, b, j, rank).wait_recv()


def backward(nodes, bits, ident, values):
    tp, seq = 1 << bits, 2 * nodes
    share, width = values["resid"].shape
    ff = values["w_gate"].shape[1] // 2
    n_q, wide, _ = values["q"].shape
    n_rows = values["kv"].shape[0]
    heads = n_q // n_rows
    tokens = tp * share
    piece = 256
    cols = (heads + 2) * HD
    small = [(piece, r * width // piece) for r in (heads * HD, heads * HD, 2 * HD)]
    shapes = [(width, 2 * ff), (width, 2 * ff), (2 * ff, width)]
    shapes += [(2 * small[0][0], small[0][1]), small[1], (2 * small[2][0], small[2][1])]
    half = (3 * width * ff + sum(r * c for r, c in small)) // (2 * piece * piece)
    slots = 2 * LAG * (nodes - 1) + 2
    vmem = pl.BlockSpec(memory_space=pltpu.VMEM)
    anywhere = pl.BlockSpec(memory_space=pl.ANY)
    dma = pltpu.SemaphoreType.DMA
    inside = ("scale", "gain_two", "gain_one", "gain_q", "gain_k")
    kv = values["kv"].shape
    total = seq * tp
    messages = 3 + 2 * (tp - 2)
    outs = shapes + [(tp, share, width)] * 2 + [(8, width // tp)]
    outs += [(2 * tp - 1, share, width)] * 3 + [(width, ff), (width, ff), (ff, width)]
    scratch = [
        (2, slots, piece, piece),
        (2, AHEAD, piece, piece),
        (tokens, width),
        (tokens, width),
        (2 * tokens, width),
        (2 * tokens, width),
        (width, 2 * tokens),
        (heads * HD, width),
        (n_q, wide, 2 * HD),
        (n_q, wide, 2 * HD),
        (n_q, 2 * HD, wide, F32),
        (nodes, n_rows, wide, 2 * HD, F32),
        (nodes,) + kv,
        (2, tokens, heads * HD),
        (2 * tokens, heads * HD),
        (n_q, 8, wide, F32),
        (2 * tokens, cols),
        small[1],
        small[2],
        small[0],
        (nodes - 1, n_rows, wide, 2 * HD),
        (nodes - 1, n_rows, wide, 2 * HD),
        (share, width, F32),
        (2, share, width),
        (8, width, F32),
        (tp, 8, width // tp, F32),
        (total, 8, width // tp, F32),
        (n_q, 1, wide, F32),
        (share, width),
        (share, width, F32),
        (2 * tokens, cols),
        (2 * tokens, 2 * HD, F32),
        (2 * tokens, 2 * HD, F32),
        (share, width),
        (2 * tokens, ff),
        (2, 2 * tokens, ff),
        (2, 2, piece, ff),
        (2, 2, width, piece),
        (2, width, piece),
        (piece, width),
    ]
    sems = [(2, AHEAD)] + [(2, half)] * 7 + [(18 + tp,), (3, 2 * tp - 1), (3, 2 * tp - 1)]
    sems += [(2, tp // 2), (messages,), (messages,), (nodes - 1,), (nodes - 1,)]
    sems += [(2, tp - 1), (2, tp - 1), (2,), (total,), (total,), (2, 3), (3,)]
    return pl.pallas_call(
        functools.partial(backward_kernel, nodes, bits),
        out_shape=[
            jax.ShapeDtypeStruct(shape, F32 if k == 8 else BF) for k, shape in enumerate(outs)
        ],
        in_specs=[vmem if k in inside else anywhere for k in values],
        out_specs=[vmem if k == 8 else anywhere for k in range(len(outs))],
        scratch_shapes=[
            pltpu.VMEM(s[:-1], F32) if s[-1] is F32 else pltpu.VMEM(s, BF) for s in scratch
        ]
        + [dma(s) for s in sems],
        compiler_params=pltpu.CompilerParams(
            collective_id=ident, has_side_effects=True, vmem_limit_bytes=62 << 20
        ),
        cost_estimate=pl.CostEstimate(
            flops=0, bytes_accessed=1 << 30, transcendentals=0
        ),
        name="backward",
    )(*values.values())[:9]


def widen(arrays):
    block = arrays[-1].shape[0]
    for array in arrays:
        block = min(block, array.shape[0])
    counts = [array.shape[0] // block for array in arrays]
    starts = [sum(counts[:k]) for k in range(len(arrays))]
    width = arrays[0].shape[1]

    def kernel(*refs):
        step = pl.program_id(0)
        for k, (start, size) in enumerate(zip(starts, counts)):

            @pl.when((step >= start) & (step < start + size))
            def _(k=k):
                refs[len(arrays) + k][...] = refs[k][...].astype(F32)

    specs = [
        pl.BlockSpec(
            (block, width), lambda i, start=start, size=size: (jnp.clip(i - start, 0, size - 1), 0)
        )
        for start, size in zip(starts, counts)
    ]
    return pl.pallas_call(
        kernel,
        grid=(sum(counts),),
        out_shape=[jax.ShapeDtypeStruct(a.shape, F32) for a in arrays],
        in_specs=specs,
        out_specs=specs,
        compiler_params=pltpu.CompilerParams(vmem_limit_bytes=56 << 20),
        cost_estimate=pl.CostEstimate(
            flops=0, bytes_accessed=6 * block * width * sum(counts), transcendentals=0
        ),
        name="widen",
    )(*arrays)


def turn_heads(mine, other, kv, q_cols, shared, width):
    side = (lax.axis_index("seq") % 2).reshape(1).astype(jnp.int32)
    chunk = 256

    def kernel(side_ref, mine_ref, other_ref, kv_ref, q_out, k_out, v_out):
        first = side_ref[0] == 0
        per = mine_ref.shape[1] // chunk
        lane = lax.broadcasted_iota(jnp.int32, (chunk, 2 * HD), 1)

        @pl.loop(0, width // chunk)
        def _(n):
            rows = pl.ds(pl.multiple_of(n * chunk, chunk), chunk)
            at = pl.ds(pl.multiple_of(n // per * q_cols, q_cols), q_cols)
            cols = pl.ds(pl.multiple_of(n % per * chunk, chunk), chunk)
            own = mine_ref[at, cols].astype(F32).T
            far = other_ref[at, cols].astype(F32).T
            q_out[rows, 0:q_cols] = jnp.where(first, own, far)
            q_out[rows, q_cols:] = jnp.where(first, far, own)

        height = 2 * HD
        per_kv = kv_ref.shape[1] // chunk
        stack = kv_ref.shape[0] // 2

        @pl.loop(0, width // chunk)
        def _(n):
            rows = pl.ds(pl.multiple_of(n * chunk, chunk), chunk)
            cols = pl.ds(pl.multiple_of(n % per_kv * chunk, chunk), chunk)
            pair = [
                kv_ref[
                    pl.ds(pl.multiple_of(s * stack + n // per_kv * height, height), height), cols
                ]
                .astype(F32)
                .T
                for s in range(2)
            ]
            if shared:
                both = pair[0] + pair[1]
                k_out[rows, :] = both[:, :HD]
                v_out[rows, :] = both[:, HD:]
            else:
                k_out[rows, :] = jnp.where(lane < HD, pair[0], pltpu.roll(pair[1], HD, 1))
                v_out[rows, :] = jnp.where(lane < HD, pltpu.roll(pair[0], HD, 1), pair[1])

    vmem = pl.BlockSpec(memory_space=pltpu.VMEM)
    k_cols = HD if shared else 2 * HD
    return pl.pallas_call(
        kernel,
        out_shape=[
            jax.ShapeDtypeStruct((width, c), F32) for c in (2 * q_cols, k_cols, k_cols)
        ],
        in_specs=[pl.BlockSpec(memory_space=pltpu.SMEM)] + [vmem] * 3,
        out_specs=[vmem] * 3,
        compiler_params=pltpu.CompilerParams(vmem_limit_bytes=40 << 20),
        name="turn_heads",
    )(side, mine, other, kv)


def per_device(
    tokens,
    positions,
    corpus,
    corpus_weight,
    gain_one,
    w_query,
    w_key,
    w_value,
    gain_query,
    gain_key,
    w_out,
    gain_two,
    w_gate,
    w_up,
    w_down,
    cotangent,
):
    net = Links()
    rows, per_row, width = tokens.shape
    count = rows * per_row
    share = count // net.tp
    total_len = per_row * net.seq
    side, node, t = net.side, net.node, net.t
    q_cols = w_query.shape[1] // 2
    shared = (w_key.shape[1] // HD) % 2 == 1
    k_cols = w_key.shape[1] if shared else w_key.shape[1] // 2
    both = 2 * count

    def lanes(v):
        return jnp.pad(v, [(0, 0)] * (v.ndim - 1) + [(0, 2 * HD - v.shape[-1])])

    pos_own = positions.reshape(count)
    corpus_own = corpus.reshape(count)
    told = net.swap_side(jnp.stack([pos_own, corpus_own]))
    cosine, sine = rope_tables(jnp.concatenate([pos_own, told[0]]))
    cosine = lanes(jnp.concatenate([cosine, cosine], axis=1))
    sine = lanes(jnp.concatenate([sine, -sine], axis=1))
    onehot = (corpus_own[:, None] == jnp.arange(NCORP, dtype=jnp.int32)).astype(F32)
    own_counts = jnp.zeros((8, 128), F32).at[0, :NCORP].set(jnp.sum(onehot, axis=0))
    token_rows = tokens.reshape(count, width)
    cot_rows = cotangent.reshape(count, width)
    head_gains = lanes(jnp.stack([gain_query, gain_key]))
    gain_q, gain_k = head_gains[0:1], head_gains[1:2]

    assert k_cols == HD

    q, kv, raw, a_one, att, log, all_counts, cot_other, resid, a_two, kv_in, a_other, w_kv = attend(
        net.nodes,
        net.bits,
        2,
        dict(
            tokens=token_rows,
            w_query=w_query,
            w_key=w_key,
            w_value=w_value,
            w_out=w_out,
            cot=cot_rows,
            gain_one=gain_one[None],
            gain_two=gain_two[None],
            gain_q=gain_q,
            gain_k=gain_k,
            cosine=cosine,
            sine=sine,
            count=own_counts,
            rows=rows,
        ),
    )
    a_two = a_two.reshape(both, width)

    counts = jnp.sum(all_counts, axis=0)[0, :NCORP]
    weight_scale = corpus_weight.astype(F32) * (rows * total_len / NCORP) / counts
    corpus_other = told[1]
    onehot_other = (corpus_other[:, None] == jnp.arange(NCORP, dtype=jnp.int32)).astype(F32)
    scale_own = jnp.sum(onehot * weight_scale, axis=-1, keepdims=True)
    scale_other = jnp.sum(onehot_other * weight_scale, axis=-1, keepdims=True)
    scale_both = jnp.concatenate([net.relative(scale_own), net.relative(scale_other)], axis=0)

    sums = backward(
        net.nodes,
        net.bits,
        3,
        dict(
            a_two=a_two,
            cot=cot_rows,
            cot_far=cot_other.reshape(count, width),
            scale=scale_both,
            w_gate=w_gate,
            w_up=w_up,
            w_down=w_down,
            resid=resid,
            tokens_in=token_rows,
            gain_two=gain_two[None],
            gain_one=gain_one[None],
            gain_q=gain_q,
            gain_k=gain_k,
            w_out=w_out,
            w_query=w_query,
            w_kv=w_kv,
            a_one=a_one,
            a_other=a_other,
            q=q,
            kv=kv,
            kv_in=kv_in,
            att=att,
            log=log,
            raw=raw,
            cosine=cosine,
            sine=sine,
        ),
    )
    q_other = net.swap_side(sums[4])
    fold = width // sums[3].shape[1]
    grad_out = sums[3].reshape(2, fold, q_cols, -1).transpose(0, 2, 1, 3).reshape(2 * q_cols, width)
    grad_gate, grad_up, grad_down, grad_out = widen([*sums[:3], grad_out])
    grad_query, grad_key, grad_value = turn_heads(
        sums[4], q_other, sums[5], q_cols, shared, width
    )
    out, d_tokens = (v.reshape(rows, per_row, width) for v in sums[6:8])
    gains = sums[8]

    head_share = HD // net.tp

    return (
        out,
        d_tokens,
        gains[0],
        grad_query,
        grad_key,
        grad_value,
        take(gains[2], t * head_share, head_share),
        take(gains[3], t * head_share, head_share),
        grad_out,
        gains[1],
        grad_gate,
        grad_up,
        grad_down,
    )


def solution(mesh):
    placed = (
        P(None, "seq", None),
        P(None, "seq"),
        P(None, "seq"),
        P(),
        P(),
        P(None, "tp"),
        P(None, "tp"),
        P(None, "tp"),
        P(),
        P(),
        P("tp", None),
        P(),
        P(None, "tp"),
        P(None, "tp"),
        P("tp", None),
        P(None, "seq", None),
    )
    return jax.shard_map(
        per_device,
        mesh=mesh,
        in_specs=placed,
        out_specs=(
            P(None, "seq", None),
            P(None, "seq", None),
            P("tp"),
            P(None, "tp"),
            P(None, "tp"),
            P(None, "tp"),
            P("tp"),
            P("tp"),
            P("tp", None),
            P("tp"),
            P(None, "tp"),
            P(None, "tp"),
            P("tp", None),
        ),
        check_vma=False,
    )
```

```python
import functools

import jax
import jax.numpy as jnp
from jax import lax
from jax.experimental import pallas as pl
from jax.experimental.pallas import tpu as pltpu
from jax.sharding import PartitionSpec as P

HD = 64
NCORP = 8


EPS = 1e-05
EPS_HEAD = 1e-06
ROPE_BASE = 10000.0
BF = jnp.bfloat16
F32 = jnp.float32
MESH = pl.DeviceIdType.MESH
LAG = 2
AHEAD = 3
KEPT = 6
ROWS_AT_ONCE = 64
SCALE_ROWS = 128


def rope_tables(positions):
    half = HD // 2
    rates = ROPE_BASE ** (-jnp.arange(half, dtype=jnp.float32) * 2.0 / HD)
    angle = positions.astype(jnp.float32)[:, None] * rates[None, :]
    return (jnp.cos(angle), jnp.sin(angle))


def rotate(vector, cosine, sine):
    half = vector.shape[-1] // 2
    first = vector[..., :half]
    second = vector[..., half:]
    return jnp.concatenate(
        [first * cosine - second * sine, second * cosine + first * sine], axis=-1
    )


def head_norm(vector, gain):
    inverse = lax.rsqrt(jnp.mean(vector * vector, axis=-1, keepdims=True) + EPS_HEAD)
    normed = vector * inverse
    return (normed, inverse, normed * gain)


def dot(a, b):
    return jnp.dot(a, b, preferred_element_type=F32)


def dot_tn(a, b):
    return lax.dot_general(a, b, (((0,), (0,)), ((), ())), preferred_element_type=F32)


def dot_nt(a, b):
    return lax.dot_general(a, b, (((1,), (1,)), ((), ())), preferred_element_type=F32)


def take(array, start, size, axis=0):
    return lax.dynamic_slice_in_dim(array, start, size, axis)


class Links:
    def __init__(self):
        self.seq = lax.axis_size("seq")
        self.tp = lax.axis_size("tp")
        self.nodes = self.seq // 2
        self.bits = self.tp.bit_length() - 1
        rank = lax.axis_index("seq")
        self.node = rank // 2
        self.side = rank % 2
        self.t = lax.axis_index("tp")

    def swap_side(self, value):
        return lax.ppermute(value, "seq", [(s, s ^ 1) for s in range(self.seq)])

    def swap_bit(self, value, bit):
        return lax.ppermute(value, "tp", [(r, r ^ (1 << bit)) for r in range(self.tp)])

    def relative(self, rows):
        share = rows.shape[0] // self.tp
        return jnp.concatenate(
            [take(rows, (self.t ^ j) * share, share) for j in range(self.tp)], axis=0
        )


def remote_copy(src, dst, send, recv, **where):
    return pltpu.make_async_remote_copy(
        src, dst, send, recv, device_id=where, device_id_type=MESH
    )


def attend_kernel(nodes, bits, *refs):
    names = (
        "tokens", "w_query", "w_key", "w_value", "w_out", "cot", "gain_one", "gain_two", "gain_q", "gain_k",
        "cosine", "sine", "count",
        "q", "kv", "raw", "a_one", "att", "log", "counts", "cot_out", "resid", "a_out", "kv_in", "a_other", "w_kv",
        "tok", "wq", "wk", "wv", "wo", "raw_other", "acc", "weight_sum", "att_in", "att_rel", "hold", "temp", "got",
        "mine", "q_in", "raw_in", "a_in", "w_in",
        "load_sem", "raw_sem", "kv_send", "kv_recv", "count_send", "count_recv", "cot_send", "cot_recv", "att_sem",
        "sum_send", "sum_recv", "all_send", "all_recv", "own_sem", "a_sem", "out_sem",
    )
    assert len(names) == len(refs)
    R = dict(zip(names, refs))
    tp, seq = 1 << bits, 2 * nodes
    top = bits - 1
    rank, t = lax.axis_index("seq"), lax.axis_index("tp")
    node, side = rank // 2, rank % 2
    across = rank + 1 - 2 * side
    n_q, wide, _ = R["q"].shape
    n_rows = R["kv"].shape[0]
    heads = n_q // n_rows
    q_cols = heads * HD
    span = wide // 2
    share, width = R["resid"].shape
    count = tp * share

    def strips(rows, step, body):
        @pl.loop(0, rows // step)
        def _(m):
            body(pl.ds(pl.multiple_of(m * step, step), step))

    def flip(bit):
        return t + (1 << bit) * (1 - 2 * ((t // (1 << bit)) % 2))

    def block_of(j):
        other = t
        for bit in range(bits):
            there = (j // (1 << bit)) % 2
            other = other + there * (1 << bit) * (1 - 2 * ((t // (1 << bit)) % 2))
        return other

    def block_rows(j):
        return pl.ds(pl.multiple_of(block_of(j) * share, share), share)

    half = R["w_out"].shape[0] // 2
    loads = [(R["tokens"], R["tok"]), (R["w_query"], R["wq"]), (R["w_key"], R["wk"])]
    loads += [(R["w_value"], R["wv"])]
    loads += [
        (
            R["w_out"].at[pl.ds(pl.multiple_of(at * half, half), half)],
            R["wo"].at[pl.ds(k * half, half)],
        )
        for k, at in enumerate((side, 1 - side))
    ]

    def load(k):
        return pltpu.make_async_copy(loads[k][0], loads[k][1], R["load_sem"].at[k])

    for k in range(6):
        load(k).start()

    leaving = [("q_in", "q"), ("raw_in", "raw"), ("a_in", "a_one"), ("w_in", "w_kv")]

    def leave(k):
        return pltpu.make_async_copy(R[leaving[k][0]], R[leaving[k][1]], R["out_sem"].at[k])

    barrier = pltpu.get_barrier_semaphore()
    for step in range(1, seq):
        pl.semaphore_signal(
            barrier, 1, device_id={"seq": (rank + step) % seq}, device_id_type=MESH
        )
    for bit in range(bits):
        pl.semaphore_signal(barrier, 1, device_id={"tp": flip(bit)}, device_id_type=MESH)

    load(0).wait()

    def first_norm(r):
        v = R["tok"][r, :].astype(F32)
        inverse = lax.rsqrt(jnp.mean(v * v, axis=-1, keepdims=True) + EPS)
        R["a_in"][r, :] = (v * inverse * R["gain_one"][...]).astype(BF)

    strips(count, 64, first_norm)
    leave(2).start()
    for k in (1, 2, 3):
        load(k).wait()

    def pair_of(k, v, first):
        if k.shape[1] == HD:
            return jnp.concatenate([k, v], axis=1)
        low = lax.broadcasted_iota(jnp.int32, k.shape, 1) < HD
        return jnp.where(
            low,
            jnp.where(first, k, pltpu.roll(k, HD, 1)),
            jnp.where(first, pltpu.roll(v, HD, 1), v),
        )

    def project(r):
        a = R["a_in"][r, :]
        k = jnp.dot(a, R["wk"][...], preferred_element_type=F32)
        v = jnp.dot(a, R["wv"][...], preferred_element_type=F32)
        R["raw_in"][r, q_cols:] = pair_of(k, v, side == 0).astype(BF)
        R["raw_other"][r, q_cols:] = pair_of(k, v, side == 1).astype(BF)

    strips(count, 256, project)

    def queries(ref, half):
        cols = pl.ds(pl.multiple_of(half * q_cols, q_cols), q_cols)

        def body(r):
            ref[r, 0:q_cols] = jnp.dot(
                R["a_in"][r, :], R["wq"][:, cols], preferred_element_type=F32
            ).astype(BF)

        strips(count, 256, body)

    queries(R["raw_other"], 1 - side)
    pl.semaphore_wait(barrier, seq - 1 + bits)
    raw_copy = remote_copy(
        R["raw_other"],
        R["raw_in"].at[pl.ds(count, count)],
        R["raw_sem"].at[0],
        R["raw_sem"].at[1],
        seq=across,
    )
    raw_copy.start()
    queries(R["raw_in"], side)
    R["counts"][0] = R["count"][...]
    count_copies = [
        remote_copy(
            R["count"],
            R["counts"].at[step],
            R["count_send"].at[step - 1],
            R["count_recv"].at[step - 1],
            seq=(rank + step) % seq,
        )
        for step in range(1, seq)
    ]
    for copy in count_copies:
        copy.start()

    lane = lax.broadcasted_iota(jnp.int32, (span, 2 * HD), 1)

    def head(v, gain, at):
        v = jnp.where(lane < HD, v, 0.0)
        inverse = lax.rsqrt(jnp.sum(v * v, axis=-1, keepdims=True) * (1.0 / HD) + EPS_HEAD)
        v = v * inverse * gain
        swapped = jnp.where(
            lane < HD // 2, pltpu.roll(v, 2 * HD - HD // 2, 1), pltpu.roll(v, HD // 2, 1)
        )
        return v * R["cosine"][at, :] - swapped * R["sine"][at, :]

    def head_rows(d):
        here = pl.ds(d * span, span)

        @pl.loop(0, n_rows)
        def _(r):
            at = pl.ds(pl.multiple_of((d * n_rows + r) * span, span), span)

            @pl.loop(0, heads // 2)
            def _(h):
                pair = R["raw_in"][at, pl.ds(pl.multiple_of(h * 2 * HD, 2 * HD), 2 * HD)].astype(F32)
                i = r * heads + 2 * h
                R["q_in"][i, here, :] = head(pair, R["gain_q"][...], at).astype(BF)
                R["q_in"][i + 1, here, :] = head(
                    pltpu.roll(pair, HD, 1), R["gain_q"][...], at
                ).astype(BF)

            pair = R["raw_in"][at, q_cols:].astype(F32)
            R["kv"][r, 0, here, :] = jnp.where(
                lane < HD, head(pair, R["gain_k"][...], at), pair
            ).astype(BF)

    def kv_copy(step, d):
        here = pl.ds(d * span, span)
        return remote_copy(
            R["kv"].at[:, :, here],
            R["kv_in"].at[step - 1, :, :, here],
            R["kv_send"].at[d, step - 1],
            R["kv_recv"].at[d, step - 1],
            seq=rank + 2 * step,
        )

    head_rows(0)
    for step in range(1, nodes):
        pl.when(node + step < nodes)(kv_copy(step, 0).start)

    def w_pairs(r):
        R["w_in"][r, :] = pair_of(
            R["wk"][r, :].astype(F32), R["wv"][r, :].astype(F32), side == 0
        ).astype(BF)

    strips(width, 256, w_pairs)
    leave(3).start()
    raw_copy.wait()
    head_rows(1)
    leave(0).start()
    leave(1).start()
    for step in range(1, nodes):
        pl.when(node + step < nodes)(kv_copy(step, 1).start)
    cot_copies = [
        remote_copy(
            R["cot"].at[block_rows(j)],
            R["cot_out"].at[j],
            R["cot_send"].at[j],
            R["cot_recv"].at[j],
            seq=across,
        )
        for j in range(0, tp, 2)
    ]
    for copy in cot_copies:
        copy.start()

    def attend(kv_at, diagonal):
        @pl.loop(0, n_q)
        def _(i):
            kv = kv_at(i // heads)
            scores = lax.dot_general(
                R["q_in"][i], kv, (((1,), (1,)), ((), ())), preferred_element_type=F32
            )
            weight = jnp.exp2(scores * (HD**-0.5 * 1.4426950408889634))
            if diagonal:
                q_at = lax.broadcasted_iota(jnp.int32, (wide, wide), 0)
                k_at = lax.broadcasted_iota(jnp.int32, (wide, wide), 1)
                q_at = jnp.where(q_at < span, q_at + span * side, q_at - span * side)
                k_at = jnp.where(k_at < span, k_at + span * side, k_at - span * side)
                weight = jnp.where(k_at <= q_at, weight, 0.0)
            sums = weight[:, :128]
            for c in range(128, wide, 128):
                sums = sums + weight[:, c : c + 128]
            values = jnp.dot(weight.astype(BF), kv, preferred_element_type=F32)
            if diagonal:
                R["weight_sum"][i] = sums
                R["acc"][i] = values
            else:
                R["weight_sum"][i] += sums
                R["acc"][i] += values

    attend(lambda r: R["kv"][r, 0], True)

    @pl.loop(1, nodes)
    def _(step):
        @pl.when(node >= step)
        def _():
            for d in range(2):
                kv_copy(step, d).wait_recv()
            attend(lambda r: R["kv_in"][step - 1, r, 0], False)

    att_copy = remote_copy(
        R["att"].at[1], R["att_in"], R["att_sem"].at[0], R["att_sem"].at[1], seq=across
    )

    def finish(d):
        at = pl.ds(d * span, span)

        @pl.loop(0, n_rows * (heads // 2))
        def _(n):
            r, h = n // (heads // 2), n % (heads // 2)
            out = []
            for k in range(2):
                i = r * heads + 2 * h + k
                total = jnp.sum(R["weight_sum"][i, at, :], axis=-1, keepdims=True)
                out.append(R["acc"][i, at, :] / total)
            both = jnp.where(lane < HD, pltpu.roll(out[0], HD, 1), out[1])
            rows = pl.ds(pl.multiple_of(r * span, span), span)
            R["att"][d, rows, pl.ds(pl.multiple_of(h * 2 * HD, 2 * HD), 2 * HD)] = both.astype(BF)

    finish(1)
    att_copy.start()
    half_rows = pl.multiple_of(t % 2 * (count // 2), count // 2)
    a_half = pl.ds(half_rows, count // 2)
    a_copy = remote_copy(
        R["a_in"].at[a_half],
        R["a_other"].at[a_half],
        R["a_sem"].at[0],
        R["a_sem"].at[1],
        seq=across,
    )
    finish(0)
    ones = jnp.ones((8, 2 * HD), F32)

    @pl.loop(0, n_q)
    def _(i):
        total = lax.dot_general(
            ones,
            R["weight_sum"][i],
            (((1,), (1,)), ((), ())),
            precision=lax.Precision.HIGHEST,
            preferred_element_type=F32,
        )
        R["log"][i] = jnp.log2(total)[0:1]

    @pl.loop(0, tp)
    def _(j):
        at = pl.ds(pl.multiple_of(j * share, share), share)
        R["att_rel"][at, 0:q_cols] = R["att"][0, block_rows(j), :]

    att_copy.wait()
    a_copy.start()

    @pl.loop(0, tp)
    def _(j):
        at = pl.ds(pl.multiple_of(j * share, share), share)
        R["att_rel"][at, q_cols:] = R["att_in"][block_rows(j), :]

    for k in (4, 5):
        load(k).wait()
    hold, temp, got, mine = R["hold"], R["temp"], R["got"], R["mine"]
    chunk = 512

    @pl.loop(0, width // chunk)
    def _(n):
        cols = pl.ds(pl.multiple_of(n * chunk, chunk), chunk)
        value = jnp.dot(
            R["att_rel"][...], R["wo"][:, cols], preferred_element_type=F32
        ).astype(BF)
        for j in range(tp):
            (temp if j % 2 else hold)[j // 2, :, cols] = value[j * share : (j + 1) * share]

    slot = 0
    for bit in range(top):
        keep = list(range(0, tp, 2 << bit))
        copies = []
        for k, j in enumerate(keep):
            src = temp.at[j // 2] if bit == 0 else hold.at[(j | 1 << bit) // 2]
            copies.append(
                remote_copy(
                    src,
                    got.at[slot + k],
                    R["sum_send"].at[slot + k],
                    R["sum_recv"].at[slot + k],
                    tp=flip(bit),
                )
            )
            copies[-1].start()
        for k, j in enumerate(keep):
            copies[k].wait()

            def add(r, k=k, j=j):
                hold[j // 2, r, :] = (
                    hold[j // 2, r, :].astype(F32) + got[slot + k, r, :].astype(F32)
                ).astype(BF)

            strips(share, 64, add)
        slot += len(keep)

    up = 1 << top
    cut = share // 2
    halves = [pl.ds(0, cut), pl.ds(cut, cut)]
    low, high = halves
    a_out = R["a_out"]
    last_copies = [
        remote_copy(
            hold.at[up // 2, rows],
            got.at[slot, rows],
            R["sum_send"].at[slot + n],
            R["sum_recv"].at[slot + n],
            tp=flip(top),
        )
        for n, rows in enumerate(halves)
    ]
    for copy in last_copies:
        copy.start()

    started = []

    def send(src, dst, k, **where):
        copy = remote_copy(src, dst, R["all_send"].at[k], R["all_recv"].at[k], **where)
        copy.start()
        started.append(copy)
        return copy

    by_side, by_top = [], []
    for n, rows in enumerate(halves):
        last_copies[n].wait()

        at = pl.ds(pl.multiple_of(t * share + n * cut, cut), cut)
        resid = (
            R["tok"][at, :].astype(F32)
            + hold[0, rows, :].astype(F32)
            + got[slot, rows, :].astype(F32)
        )
        R["resid"][rows, :] = resid
        inverse = lax.rsqrt(jnp.mean(resid * resid, axis=-1, keepdims=True) + EPS)
        mine[rows, :] = (resid * inverse * R["gain_two"][...]).astype(BF)
        by_side.append(send(mine.at[rows], a_out.at[1, 0, rows], 2 * n, seq=across))
        by_top.append(send(mine.at[rows], a_out.at[0, up, rows], 2 * n + 1, tp=flip(top)))
    put = pltpu.make_async_copy(mine, a_out.at[0, 0], R["own_sem"])
    put.start()
    k = 6
    for copy in cot_copies:
        copy.wait()
    cot_copies = []
    for j in range(0, tp, 2):
        cot_copies.append(
            remote_copy(
                R["cot_out"].at[j],
                R["cot_out"].at[j + 1],
                R["cot_send"].at[j + 1],
                R["cot_recv"].at[j + 1],
                tp=flip(0),
            )
        )
        cot_copies[-1].start()
    pending = {}
    for bit in reversed(range(top)):
        have = [j for j in range(tp) if j % (2 << bit) == 0]
        if bit == top - 1:
            pending[0, 0] = send(mine, a_out.at[0, 1 << bit], k, tp=flip(bit))
            k += 1
            by_side[0].wait_recv()
            far_low = send(a_out.at[1, 0, low], a_out.at[1, up, low], 4, tp=flip(top))
            by_side[1].wait_recv()
            pending[1, 0] = send(a_out.at[1, 0], a_out.at[1, 1 << bit], k, tp=flip(bit))
            k += 1
            by_top[0].wait_recv()
            by_top[1].wait_recv()
            far_high = send(a_out.at[0, up, high], a_out.at[1, up, high], 5, seq=across)
            pending[0, up] = send(a_out.at[0, up], a_out.at[0, up | 1 << bit], k, tp=flip(bit))
            k += 1
            far_low.wait_recv()
            far_high.wait_recv()
            pending[1, up] = send(a_out.at[1, up], a_out.at[1, up | 1 << bit], k, tp=flip(bit))
            k += 1
        else:
            for d in range(2):
                for j in have:
                    pending[d, j] = send(
                        a_out.at[d, j], a_out.at[d, j | 1 << bit], k, tp=flip(bit)
                    )
                    k += 1
        for copy in pending.values():
            copy.wait_recv()
        pending = {}
    a_copy.wait()
    a_next = remote_copy(
        R["a_other"].at[a_half],
        R["a_other"].at[a_half],
        R["a_sem"].at[2],
        R["a_sem"].at[3],
        tp=flip(0),
    )
    a_next.start()
    for copy in started:
        copy.wait_send()
    put.wait()
    for copy in count_copies + cot_copies:
        copy.wait()
    a_next.wait()
    for k in range(4):
        leave(k).wait()
    for step in range(1, nodes):
        for d in range(2):
            pl.when(node + step < nodes)(kv_copy(step, d).wait_send)


def attend(nodes, bits, ident, values):
    tp, seq = 1 << bits, 2 * nodes
    tokens, width = values["tokens"].shape
    share = tokens // tp
    q_all, k_all = values["w_query"].shape[1], values["w_key"].shape[1]
    heads = q_all // 2 // HD
    rows, wide = values["rows"], 2 * tokens // values["rows"]
    n_q = rows * heads
    cols = (heads + 2) * HD
    inputs = {k: v for k, v in values.items() if k != "rows"}
    inside = ("gain_one", "gain_two", "gain_q", "gain_k", "cosine", "sine", "count")
    vmem = pl.BlockSpec(memory_space=pltpu.VMEM)
    anywhere = pl.BlockSpec(memory_space=pl.ANY)
    dma = pltpu.SemaphoreType.DMA
    messages = 6 + 2 * (tp - 2)
    kv = (rows, 1, wide, 2 * HD)
    outs = [
        ((n_q, wide, 2 * HD), BF, anywhere),
        (kv, BF, vmem),
        ((2 * tokens, cols), BF, anywhere),
        ((tokens, width), BF, anywhere),
        ((2, tokens, heads * HD), BF, vmem),
        ((n_q, 1, wide), F32, vmem),
        ((seq,) + values["count"].shape, F32, vmem),
        ((tp, share, width), BF, anywhere),
        ((share, width), F32, vmem),
        ((2, tp, share, width), BF, anywhere),
        ((nodes - 1,) + kv, BF, vmem),
        ((tokens, width), BF, anywhere),
        ((width, 2 * HD), BF, anywhere),
    ]
    scratch = [
        ((tokens, width), BF),
        ((width, q_all), BF),
        ((width, k_all), BF),
        ((width, k_all), BF),
        ((q_all, width), BF),
        ((tokens, cols), BF),
        ((n_q, wide, 2 * HD), F32),
        ((n_q, wide, 128), F32),
        ((tokens, heads * HD), BF),
        ((tokens, q_all), BF),
        ((tp // 2, share, width), BF),
        ((tp // 2, share, width), BF),
        ((tp - 1, share, width), BF),
        ((share, width), BF),
        ((n_q, wide, 2 * HD), BF),
        ((2 * tokens, cols), BF),
        ((tokens, width), BF),
        ((width, 2 * HD), BF),
    ]
    sems = [(6,), (2,), (2, nodes - 1), (2, nodes - 1), (seq - 1,), (seq - 1,), (tp,), (tp,), (2,)]
    sems += [(tp,), (tp,), (messages,), (messages,), (), (4,), (4,)]
    return pl.pallas_call(
        functools.partial(attend_kernel, nodes, bits),
        out_shape=[jax.ShapeDtypeStruct(shape, kind) for shape, kind, _ in outs],
        in_specs=[vmem if k in inside else anywhere for k in inputs],
        out_specs=[place for _, _, place in outs],
        scratch_shapes=[pltpu.VMEM(shape, kind) for shape, kind in scratch]
        + [dma(s) for s in sems],
        compiler_params=pltpu.CompilerParams(
            collective_id=ident, has_side_effects=True, vmem_limit_bytes=56 << 20
        ),
        cost_estimate=pl.CostEstimate(
            flops=0, bytes_accessed=200 << 20, transcendentals=0
        ),
        name="attend",
    )(*inputs.values())


def backward_kernel(nodes, bits, *refs):
    names = (
        "a_two", "cot", "cot_far", "scale", "w_gate", "w_up", "w_down", "resid", "tokens_in", "gain_two",
        "gain_one", "gain_q", "gain_k", "w_out", "w_query", "w_kv", "a_one", "a_other", "q", "kv", "kv_in", "att",
        "log", "raw", "cosine", "sine", "gate_sum", "up_sum", "down_sum", "out_sum",
        "q_sum", "kv_sum", "out", "tokens", "gains", "two_in", "ffn_in", "one_in", "gate_part",
        "up_part", "down_part", "red", "own", "hold", "temp", "low", "a_in", "a_t", "w_rows",
        "q_in", "d_out", "d_q", "d_kv", "kv_all", "att_in", "d_att", "delta", "d_raw", "q_part",
        "kv_part", "out_part", "kv_back", "kv_far", "d_resid", "fresh", "gain_rows", "gain_box",
        "gain_all", "log_in", "cot_in", "resid_in", "raw_in", "cos_in", "sin_in", "x_in", "hidden", "d_pair", "w_strip", "w_cols", "stage", "stage_down",
        "own_sem", "red_send", "red_recv", "fin_send", "fin_recv", "x_send", "x_recv", "put_sem",
        "load_sem", "sum_send", "sum_recv", "temp_sem", "low_send", "low_recv", "kv_send",
        "kv_recv", "tok_send", "tok_recv", "tok_put", "gain_send", "gain_recv", "w_sem",
        "stage_sem",
    )
    assert len(names) == len(refs)
    R = dict(zip(names, refs))
    tp, seq = 1 << bits, 2 * nodes
    top = bits - 1
    rank, t = lax.axis_index("seq"), lax.axis_index("tp")
    node, side = rank // 2, rank % 2
    across = rank + 1 - 2 * side
    last = nodes - 1
    me = rank * tp + t
    total = seq * tp
    share, width = R["resid"].shape
    n_q, wide, _ = R["q"].shape
    n_rows = R["kv"].shape[0]
    heads = n_q // n_rows
    span = wide // 2
    slots, prow, pcol = R["red"].shape[1:]
    half = R["red_send"].shape[1]
    ff = R["gate_part"].shape[1]
    chunks = ff // pcol
    tall = width // prow
    per_chunk = 3 * tall
    fed = chunks * per_chunk

    def strips(rows, step, body):
        @pl.loop(0, rows // step)
        def _(m):
            body(pl.ds(pl.multiple_of(m * step, step), step))

    def flip(bit):
        return t + (1 << bit) * (1 - 2 * ((t // (1 << bit)) % 2))

    def block_of(j):
        other = t
        for bit in range(bits):
            there = (j // (1 << bit)) % 2
            other = other + there * (1 << bit) * (1 - 2 * ((t // (1 << bit)) % 2))
        return other

    def block_rows(j):
        return pl.ds(pl.multiple_of(block_of(j) * share, share), share)

    barrier = pltpu.get_barrier_semaphore()

    @pl.loop(1, total)
    def _(k):
        other = (me + k) % total
        pl.semaphore_signal(
            barrier, 1, device_id={"seq": other // tp, "tp": other % tp}, device_id_type=MESH
        )

    pl.semaphore_wait(barrier, total - 1)

    red, own = R["red"], R["own"]
    own_sem, put_sem = R["own_sem"], R["put_sem"]
    red_sems = R["red_send"], R["red_recv"]
    fin_sems = R["fin_send"], R["fin_recv"]
    x_sems = R["x_send"], R["x_recv"]

    def with_piece(b, j, act):
        p = 2 * j + b
        chunk, k, kind = p // per_chunk, p % tall, (p % per_chunk) // tall
        along_chunk = pl.multiple_of(chunk * pcol, pcol)
        along_side = pl.multiple_of(side * ff + chunk * pcol, pcol)
        along_width = pl.ds(pl.multiple_of(k * prow, prow), prow)
        for i, name in enumerate(("gate", "up", "down")):

            @pl.when((p < fed) & (kind == i))
            def _(name=name):
                part, whole = R[name + "_part"], R[name + "_sum"]
                if name == "down":
                    act(
                        part.at[pl.ds(along_chunk, prow), along_width],
                        whole.at[pl.ds(along_side, prow), along_width],
                    )
                else:
                    act(
                        part.at[along_width, pl.ds(along_chunk, pcol)],
                        whole.at[along_width, pl.ds(along_side, pcol)],
                    )

        base = fed
        for name in ("out", "q", "kv"):
            part, whole = R[name + "_part"], R[name + "_sum"]
            size = part.shape[1] // pcol

            @pl.when((p >= base) & (p < base + size))
            def _(part=part, whole=whole, base=base, name=name):
                col = pl.ds(pl.multiple_of((p - base) * pcol, pcol), pcol)
                row = 0 if name == "q" else side * prow
                act(part.at[:, col], whole.at[pl.ds(pl.multiple_of(row, prow), prow), col])

            base += size

    def along(src, dst, sems, b, j, target):
        return remote_copy(src, dst, sems[0].at[b, j], sems[1].at[b, j], seq=target)

    def placed(j):
        if gap == 0:
            return j, (j >= 0) & (j < half)
        after = j >= late + gap
        return jnp.where(after, j - gap, j), ((j >= 0) & (j < late)) | (
            after & (j < half + gap)
        )

    def crosses(j):
        return (j < late) | (j >= late_end)

    def stream(b, i):
        v = node if b == 0 else last - node
        ahead = rank + 2 if b == 0 else rank - 2
        behind = rank - 2 if b == 0 else rank + 2
        f, there = placed(i - LAG * v + AHEAD - 1)

        @pl.when((v > 0) & there)
        def _():
            with_piece(
                b,
                f,
                lambda src, dst: pltpu.make_async_copy(
                    src, own.at[b, f % AHEAD], own_sem.at[b, f % AHEAD]
                ).start(),
            )

        j, there = placed(i - LAG * v)

        @pl.when((v == 0) & there)
        def _():
            with_piece(
                b, j, lambda src, dst: along(src, red.at[b, j % slots], red_sems, b, j, ahead).start()
            )

        @pl.when((v > 0) & there)
        def _():
            mine = own.at[b, j % AHEAD]
            pltpu.make_async_copy(mine, mine, own_sem.at[b, j % AHEAD]).wait()
            along(red.at[b, j % slots], red.at[b, j % slots], red_sems, b, j, behind).wait_recv()
            at = j % slots

            def add(r):
                red[b, at, r] = (
                    red[b, at, r].astype(F32) + own[b, j % AHEAD, r].astype(F32)
                ).astype(BF)

            strips(prow, 64, add)

            @pl.when(v < last)
            def _():
                along(red.at[b, j % slots], red.at[b, j % slots], red_sems, b, j, ahead).start()

            @pl.when((v == last) & (j >= KEPT))
            def _():
                @pl.when(crosses(j - KEPT))
                def _():
                    along(red.at[b, 0], red.at[b, 0], x_sems, b, j - KEPT, across).wait_send()

                along(red.at[b, 0], red.at[b, 0], fin_sems, b, j - KEPT, behind).wait_send()
                pltpu.make_async_copy(red.at[b, 0], red.at[b, 0], put_sem.at[b, j - KEPT]).wait()

            @pl.when(v == last)
            def _():
                def act(src, dst):
                    along(red.at[b, j % slots], dst, fin_sems, b, j, behind).start()

                    @pl.when(crosses(j))
                    def _():
                        along(red.at[b, j % slots], dst, x_sems, b, j, across).start()

                    pltpu.make_async_copy(red.at[b, j % slots], dst, put_sem.at[b, j]).start()

                with_piece(b, j, act)

        g, there = placed(i - LAG * last - LAG * (last - v))

        @pl.when((v < last) & there)
        def _():
            along(red.at[b, 0], red.at[b, 0], fin_sems, b, g, ahead).wait_recv()

            @pl.when(v > 0)
            def _():
                along(red.at[b, 0], red.at[b, 0], red_sems, b, g, ahead).wait_send()

            def act(src, dst):
                @pl.when(v > 0)
                def _():
                    along(dst, dst, fin_sems, b, g, behind).start()

                @pl.when(crosses(g))
                def _():
                    along(dst, dst, x_sems, b, g, across).start()

            with_piece(b, g, act)

    hold, temp = R["hold"], R["temp"]
    boxes = [R["two_in"], R["ffn_in"], R["one_in"]]

    def held(ref, d, k):
        return ref.at[pl.ds((d * (tp // 2) + k) * share, share)]

    def messages(bit):
        base = sum(tp >> b for b in range(bit))
        keep = [(d, j) for d in range(2) for j in range(0, tp, 2 << bit)]
        return [(base + k, d, j) for k, (d, j) in enumerate(keep)]

    def sum_copy(n, m, src, **where):
        return remote_copy(
            src, boxes[n].at[m], R["sum_send"].at[n, m], R["sum_recv"].at[n, m], **where
        )

    def sum_start(n, bit):
        for m, d, j in messages(bit):
            src = held(temp, d, j // 2) if bit == 0 else held(hold, d, (j | 1 << bit) // 2)
            sum_copy(n, m, src, tp=flip(bit)).start()

    def sum_add(n, bit):
        for m, d, j in messages(bit):
            sum_copy(n, m, held(temp, d, j // 2), tp=flip(bit)).wait()
        loads = []
        for m, d, j in messages(bit):
            k = j // 2
            loads.append(
                pltpu.make_async_copy(boxes[n].at[m], held(temp, d, k), R["temp_sem"].at[d, k])
            )
            loads[-1].start()
        for copy, (m, d, j) in zip(loads, messages(bit)):
            copy.wait()
            base = (d * (tp // 2) + j // 2) * share

            def add(r, base=base):
                at = pl.ds(pl.multiple_of(base + r.start, ROWS_AT_ONCE), ROWS_AT_ONCE)
                hold[at, :] = (hold[at, :].astype(F32) + temp[at, :].astype(F32)).astype(BF)

            strips(share, ROWS_AT_ONCE, add)

    final = 2 * (tp - 1)

    def side_start(n):
        sum_copy(n, final, held(hold, 1, 0), seq=across).start()

    def side_finish(n):
        sum_copy(n, final, held(hold, 1, 0), seq=across).wait()
        load = pltpu.make_async_copy(boxes[n].at[final], held(temp, 0, 0), R["temp_sem"].at[0, 0])
        load.start()
        load.wait()

    def side_sum(r):
        return hold[r, :].astype(F32) + temp[r, :].astype(F32)

    ends = [R["out"], R["tokens"]]

    def token_copy(n, k, src, j, bit):
        return remote_copy(
            src,
            ends[n].at[block_of(j)],
            R["tok_send"].at[n, k],
            R["tok_recv"].at[n, k],
            tp=flip(bit),
        )

    def token_messages(bit):
        base = sum(tp >> (b + 1) for b in range(bit + 1, bits))
        return [(base + k, j) for k, j in enumerate(range(0, tp, 2 << bit))]

    def tokens_start(n, bit):
        for k, j in token_messages(bit):
            src = R["fresh"].at[n] if j == 0 else ends[n].at[block_of(j)]
            token_copy(n, k, src, j, bit).start()

    def tokens_wait(n, bit):
        for k, j in token_messages(bit):
            token_copy(n, k, R["fresh"].at[n], j, bit).wait()

    def tokens_put(n):
        return pltpu.make_async_copy(R["fresh"].at[n], ends[n].at[t], R["tok_put"].at[n])

    def block(d, j):
        return pl.ds((d * tp + j) * share, share)

    loads = [
        (R["w_out"].at[pl.ds(pl.multiple_of(side * heads * HD, heads * HD), heads * HD)], R["w_rows"]),
        (
            R["w_query"].at[:, pl.ds(pl.multiple_of(side * heads * HD, heads * HD), heads * HD)],
            R["a_t"].at[:, pl.ds(0, heads * HD)],
        ),
        (R["a_one"], R["a_in"].at[pl.ds(0, tp * share)]),
        (R["q"], R["q_in"]),
        (R["kv"], R["kv_all"].at[0]),
        (R["kv_in"], R["kv_all"].at[pl.ds(1, nodes - 1)]),
        (R["att"], R["att_in"]),
        (R["log"], R["log_in"]),
        (R["a_two"], R["low"]),
        (R["cot_far"], R["a_in"].at[pl.ds(tp * share, tp * share)]),
        (R["cot"].at[block_rows(0)], R["cot_in"]),
        (R["a_other"], R["a_in"].at[pl.ds(tp * share, tp * share)]),
        (R["w_kv"], R["a_t"].at[:, pl.ds(heads * HD, 2 * HD)]),
    ] + [(R["cot"].at[block_rows(j)], R["a_in"].at[block(0, j)]) for j in range(tp)]
    first_plain = len(loads)
    loads += [(R["resid"], R["resid_in"]), (R["raw"], R["raw_in"])]
    loads += [(R["cosine"], R["cos_in"]), (R["sine"], R["sin_in"])]
    loads += [(R["tokens_in"].at[block_rows(0)], R["x_in"])]
    plain = range(first_plain, len(loads))

    def load(k):
        return pltpu.make_async_copy(loads[k][0], loads[k][1], R["load_sem"].at[k])

    w_cols, w_sem = R["w_cols"], R["w_sem"]
    both = 2 * tp * share
    nt = (((1,), (1,)), ((), ()))
    tn = (((0,), (0,)), ((), ()))

    def chunk_loads(c):
        at = pl.multiple_of(side * ff + c * pcol, pcol)
        slot = c % 2
        down_at = pl.multiple_of(slot * pcol, pcol)
        return [
            pltpu.make_async_copy(
                R["w_gate"].at[:, pl.ds(at, pcol)], w_cols.at[slot, 0], w_sem.at[slot, 0]
            ),
            pltpu.make_async_copy(
                R["w_up"].at[:, pl.ds(at, pcol)], w_cols.at[slot, 1], w_sem.at[slot, 1]
            ),
            pltpu.make_async_copy(
                R["w_down"].at[pl.ds(at, pcol)],
                hold.at[pl.ds(down_at, pcol)],
                w_sem.at[slot, 2],
            ),
        ]

    def begin():
        load(8).start()
        for copy in chunk_loads(0):
            copy.start()
        early = (9, *range(13, 13 + tp))
        for k in early:
            load(k).start()
        load(8).wait()
        for k in early:
            load(k).wait()

        def body(r):
            R["a_in"][r, :] = (R["a_in"][r, :].astype(F32) * R["scale"][r, :]).astype(BF)

        strips(both, SCALE_ROWS, body)
        for copy in chunk_loads(1):
            copy.start()
        for k in (0, 3, 4, 5, 6, 7, 10, *plain):
            load(k).start()

    def chunk_ready(c):
        for copy in chunk_loads(c):
            copy.wait()

    def chunk_next(c):
        @pl.when(c + 2 < chunks)
        def _():
            for copy in chunk_loads(c + 2):
                copy.start()

    def chunk_forward(c, at):
        slot = c % 2
        cols = pl.ds(pl.multiple_of(c * pcol, pcol), pcol)
        w_rows = hold.at[pl.ds(pl.multiple_of(slot * pcol, pcol), pcol)]

        gate = jnp.dot(R["low"][at, :], w_cols[slot, 0], preferred_element_type=F32)
        up = jnp.dot(R["low"][at, :], w_cols[slot, 1], preferred_element_type=F32)
        d_hidden = lax.dot_general(R["a_in"][at, :], w_rows[...], nt, preferred_element_type=F32)
        sigma = 1.0 / (1.0 + jnp.exp(-gate))
        smooth = gate * sigma
        R["hidden"][at, cols] = (smooth * up).astype(BF)
        R["d_pair"][1, at, cols] = (d_hidden * smooth).astype(BF)
        R["d_pair"][0, at, cols] = (d_hidden * up * (sigma * (1.0 + gate - smooth))).astype(BF)

    def turn():
        def body(at):
            R["a_t"][:, at] = R["low"][at, :].T

        strips(both, 256, body)

    def stage_copies(c):
        at = pl.ds(pl.multiple_of(c * pcol, pcol), pcol)
        sem = R["stage_sem"]
        return [
            pltpu.make_async_copy(R["stage"].at[0], R["gate_part"].at[:, at], sem.at[0]),
            pltpu.make_async_copy(R["stage"].at[1], R["up_part"].at[:, at], sem.at[1]),
            pltpu.make_async_copy(R["stage_down"], R["down_part"].at[at], sem.at[2]),
        ]

    def chunk_gradients(c, low_k, high_k):
        cols = pl.ds(pl.multiple_of(c * pcol, pcol), pcol)

        @pl.loop(low_k, high_k)
        def _(k):
            def body(at):
                R["stage"][k, at, :] = jnp.dot(
                    R["a_t"][at, :], R["d_pair"][k, :, cols], preferred_element_type=F32
                ).astype(BF)

            strips(width, 1024, body)
            for n, copy in enumerate(stage_copies(c)[:2]):
                pl.when(k == n)(copy.start)

        for n, copy in enumerate(stage_copies(c)[:2]):
            pl.when((low_k <= n) & (high_k > n))(copy.wait)

    def chunk_down(c):
        cols = pl.ds(pl.multiple_of(c * pcol, pcol), pcol)

        def body(at):
            R["stage_down"][:, at] = lax.dot_general(
                R["hidden"][:, cols], R["a_in"][:, at], tn, preferred_element_type=F32
            ).astype(BF)

        strips(width, 1024, body)
        stage_copies(c)[2].start()

    def row_loads(n):
        rows = pl.ds(pl.multiple_of(n * pcol, pcol), pcol)
        cols = pl.ds(pl.multiple_of(side * ff, ff), ff)
        return [
            pltpu.make_async_copy(
                R[name].at[rows, cols], R["w_strip"].at[n % 2, k], w_sem.at[n % 2, k]
            )
            for k, name in enumerate(("w_gate", "w_up"))
        ]

    def down_loads(n):
        return [
            pltpu.make_async_copy(
                R["w_down"].at[
                    pl.ds(pl.multiple_of(side * ff, ff), ff),
                    pl.ds(pl.multiple_of(n * pcol, pcol), pcol),
                ],
                w_cols.at[n % 2, 0, pl.ds(0, ff)],
                w_sem.at[n % 2, 0],
            )
        ]

    def start_all(copies):
        for copy in copies:
            copy.start()

    def by_columns(low_n, high_n, loads, product):
        @pl.loop(low_n, high_n)
        def _(n):
            for copy in loads(n):
                copy.wait()
            cols = pl.ds(pl.multiple_of(n * pcol, pcol), pcol)

            @pl.loop(0, 2)
            def _(d):
                at = pl.ds(pl.multiple_of(d * tp * share, tp * share), tp * share)
                value = product(at, n % 2).astype(BF)
                for j in range(tp):
                    rows = pl.ds(
                        pl.multiple_of((d * (tp // 2) + j // 2) * share, share), share
                    )
                    (temp if j % 2 else hold)[rows, cols] = value[j * share : (j + 1) * share]

            @pl.when(n + 2 < width // pcol)
            def _():
                start_all(loads(n + 2))

    def second_part(low_n, high_n):
        def product(at, slot):
            value = lax.dot_general(
                R["d_pair"][0, at, :], R["w_strip"][slot, 0], nt, preferred_element_type=F32
            )
            return value + lax.dot_general(
                R["d_pair"][1, at, :], R["w_strip"][slot, 1], nt, preferred_element_type=F32
            )

        by_columns(low_n, high_n, row_loads, product)

    def ffn_part(low_n, high_n):
        def product(at, slot):
            return jnp.dot(
                R["hidden"][at, :], w_cols[slot, 0, 0:ff, :], preferred_element_type=F32
            )

        by_columns(low_n, high_n, down_loads, product)

    def normed(v):
        inverse = lax.rsqrt(jnp.mean(v * v, axis=-1, keepdims=True) + EPS)
        return v * inverse, inverse

    low = R["low"]

    def low_at(d, j):
        return low.at[block(d, j)]

    def low_copy(k, src, dst, **where):
        return remote_copy(src, dst, R["low_send"].at[k], R["low_recv"].at[k], **where)

    up = 1 << top
    low_side = low_copy(0, low_at(0, 0), low_at(1, 0), seq=across)
    low_top = low_copy(1, low_at(0, 0), low_at(0, up), tp=flip(top))
    low_far = low_copy(2, low_at(1, 0), low_at(1, up), tp=flip(top))

    def low_bit(bit):
        base = 3 + sum(tp >> b for b in range(bit + 1, top))
        return [
            low_copy(base + k, low_at(d, j), low_at(d, j | 1 << bit), tp=flip(bit))
            for k, (d, j) in enumerate(
                (d, j) for d in range(2) for j in range(0, tp, 2 << bit)
            )
        ]

    def second_norm():
        side_finish(0)
        for k in (10, *plain):
            load(k).wait()
        R["gain_rows"][...] = jnp.zeros_like(R["gain_rows"])

        def body(r):
            d_a = side_sum(r)
            n_two, inverse = normed(R["resid_in"][r, :])
            R["gain_rows"][1:2, :] += jnp.sum(d_a * n_two, axis=0, keepdims=True)
            e = d_a * R["gain_two"][...]
            d_resid = R["cot_in"][r, :].astype(F32) * R["scale"][r, :] + inverse * (
                e - n_two * jnp.mean(e * n_two, axis=-1, keepdims=True)
            )
            R["d_resid"][r, :] = d_resid
            low[r, :] = d_resid.astype(BF)

        strips(share, ROWS_AT_ONCE, body)
        low_side.start()
        low_top.start()

    lane = lax.broadcasted_iota(jnp.int32, (span, 2 * HD), 1)

    def attended_back():
        for k in (0, 6):
            load(k).wait()
        R["d_kv"][...] = jnp.zeros_like(R["d_kv"])
        R["d_q"][...] = jnp.zeros_like(R["d_q"])
        @pl.loop(0, 2)
        def _(d):
            value = lax.dot_general(
                low[pl.ds(pl.multiple_of(d * tp * share, tp * share), tp * share), :],
                R["w_rows"][...],
                nt,
                preferred_element_type=F32,
            ).astype(BF)
            for j in range(tp):
                at = pl.ds(pl.multiple_of((d * tp + block_of(j)) * share, share), share)
                R["d_att"][at, :] = value[j * share : (j + 1) * share]

        ones = jnp.ones((8, 2 * HD), F32)
        pairs = heads // 2

        @pl.loop(0, 2 * n_rows * pairs)
        def _(n):
            d, r, h = n // (n_rows * pairs), n // pairs % n_rows, n % pairs
            cols = pl.ds(pl.multiple_of(h * 2 * HD, 2 * HD), 2 * HD)
            rows = pl.ds(pl.multiple_of(r * span, span), span)
            at = pl.ds(pl.multiple_of(d * span, span), span)
            d_rows = pl.ds(pl.multiple_of((d * n_rows + r) * span, span), span)
            for k in range(2):
                grads = R["d_att"][d_rows, cols].astype(F32)
                values = R["att_in"][d, rows, cols].astype(F32)
                if k == 0:
                    grads = pltpu.roll(grads, HD, 1)
                    values = pltpu.roll(values, HD, 1)
                grads = jnp.where(lane < HD, 0.0, grads)
                i = r * heads + 2 * h + k
                R["d_out"][i, at, :] = grads.astype(BF)
                R["delta"][i, :, at] = lax.dot_general(
                    ones,
                    grads * values,
                    nt,
                    precision=lax.Precision.HIGHEST,
                    preferred_element_type=F32,
                )

    def put_folded(ref, c, value):
        rows, cols = value.shape
        at = pl.ds(pl.multiple_of(c // ref.shape[1] * rows, rows), rows)
        ref[at, pl.ds(pl.multiple_of(c % ref.shape[1], cols), cols)] = value.astype(BF)

    def out_gradient():
        chunk = width // 2

        @pl.loop(0, 2 * tp)
        def _(n):
            R["d_att"][pl.ds(pl.multiple_of(n * share, share), share), :] = R["att_in"][
                n // tp, block_rows(n % tp), :
            ]

        @pl.loop(0, width // chunk)
        def _(n):
            c = pl.multiple_of(n * chunk, chunk)
            value = lax.dot_general(
                R["d_att"][...], low[:, pl.ds(c, chunk)], tn, preferred_element_type=F32
            )
            put_folded(R["out_part"], c, value)

    def attention_block(piece, i, diagonal):
        r = i // heads
        kv = R["kv_all"][piece, r, 0]
        q, d_out = R["q_in"][i], R["d_out"][i]
        scores = lax.dot_general(kv, q, nt, preferred_element_type=F32)
        probs = jnp.exp2(scores * (HD**-0.5 * 1.4426950408889634) - R["log_in"][i])
        if diagonal:
            k_at = lax.broadcasted_iota(jnp.int32, (wide, wide), 0)
            q_at = lax.broadcasted_iota(jnp.int32, (wide, wide), 1)
            q_at = jnp.where(q_at < span, q_at + span * side, q_at - span * side)
            k_at = jnp.where(k_at < span, k_at + span * side, k_at - span * side)
            probs = jnp.where(k_at <= q_at, probs, 0.0)
        d_probs = lax.dot_general(kv, d_out, nt, preferred_element_type=F32)
        d_scores = (probs * (d_probs - R["delta"][i, 0:1, :])).astype(BF)
        R["d_kv"][piece, r] += jnp.dot(d_scores, q, preferred_element_type=F32) + jnp.dot(
            probs.astype(BF), d_out, preferred_element_type=F32
        ) * (HD**0.5)
        R["d_q"][i] += lax.dot_general(
            kv, d_scores, (((0,), (0,)), ((), ())), preferred_element_type=F32
        )

    def kv_copy(step):
        return remote_copy(
            R["kv_back"].at[step - 1],
            R["kv_far"].at[step - 1],
            R["kv_send"].at[step - 1],
            R["kv_recv"].at[step - 1],
            seq=rank - 2 * step,
        )

    def kv_send():
        for step in range(1, nodes):

            @pl.when(node >= step)
            def _():
                R["kv_back"][step - 1] = R["d_kv"][step].astype(BF)
                kv_copy(step).start()

    def kv_sum():
        for step in range(1, nodes):

            @pl.when(node + step < nodes)
            def _():
                kv_copy(step).wait_recv()
                R["d_kv"][0] += R["kv_far"][step - 1].astype(F32)

            @pl.when(node >= step)
            def _():
                kv_copy(step).wait_send()

    def head_back(grads, raw, gain, at):
        lanes = 2 * HD
        low_lane = lane < HD // 2
        raw = jnp.where(lane < HD, raw, 0.0)
        swapped = jnp.where(
            low_lane, pltpu.roll(grads, lanes - HD // 2, 1), pltpu.roll(grads, HD // 2, 1)
        )
        rotated = grads * R["cos_in"][at, :] + swapped * R["sin_in"][at, :]
        inverse = lax.rsqrt(jnp.sum(raw * raw, axis=-1, keepdims=True) * (1.0 / HD) + EPS_HEAD)
        n = raw * inverse
        e = rotated * gain
        back = inverse * (e - n * (jnp.sum(e * n, axis=-1, keepdims=True) * (1.0 / HD)))
        return back, jnp.sum(rotated * n, axis=0, keepdims=True)

    def heads_back():
        scale = HD**-0.5
        pairs = heads // 2

        @pl.loop(0, 2 * n_rows)
        def _(n):
            r, d = n // 2, n % 2
            at = pl.ds(pl.multiple_of((d * n_rows + r) * span, span), span)
            here = pl.ds(pl.multiple_of(d * span, span), span)

            @pl.loop(0, pairs)
            def _(h):
                pair = []
                both_raw = R["raw_in"][at, pl.ds(pl.multiple_of(h * 2 * HD, 2 * HD), 2 * HD)].astype(F32)
                for k in range(2):
                    i = r * heads + 2 * h + k
                    grads = R["d_q"][i, :, here].T * scale
                    raw = both_raw if k == 0 else pltpu.roll(both_raw, HD, 1)
                    back, gain = head_back(grads, raw, R["gain_q"][...], at)
                    R["gain_rows"][2:3, 0 : 2 * HD] += gain
                    pair.append(back)
                R["d_raw"][at, pl.ds(pl.multiple_of(h * 2 * HD, 2 * HD), 2 * HD)] = jnp.where(
                    lane < HD, pair[0], pltpu.roll(pair[1], HD, 1)
                ).astype(BF)

            grads = R["d_kv"][0, r, here, :] * scale
            raw = R["raw_in"][at, heads * HD :].astype(F32)
            back, gain = head_back(grads, raw, R["gain_k"][...], at)
            R["gain_rows"][3:4, 0 : 2 * HD] += gain
            R["d_raw"][at, pl.ds(heads * HD, 2 * HD)] = jnp.where(lane < HD, back, grads).astype(
                BF
            )

    def raw_gradient():
        for k in (2, 11):
            load(k).wait()
        chunk = width // 2
        cut = heads * HD

        @pl.loop(0, width // chunk)
        def _(n):
            c = pl.multiple_of(n * chunk, chunk)
            value = lax.dot_general(
                R["d_raw"][...], R["a_in"][:, pl.ds(c, chunk)], tn, preferred_element_type=F32
            )
            put_folded(R["q_part"], c, value[:cut])
            put_folded(R["kv_part"], c, value[cut:])

    def first_part(low_n, high_n):
        inner = (heads + 2) * HD
        rel = R["hidden"]
        chunk = 512

        if low_n == 0:
            load(1).wait()
            load(12).wait()

            @pl.loop(0, 2 * tp)
            def _(n):
                rows = pl.multiple_of((n // tp * tp + block_of(n % tp)) * share, share)
                rel[pl.ds(pl.multiple_of(n * share, share), share), 0:inner] = R["d_raw"][
                    pl.ds(rows, share), :
                ]

        @pl.loop(low_n, high_n)
        def _(n):
            cols = pl.ds(pl.multiple_of(n * chunk, chunk), chunk)

            @pl.loop(0, 2)
            def _(d):
                at = pl.ds(pl.multiple_of(d * tp * share, tp * share), tp * share)
                value = lax.dot_general(
                    rel[at, 0:inner], R["a_t"][cols, 0:inner], nt, preferred_element_type=F32
                ).astype(BF)
                for j in range(tp):
                    rows = pl.ds(
                        pl.multiple_of((d * (tp // 2) + j // 2) * share, share), share
                    )
                    (temp if j % 2 else hold)[rows, cols] = value[j * share : (j + 1) * share]

    def out_end():
        side_finish(1)

        def body(r):
            R["fresh"][0, r, :] = (R["resid_in"][r, :] + side_sum(r)).astype(BF)

        strips(share, ROWS_AT_ONCE, body)
        tokens_put(0).start()
        tokens_start(0, top)

    def first_norm():
        side_finish(2)

        def body(r):
            d_a = side_sum(r)
            n_one, inverse = normed(R["x_in"][r, :].astype(F32))
            R["gain_rows"][0:1, :] += jnp.sum(d_a * n_one, axis=0, keepdims=True)
            e = d_a * R["gain_one"][...]
            d_x = R["d_resid"][r, :] + inverse * (
                e - n_one * jnp.mean(e * n_one, axis=-1, keepdims=True)
            )
            R["fresh"][1, r, :] = d_x.astype(BF)

        strips(share, ROWS_AT_ONCE, body)
        tokens_put(1).start()
        tokens_start(1, top)
        part = width // tp
        for k in range(tp):
            R["gain_box"][k] = jnp.zeros((8, part), F32)
            R["gain_box"][k, 0:2, :] = R["gain_rows"][0:2, k * part : (k + 1) * part]
            R["gain_box"][k, 2:4, 0 : 2 * HD] = R["gain_rows"][2:4, 0 : 2 * HD]

        @pl.loop(1, total)
        def _(k):
            other = (me + k) % total
            remote_copy(
                R["gain_box"].at[other % tp],
                R["gain_all"].at[k],
                R["gain_send"].at[k],
                R["gain_recv"].at[k],
                seq=other // tp,
                tp=other % tp,
            ).start()

        R["gain_all"][0] = R["gain_box"][t]

    def gains_end():
        @pl.loop(1, total)
        def _(k):
            remote_copy(
                R["gain_box"].at[0],
                R["gain_all"].at[k],
                R["gain_send"].at[k],
                R["gain_recv"].at[k],
                seq=rank,
                tp=t,
            ).wait()

        R["gains"][...] = jnp.zeros_like(R["gains"])

        @pl.loop(0, total)
        def _(k):
            R["gains"][...] += R["gain_all"][k]

    tasks = {}

    def task(step, *acts):
        tasks.setdefault(step, []).extend(acts)
        return step

    def sums_tasks(n, step):
        for bit in range(bits):
            step += 2 if bit == 0 else 5
            following = (
                (lambda bit=bit: sum_start(n, bit + 1)) if bit < top else (lambda: side_start(n))
            )
            task(step, lambda bit=bit: sum_add(n, bit), following)
        return step + 5

    def token_tasks(n, step):
        for bit in reversed(range(bits)):
            step += 3
            task(step, lambda bit=bit: tokens_wait(n, bit))
            if bit:
                task(step, lambda bit=bit: tokens_start(n, bit - 1))
        task(step, lambda: tokens_put(n).wait())
        return step

    n_rows_w = width // pcol
    first_move = 1
    halves = 2 * chunks - 1
    task(0, begin)
    step = halves
    task(step, lambda: start_all(row_loads(0)), lambda: start_all(row_loads(1)))
    for k in range(4):
        step = task(
            halves + k, lambda k=k: second_part(n_rows_w * k // 4, n_rows_w * (k + 1) // 4)
        )
    task(step, lambda: sum_start(0, 0))
    task(step, lambda: start_all(down_loads(0)), lambda: start_all(down_loads(1)))
    grads_at = step + 1
    grads_end = grads_at + 2 * (chunks - 1)
    assert grads_at + 1 < first_move + per_chunk // 2
    task(grads_end, load(1).start, load(2).start, load(11).start, load(12).start)
    step = task(sums_tasks(0, step), second_norm)
    task(max(step, grads_end) + 1, lambda: ffn_part(0, n_rows_w // 2))
    ffn_at = task(
        max(step, grads_end) + 2,
        lambda: ffn_part(n_rows_w // 2, n_rows_w),
        lambda: sum_start(1, 0),
    )
    step = task(step + 4, low_side.wait, low_top.wait, low_far.start)
    step += 3
    task(step, low_far.wait)
    for bit in reversed(range(top)):
        task(step, lambda bit=bit: [c.start() for c in low_bit(bit)])
        step += 2
        task(step, lambda bit=bit: [c.wait() for c in low_bit(bit)])
    task(step, attended_back)
    ffn_end = task(sums_tasks(1, ffn_at), out_end)
    token_tasks(0, ffn_end)
    step = task(step + 1, *[load(k).wait for k in (3, 4, 5, 7)])
    first_block = step
    per_step = 4
    step += -(-(nodes * n_q) // per_step)
    last_block = step
    task(step, kv_send)
    task(step + 2, out_gradient)
    step = task(step + 5, kv_sum, heads_back)
    step = task(step + 1, raw_gradient)
    raw_ready = step
    assert raw_ready > ffn_end
    task(step + 1, lambda: first_part(0, width // 1024))
    step = task(
        step + 2, lambda: first_part(width // 1024, width // 512), lambda: sum_start(2, 0)
    )
    step = task(sums_tasks(2, step), first_norm)
    task(token_tasks(1, step), gains_end)

    late = half - (R["q_part"].shape[1] + R["kv_part"].shape[1]) // pcol // 2
    late_end = late + R["q_part"].shape[1] // pcol // 2
    gap = max(0, raw_ready + 1 - late - first_move)
    steps = max(first_move + half + gap + 2 * LAG * last, max(tasks) + 1)

    @pl.loop(0, steps)
    def _(i):
        for b in range(2):
            stream(b, i - first_move)
        for at, acts in sorted(tasks.items()):

            @pl.when(i == at)
            def _(acts=acts):
                for act in acts:
                    act()

        @pl.when(i < halves)
        def _():
            c = (i + 1) // 2

            @pl.when((i == 0) | (i % 2 == 1))
            def _():
                chunk_ready(c)

            @pl.loop(jnp.where((i == 0) | (i % 2 == 1), 0, 1), jnp.where(i % 2 == 1, 1, 2))
            def _(m):
                chunk_forward(c, pl.ds(pl.multiple_of(m * (both // 2), both // 2), both // 2))

            @pl.when(i % 2 == 0)
            def _():
                chunk_next(c)

        pl.when(i == 0)(turn)
        g = i - grads_at
        c = jnp.where(i < 3, 0, g // 2 + 1)
        within = (g >= 0) & (i < grads_end)

        @pl.when((i < 2) | (within & (g % 2 == 0)))
        def _():
            chunk_gradients(c, jnp.where(i == 1, 1, 0), jnp.where(i == 0, 1, 2))

        @pl.when((i == 2) | (within & (g % 2 == 1)))
        def _():
            chunk_down(c)
            stage_copies(c)[2].wait()

        @pl.when((i >= first_block) & (i < last_block))
        def _():
            @pl.loop(0, per_step)
            def _(k):
                n = (i - first_block) * per_step + k
                piece = n // n_q

                @pl.when(n < n_q)
                def _():
                    attention_block(0, n, True)

                @pl.when((n >= n_q) & (n < n_q * nodes) & (node >= piece))
                def _():
                    attention_block(piece, n % n_q, False)

    @pl.loop(0, half)
    def _(j):
        for b in range(2):
            v = node if b == 0 else last - node
            probe = red.at[b, 0]

            @pl.when(v == 0)
            def _():
                along(probe, probe, red_sems, b, j, rank).wait_send()

            @pl.when((v > 0) & ((v < last) | (j >= half - KEPT)))
            def _():
                along(probe, probe, fin_sems, b, j, rank).wait_send()

            @pl.when((v == last) & (j >= half - KEPT))
            def _():
                pltpu.make_async_copy(probe, probe, put_sem.at[b, j]).wait()

            @pl.when(crosses(j) & ((v < last) | (j >= half - KEPT)))
            def _():
                along(probe, probe, x_sems, b, j, rank).wait_send()

            @pl.when(crosses(j))
            def _():
                along(probe, probe, x_sems, b, j, rank).wait_recv()


def backward(nodes, bits, ident, values):
    tp, seq = 1 << bits, 2 * nodes
    share, width = values["resid"].shape
    ff = values["w_gate"].shape[1] // 2
    n_q, wide, _ = values["q"].shape
    n_rows = values["kv"].shape[0]
    heads = n_q // n_rows
    tokens = tp * share
    piece = 256
    cols = (heads + 2) * HD
    small = [(piece, r * width // piece) for r in (heads * HD, heads * HD, 2 * HD)]
    shapes = [(width, 2 * ff), (width, 2 * ff), (2 * ff, width)]
    shapes += [(2 * small[0][0], small[0][1]), small[1], (2 * small[2][0], small[2][1])]
    half = (3 * width * ff + sum(r * c for r, c in small)) // (2 * piece * piece)
    slots = 2 * LAG * (nodes - 1) + 2
    vmem = pl.BlockSpec(memory_space=pltpu.VMEM)
    anywhere = pl.BlockSpec(memory_space=pl.ANY)
    dma = pltpu.SemaphoreType.DMA
    inside = ("scale", "gain_two", "gain_one", "gain_q", "gain_k")
    kv = values["kv"].shape
    total = seq * tp
    messages = 3 + 2 * (tp - 2)
    outs = shapes + [(tp, share, width)] * 2 + [(8, width // tp)]
    outs += [(2 * tp - 1, share, width)] * 3 + [(width, ff), (width, ff), (ff, width)]
    scratch = [
        (2, slots, piece, piece),
        (2, AHEAD, piece, piece),
        (tokens, width),
        (tokens, width),
        (2 * tokens, width),
        (2 * tokens, width),
        (width, 2 * tokens),
        (heads * HD, width),
        (n_q, wide, 2 * HD),
        (n_q, wide, 2 * HD),
        (n_q, 2 * HD, wide, F32),
        (nodes, n_rows, wide, 2 * HD, F32),
        (nodes,) + kv,
        (2, tokens, heads * HD),
        (2 * tokens, heads * HD),
        (n_q, 8, wide, F32),
        (2 * tokens, cols),
        small[1],
        small[2],
        small[0],
        (nodes - 1, n_rows, wide, 2 * HD),
        (nodes - 1, n_rows, wide, 2 * HD),
        (share, width, F32),
        (2, share, width),
        (8, width, F32),
        (tp, 8, width // tp, F32),
        (total, 8, width // tp, F32),
        (n_q, 1, wide, F32),
        (share, width),
        (share, width, F32),
        (2 * tokens, cols),
        (2 * tokens, 2 * HD, F32),
        (2 * tokens, 2 * HD, F32),
        (share, width),
        (2 * tokens, ff),
        (2, 2 * tokens, ff),
        (2, 2, piece, ff),
        (2, 2, width, piece),
        (2, width, piece),
        (piece, width),
    ]
    sems = [(2, AHEAD)] + [(2, half)] * 7 + [(18 + tp,), (3, 2 * tp - 1), (3, 2 * tp - 1)]
    sems += [(2, tp // 2), (messages,), (messages,), (nodes - 1,), (nodes - 1,)]
    sems += [(2, tp - 1), (2, tp - 1), (2,), (total,), (total,), (2, 3), (3,)]
    return pl.pallas_call(
        functools.partial(backward_kernel, nodes, bits),
        out_shape=[
            jax.ShapeDtypeStruct(shape, F32 if k == 8 else BF) for k, shape in enumerate(outs)
        ],
        in_specs=[vmem if k in inside else anywhere for k in values],
        out_specs=[vmem if k == 8 else anywhere for k in range(len(outs))],
        scratch_shapes=[
            pltpu.VMEM(s[:-1], F32) if s[-1] is F32 else pltpu.VMEM(s, BF) for s in scratch
        ]
        + [dma(s) for s in sems],
        compiler_params=pltpu.CompilerParams(
            collective_id=ident, has_side_effects=True, vmem_limit_bytes=62 << 20
        ),
        cost_estimate=pl.CostEstimate(
            flops=0, bytes_accessed=1 << 30, transcendentals=0
        ),
        name="backward",
    )(*values.values())[:9]


def widen(arrays):
    block = arrays[-1].shape[0]
    for array in arrays:
        block = min(block, array.shape[0])
    counts = [array.shape[0] // block for array in arrays]
    starts = [sum(counts[:k]) for k in range(len(arrays))]
    width = arrays[0].shape[1]

    def kernel(*refs):
        step = pl.program_id(0)
        for k, (start, size) in enumerate(zip(starts, counts)):

            @pl.when((step >= start) & (step < start + size))
            def _(k=k):
                refs[len(arrays) + k][...] = refs[k][...].astype(F32)

    specs = [
        pl.BlockSpec(
            (block, width), lambda i, start=start, size=size: (jnp.clip(i - start, 0, size - 1), 0)
        )
        for start, size in zip(starts, counts)
    ]
    return pl.pallas_call(
        kernel,
        grid=(sum(counts),),
        out_shape=[jax.ShapeDtypeStruct(a.shape, F32) for a in arrays],
        in_specs=specs,
        out_specs=specs,
        compiler_params=pltpu.CompilerParams(vmem_limit_bytes=56 << 20),
        cost_estimate=pl.CostEstimate(
            flops=0, bytes_accessed=6 * block * width * sum(counts), transcendentals=0
        ),
        name="widen",
    )(*arrays)


def turn_heads(mine, other, kv, q_cols, shared, width):
    side = (lax.axis_index("seq") % 2).reshape(1).astype(jnp.int32)
    chunk = 256

    def kernel(side_ref, mine_ref, other_ref, kv_ref, q_out, k_out, v_out):
        first = side_ref[0] == 0
        per = mine_ref.shape[1] // chunk
        lane = lax.broadcasted_iota(jnp.int32, (chunk, 2 * HD), 1)

        @pl.loop(0, width // chunk)
        def _(n):
            rows = pl.ds(pl.multiple_of(n * chunk, chunk), chunk)
            at = pl.ds(pl.multiple_of(n // per * q_cols, q_cols), q_cols)
            cols = pl.ds(pl.multiple_of(n % per * chunk, chunk), chunk)
            own = mine_ref[at, cols].astype(F32).T
            far = other_ref[at, cols].astype(F32).T
            q_out[rows, 0:q_cols] = jnp.where(first, own, far)
            q_out[rows, q_cols:] = jnp.where(first, far, own)

        height = 2 * HD
        per_kv = kv_ref.shape[1] // chunk
        stack = kv_ref.shape[0] // 2

        @pl.loop(0, width // chunk)
        def _(n):
            rows = pl.ds(pl.multiple_of(n * chunk, chunk), chunk)
            cols = pl.ds(pl.multiple_of(n % per_kv * chunk, chunk), chunk)
            pair = [
                kv_ref[
                    pl.ds(pl.multiple_of(s * stack + n // per_kv * height, height), height), cols
                ]
                .astype(F32)
                .T
                for s in range(2)
            ]
            if shared:
                both = pair[0] + pair[1]
                k_out[rows, :] = both[:, :HD]
                v_out[rows, :] = both[:, HD:]
            else:
                k_out[rows, :] = jnp.where(lane < HD, pair[0], pltpu.roll(pair[1], HD, 1))
                v_out[rows, :] = jnp.where(lane < HD, pltpu.roll(pair[0], HD, 1), pair[1])

    vmem = pl.BlockSpec(memory_space=pltpu.VMEM)
    k_cols = HD if shared else 2 * HD
    return pl.pallas_call(
        kernel,
        out_shape=[
            jax.ShapeDtypeStruct((width, c), F32) for c in (2 * q_cols, k_cols, k_cols)
        ],
        in_specs=[pl.BlockSpec(memory_space=pltpu.SMEM)] + [vmem] * 3,
        out_specs=[vmem] * 3,
        compiler_params=pltpu.CompilerParams(vmem_limit_bytes=40 << 20),
        name="turn_heads",
    )(side, mine, other, kv)


def per_device(
    tokens,
    positions,
    corpus,
    corpus_weight,
    gain_one,
    w_query,
    w_key,
    w_value,
    gain_query,
    gain_key,
    w_out,
    gain_two,
    w_gate,
    w_up,
    w_down,
    cotangent,
):
    net = Links()
    rows, per_row, width = tokens.shape
    count = rows * per_row
    share = count // net.tp
    total_len = per_row * net.seq
    side, node, t = net.side, net.node, net.t
    q_cols = w_query.shape[1] // 2
    shared = (w_key.shape[1] // HD) % 2 == 1
    k_cols = w_key.shape[1] if shared else w_key.shape[1] // 2
    both = 2 * count

    def lanes(v):
        return jnp.pad(v, [(0, 0)] * (v.ndim - 1) + [(0, 2 * HD - v.shape[-1])])

    pos_own = positions.reshape(count)
    corpus_own = corpus.reshape(count)
    told = net.swap_side(jnp.stack([pos_own, corpus_own]))
    cosine, sine = rope_tables(jnp.concatenate([pos_own, told[0]]))
    cosine = lanes(jnp.concatenate([cosine, cosine], axis=1))
    sine = lanes(jnp.concatenate([sine, -sine], axis=1))
    onehot = (corpus_own[:, None] == jnp.arange(NCORP, dtype=jnp.int32)).astype(F32)
    own_counts = jnp.zeros((8, 128), F32).at[0, :NCORP].set(jnp.sum(onehot, axis=0))
    token_rows = tokens.reshape(count, width)
    cot_rows = cotangent.reshape(count, width)
    head_gains = lanes(jnp.stack([gain_query, gain_key]))
    gain_q, gain_k = head_gains[0:1], head_gains[1:2]

    assert k_cols == HD

    q, kv, raw, a_one, att, log, all_counts, cot_other, resid, a_two, kv_in, a_other, w_kv = attend(
        net.nodes,
        net.bits,
        2,
        dict(
            tokens=token_rows,
            w_query=w_query,
            w_key=w_key,
            w_value=w_value,
            w_out=w_out,
            cot=cot_rows,
            gain_one=gain_one[None],
            gain_two=gain_two[None],
            gain_q=gain_q,
            gain_k=gain_k,
            cosine=cosine,
            sine=sine,
            count=own_counts,
            rows=rows,
        ),
    )
    a_two = a_two.reshape(both, width)

    counts = jnp.sum(all_counts, axis=0)[0, :NCORP]
    weight_scale = corpus_weight.astype(F32) * (rows * total_len / NCORP) / counts
    corpus_other = told[1]
    onehot_other = (corpus_other[:, None] == jnp.arange(NCORP, dtype=jnp.int32)).astype(F32)
    scale_own = jnp.sum(onehot * weight_scale, axis=-1, keepdims=True)
    scale_other = jnp.sum(onehot_other * weight_scale, axis=-1, keepdims=True)
    scale_both = jnp.concatenate([net.relative(scale_own), net.relative(scale_other)], axis=0)

    sums = backward(
        net.nodes,
        net.bits,
        3,
        dict(
            a_two=a_two,
            cot=cot_rows,
            cot_far=cot_other.reshape(count, width),
            scale=scale_both,
            w_gate=w_gate,
            w_up=w_up,
            w_down=w_down,
            resid=resid,
            tokens_in=token_rows,
            gain_two=gain_two[None],
            gain_one=gain_one[None],
            gain_q=gain_q,
            gain_k=gain_k,
            w_out=w_out,
            w_query=w_query,
            w_kv=w_kv,
            a_one=a_one,
            a_other=a_other,
            q=q,
            kv=kv,
            kv_in=kv_in,
            att=att,
            log=log,
            raw=raw,
            cosine=cosine,
            sine=sine,
        ),
    )
    q_other = net.swap_side(sums[4])
    fold = width // sums[3].shape[1]
    grad_out = sums[3].reshape(2, fold, q_cols, -1).transpose(0, 2, 1, 3).reshape(2 * q_cols, width)
    grad_gate, grad_up, grad_down, grad_out = widen([*sums[:3], grad_out])
    grad_query, grad_key, grad_value = turn_heads(
        sums[4], q_other, sums[5], q_cols, shared, width
    )
    out, d_tokens = (v.reshape(rows, per_row, width) for v in sums[6:8])
    gains = sums[8]

    head_share = HD // net.tp

    return (
        out,
        d_tokens,
        gains[0],
        grad_query,
        grad_key,
        grad_value,
        take(gains[2], t * head_share, head_share),
        take(gains[3], t * head_share, head_share),
        grad_out,
        gains[1],
        grad_gate,
        grad_up,
        grad_down,
    )


def solution(mesh):
    placed = (
        P(None, "seq", None),
        P(None, "seq"),
        P(None, "seq"),
        P(),
        P(),
        P(None, "tp"),
        P(None, "tp"),
        P(None, "tp"),
        P(),
        P(),
        P("tp", None),
        P(),
        P(None, "tp"),
        P(None, "tp"),
        P("tp", None),
        P(None, "seq", None),
    )
    return jax.shard_map(
        per_device,
        mesh=mesh,
        in_specs=placed,
        out_specs=(
            P(None, "seq", None),
            P(None, "seq", None),
            P("tp"),
            P(None, "tp"),
            P(None, "tp"),
            P(None, "tp"),
            P("tp"),
            P("tp"),
            P("tp", None),
            P("tp"),
            P(None, "tp"),
            P(None, "tp"),
            P("tp", None),
        ),
        check_vma=False,
    )
```

```python
import functools

import jax
import jax.numpy as jnp
from jax import lax
from jax.experimental import pallas as pl
from jax.experimental.pallas import tpu as pltpu
from jax.sharding import PartitionSpec as P

HD = 64
NCORP = 8


EPS = 1e-05
EPS_HEAD = 1e-06
ROPE_BASE = 10000.0
BF = jnp.bfloat16
F32 = jnp.float32
MESH = pl.DeviceIdType.MESH
LAG = 2
AHEAD = 3
KEPT = 15
ROWS_AT_ONCE = 64
SCALE_ROWS = 128


def rope_tables(positions):
    half = HD // 2
    rates = ROPE_BASE ** (-jnp.arange(half, dtype=jnp.float32) * 2.0 / HD)
    angle = positions.astype(jnp.float32)[:, None] * rates[None, :]
    return (jnp.cos(angle), jnp.sin(angle))


def rotate(vector, cosine, sine):
    half = vector.shape[-1] // 2
    first = vector[..., :half]
    second = vector[..., half:]
    return jnp.concatenate(
        [first * cosine - second * sine, second * cosine + first * sine], axis=-1
    )


def head_norm(vector, gain):
    inverse = lax.rsqrt(jnp.mean(vector * vector, axis=-1, keepdims=True) + EPS_HEAD)
    normed = vector * inverse
    return (normed, inverse, normed * gain)


def dot(a, b):
    return jnp.dot(a, b, preferred_element_type=F32)


def dot_tn(a, b):
    return lax.dot_general(a, b, (((0,), (0,)), ((), ())), preferred_element_type=F32)


def dot_nt(a, b):
    return lax.dot_general(a, b, (((1,), (1,)), ((), ())), preferred_element_type=F32)


def take(array, start, size, axis=0):
    return lax.dynamic_slice_in_dim(array, start, size, axis)


class Links:
    def __init__(self):
        self.seq = lax.axis_size("seq")
        self.tp = lax.axis_size("tp")
        self.nodes = self.seq // 2
        self.bits = self.tp.bit_length() - 1
        rank = lax.axis_index("seq")
        self.node = rank // 2
        self.side = rank % 2
        self.t = lax.axis_index("tp")

    def swap_side(self, value):
        return lax.ppermute(value, "seq", [(s, s ^ 1) for s in range(self.seq)])

    def swap_bit(self, value, bit):
        return lax.ppermute(value, "tp", [(r, r ^ (1 << bit)) for r in range(self.tp)])

    def relative(self, rows):
        share = rows.shape[0] // self.tp
        return jnp.concatenate(
            [take(rows, (self.t ^ j) * share, share) for j in range(self.tp)], axis=0
        )


def remote_copy(src, dst, send, recv, **where):
    return pltpu.make_async_remote_copy(
        src, dst, send, recv, device_id=where, device_id_type=MESH
    )


def attend_kernel(nodes, bits, *refs):
    names = (
        "tokens", "w_query", "w_key", "w_value", "w_out", "cot", "gain_one", "gain_two", "gain_q", "gain_k",
        "cosine", "sine", "count",
        "q", "kv", "raw", "a_one", "att", "log", "counts", "cot_out", "resid", "a_out", "kv_in", "a_other", "w_kv",
        "tok", "wq", "wk", "wv", "wo", "raw_other", "acc", "weight_sum", "att_in", "att_rel", "hold", "temp", "got",
        "mine", "q_in", "raw_in", "a_in", "w_in",
        "load_sem", "raw_sem", "kv_send", "kv_recv", "count_send", "count_recv", "cot_send", "cot_recv", "att_sem",
        "sum_send", "sum_recv", "all_send", "all_recv", "own_sem", "a_sem", "out_sem",
    )
    assert len(names) == len(refs)
    R = dict(zip(names, refs))
    tp, seq = 1 << bits, 2 * nodes
    top = bits - 1
    rank, t = lax.axis_index("seq"), lax.axis_index("tp")
    node, side = rank // 2, rank % 2
    across = rank + 1 - 2 * side
    n_q, wide, _ = R["q"].shape
    n_rows = R["kv"].shape[0]
    heads = n_q // n_rows
    q_cols = heads * HD
    span = wide // 2
    share, width = R["resid"].shape
    count = tp * share

    def strips(rows, step, body):
        @pl.loop(0, rows // step)
        def _(m):
            body(pl.ds(pl.multiple_of(m * step, step), step))

    def flip(bit):
        return t + (1 << bit) * (1 - 2 * ((t // (1 << bit)) % 2))

    def block_of(j):
        other = t
        for bit in range(bits):
            there = (j // (1 << bit)) % 2
            other = other + there * (1 << bit) * (1 - 2 * ((t // (1 << bit)) % 2))
        return other

    def block_rows(j):
        return pl.ds(pl.multiple_of(block_of(j) * share, share), share)

    half = R["w_out"].shape[0] // 2
    loads = [(R["tokens"], R["tok"]), (R["w_query"], R["wq"]), (R["w_key"], R["wk"])]
    loads += [(R["w_value"], R["wv"])]
    loads += [
        (
            R["w_out"].at[pl.ds(pl.multiple_of(at * half, half), half)],
            R["wo"].at[pl.ds(k * half, half)],
        )
        for k, at in enumerate((side, 1 - side))
    ]

    def load(k):
        return pltpu.make_async_copy(loads[k][0], loads[k][1], R["load_sem"].at[k])

    for k in range(6):
        load(k).start()

    leaving = [("q_in", "q"), ("raw_in", "raw"), ("a_in", "a_one"), ("w_in", "w_kv")]

    def leave(k):
        return pltpu.make_async_copy(R[leaving[k][0]], R[leaving[k][1]], R["out_sem"].at[k])

    barrier = pltpu.get_barrier_semaphore()
    for step in range(1, seq):
        pl.semaphore_signal(
            barrier, 1, device_id={"seq": (rank + step) % seq}, device_id_type=MESH
        )
    for bit in range(bits):
        pl.semaphore_signal(barrier, 1, device_id={"tp": flip(bit)}, device_id_type=MESH)

    load(0).wait()

    def first_norm(r):
        v = R["tok"][r, :].astype(F32)
        inverse = lax.rsqrt(jnp.mean(v * v, axis=-1, keepdims=True) + EPS)
        R["a_in"][r, :] = (v * inverse * R["gain_one"][...]).astype(BF)

    strips(count, 64, first_norm)
    leave(2).start()
    for k in (1, 2, 3):
        load(k).wait()

    def pair_of(k, v, first):
        if k.shape[1] == HD:
            return jnp.concatenate([k, v], axis=1)
        low = lax.broadcasted_iota(jnp.int32, k.shape, 1) < HD
        return jnp.where(
            low,
            jnp.where(first, k, pltpu.roll(k, HD, 1)),
            jnp.where(first, pltpu.roll(v, HD, 1), v),
        )

    def project(r):
        a = R["a_in"][r, :]
        k = jnp.dot(a, R["wk"][...], preferred_element_type=F32)
        v = jnp.dot(a, R["wv"][...], preferred_element_type=F32)
        R["raw_in"][r, q_cols:] = pair_of(k, v, side == 0).astype(BF)
        R["raw_other"][r, q_cols:] = pair_of(k, v, side == 1).astype(BF)

    strips(count, 256, project)

    def queries(ref, half):
        cols = pl.ds(pl.multiple_of(half * q_cols, q_cols), q_cols)

        def body(r):
            ref[r, 0:q_cols] = jnp.dot(
                R["a_in"][r, :], R["wq"][:, cols], preferred_element_type=F32
            ).astype(BF)

        strips(count, 256, body)

    queries(R["raw_other"], 1 - side)
    pl.semaphore_wait(barrier, seq - 1 + bits)
    raw_copy = remote_copy(
        R["raw_other"],
        R["raw_in"].at[pl.ds(count, count)],
        R["raw_sem"].at[0],
        R["raw_sem"].at[1],
        seq=across,
    )
    raw_copy.start()
    queries(R["raw_in"], side)
    R["counts"][0] = R["count"][...]
    count_copies = [
        remote_copy(
            R["count"],
            R["counts"].at[step],
            R["count_send"].at[step - 1],
            R["count_recv"].at[step - 1],
            seq=(rank + step) % seq,
        )
        for step in range(1, seq)
    ]
    for copy in count_copies:
        copy.start()

    lane = lax.broadcasted_iota(jnp.int32, (span, 2 * HD), 1)

    def head(v, gain, at):
        v = jnp.where(lane < HD, v, 0.0)
        inverse = lax.rsqrt(jnp.sum(v * v, axis=-1, keepdims=True) * (1.0 / HD) + EPS_HEAD)
        v = v * inverse * gain
        swapped = jnp.where(
            lane < HD // 2, pltpu.roll(v, 2 * HD - HD // 2, 1), pltpu.roll(v, HD // 2, 1)
        )
        return v * R["cosine"][at, :] - swapped * R["sine"][at, :]

    def head_rows(d):
        here = pl.ds(d * span, span)

        @pl.loop(0, n_rows)
        def _(r):
            at = pl.ds(pl.multiple_of((d * n_rows + r) * span, span), span)

            @pl.loop(0, heads // 2)
            def _(h):
                pair = R["raw_in"][at, pl.ds(pl.multiple_of(h * 2 * HD, 2 * HD), 2 * HD)].astype(F32)
                i = r * heads + 2 * h
                R["q_in"][i, here, :] = head(pair, R["gain_q"][...], at).astype(BF)
                R["q_in"][i + 1, here, :] = head(
                    pltpu.roll(pair, HD, 1), R["gain_q"][...], at
                ).astype(BF)

            pair = R["raw_in"][at, q_cols:].astype(F32)
            R["kv"][r, 0, here, :] = jnp.where(
                lane < HD, head(pair, R["gain_k"][...], at), pair
            ).astype(BF)

    def kv_copy(step, d):
        here = pl.ds(d * span, span)
        return remote_copy(
            R["kv"].at[:, :, here],
            R["kv_in"].at[step - 1, :, :, here],
            R["kv_send"].at[d, step - 1],
            R["kv_recv"].at[d, step - 1],
            seq=rank + 2 * step,
        )

    head_rows(0)
    for step in range(1, nodes):
        pl.when(node + step < nodes)(kv_copy(step, 0).start)

    def w_pairs(r):
        R["w_in"][r, :] = pair_of(
            R["wk"][r, :].astype(F32), R["wv"][r, :].astype(F32), side == 0
        ).astype(BF)

    strips(width, 256, w_pairs)
    leave(3).start()
    raw_copy.wait()
    head_rows(1)
    leave(0).start()
    leave(1).start()
    for step in range(1, nodes):
        pl.when(node + step < nodes)(kv_copy(step, 1).start)
    cot_copies = [
        remote_copy(
            R["cot"].at[block_rows(j)],
            R["cot_out"].at[j],
            R["cot_send"].at[j],
            R["cot_recv"].at[j],
            seq=across,
        )
        for j in range(0, tp, 2)
    ]
    for copy in cot_copies:
        copy.start()

    def attend(kv_at, diagonal):
        @pl.loop(0, n_q)
        def _(i):
            kv = kv_at(i // heads)
            scores = lax.dot_general(
                R["q_in"][i], kv, (((1,), (1,)), ((), ())), preferred_element_type=F32
            )
            weight = jnp.exp2(scores * (HD**-0.5 * 1.4426950408889634))
            if diagonal:
                q_at = lax.broadcasted_iota(jnp.int32, (wide, wide), 0)
                k_at = lax.broadcasted_iota(jnp.int32, (wide, wide), 1)
                q_at = jnp.where(q_at < span, q_at + span * side, q_at - span * side)
                k_at = jnp.where(k_at < span, k_at + span * side, k_at - span * side)
                weight = jnp.where(k_at <= q_at, weight, 0.0)
            sums = weight[:, :128]
            for c in range(128, wide, 128):
                sums = sums + weight[:, c : c + 128]
            values = jnp.dot(weight.astype(BF), kv, preferred_element_type=F32)
            if diagonal:
                R["weight_sum"][i] = sums
                R["acc"][i] = values
            else:
                R["weight_sum"][i] += sums
                R["acc"][i] += values

    attend(lambda r: R["kv"][r, 0], True)

    @pl.loop(1, nodes)
    def _(step):
        @pl.when(node >= step)
        def _():
            for d in range(2):
                kv_copy(step, d).wait_recv()
            attend(lambda r: R["kv_in"][step - 1, r, 0], False)

    att_copy = remote_copy(
        R["att"].at[1], R["att_in"], R["att_sem"].at[0], R["att_sem"].at[1], seq=across
    )

    def finish(d):
        at = pl.ds(d * span, span)

        @pl.loop(0, n_rows * (heads // 2))
        def _(n):
            r, h = n // (heads // 2), n % (heads // 2)
            out = []
            for k in range(2):
                i = r * heads + 2 * h + k
                total = jnp.sum(R["weight_sum"][i, at, :], axis=-1, keepdims=True)
                out.append(R["acc"][i, at, :] / total)
            both = jnp.where(lane < HD, pltpu.roll(out[0], HD, 1), out[1])
            rows = pl.ds(pl.multiple_of(r * span, span), span)
            R["att"][d, rows, pl.ds(pl.multiple_of(h * 2 * HD, 2 * HD), 2 * HD)] = both.astype(BF)

    finish(1)
    att_copy.start()
    half_rows = pl.multiple_of(t % 2 * (count // 2), count // 2)
    a_half = pl.ds(half_rows, count // 2)
    a_copy = remote_copy(
        R["a_in"].at[a_half],
        R["a_other"].at[a_half],
        R["a_sem"].at[0],
        R["a_sem"].at[1],
        seq=across,
    )
    finish(0)
    ones = jnp.ones((8, 2 * HD), F32)

    @pl.loop(0, n_q)
    def _(i):
        total = lax.dot_general(
            ones,
            R["weight_sum"][i],
            (((1,), (1,)), ((), ())),
            precision=lax.Precision.HIGHEST,
            preferred_element_type=F32,
        )
        R["log"][i] = jnp.log2(total)[0:1]

    @pl.loop(0, tp)
    def _(j):
        at = pl.ds(pl.multiple_of(j * share, share), share)
        R["att_rel"][at, 0:q_cols] = R["att"][0, block_rows(j), :]

    att_copy.wait()
    a_copy.start()

    @pl.loop(0, tp)
    def _(j):
        at = pl.ds(pl.multiple_of(j * share, share), share)
        R["att_rel"][at, q_cols:] = R["att_in"][block_rows(j), :]

    for k in (4, 5):
        load(k).wait()
    hold, temp, got, mine = R["hold"], R["temp"], R["got"], R["mine"]
    chunk = 512

    @pl.loop(0, width // chunk)
    def _(n):
        cols = pl.ds(pl.multiple_of(n * chunk, chunk), chunk)
        value = jnp.dot(
            R["att_rel"][...], R["wo"][:, cols], preferred_element_type=F32
        ).astype(BF)
        for j in range(tp):
            (temp if j % 2 else hold)[j // 2, :, cols] = value[j * share : (j + 1) * share]

    slot = 0
    for bit in range(top):
        keep = list(range(0, tp, 2 << bit))
        copies = []
        for k, j in enumerate(keep):
            src = temp.at[j // 2] if bit == 0 else hold.at[(j | 1 << bit) // 2]
            copies.append(
                remote_copy(
                    src,
                    got.at[slot + k],
                    R["sum_send"].at[slot + k],
                    R["sum_recv"].at[slot + k],
                    tp=flip(bit),
                )
            )
            copies[-1].start()
        for k, j in enumerate(keep):
            copies[k].wait()

            def add(r, k=k, j=j):
                hold[j // 2, r, :] = (
                    hold[j // 2, r, :].astype(F32) + got[slot + k, r, :].astype(F32)
                ).astype(BF)

            strips(share, 64, add)
        slot += len(keep)

    up = 1 << top
    cut = share // 2
    halves = [pl.ds(0, cut), pl.ds(cut, cut)]
    low, high = halves
    a_out = R["a_out"]
    last_copies = [
        remote_copy(
            hold.at[up // 2, rows],
            got.at[slot, rows],
            R["sum_send"].at[slot + n],
            R["sum_recv"].at[slot + n],
            tp=flip(top),
        )
        for n, rows in enumerate(halves)
    ]
    for copy in last_copies:
        copy.start()

    started = []

    def send(src, dst, k, **where):
        copy = remote_copy(src, dst, R["all_send"].at[k], R["all_recv"].at[k], **where)
        copy.start()
        started.append(copy)
        return copy

    by_side, by_top = [], []
    for n, rows in enumerate(halves):
        last_copies[n].wait()

        at = pl.ds(pl.multiple_of(t * share + n * cut, cut), cut)
        resid = (
            R["tok"][at, :].astype(F32)
            + hold[0, rows, :].astype(F32)
            + got[slot, rows, :].astype(F32)
        )
        R["resid"][rows, :] = resid
        inverse = lax.rsqrt(jnp.mean(resid * resid, axis=-1, keepdims=True) + EPS)
        mine[rows, :] = (resid * inverse * R["gain_two"][...]).astype(BF)
        by_side.append(send(mine.at[rows], a_out.at[1, 0, rows], 2 * n, seq=across))
        by_top.append(send(mine.at[rows], a_out.at[0, up, rows], 2 * n + 1, tp=flip(top)))
    put = pltpu.make_async_copy(mine, a_out.at[0, 0], R["own_sem"])
    put.start()
    k = 6
    for copy in cot_copies:
        copy.wait()
    cot_copies = []
    for j in range(0, tp, 2):
        cot_copies.append(
            remote_copy(
                R["cot_out"].at[j],
                R["cot_out"].at[j + 1],
                R["cot_send"].at[j + 1],
                R["cot_recv"].at[j + 1],
                tp=flip(0),
            )
        )
        cot_copies[-1].start()
    pending = {}
    for bit in reversed(range(top)):
        have = [j for j in range(tp) if j % (2 << bit) == 0]
        if bit == top - 1:
            pending[0, 0] = send(mine, a_out.at[0, 1 << bit], k, tp=flip(bit))
            k += 1
            by_side[0].wait_recv()
            far_low = send(a_out.at[1, 0, low], a_out.at[1, up, low], 4, tp=flip(top))
            by_side[1].wait_recv()
            pending[1, 0] = send(a_out.at[1, 0], a_out.at[1, 1 << bit], k, tp=flip(bit))
            k += 1
            by_top[0].wait_recv()
            by_top[1].wait_recv()
            far_high = send(a_out.at[0, up, high], a_out.at[1, up, high], 5, seq=across)
            pending[0, up] = send(a_out.at[0, up], a_out.at[0, up | 1 << bit], k, tp=flip(bit))
            k += 1
            far_low.wait_recv()
            far_high.wait_recv()
            pending[1, up] = send(a_out.at[1, up], a_out.at[1, up | 1 << bit], k, tp=flip(bit))
            k += 1
        else:
            for d in range(2):
                for j in have:
                    pending[d, j] = send(
                        a_out.at[d, j], a_out.at[d, j | 1 << bit], k, tp=flip(bit)
                    )
                    k += 1
        for copy in pending.values():
            copy.wait_recv()
        pending = {}
    a_copy.wait()
    a_next = remote_copy(
        R["a_other"].at[a_half],
        R["a_other"].at[a_half],
        R["a_sem"].at[2],
        R["a_sem"].at[3],
        tp=flip(0),
    )
    a_next.start()
    for copy in started:
        copy.wait_send()
    put.wait()
    for copy in count_copies + cot_copies:
        copy.wait()
    a_next.wait()
    for k in range(4):
        leave(k).wait()
    for step in range(1, nodes):
        for d in range(2):
            pl.when(node + step < nodes)(kv_copy(step, d).wait_send)


def attend(nodes, bits, ident, values):
    tp, seq = 1 << bits, 2 * nodes
    tokens, width = values["tokens"].shape
    share = tokens // tp
    q_all, k_all = values["w_query"].shape[1], values["w_key"].shape[1]
    heads = q_all // 2 // HD
    rows, wide = values["rows"], 2 * tokens // values["rows"]
    n_q = rows * heads
    cols = (heads + 2) * HD
    inputs = {k: v for k, v in values.items() if k != "rows"}
    inside = ("gain_one", "gain_two", "gain_q", "gain_k", "cosine", "sine", "count")
    vmem = pl.BlockSpec(memory_space=pltpu.VMEM)
    anywhere = pl.BlockSpec(memory_space=pl.ANY)
    dma = pltpu.SemaphoreType.DMA
    messages = 6 + 2 * (tp - 2)
    kv = (rows, 1, wide, 2 * HD)
    outs = [
        ((n_q, wide, 2 * HD), BF, anywhere),
        (kv, BF, vmem),
        ((2 * tokens, cols), BF, anywhere),
        ((tokens, width), BF, anywhere),
        ((2, tokens, heads * HD), BF, vmem),
        ((n_q, 1, wide), F32, vmem),
        ((seq,) + values["count"].shape, F32, vmem),
        ((tp, share, width), BF, anywhere),
        ((share, width), F32, vmem),
        ((2, tp, share, width), BF, anywhere),
        ((nodes - 1,) + kv, BF, vmem),
        ((tokens, width), BF, anywhere),
        ((width, 2 * HD), BF, anywhere),
    ]
    scratch = [
        ((tokens, width), BF),
        ((width, q_all), BF),
        ((width, k_all), BF),
        ((width, k_all), BF),
        ((q_all, width), BF),
        ((tokens, cols), BF),
        ((n_q, wide, 2 * HD), F32),
        ((n_q, wide, 128), F32),
        ((tokens, heads * HD), BF),
        ((tokens, q_all), BF),
        ((tp // 2, share, width), BF),
        ((tp // 2, share, width), BF),
        ((tp - 1, share, width), BF),
        ((share, width), BF),
        ((n_q, wide, 2 * HD), BF),
        ((2 * tokens, cols), BF),
        ((tokens, width), BF),
        ((width, 2 * HD), BF),
    ]
    sems = [(6,), (2,), (2, nodes - 1), (2, nodes - 1), (seq - 1,), (seq - 1,), (tp,), (tp,), (2,)]
    sems += [(tp,), (tp,), (messages,), (messages,), (), (4,), (4,)]
    return pl.pallas_call(
        functools.partial(attend_kernel, nodes, bits),
        out_shape=[jax.ShapeDtypeStruct(shape, kind) for shape, kind, _ in outs],
        in_specs=[vmem if k in inside else anywhere for k in inputs],
        out_specs=[place for _, _, place in outs],
        scratch_shapes=[pltpu.VMEM(shape, kind) for shape, kind in scratch]
        + [dma(s) for s in sems],
        compiler_params=pltpu.CompilerParams(
            collective_id=ident, has_side_effects=True, vmem_limit_bytes=56 << 20
        ),
        cost_estimate=pl.CostEstimate(
            flops=0, bytes_accessed=200 << 20, transcendentals=0
        ),
        name="attend",
    )(*inputs.values())


def backward_kernel(nodes, bits, *refs):
    names = (
        "a_two", "cot", "cot_far", "scale", "w_gate", "w_up", "w_down", "resid", "tokens_in", "gain_two",
        "gain_one", "gain_q", "gain_k", "w_out", "w_query", "w_kv", "a_one", "a_other", "q", "kv", "kv_in", "att",
        "log", "raw", "cosine", "sine", "gate_sum", "up_sum", "down_sum", "out_sum",
        "q_sum", "kv_sum", "out", "tokens", "gains", "two_in", "ffn_in", "one_in", "gate_part",
        "up_part", "down_part", "red", "own", "hold", "temp", "low", "a_in", "a_t", "w_rows",
        "q_in", "d_out", "d_q", "d_kv", "kv_all", "att_in", "d_att", "delta", "d_raw", "q_part",
        "kv_part", "out_part", "kv_back", "kv_far", "d_resid", "fresh", "gain_rows", "gain_box",
        "gain_all", "log_in", "cot_in", "resid_in", "raw_in", "cos_in", "sin_in", "x_in", "hidden", "d_pair", "w_strip", "w_cols", "stage", "stage_down",
        "own_sem", "red_send", "red_recv", "fin_send", "fin_recv", "x_send", "x_recv", "put_sem",
        "load_sem", "sum_send", "sum_recv", "temp_sem", "low_send", "low_recv", "kv_send",
        "kv_recv", "tok_send", "tok_recv", "tok_put", "gain_send", "gain_recv", "w_sem",
        "stage_sem",
    )
    assert len(names) == len(refs)
    R = dict(zip(names, refs))
    tp, seq = 1 << bits, 2 * nodes
    top = bits - 1
    rank, t = lax.axis_index("seq"), lax.axis_index("tp")
    node, side = rank // 2, rank % 2
    across = rank + 1 - 2 * side
    last = nodes - 1
    me = rank * tp + t
    total = seq * tp
    share, width = R["resid"].shape
    n_q, wide, _ = R["q"].shape
    n_rows = R["kv"].shape[0]
    heads = n_q // n_rows
    span = wide // 2
    slots, prow, pcol = R["red"].shape[1:]
    half = R["red_send"].shape[1]
    ff = R["gate_part"].shape[1]
    chunks = ff // pcol
    tall = width // prow
    per_chunk = 3 * tall
    fed = chunks * per_chunk

    def strips(rows, step, body):
        @pl.loop(0, rows // step)
        def _(m):
            body(pl.ds(pl.multiple_of(m * step, step), step))

    def flip(bit):
        return t + (1 << bit) * (1 - 2 * ((t // (1 << bit)) % 2))

    def block_of(j):
        other = t
        for bit in range(bits):
            there = (j // (1 << bit)) % 2
            other = other + there * (1 << bit) * (1 - 2 * ((t // (1 << bit)) % 2))
        return other

    def block_rows(j):
        return pl.ds(pl.multiple_of(block_of(j) * share, share), share)

    barrier = pltpu.get_barrier_semaphore()

    @pl.loop(1, total)
    def _(k):
        other = (me + k) % total
        pl.semaphore_signal(
            barrier, 1, device_id={"seq": other // tp, "tp": other % tp}, device_id_type=MESH
        )

    pl.semaphore_wait(barrier, total - 1)

    red, own = R["red"], R["own"]
    own_sem, put_sem = R["own_sem"], R["put_sem"]
    red_sems = R["red_send"], R["red_recv"]
    fin_sems = R["fin_send"], R["fin_recv"]
    x_sems = R["x_send"], R["x_recv"]

    def with_piece(b, j, act):
        p = 2 * j + b
        chunk, k, kind = p // per_chunk, p % tall, (p % per_chunk) // tall
        along_chunk = pl.multiple_of(chunk * pcol, pcol)
        along_side = pl.multiple_of(side * ff + chunk * pcol, pcol)
        along_width = pl.ds(pl.multiple_of(k * prow, prow), prow)
        for i, name in enumerate(("gate", "up", "down")):

            @pl.when((p < fed) & (kind == i))
            def _(name=name):
                part, whole = R[name + "_part"], R[name + "_sum"]
                if name == "down":
                    act(
                        part.at[pl.ds(along_chunk, prow), along_width],
                        whole.at[pl.ds(along_side, prow), along_width],
                    )
                else:
                    act(
                        part.at[along_width, pl.ds(along_chunk, pcol)],
                        whole.at[along_width, pl.ds(along_side, pcol)],
                    )

        base = fed
        for name in ("out", "q", "kv"):
            part, whole = R[name + "_part"], R[name + "_sum"]
            size = part.shape[1] // pcol

            @pl.when((p >= base) & (p < base + size))
            def _(part=part, whole=whole, base=base, name=name):
                col = pl.ds(pl.multiple_of((p - base) * pcol, pcol), pcol)
                row = 0 if name == "q" else side * prow
                act(part.at[:, col], whole.at[pl.ds(pl.multiple_of(row, prow), prow), col])

            base += size

    def along(src, dst, sems, b, j, target):
        return remote_copy(src, dst, sems[0].at[b, j], sems[1].at[b, j], seq=target)

    def placed(j):
        if gap == 0:
            return j, (j >= 0) & (j < half)
        after = j >= late + gap
        return jnp.where(after, j - gap, j), ((j >= 0) & (j < late)) | (
            after & (j < half + gap)
        )

    def crosses(j):
        return (j < late) | (j >= late_end)

    def stream(b, i):
        v = node if b == 0 else last - node
        ahead = rank + 2 if b == 0 else rank - 2
        behind = rank - 2 if b == 0 else rank + 2
        f, there = placed(i - LAG * v + AHEAD - 1)

        @pl.when((v > 0) & there)
        def _():
            with_piece(
                b,
                f,
                lambda src, dst: pltpu.make_async_copy(
                    src, own.at[b, f % AHEAD], own_sem.at[b, f % AHEAD]
                ).start(),
            )

        j, there = placed(i - LAG * v)

        @pl.when((v == 0) & there)
        def _():
            with_piece(
                b, j, lambda src, dst: along(src, red.at[b, j % slots], red_sems, b, j, ahead).start()
            )

        @pl.when((v > 0) & there)
        def _():
            mine = own.at[b, j % AHEAD]
            pltpu.make_async_copy(mine, mine, own_sem.at[b, j % AHEAD]).wait()
            along(red.at[b, j % slots], red.at[b, j % slots], red_sems, b, j, behind).wait_recv()
            at = j % slots

            def add(r):
                red[b, at, r] = (
                    red[b, at, r].astype(F32) + own[b, j % AHEAD, r].astype(F32)
                ).astype(BF)

            strips(prow, 64, add)

            @pl.when(v < last)
            def _():
                along(red.at[b, j % slots], red.at[b, j % slots], red_sems, b, j, ahead).start()

            @pl.when((v == last) & (j >= KEPT))
            def _():
                @pl.when(crosses(j - KEPT))
                def _():
                    along(red.at[b, 0], red.at[b, 0], x_sems, b, j - KEPT, across).wait_send()

                along(red.at[b, 0], red.at[b, 0], fin_sems, b, j - KEPT, behind).wait_send()
                pltpu.make_async_copy(red.at[b, 0], red.at[b, 0], put_sem.at[b, j - KEPT]).wait()

            @pl.when(v == last)
            def _():
                def act(src, dst):
                    along(red.at[b, j % slots], dst, fin_sems, b, j, behind).start()

                    @pl.when(crosses(j))
                    def _():
                        along(red.at[b, j % slots], dst, x_sems, b, j, across).start()

                    pltpu.make_async_copy(red.at[b, j % slots], dst, put_sem.at[b, j]).start()

                with_piece(b, j, act)

        g, there = placed(i - LAG * last - LAG * (last - v))

        @pl.when((v < last) & there)
        def _():
            along(red.at[b, 0], red.at[b, 0], fin_sems, b, g, ahead).wait_recv()

            @pl.when(v > 0)
            def _():
                along(red.at[b, 0], red.at[b, 0], red_sems, b, g, ahead).wait_send()

            def act(src, dst):
                @pl.when(v > 0)
                def _():
                    along(dst, dst, fin_sems, b, g, behind).start()

                @pl.when(crosses(g))
                def _():
                    along(dst, dst, x_sems, b, g, across).start()

            with_piece(b, g, act)

    hold, temp = R["hold"], R["temp"]
    boxes = [R["two_in"], R["ffn_in"], R["one_in"]]

    def held(ref, d, k):
        return ref.at[pl.ds((d * (tp // 2) + k) * share, share)]

    def messages(bit):
        base = sum(tp >> b for b in range(bit))
        keep = [(d, j) for d in range(2) for j in range(0, tp, 2 << bit)]
        return [(base + k, d, j) for k, (d, j) in enumerate(keep)]

    def sum_copy(n, m, src, **where):
        return remote_copy(
            src, boxes[n].at[m], R["sum_send"].at[n, m], R["sum_recv"].at[n, m], **where
        )

    def sum_start(n, bit):
        for m, d, j in messages(bit):
            src = held(temp, d, j // 2) if bit == 0 else held(hold, d, (j | 1 << bit) // 2)
            sum_copy(n, m, src, tp=flip(bit)).start()

    def sum_add(n, bit):
        for m, d, j in messages(bit):
            sum_copy(n, m, held(temp, d, j // 2), tp=flip(bit)).wait()
        loads = []
        for m, d, j in messages(bit):
            k = j // 2
            loads.append(
                pltpu.make_async_copy(boxes[n].at[m], held(temp, d, k), R["temp_sem"].at[d, k])
            )
            loads[-1].start()
        for copy, (m, d, j) in zip(loads, messages(bit)):
            copy.wait()
            base = (d * (tp // 2) + j // 2) * share

            def add(r, base=base):
                at = pl.ds(pl.multiple_of(base + r.start, ROWS_AT_ONCE), ROWS_AT_ONCE)
                hold[at, :] = (hold[at, :].astype(F32) + temp[at, :].astype(F32)).astype(BF)

            strips(share, ROWS_AT_ONCE, add)

    final = 2 * (tp - 1)

    def side_start(n):
        sum_copy(n, final, held(hold, 1, 0), seq=across).start()

    def side_finish(n):
        sum_copy(n, final, held(hold, 1, 0), seq=across).wait()
        load = pltpu.make_async_copy(boxes[n].at[final], held(temp, 0, 0), R["temp_sem"].at[0, 0])
        load.start()
        load.wait()

    def side_sum(r):
        return hold[r, :].astype(F32) + temp[r, :].astype(F32)

    ends = [R["out"], R["tokens"]]

    def token_copy(n, k, src, j, bit):
        return remote_copy(
            src,
            ends[n].at[block_of(j)],
            R["tok_send"].at[n, k],
            R["tok_recv"].at[n, k],
            tp=flip(bit),
        )

    def token_messages(bit):
        base = sum(tp >> (b + 1) for b in range(bit + 1, bits))
        return [(base + k, j) for k, j in enumerate(range(0, tp, 2 << bit))]

    def tokens_start(n, bit):
        for k, j in token_messages(bit):
            src = R["fresh"].at[n] if j == 0 else ends[n].at[block_of(j)]
            token_copy(n, k, src, j, bit).start()

    def tokens_wait(n, bit):
        for k, j in token_messages(bit):
            token_copy(n, k, R["fresh"].at[n], j, bit).wait()

    def tokens_put(n):
        return pltpu.make_async_copy(R["fresh"].at[n], ends[n].at[t], R["tok_put"].at[n])

    def block(d, j):
        return pl.ds((d * tp + j) * share, share)

    loads = [
        (R["w_out"].at[pl.ds(pl.multiple_of(side * heads * HD, heads * HD), heads * HD)], R["w_rows"]),
        (
            R["w_query"].at[:, pl.ds(pl.multiple_of(side * heads * HD, heads * HD), heads * HD)],
            R["a_t"].at[:, pl.ds(0, heads * HD)],
        ),
        (R["a_one"], R["a_in"].at[pl.ds(0, tp * share)]),
        (R["q"], R["q_in"]),
        (R["kv"], R["kv_all"].at[0]),
        (R["kv_in"], R["kv_all"].at[pl.ds(1, nodes - 1)]),
        (R["att"], R["att_in"]),
        (R["log"], R["log_in"]),
        (R["a_two"], R["low"]),
        (R["cot_far"], R["a_in"].at[pl.ds(tp * share, tp * share)]),
        (R["cot"].at[block_rows(0)], R["cot_in"]),
        (R["a_other"], R["a_in"].at[pl.ds(tp * share, tp * share)]),
        (R["w_kv"], R["a_t"].at[:, pl.ds(heads * HD, 2 * HD)]),
    ] + [(R["cot"].at[block_rows(j)], R["a_in"].at[block(0, j)]) for j in range(tp)]
    first_plain = len(loads)
    loads += [(R["resid"], R["resid_in"]), (R["raw"], R["raw_in"])]
    loads += [(R["cosine"], R["cos_in"]), (R["sine"], R["sin_in"])]
    loads += [(R["tokens_in"].at[block_rows(0)], R["x_in"])]
    plain = range(first_plain, len(loads))

    def load(k):
        return pltpu.make_async_copy(loads[k][0], loads[k][1], R["load_sem"].at[k])

    w_cols, w_sem = R["w_cols"], R["w_sem"]
    both = 2 * tp * share
    nt = (((1,), (1,)), ((), ()))
    tn = (((0,), (0,)), ((), ()))

    def chunk_loads(c):
        at = pl.multiple_of(side * ff + c * pcol, pcol)
        slot = c % 2
        down_at = pl.multiple_of(slot * pcol, pcol)
        return [
            pltpu.make_async_copy(
                R["w_gate"].at[:, pl.ds(at, pcol)], w_cols.at[slot, 0], w_sem.at[slot, 0]
            ),
            pltpu.make_async_copy(
                R["w_up"].at[:, pl.ds(at, pcol)], w_cols.at[slot, 1], w_sem.at[slot, 1]
            ),
            pltpu.make_async_copy(
                R["w_down"].at[pl.ds(at, pcol)],
                hold.at[pl.ds(down_at, pcol)],
                w_sem.at[slot, 2],
            ),
        ]

    def begin():
        load(8).start()
        for copy in chunk_loads(0):
            copy.start()
        early = (9, *range(13, 13 + tp))
        for k in early:
            load(k).start()
        load(8).wait()
        for k in early:
            load(k).wait()

        def body(r):
            R["a_in"][r, :] = (R["a_in"][r, :].astype(F32) * R["scale"][r, :]).astype(BF)

        strips(both, SCALE_ROWS, body)
        for copy in chunk_loads(1):
            copy.start()
        for k in (0, 3, 4, 5, 6, 7, 10, *plain):
            load(k).start()

    def chunk_ready(c):
        for copy in chunk_loads(c):
            copy.wait()

    def chunk_next(c):
        @pl.when(c + 2 < chunks)
        def _():
            for copy in chunk_loads(c + 2):
                copy.start()

    def chunk_forward(c, at):
        slot = c % 2
        cols = pl.ds(pl.multiple_of(c * pcol, pcol), pcol)
        w_rows = hold.at[pl.ds(pl.multiple_of(slot * pcol, pcol), pcol)]

        gate = jnp.dot(R["low"][at, :], w_cols[slot, 0], preferred_element_type=F32)
        up = jnp.dot(R["low"][at, :], w_cols[slot, 1], preferred_element_type=F32)
        d_hidden = lax.dot_general(R["a_in"][at, :], w_rows[...], nt, preferred_element_type=F32)
        sigma = 1.0 / (1.0 + jnp.exp(-gate))
        smooth = gate * sigma
        R["hidden"][at, cols] = (smooth * up).astype(BF)
        R["d_pair"][1, at, cols] = (d_hidden * smooth).astype(BF)
        R["d_pair"][0, at, cols] = (d_hidden * up * (sigma * (1.0 + gate - smooth))).astype(BF)

    def turn():
        def body(at):
            R["a_t"][:, at] = R["low"][at, :].T

        strips(both, 256, body)

    def stage_copies(c):
        at = pl.ds(pl.multiple_of(c * pcol, pcol), pcol)
        sem = R["stage_sem"]
        return [
            pltpu.make_async_copy(R["stage"].at[0], R["gate_part"].at[:, at], sem.at[0]),
            pltpu.make_async_copy(R["stage"].at[1], R["up_part"].at[:, at], sem.at[1]),
            pltpu.make_async_copy(R["stage_down"], R["down_part"].at[at], sem.at[2]),
        ]

    def chunk_gradients(c, low_k, high_k):
        cols = pl.ds(pl.multiple_of(c * pcol, pcol), pcol)

        @pl.loop(low_k, high_k)
        def _(k):
            def body(at):
                R["stage"][k, at, :] = jnp.dot(
                    R["a_t"][at, :], R["d_pair"][k, :, cols], preferred_element_type=F32
                ).astype(BF)

            strips(width, 1024, body)
            for n, copy in enumerate(stage_copies(c)[:2]):
                pl.when(k == n)(copy.start)

        for n, copy in enumerate(stage_copies(c)[:2]):
            pl.when((low_k <= n) & (high_k > n))(copy.wait)

    def chunk_down(c):
        cols = pl.ds(pl.multiple_of(c * pcol, pcol), pcol)

        def body(at):
            R["stage_down"][:, at] = lax.dot_general(
                R["hidden"][:, cols], R["a_in"][:, at], tn, preferred_element_type=F32
            ).astype(BF)

        strips(width, 1024, body)
        stage_copies(c)[2].start()

    def row_loads(n):
        rows = pl.ds(pl.multiple_of(n * pcol, pcol), pcol)
        cols = pl.ds(pl.multiple_of(side * ff, ff), ff)
        return [
            pltpu.make_async_copy(
                R[name].at[rows, cols], R["w_strip"].at[n % 2, k], w_sem.at[n % 2, k]
            )
            for k, name in enumerate(("w_gate", "w_up"))
        ]

    def down_loads(n):
        return [
            pltpu.make_async_copy(
                R["w_down"].at[
                    pl.ds(pl.multiple_of(side * ff, ff), ff),
                    pl.ds(pl.multiple_of(n * pcol, pcol), pcol),
                ],
                w_cols.at[n % 2, 0, pl.ds(0, ff)],
                w_sem.at[n % 2, 0],
            )
        ]

    def start_all(copies):
        for copy in copies:
            copy.start()

    def by_columns(low_n, high_n, loads, product):
        @pl.loop(low_n, high_n)
        def _(n):
            for copy in loads(n):
                copy.wait()
            cols = pl.ds(pl.multiple_of(n * pcol, pcol), pcol)

            @pl.loop(0, 2)
            def _(d):
                at = pl.ds(pl.multiple_of(d * tp * share, tp * share), tp * share)
                value = product(at, n % 2).astype(BF)
                for j in range(tp):
                    rows = pl.ds(
                        pl.multiple_of((d * (tp // 2) + j // 2) * share, share), share
                    )
                    (temp if j % 2 else hold)[rows, cols] = value[j * share : (j + 1) * share]

            @pl.when(n + 2 < width // pcol)
            def _():
                start_all(loads(n + 2))

    def second_part(low_n, high_n):
        def product(at, slot):
            value = lax.dot_general(
                R["d_pair"][0, at, :], R["w_strip"][slot, 0], nt, preferred_element_type=F32
            )
            return value + lax.dot_general(
                R["d_pair"][1, at, :], R["w_strip"][slot, 1], nt, preferred_element_type=F32
            )

        by_columns(low_n, high_n, row_loads, product)

    def ffn_part(low_n, high_n):
        def product(at, slot):
            return jnp.dot(
                R["hidden"][at, :], w_cols[slot, 0, 0:ff, :], preferred_element_type=F32
            )

        by_columns(low_n, high_n, down_loads, product)

    def normed(v):
        inverse = lax.rsqrt(jnp.mean(v * v, axis=-1, keepdims=True) + EPS)
        return v * inverse, inverse

    low = R["low"]

    def low_at(d, j):
        return low.at[block(d, j)]

    def low_copy(k, src, dst, **where):
        return remote_copy(src, dst, R["low_send"].at[k], R["low_recv"].at[k], **where)

    up = 1 << top
    low_side = low_copy(0, low_at(0, 0), low_at(1, 0), seq=across)
    low_top = low_copy(1, low_at(0, 0), low_at(0, up), tp=flip(top))
    low_far = low_copy(2, low_at(1, 0), low_at(1, up), tp=flip(top))

    def low_bit(bit):
        base = 3 + sum(tp >> b for b in range(bit + 1, top))
        return [
            low_copy(base + k, low_at(d, j), low_at(d, j | 1 << bit), tp=flip(bit))
            for k, (d, j) in enumerate(
                (d, j) for d in range(2) for j in range(0, tp, 2 << bit)
            )
        ]

    def second_norm():
        side_finish(0)
        for k in (10, *plain):
            load(k).wait()
        R["gain_rows"][...] = jnp.zeros_like(R["gain_rows"])

        def body(r):
            d_a = side_sum(r)
            n_two, inverse = normed(R["resid_in"][r, :])
            R["gain_rows"][1:2, :] += jnp.sum(d_a * n_two, axis=0, keepdims=True)
            e = d_a * R["gain_two"][...]
            d_resid = R["cot_in"][r, :].astype(F32) * R["scale"][r, :] + inverse * (
                e - n_two * jnp.mean(e * n_two, axis=-1, keepdims=True)
            )
            R["d_resid"][r, :] = d_resid
            low[r, :] = d_resid.astype(BF)

        strips(share, ROWS_AT_ONCE, body)
        low_side.start()
        low_top.start()

    lane = lax.broadcasted_iota(jnp.int32, (span, 2 * HD), 1)

    def attended_back():
        for k in (0, 6):
            load(k).wait()
        R["d_kv"][...] = jnp.zeros_like(R["d_kv"])
        R["d_q"][...] = jnp.zeros_like(R["d_q"])
        @pl.loop(0, 2)
        def _(d):
            value = lax.dot_general(
                low[pl.ds(pl.multiple_of(d * tp * share, tp * share), tp * share), :],
                R["w_rows"][...],
                nt,
                preferred_element_type=F32,
            ).astype(BF)
            for j in range(tp):
                at = pl.ds(pl.multiple_of((d * tp + block_of(j)) * share, share), share)
                R["d_att"][at, :] = value[j * share : (j + 1) * share]

        ones = jnp.ones((8, 2 * HD), F32)
        pairs = heads // 2

        @pl.loop(0, 2 * n_rows * pairs)
        def _(n):
            d, r, h = n // (n_rows * pairs), n // pairs % n_rows, n % pairs
            cols = pl.ds(pl.multiple_of(h * 2 * HD, 2 * HD), 2 * HD)
            rows = pl.ds(pl.multiple_of(r * span, span), span)
            at = pl.ds(pl.multiple_of(d * span, span), span)
            d_rows = pl.ds(pl.multiple_of((d * n_rows + r) * span, span), span)
            for k in range(2):
                grads = R["d_att"][d_rows, cols].astype(F32)
                values = R["att_in"][d, rows, cols].astype(F32)
                if k == 0:
                    grads = pltpu.roll(grads, HD, 1)
                    values = pltpu.roll(values, HD, 1)
                grads = jnp.where(lane < HD, 0.0, grads)
                i = r * heads + 2 * h + k
                R["d_out"][i, at, :] = grads.astype(BF)
                R["delta"][i, :, at] = lax.dot_general(
                    ones,
                    grads * values,
                    nt,
                    precision=lax.Precision.HIGHEST,
                    preferred_element_type=F32,
                )

    def put_folded(ref, c, value):
        rows, cols = value.shape
        at = pl.ds(pl.multiple_of(c // ref.shape[1] * rows, rows), rows)
        ref[at, pl.ds(pl.multiple_of(c % ref.shape[1], cols), cols)] = value.astype(BF)

    def out_gradient():
        chunk = width // 2

        @pl.loop(0, 2 * tp)
        def _(n):
            R["d_att"][pl.ds(pl.multiple_of(n * share, share), share), :] = R["att_in"][
                n // tp, block_rows(n % tp), :
            ]

        @pl.loop(0, width // chunk)
        def _(n):
            c = pl.multiple_of(n * chunk, chunk)
            value = lax.dot_general(
                R["d_att"][...], low[:, pl.ds(c, chunk)], tn, preferred_element_type=F32
            )
            put_folded(R["out_part"], c, value)

    def attention_block(piece, i, diagonal):
        r = i // heads
        kv = R["kv_all"][piece, r, 0]
        q, d_out = R["q_in"][i], R["d_out"][i]
        scores = lax.dot_general(kv, q, nt, preferred_element_type=F32)
        probs = jnp.exp2(scores * (HD**-0.5 * 1.4426950408889634) - R["log_in"][i])
        if diagonal:
            k_at = lax.broadcasted_iota(jnp.int32, (wide, wide), 0)
            q_at = lax.broadcasted_iota(jnp.int32, (wide, wide), 1)
            q_at = jnp.where(q_at < span, q_at + span * side, q_at - span * side)
            k_at = jnp.where(k_at < span, k_at + span * side, k_at - span * side)
            probs = jnp.where(k_at <= q_at, probs, 0.0)
        d_probs = lax.dot_general(kv, d_out, nt, preferred_element_type=F32)
        d_scores = (probs * (d_probs - R["delta"][i, 0:1, :])).astype(BF)
        R["d_kv"][piece, r] += jnp.dot(d_scores, q, preferred_element_type=F32) + jnp.dot(
            probs.astype(BF), d_out, preferred_element_type=F32
        ) * (HD**0.5)
        R["d_q"][i] += lax.dot_general(
            kv, d_scores, (((0,), (0,)), ((), ())), preferred_element_type=F32
        )

    def kv_copy(step):
        return remote_copy(
            R["kv_back"].at[step - 1],
            R["kv_far"].at[step - 1],
            R["kv_send"].at[step - 1],
            R["kv_recv"].at[step - 1],
            seq=rank - 2 * step,
        )

    def kv_send():
        for step in range(1, nodes):

            @pl.when(node >= step)
            def _():
                R["kv_back"][step - 1] = R["d_kv"][step].astype(BF)
                kv_copy(step).start()

    def kv_sum():
        for step in range(1, nodes):

            @pl.when(node + step < nodes)
            def _():
                kv_copy(step).wait_recv()
                R["d_kv"][0] += R["kv_far"][step - 1].astype(F32)

            @pl.when(node >= step)
            def _():
                kv_copy(step).wait_send()

    def head_back(grads, raw, gain, at):
        lanes = 2 * HD
        low_lane = lane < HD // 2
        raw = jnp.where(lane < HD, raw, 0.0)
        swapped = jnp.where(
            low_lane, pltpu.roll(grads, lanes - HD // 2, 1), pltpu.roll(grads, HD // 2, 1)
        )
        rotated = grads * R["cos_in"][at, :] + swapped * R["sin_in"][at, :]
        inverse = lax.rsqrt(jnp.sum(raw * raw, axis=-1, keepdims=True) * (1.0 / HD) + EPS_HEAD)
        n = raw * inverse
        e = rotated * gain
        back = inverse * (e - n * (jnp.sum(e * n, axis=-1, keepdims=True) * (1.0 / HD)))
        return back, jnp.sum(rotated * n, axis=0, keepdims=True)

    def heads_back():
        scale = HD**-0.5
        pairs = heads // 2

        @pl.loop(0, 2 * n_rows)
        def _(n):
            r, d = n // 2, n % 2
            at = pl.ds(pl.multiple_of((d * n_rows + r) * span, span), span)
            here = pl.ds(pl.multiple_of(d * span, span), span)

            @pl.loop(0, pairs)
            def _(h):
                pair = []
                both_raw = R["raw_in"][at, pl.ds(pl.multiple_of(h * 2 * HD, 2 * HD), 2 * HD)].astype(F32)
                for k in range(2):
                    i = r * heads + 2 * h + k
                    grads = R["d_q"][i, :, here].T * scale
                    raw = both_raw if k == 0 else pltpu.roll(both_raw, HD, 1)
                    back, gain = head_back(grads, raw, R["gain_q"][...], at)
                    R["gain_rows"][2:3, 0 : 2 * HD] += gain
                    pair.append(back)
                R["d_raw"][at, pl.ds(pl.multiple_of(h * 2 * HD, 2 * HD), 2 * HD)] = jnp.where(
                    lane < HD, pair[0], pltpu.roll(pair[1], HD, 1)
                ).astype(BF)

            grads = R["d_kv"][0, r, here, :] * scale
            raw = R["raw_in"][at, heads * HD :].astype(F32)
            back, gain = head_back(grads, raw, R["gain_k"][...], at)
            R["gain_rows"][3:4, 0 : 2 * HD] += gain
            R["d_raw"][at, pl.ds(heads * HD, 2 * HD)] = jnp.where(lane < HD, back, grads).astype(
                BF
            )

    def raw_gradient():
        for k in (2, 11):
            load(k).wait()
        chunk = width // 2
        cut = heads * HD

        @pl.loop(0, width // chunk)
        def _(n):
            c = pl.multiple_of(n * chunk, chunk)
            value = lax.dot_general(
                R["d_raw"][...], R["a_in"][:, pl.ds(c, chunk)], tn, preferred_element_type=F32
            )
            put_folded(R["q_part"], c, value[:cut])
            put_folded(R["kv_part"], c, value[cut:])

    def first_part(low_n, high_n):
        inner = (heads + 2) * HD
        rel = R["hidden"]
        chunk = 512

        if low_n == 0:
            load(1).wait()
            load(12).wait()

            @pl.loop(0, 2 * tp)
            def _(n):
                rows = pl.multiple_of((n // tp * tp + block_of(n % tp)) * share, share)
                rel[pl.ds(pl.multiple_of(n * share, share), share), 0:inner] = R["d_raw"][
                    pl.ds(rows, share), :
                ]

        @pl.loop(low_n, high_n)
        def _(n):
            cols = pl.ds(pl.multiple_of(n * chunk, chunk), chunk)

            @pl.loop(0, 2)
            def _(d):
                at = pl.ds(pl.multiple_of(d * tp * share, tp * share), tp * share)
                value = lax.dot_general(
                    rel[at, 0:inner], R["a_t"][cols, 0:inner], nt, preferred_element_type=F32
                ).astype(BF)
                for j in range(tp):
                    rows = pl.ds(
                        pl.multiple_of((d * (tp // 2) + j // 2) * share, share), share
                    )
                    (temp if j % 2 else hold)[rows, cols] = value[j * share : (j + 1) * share]

    def out_end():
        side_finish(1)

        def body(r):
            R["fresh"][0, r, :] = (R["resid_in"][r, :] + side_sum(r)).astype(BF)

        strips(share, ROWS_AT_ONCE, body)
        tokens_put(0).start()
        tokens_start(0, top)

    def first_norm():
        side_finish(2)

        def body(r):
            d_a = side_sum(r)
            n_one, inverse = normed(R["x_in"][r, :].astype(F32))
            R["gain_rows"][0:1, :] += jnp.sum(d_a * n_one, axis=0, keepdims=True)
            e = d_a * R["gain_one"][...]
            d_x = R["d_resid"][r, :] + inverse * (
                e - n_one * jnp.mean(e * n_one, axis=-1, keepdims=True)
            )
            R["fresh"][1, r, :] = d_x.astype(BF)

        strips(share, ROWS_AT_ONCE, body)
        tokens_put(1).start()
        tokens_start(1, top)
        part = width // tp
        for k in range(tp):
            R["gain_box"][k] = jnp.zeros((8, part), F32)
            R["gain_box"][k, 0:2, :] = R["gain_rows"][0:2, k * part : (k + 1) * part]
            R["gain_box"][k, 2:4, 0 : 2 * HD] = R["gain_rows"][2:4, 0 : 2 * HD]

        @pl.loop(1, total)
        def _(k):
            other = (me + k) % total
            remote_copy(
                R["gain_box"].at[other % tp],
                R["gain_all"].at[k],
                R["gain_send"].at[k],
                R["gain_recv"].at[k],
                seq=other // tp,
                tp=other % tp,
            ).start()

        R["gain_all"][0] = R["gain_box"][t]

    def gains_end():
        @pl.loop(1, total)
        def _(k):
            remote_copy(
                R["gain_box"].at[0],
                R["gain_all"].at[k],
                R["gain_send"].at[k],
                R["gain_recv"].at[k],
                seq=rank,
                tp=t,
            ).wait()

        R["gains"][...] = jnp.zeros_like(R["gains"])

        @pl.loop(0, total)
        def _(k):
            R["gains"][...] += R["gain_all"][k]

    tasks = {}

    def task(step, *acts):
        tasks.setdefault(step, []).extend(acts)
        return step

    def sums_tasks(n, step):
        for bit in range(bits):
            step += 2 if bit == 0 else 5
            following = (
                (lambda bit=bit: sum_start(n, bit + 1)) if bit < top else (lambda: side_start(n))
            )
            task(step, lambda bit=bit: sum_add(n, bit), following)
        return step + 5

    def token_tasks(n, step):
        for bit in reversed(range(bits)):
            step += 3
            task(step, lambda bit=bit: tokens_wait(n, bit))
            if bit:
                task(step, lambda bit=bit: tokens_start(n, bit - 1))
        task(step, lambda: tokens_put(n).wait())
        return step

    n_rows_w = width // pcol
    first_move = 1
    halves = 2 * chunks - 1
    task(0, begin)
    step = halves
    task(step, lambda: start_all(row_loads(0)), lambda: start_all(row_loads(1)))
    for k in range(4):
        step = task(
            halves + k, lambda k=k: second_part(n_rows_w * k // 4, n_rows_w * (k + 1) // 4)
        )
    task(step, lambda: sum_start(0, 0))
    task(step, lambda: start_all(down_loads(0)), lambda: start_all(down_loads(1)))
    grads_at = step + 1
    grads_end = grads_at + 2 * (chunks - 1)
    assert grads_at + 1 < first_move + per_chunk // 2
    task(grads_end, load(1).start, load(2).start, load(11).start, load(12).start)
    step = task(sums_tasks(0, step), second_norm)
    task(max(step, grads_end) + 1, lambda: ffn_part(0, n_rows_w // 2))
    ffn_at = task(
        max(step, grads_end) + 2,
        lambda: ffn_part(n_rows_w // 2, n_rows_w),
        lambda: sum_start(1, 0),
    )
    step = task(step + 4, low_side.wait, low_top.wait, low_far.start)
    step += 3
    task(step, low_far.wait)
    for bit in reversed(range(top)):
        task(step, lambda bit=bit: [c.start() for c in low_bit(bit)])
        step += 2
        task(step, lambda bit=bit: [c.wait() for c in low_bit(bit)])
    task(step, attended_back)
    ffn_end = task(sums_tasks(1, ffn_at), out_end)
    token_tasks(0, ffn_end)
    step = task(step + 1, *[load(k).wait for k in (3, 4, 5, 7)])
    first_block = step
    per_step = 4
    step += -(-(nodes * n_q) // per_step)
    last_block = step
    task(step, kv_send)
    task(step + 2, out_gradient)
    step = task(step + 5, kv_sum, heads_back)
    step = task(step + 1, raw_gradient)
    raw_ready = step
    assert raw_ready > ffn_end
    task(step + 1, lambda: first_part(0, width // 1024))
    step = task(
        step + 2, lambda: first_part(width // 1024, width // 512), lambda: sum_start(2, 0)
    )
    step = task(sums_tasks(2, step), first_norm)
    task(token_tasks(1, step), gains_end)

    late = half - (R["q_part"].shape[1] + R["kv_part"].shape[1]) // pcol // 2
    late_end = late + R["q_part"].shape[1] // pcol // 2
    gap = max(0, raw_ready + 1 - late - first_move)
    steps = max(first_move + half + gap + 2 * LAG * last, max(tasks) + 1)

    @pl.loop(0, steps)
    def _(i):
        for b in range(2):
            stream(b, i - first_move)
        for at, acts in sorted(tasks.items()):

            @pl.when(i == at)
            def _(acts=acts):
                for act in acts:
                    act()

        @pl.when(i < halves)
        def _():
            c = (i + 1) // 2

            @pl.when((i == 0) | (i % 2 == 1))
            def _():
                chunk_ready(c)

            @pl.loop(jnp.where((i == 0) | (i % 2 == 1), 0, 1), jnp.where(i % 2 == 1, 1, 2))
            def _(m):
                chunk_forward(c, pl.ds(pl.multiple_of(m * (both // 2), both // 2), both // 2))

            @pl.when(i % 2 == 0)
            def _():
                chunk_next(c)

        pl.when(i == 0)(turn)
        g = i - grads_at
        c = jnp.where(i < 3, 0, g // 2 + 1)
        within = (g >= 0) & (i < grads_end)

        @pl.when((i < 2) | (within & (g % 2 == 0)))
        def _():
            chunk_gradients(c, jnp.where(i == 1, 1, 0), jnp.where(i == 0, 1, 2))

        @pl.when((i == 2) | (within & (g % 2 == 1)))
        def _():
            chunk_down(c)
            stage_copies(c)[2].wait()

        @pl.when((i >= first_block) & (i < last_block))
        def _():
            @pl.loop(0, per_step)
            def _(k):
                n = (i - first_block) * per_step + k
                piece = n // n_q

                @pl.when(n < n_q)
                def _():
                    attention_block(0, n, True)

                @pl.when((n >= n_q) & (n < n_q * nodes) & (node >= piece))
                def _():
                    attention_block(piece, n % n_q, False)

    @pl.loop(0, half)
    def _(j):
        for b in range(2):
            v = node if b == 0 else last - node
            probe = red.at[b, 0]

            @pl.when(v == 0)
            def _():
                along(probe, probe, red_sems, b, j, rank).wait_send()

            @pl.when((v > 0) & ((v < last) | (j >= half - KEPT)))
            def _():
                along(probe, probe, fin_sems, b, j, rank).wait_send()

            @pl.when((v == last) & (j >= half - KEPT))
            def _():
                pltpu.make_async_copy(probe, probe, put_sem.at[b, j]).wait()

            @pl.when(crosses(j) & ((v < last) | (j >= half - KEPT)))
            def _():
                along(probe, probe, x_sems, b, j, rank).wait_send()

            @pl.when(crosses(j))
            def _():
                along(probe, probe, x_sems, b, j, rank).wait_recv()


def backward(nodes, bits, ident, values):
    tp, seq = 1 << bits, 2 * nodes
    share, width = values["resid"].shape
    ff = values["w_gate"].shape[1] // 2
    n_q, wide, _ = values["q"].shape
    n_rows = values["kv"].shape[0]
    heads = n_q // n_rows
    tokens = tp * share
    piece = 256
    cols = (heads + 2) * HD
    small = [(piece, r * width // piece) for r in (heads * HD, heads * HD, 2 * HD)]
    shapes = [(width, 2 * ff), (width, 2 * ff), (2 * ff, width)]
    shapes += [(2 * small[0][0], small[0][1]), small[1], (2 * small[2][0], small[2][1])]
    half = (3 * width * ff + sum(r * c for r, c in small)) // (2 * piece * piece)
    slots = 2 * LAG * (nodes - 1) + 8
    vmem = pl.BlockSpec(memory_space=pltpu.VMEM)
    anywhere = pl.BlockSpec(memory_space=pl.ANY)
    dma = pltpu.SemaphoreType.DMA
    inside = ("scale", "gain_two", "gain_one", "gain_q", "gain_k")
    kv = values["kv"].shape
    total = seq * tp
    messages = 3 + 2 * (tp - 2)
    outs = shapes + [(tp, share, width)] * 2 + [(8, width // tp)]
    outs += [(2 * tp - 1, share, width)] * 3 + [(width, ff), (width, ff), (ff, width)]
    scratch = [
        (2, slots, piece, piece),
        (2, AHEAD, piece, piece),
        (tokens, width),
        (tokens, width),
        (2 * tokens, width),
        (2 * tokens, width),
        (width, 2 * tokens),
        (heads * HD, width),
        (n_q, wide, 2 * HD),
        (n_q, wide, 2 * HD),
        (n_q, 2 * HD, wide, F32),
        (nodes, n_rows, wide, 2 * HD, F32),
        (nodes,) + kv,
        (2, tokens, heads * HD),
        (2 * tokens, heads * HD),
        (n_q, 8, wide, F32),
        (2 * tokens, cols),
        small[1],
        small[2],
        small[0],
        (nodes - 1, n_rows, wide, 2 * HD),
        (nodes - 1, n_rows, wide, 2 * HD),
        (share, width, F32),
        (2, share, width),
        (8, width, F32),
        (tp, 8, width // tp, F32),
        (total, 8, width // tp, F32),
        (n_q, 1, wide, F32),
        (share, width),
        (share, width, F32),
        (2 * tokens, cols),
        (2 * tokens, 2 * HD, F32),
        (2 * tokens, 2 * HD, F32),
        (share, width),
        (2 * tokens, ff),
        (2, 2 * tokens, ff),
        (2, 2, piece, ff),
        (2, 2, width, piece),
        (2, width, piece),
        (piece, width),
    ]
    sems = [(2, AHEAD)] + [(2, half)] * 7 + [(18 + tp,), (3, 2 * tp - 1), (3, 2 * tp - 1)]
    sems += [(2, tp // 2), (messages,), (messages,), (nodes - 1,), (nodes - 1,)]
    sems += [(2, tp - 1), (2, tp - 1), (2,), (total,), (total,), (2, 3), (3,)]
    return pl.pallas_call(
        functools.partial(backward_kernel, nodes, bits),
        out_shape=[
            jax.ShapeDtypeStruct(shape, F32 if k == 8 else BF) for k, shape in enumerate(outs)
        ],
        in_specs=[vmem if k in inside else anywhere for k in values],
        out_specs=[vmem if k == 8 else anywhere for k in range(len(outs))],
        scratch_shapes=[
            pltpu.VMEM(s[:-1], F32) if s[-1] is F32 else pltpu.VMEM(s, BF) for s in scratch
        ]
        + [dma(s) for s in sems],
        compiler_params=pltpu.CompilerParams(
            collective_id=ident, has_side_effects=True, vmem_limit_bytes=62 << 20
        ),
        cost_estimate=pl.CostEstimate(
            flops=0, bytes_accessed=1 << 30, transcendentals=0
        ),
        name="backward",
    )(*values.values())[:9]


def widen(arrays):
    block = arrays[-1].shape[0]
    for array in arrays:
        block = min(block, array.shape[0])
    counts = [array.shape[0] // block for array in arrays]
    starts = [sum(counts[:k]) for k in range(len(arrays))]
    width = arrays[0].shape[1]

    def kernel(*refs):
        step = pl.program_id(0)
        for k, (start, size) in enumerate(zip(starts, counts)):

            @pl.when((step >= start) & (step < start + size))
            def _(k=k):
                refs[len(arrays) + k][...] = refs[k][...].astype(F32)

    specs = [
        pl.BlockSpec(
            (block, width), lambda i, start=start, size=size: (jnp.clip(i - start, 0, size - 1), 0)
        )
        for start, size in zip(starts, counts)
    ]
    return pl.pallas_call(
        kernel,
        grid=(sum(counts),),
        out_shape=[jax.ShapeDtypeStruct(a.shape, F32) for a in arrays],
        in_specs=specs,
        out_specs=specs,
        compiler_params=pltpu.CompilerParams(vmem_limit_bytes=56 << 20),
        cost_estimate=pl.CostEstimate(
            flops=0, bytes_accessed=6 * block * width * sum(counts), transcendentals=0
        ),
        name="widen",
    )(*arrays)


def turn_heads(mine, other, kv, q_cols, shared, width):
    side = (lax.axis_index("seq") % 2).reshape(1).astype(jnp.int32)
    chunk = 256

    def kernel(side_ref, mine_ref, other_ref, kv_ref, q_out, k_out, v_out):
        first = side_ref[0] == 0
        per = mine_ref.shape[1] // chunk
        lane = lax.broadcasted_iota(jnp.int32, (chunk, 2 * HD), 1)

        @pl.loop(0, width // chunk)
        def _(n):
            rows = pl.ds(pl.multiple_of(n * chunk, chunk), chunk)
            at = pl.ds(pl.multiple_of(n // per * q_cols, q_cols), q_cols)
            cols = pl.ds(pl.multiple_of(n % per * chunk, chunk), chunk)
            own = mine_ref[at, cols].astype(F32).T
            far = other_ref[at, cols].astype(F32).T
            q_out[rows, 0:q_cols] = jnp.where(first, own, far)
            q_out[rows, q_cols:] = jnp.where(first, far, own)

        height = 2 * HD
        per_kv = kv_ref.shape[1] // chunk
        stack = kv_ref.shape[0] // 2

        @pl.loop(0, width // chunk)
        def _(n):
            rows = pl.ds(pl.multiple_of(n * chunk, chunk), chunk)
            cols = pl.ds(pl.multiple_of(n % per_kv * chunk, chunk), chunk)
            pair = [
                kv_ref[
                    pl.ds(pl.multiple_of(s * stack + n // per_kv * height, height), height), cols
                ]
                .astype(F32)
                .T
                for s in range(2)
            ]
            if shared:
                both = pair[0] + pair[1]
                k_out[rows, :] = both[:, :HD]
                v_out[rows, :] = both[:, HD:]
            else:
                k_out[rows, :] = jnp.where(lane < HD, pair[0], pltpu.roll(pair[1], HD, 1))
                v_out[rows, :] = jnp.where(lane < HD, pltpu.roll(pair[0], HD, 1), pair[1])

    vmem = pl.BlockSpec(memory_space=pltpu.VMEM)
    k_cols = HD if shared else 2 * HD
    return pl.pallas_call(
        kernel,
        out_shape=[
            jax.ShapeDtypeStruct((width, c), F32) for c in (2 * q_cols, k_cols, k_cols)
        ],
        in_specs=[pl.BlockSpec(memory_space=pltpu.SMEM)] + [vmem] * 3,
        out_specs=[vmem] * 3,
        compiler_params=pltpu.CompilerParams(vmem_limit_bytes=40 << 20),
        name="turn_heads",
    )(side, mine, other, kv)


def per_device(
    tokens,
    positions,
    corpus,
    corpus_weight,
    gain_one,
    w_query,
    w_key,
    w_value,
    gain_query,
    gain_key,
    w_out,
    gain_two,
    w_gate,
    w_up,
    w_down,
    cotangent,
):
    net = Links()
    rows, per_row, width = tokens.shape
    count = rows * per_row
    share = count // net.tp
    total_len = per_row * net.seq
    side, node, t = net.side, net.node, net.t
    q_cols = w_query.shape[1] // 2
    shared = (w_key.shape[1] // HD) % 2 == 1
    k_cols = w_key.shape[1] if shared else w_key.shape[1] // 2
    both = 2 * count

    def lanes(v):
        return jnp.pad(v, [(0, 0)] * (v.ndim - 1) + [(0, 2 * HD - v.shape[-1])])

    pos_own = positions.reshape(count)
    corpus_own = corpus.reshape(count)
    told = net.swap_side(jnp.stack([pos_own, corpus_own]))
    cosine, sine = rope_tables(jnp.concatenate([pos_own, told[0]]))
    cosine = lanes(jnp.concatenate([cosine, cosine], axis=1))
    sine = lanes(jnp.concatenate([sine, -sine], axis=1))
    onehot = (corpus_own[:, None] == jnp.arange(NCORP, dtype=jnp.int32)).astype(F32)
    own_counts = jnp.zeros((8, 128), F32).at[0, :NCORP].set(jnp.sum(onehot, axis=0))
    token_rows = tokens.reshape(count, width)
    cot_rows = cotangent.reshape(count, width)
    head_gains = lanes(jnp.stack([gain_query, gain_key]))
    gain_q, gain_k = head_gains[0:1], head_gains[1:2]

    assert k_cols == HD

    q, kv, raw, a_one, att, log, all_counts, cot_other, resid, a_two, kv_in, a_other, w_kv = attend(
        net.nodes,
        net.bits,
        2,
        dict(
            tokens=token_rows,
            w_query=w_query,
            w_key=w_key,
            w_value=w_value,
            w_out=w_out,
            cot=cot_rows,
            gain_one=gain_one[None],
            gain_two=gain_two[None],
            gain_q=gain_q,
            gain_k=gain_k,
            cosine=cosine,
            sine=sine,
            count=own_counts,
            rows=rows,
        ),
    )
    a_two = a_two.reshape(both, width)

    counts = jnp.sum(all_counts, axis=0)[0, :NCORP]
    weight_scale = corpus_weight.astype(F32) * (rows * total_len / NCORP) / counts
    corpus_other = told[1]
    onehot_other = (corpus_other[:, None] == jnp.arange(NCORP, dtype=jnp.int32)).astype(F32)
    scale_own = jnp.sum(onehot * weight_scale, axis=-1, keepdims=True)
    scale_other = jnp.sum(onehot_other * weight_scale, axis=-1, keepdims=True)
    scale_both = jnp.concatenate([net.relative(scale_own), net.relative(scale_other)], axis=0)

    sums = backward(
        net.nodes,
        net.bits,
        3,
        dict(
            a_two=a_two,
            cot=cot_rows,
            cot_far=cot_other.reshape(count, width),
            scale=scale_both,
            w_gate=w_gate,
            w_up=w_up,
            w_down=w_down,
            resid=resid,
            tokens_in=token_rows,
            gain_two=gain_two[None],
            gain_one=gain_one[None],
            gain_q=gain_q,
            gain_k=gain_k,
            w_out=w_out,
            w_query=w_query,
            w_kv=w_kv,
            a_one=a_one,
            a_other=a_other,
            q=q,
            kv=kv,
            kv_in=kv_in,
            att=att,
            log=log,
            raw=raw,
            cosine=cosine,
            sine=sine,
        ),
    )
    q_other = net.swap_side(sums[4])
    fold = width // sums[3].shape[1]
    grad_out = sums[3].reshape(2, fold, q_cols, -1).transpose(0, 2, 1, 3).reshape(2 * q_cols, width)
    grad_gate, grad_up, grad_down, grad_out = widen([*sums[:3], grad_out])
    grad_query, grad_key, grad_value = turn_heads(
        sums[4], q_other, sums[5], q_cols, shared, width
    )
    out, d_tokens = (v.reshape(rows, per_row, width) for v in sums[6:8])
    gains = sums[8]

    head_share = HD // net.tp

    return (
        out,
        d_tokens,
        gains[0],
        grad_query,
        grad_key,
        grad_value,
        take(gains[2], t * head_share, head_share),
        take(gains[3], t * head_share, head_share),
        grad_out,
        gains[1],
        grad_gate,
        grad_up,
        grad_down,
    )


def solution(mesh):
    placed = (
        P(None, "seq", None),
        P(None, "seq"),
        P(None, "seq"),
        P(),
        P(),
        P(None, "tp"),
        P(None, "tp"),
        P(None, "tp"),
        P(),
        P(),
        P("tp", None),
        P(),
        P(None, "tp"),
        P(None, "tp"),
        P("tp", None),
        P(None, "seq", None),
    )
    return jax.shard_map(
        per_device,
        mesh=mesh,
        in_specs=placed,
        out_specs=(
            P(None, "seq", None),
            P(None, "seq", None),
            P("tp"),
            P(None, "tp"),
            P(None, "tp"),
            P(None, "tp"),
            P("tp"),
            P("tp"),
            P("tp", None),
            P("tp"),
            P(None, "tp"),
            P(None, "tp"),
            P("tp", None),
        ),
        check_vma=False,
    )
```
